32 devices in a mesh: ep: 4 (over y, x), dp: 4 (over z), fs: 2 (over core).
Axes of the slice: x: 2, y: 2, z: 4, core: 2. Of those that a mesh axis runs over, the one named last changes fastest.
Arguments:
- tokens: bfloat16 [16, 1024, 768], P(('dp', 'fs'), 'ep'), may hold values from -6 to 6
- prev_logits: float32 [16, 1024, 6], P(('dp', 'fs'), 'ep'), may hold values from -3 to 3
- segments: int32 [16, 1024], P(('dp', 'fs')), may hold values from 0 to 3, never falling along the last dimension, each value on 1 to 512 neighbouring positions
- routes: int32 [16, 1024, 2], P(('dp', 'fs'), 'ep'), may hold values from 0 to 5, all different within a row; in each aligned block of 256 rows (0 to 255, 256 to 511, ..., all dimensions but the last counted through in order) at most 128 rows name the same one
- cotangent: bfloat16 [16, 1024, 768], P(('dp', 'fs'), 'ep'), may hold values from -6 to 6
- gain_attn: bfloat16 [768], P('fs'), may hold values from 0.5 to 1.5
- w_qkv: bfloat16 [768, 2304], P('fs'), may hold values from -0.21875 to 0.21875
- w_out: bfloat16 [768, 768], P('fs'), may hold values from -0.625 to 0.625
- gain_moe: bfloat16 [768], P('fs'), may hold values from 0.5 to 1.5
- w_router: bfloat16 [768, 6], P('fs'), may hold values from -0.15625 to 0.15625
- const_proj: bfloat16 [768, 4], P('fs'), may hold values from -0.21875 to 0.21875
- const_vec: bfloat16 [768, 2], P('fs'), may hold values from -24 to 24
- w_gate: bfloat16 [4, 768, 1024], P('ep', 'fs'), may hold values from -0.21875 to 0.21875
- w_up: bfloat16 [4, 768, 1024], P('ep', 'fs'), may hold values from -0.21875 to 0.21875
- w_down: bfloat16 [4, 1024, 768], P('ep', 'fs'), may hold values from -0.75 to 0.75
Outputs:
- block_out: bfloat16 [16, 1024, 768], P(('dp', 'fs'), 'ep')
- grad_tokens: float32 [16, 1024, 768], P(('dp', 'fs'), 'ep')
- grad_prev: float32 [16, 1024, 6], P(('dp', 'fs'), 'ep')
- grad_gain_attn: float32 [768], P(('ep', 'dp', 'fs'))
- grad_w_qkv: float32 [768, 2304], P(('ep', 'dp', 'fs'))
- grad_w_out: float32 [768, 768], P(('ep', 'dp', 'fs'))
- grad_gain_moe: float32 [768], P(('ep', 'dp', 'fs'))
- grad_w_router: float32 [768, 6], P(('ep', 'dp', 'fs'))
- grad_const_proj: float32 [768, 4], P(('ep', 'dp', 'fs'))
- grad_const_vec: float32 [768, 2], P(('ep', 'dp', 'fs'))
- grad_w_gate: float32 [4, 768, 1024], P('ep', ('dp', 'fs'))
- grad_w_up: float32 [4, 768, 1024], P('ep', ('dp', 'fs'))
- grad_w_down: float32 [4, 1024, 768], P('ep', ('dp', 'fs'))
The draws below stay inside these ranges and needn't reach their ends.
Inputs may be any that keep to these rules, and one draw needn't show every extreme that they name: `routes`: each token names two different route numbers. In each aligned block of 256 tokens of a sequence, no route number is named more than 128 times, a bound that some block reaches. `segments`: along a sequence segment numbers never fall; each of the 4 numbers occurs, no segment is longer than half of 1024 tokens, and one is exactly that long.
All inputs are finite; a program needn't handle non-finite values.
Results may differ from the reference program's by a relative error of at most 0.015.
Values may be sent and summed in bfloat16 or wider, within the bound.
A program may use at most 256 MiB of HBM per device.

```python
import math
import jax
import jax.numpy as jnp
import numpy as np
from jax import lax

D = 768
HEADS = 12
HEAD = 64
FF = 2048
HSPLIT = 2
SEGS = 4
LEN = 1024
EXPERTS = 2
NROUTE = 6
OWNERS = 4
HALF = 1024
TOK_DEV = 256
CAP = 128
SEQS = 16


def block_levels(key, shape, shards, least, high):
    loudness = 1.0
    for dim, shards_of in shards:
        steps = jax.random.uniform(jax.random.fold_in(jax.random.fold_in(key, 6), dim), (shards_of,), jnp.float32, least / len(shards), high / len(shards))
        loudness = loudness * jnp.repeat(jnp.exp(steps), shape[dim] // shards_of).reshape((-1,) + (1,) * (len(shape) - 1 - dim))
    return loudness


def length_profile(count, total, bound, slope):
    portions = [(1 << 20) // math.isqrt(standing ** slope) + 1 for standing in range(2, count + 1)]
    rest, holding = total - bound - (count - 1), [1] * (count - 1)
    while rest > 0:
        free = [i for i in range(count - 1) if holding[i] < bound]
        pool, left = sum([portions[i] for i in free]), rest
        for i in free:
            extra = min(bound - holding[i], max(1, left * portions[i] // pool), rest)
            holding[i] = holding[i] + extra
            rest = rest - extra
    return np.array([bound] + holding)


def uneven_parts(key, number_of, total, bound, skew):
    if number_of == 2:
        one = jax.random.randint(key, (), max(1, total - bound), min(bound, total - 1) + 1)
        return jnp.stack([one, total - one])
    tallies = jnp.asarray(length_profile(number_of, total, bound, skew), jnp.int32)
    couples = (number_of - 1) // 2
    donor, sink = tallies[1:1 + 2 * couples:2], tallies[2:2 + 2 * couples:2]
    margin = jnp.minimum(donor - 1, bound - sink)
    moved = jax.random.randint(jax.random.fold_in(key, 1), (couples,), 0, 1 << 20) % (margin + 1)
    tallies = tallies.at[1:1 + 2 * couples:2].set(donor - moved).at[2:2 + 2 * couples:2].set(sink + moved)
    return tallies[jax.random.permutation(jax.random.fold_in(key, 2), number_of)]


def shared_out(own_key, own, number, rows, count, top, reach, skew):
    order = jax.random.permutation(own_key, count)
    crowded, ordinary = portions_of(count, rows * top, reach, skew, True), portions_of(count, rows * top, reach, skew, False)
    places = jnp.arange(count)

    def named(tallies, turn):
        used = int((tallies > 0).sum())
        fixed = max(1, used // 4)
        moved = fixed + (places - fixed + turn * (used - fixed)) % max(1, count - fixed)
        return jnp.zeros((count,), jnp.int32).at[order[jnp.where(places < fixed, places, moved)]].set(jnp.asarray(tallies, jnp.int32))

    tallies = jnp.where(number % 4 == 0, named(crowded, number // 4), named(ordinary, number - number // 4 - 1))
    mixed = jax.random.permutation(jax.random.fold_in(own, 3), count)
    donor, receiver = mixed[0:count // 2 * 2:2], mixed[1:count // 2 * 2:2]
    margin = jnp.minimum(tallies[donor] - 1, reach - tallies[receiver]) // 2
    margin = jnp.where((donor == order[0]) | (receiver == order[0]) | (tallies[receiver] == 0), 0, jnp.maximum(margin, 0))
    moved = jax.random.randint(jax.random.fold_in(own, 4), (count // 2,), 0, 1 << 20) % (margin + 1)
    tallies = tallies.at[donor].add(-moved).at[receiver].add(moved)
    labels = jnp.searchsorted(jnp.cumsum(tallies), jnp.arange(rows * top), side="right").astype(jnp.int32)
    listing = labels.reshape(top, rows).T
    listing = listing[jax.random.permutation(jax.random.fold_in(own, 1), rows)]
    turn = jax.random.randint(jax.random.fold_in(own, 2), (rows, 1), 0, top)
    return jnp.take_along_axis(listing, (jnp.arange(top)[None, :] + turn) % top, axis=1)


def portions_of(amount, total, most, slope, full):
    weights = [(1 << 20) // math.isqrt(grade ** slope) + 1 for grade in range(1, amount + 1)]
    largest = most if full else min(most, max(-(-total // amount), total * weights[0] // sum(weights)))
    least = 1 if total - largest >= amount - 1 else 0
    counts, surplus = [largest] + [least] * (amount - 1), total - largest - least * (amount - 1)
    while surplus > 0:
        candidates = [i for i in range(1, amount) if counts[i] < largest] or [i for i in range(1, amount) if counts[i] < most]
        whole, left = sum([weights[i] for i in candidates]), surplus
        for i in candidates:
            addition = min(most - counts[i], max(1, left * weights[i] // whole), surplus)
            counts[i] = counts[i] + addition
            surplus = surplus - addition
    return np.array(counts)


def bell_draw(rng, dims, deviation, limit, shards=(), kind=jnp.bfloat16):
    loudness = block_levels(rng, dims, shards, -0.22, 0.18) if shards else 1.0
    array = jax.random.normal(rng, dims, jnp.float32) * deviation * loudness
    return jnp.minimum(jnp.maximum(array, -limit), limit).astype(kind)


def setup_inputs(seed: int = 0) -> dict:
    keys = jax.random.split(jax.random.key(seed), 16)
    tokens = bell_draw(keys[0], (SEQS, LEN, D), 1.0, 6.0, ((0, 8), (1, 4)))
    prev_logits = bell_draw(keys[1], (SEQS, LEN, NROUTE), 0.5, 3.0, ((0, 8), (1, 4)), jnp.float32)
    segments = jax.vmap(lambda own: jnp.searchsorted(jnp.cumsum(uneven_parts(own, SEGS, LEN, LEN // 2, 2)), jnp.arange(LEN), side="right"))(jax.random.split(keys[2], SEQS)).reshape((SEQS, LEN)).astype(jnp.int32)
    routes_keys = jax.random.split(jax.random.fold_in(keys[3], 1), SEQS * LEN // TOK_DEV)
    routes_turns = jax.random.permutation(jax.random.fold_in(keys[3], 3), SEQS * LEN // TOK_DEV)
    routes = jax.vmap(lambda own, number: shared_out(jax.random.fold_in(keys[3], 2), own, number, TOK_DEV, NROUTE, 2, CAP, 1))(routes_keys, routes_turns).reshape((SEQS, LEN, 2))
    cotangent = bell_draw(keys[4], (SEQS, LEN, D), 1.0, 6.0, ((0, 8), (1, 4)))
    gain_attn = jnp.clip(1.0 + 0.1 * jax.random.normal(keys[5], (D,), jnp.float32), 0.5, 1.5).astype(jnp.bfloat16)
    w_qkv = bell_draw(keys[6], (D, 3 * D), D ** -0.5, 0.21875, ((0, 2),))
    w_out = bell_draw(keys[7], (D, D), (D // 8) ** -0.5, 0.625, ((0, 2),))
    gain_moe = jnp.clip(1.0 + 0.1 * jax.random.normal(keys[8], (D,), jnp.float32), 0.5, 1.5).astype(jnp.bfloat16)
    w_router = bell_draw(keys[9], (D, NROUTE), (2 * D) ** -0.5, 0.15625, ((0, 2),))
    const_proj = bell_draw(keys[10], (D, 4), D ** -0.5, 0.21875, ((0, 2),))
    const_vec = bell_draw(keys[11], (D, 2), 4.0, 24.0, ((0, 2),))
    w_gate = bell_draw(keys[12], (OWNERS, D, HALF), D ** -0.5, 0.21875, ((0, 4), (1, 2)))
    w_up = bell_draw(keys[13], (OWNERS, D, HALF), D ** -0.5, 0.21875, ((0, 4), (1, 2)))
    w_down = bell_draw(keys[14], (OWNERS, HALF, D), (FF // 32) ** -0.5, 0.75, ((0, 4), (1, 2)))
    return dict(tokens=tokens, prev_logits=prev_logits, segments=segments, routes=routes, cotangent=cotangent, gain_attn=gain_attn, w_qkv=w_qkv, w_out=w_out, gain_moe=gain_moe, w_router=w_router, const_proj=const_proj, const_vec=const_vec, w_gate=w_gate, w_up=w_up, w_down=w_down)


NORM_EPS = 1e-06
MASK_FILL = -1e+30
HIGHEST = lax.Precision.HIGHEST

@jax.custom_vjp
def low(v):
    return lax.optimization_barrier(v.astype(jnp.bfloat16)).astype(jnp.float32)

@jax.custom_vjp
def low_back(v):
    return v

def low_keep(v):
    return (low(v), None)

def low_pass(kept, grad):
    return (grad,)

def back_keep(v):
    return (v, None)

def back_low(kept, grad):
    return (low(grad),)
low.defvjp(low_keep, low_pass)
low_back.defvjp(back_keep, back_low)

def rms_scale(values, gains):
    inverse = lax.rsqrt(lax.optimization_barrier(jnp.mean(values * values, axis=-1, keepdims=True)) + NORM_EPS)
    return values * inverse * gains

def attend_block(query_block, pos_block, seg_block, key_heads, value_heads, seg_all, pos_all):
    scores = low_back(jnp.einsum('qhd,khd->hqk', query_block, key_heads, precision=HIGHEST) * 0.125)
    allowed = (seg_block[:, None] == seg_all[None, :]) & (pos_all[None, :] <= pos_block[:, None])
    scores = jnp.where(allowed[None], scores, MASK_FILL)
    largest = lax.optimization_barrier(jnp.max(scores, axis=-1, keepdims=True))
    powers = jnp.exp(scores - largest)
    weights = powers / lax.optimization_barrier(jnp.sum(powers, axis=-1, keepdims=True))
    return jnp.einsum('hqk,khd->qhd', low(weights), value_heads, precision=HIGHEST)

def expert_rows(mixed, route_row, gate_weight, up_weight, down_weight):
    seq_length = mixed.shape[0]
    block_count = seq_length // TOK_DEV
    pair_route = route_row.reshape(-1)
    expert_hit = (pair_route[:, None] == jnp.arange(EXPERTS, dtype=jnp.int32)[None, :]).astype(jnp.int32)
    per_block = expert_hit.reshape(block_count, 2 * TOK_DEV, EXPERTS)
    before = (jnp.cumsum(per_block, axis=1) - per_block).reshape(2 * seq_length, EXPERTS)
    slot_index = lax.optimization_barrier(jnp.sum(before * expert_hit, axis=1))
    expert_index = lax.optimization_barrier(jnp.sum(expert_hit * jnp.arange(EXPERTS, dtype=jnp.int32)[None, :], axis=1))
    ffn_used = lax.optimization_barrier(jnp.sum(expert_hit, axis=1))
    block_index = jnp.arange(2 * seq_length, dtype=jnp.int32) // (2 * TOK_DEV)
    slot_width = block_count * CAP
    slot_place = jnp.where(ffn_used > 0, expert_index * slot_width + block_index * CAP + slot_index, EXPERTS * slot_width).astype(jnp.int32)
    pair_rows = jnp.repeat(mixed, 2, axis=0)
    buffer_rows = jnp.zeros((EXPERTS * slot_width + 1, D), jnp.float32).at[slot_place].add(pair_rows)
    buffer_rows = buffer_rows[:EXPERTS * slot_width].reshape(EXPERTS, slot_width, D)
    gate_blocks = gate_weight.reshape(EXPERTS, HSPLIT, D, HALF)
    up_blocks = up_weight.reshape(EXPERTS, HSPLIT, D, HALF)
    down_blocks = down_weight.reshape(EXPERTS, HSPLIT, HALF, D)
    result_rows = jnp.zeros((EXPERTS, slot_width, D), jnp.float32)
    for half_index in range(HSPLIT):
        input_rows = low_back(buffer_rows)
        gate_part = low_back(jnp.einsum('ewd,edf->ewf', input_rows, gate_blocks[:, half_index], precision=HIGHEST))
        up_part = low_back(jnp.einsum('ewd,edf->ewf', input_rows, up_blocks[:, half_index], precision=HIGHEST))
        hidden = low(jax.nn.silu(gate_part) * up_part)
        part_out = low(low_back(jnp.einsum('ewf,efd->ewd', hidden, down_blocks[:, half_index], precision=HIGHEST)))
        result_rows = result_rows + part_out
    flat_rows = jnp.concatenate([result_rows.reshape(EXPERTS * slot_width, D), jnp.zeros((1, D), jnp.float32)], axis=0)
    return flat_rows[slot_place].reshape(seq_length, 2, D)

def layer(token_rows, prev_rows, params, seg_row, route_row):
    attn_gain, qkv_weight, out_weight, moe_gain, router_weight, cproj_weight, cvec_weight, gate_weight, up_weight, down_weight = params
    seq_length = token_rows.shape[0]
    normed = low(rms_scale(token_rows, attn_gain))
    qkv_rows = low_back(low(jnp.dot(normed, qkv_weight, precision=HIGHEST)))
    queries = qkv_rows[:, :D].reshape(seq_length, HEADS, HEAD)
    key_heads = qkv_rows[:, D:2 * D].reshape(seq_length, HEADS, HEAD)
    value_heads = qkv_rows[:, 2 * D:].reshape(seq_length, HEADS, HEAD)
    pos_all = jnp.arange(seq_length, dtype=jnp.int32)
    block_rows = math.gcd(seq_length, 512)
    block_count = seq_length // block_rows

    def one_block(pieces):
        return attend_block(pieces[0], pieces[1], pieces[2], key_heads, value_heads, seg_row, pos_all)
    attended = lax.map(jax.checkpoint(one_block), (queries.reshape(block_count, block_rows, HEADS, HEAD), pos_all.reshape(block_count, block_rows), seg_row.reshape(block_count, block_rows)))
    attended = attended.reshape(seq_length, D)
    valid_rows = (seg_row != SEGS - 1).astype(jnp.float32)[:, None]
    attended = low_back(low(attended * valid_rows))
    residual = token_rows + low_back(jnp.dot(attended, out_weight, precision=HIGHEST))
    mixed = low(rms_scale(residual, moe_gain))
    logits = jnp.dot(mixed, router_weight, precision=HIGHEST) + prev_rows
    router_probs = jax.nn.softmax(logits, axis=-1)
    choose = (route_row[:, :, None] == jnp.arange(NROUTE, dtype=jnp.int32)[None, None, :]).astype(jnp.float32)
    gate_values = lax.optimization_barrier(jnp.sum(choose * router_probs[:, None, :], axis=-1))
    const_logits = jnp.dot(mixed, cproj_weight, precision=HIGHEST)
    expert_out = expert_rows(mixed, route_row, gate_weight, up_weight, down_weight)
    expert_out = expert_out + choose[:, :, EXPERTS + 1:EXPERTS + 2] * mixed[:, None, :]
    for const_index in range(2):
        mixing = jax.nn.softmax(const_logits[:, 2 * const_index:2 * const_index + 2], axis=-1)
        const_out = mixing[:, :1] * mixed + mixing[:, 1:] * cvec_weight[:, const_index][None, :]
        column = EXPERTS + 2 + const_index
        expert_out = expert_out + choose[:, :, column:column + 1] * const_out[:, None, :]
    return residual + lax.optimization_barrier(jnp.sum(gate_values[:, :, None] * expert_out, axis=1))

def reference(tokens, prev_logits, segments, routes, cotangent, gain_attn, w_qkv, w_out, gain_moe, w_router, const_proj, const_vec, w_gate, w_up, w_down):
    params = tuple((weight.astype(jnp.float32) for weight in (gain_attn, w_qkv, w_out, gain_moe, w_router, const_proj, const_vec, w_gate, w_up, w_down)))

    def per_sequence(carry_grads, item_arrays):
        token_rows, prev_rows, seg_row, route_row, grad_rows = item_arrays

        def forward(first_arg, second_arg, weights):
            return layer(first_arg, second_arg, weights, seg_row, route_row)
        layer_out, pull_back = jax.vjp(forward, token_rows, prev_rows, params)
        grad_input, grad_prev_rows, grad_params = pull_back(grad_rows)
        carry_grads = jax.tree.map(lambda first_term, second_term: first_term + second_term, carry_grads, grad_params)
        return (carry_grads, (layer_out.astype(jnp.bfloat16), grad_input, grad_prev_rows))
    zero_grads = jax.tree.map(jnp.zeros_like, params)
    grads, (block_out, grad_tokens, grad_prev) = lax.scan(per_sequence, zero_grads, (tokens.astype(jnp.float32), prev_logits, segments, routes, cotangent.astype(jnp.float32)))
    return (block_out, grad_tokens, grad_prev, grads[0], grads[1], grads[2], grads[3], grads[4], grads[5], grads[6], grads[7], grads[8], grads[9])
```

```python
import functools

import jax
import jax.numpy as jnp
from jax import lax
from jax.experimental import pallas as pl
from jax.experimental.pallas import tpu as pltpu
from jax.sharding import PartitionSpec as P

HEAD = 64
SEGS = 4


NORM_EPS = 1e-06
MASK_FILL = -1e30
HIGHEST = lax.Precision.HIGHEST


def rms_scale(values, gains):
    inverse = lax.rsqrt(jnp.mean(values * values, axis=-1, keepdims=True) + NORM_EPS)
    return values * inverse * gains


def small_softmax(logit_rows):
    largest = jnp.max(logit_rows, axis=-1, keepdims=True)
    powers = jnp.exp(logit_rows - largest)
    return powers / jnp.sum(powers, axis=-1, keepdims=True)


def add_tuple(first_tuple, second_tuple):
    if first_tuple is None:
        return second_tuple
    return tuple(
        (first_term + second_term for first_term, second_term in zip(first_tuple, second_tuple))
    )


def shards(
    tokens,
    prev_logits,
    segments,
    routes,
    cotangent,
    gain_attn,
    w_qkv,
    w_out,
    gain_moe,
    w_router,
    const_proj,
    const_vec,
    w_gate,
    w_up,
    w_down,
):
    micro_count, row_count, model_width = tokens.shape
    head_count = model_width // HEAD
    peer_count = lax.axis_size("ep")
    my_index = lax.axis_index("ep")
    route_count = w_router.shape[1]
    expert_count = route_count - 4
    half_count = peer_count // expert_count
    capacity = (3 * row_count // route_count + 7) // 8 * 8
    seq_length = row_count * peer_count
    slot_count = expert_count * capacity
    pos_all = jnp.arange(seq_length, dtype=jnp.int32)
    pos_mine = my_index * row_count + jnp.arange(row_count, dtype=jnp.int32)
    expert_ids = jnp.arange(expert_count, dtype=jnp.int32)
    slot_ids = jnp.arange(slot_count, dtype=jnp.int32)
    route_ids = jnp.arange(route_count, dtype=jnp.int32)
    layer_outputs = []
    input_grads = []
    prev_grads = []
    dense_acc = None
    expert_acc = None
    for step_index in range(micro_count):
        gathered = (
            lax.all_gather(w_qkv, "fs", axis=0, tiled=True),
            lax.all_gather(w_out, "fs", axis=0, tiled=True),
            lax.all_gather(w_router, "fs", axis=0, tiled=True),
            lax.all_gather(const_proj, "fs", axis=0, tiled=True),
            lax.all_gather(const_vec, "fs", axis=0, tiled=True),
            lax.all_gather(gain_attn, "fs", axis=0, tiled=True),
            lax.all_gather(gain_moe, "fs", axis=0, tiled=True),
            lax.all_gather(w_gate, "fs", axis=1, tiled=True),
            lax.all_gather(w_up, "fs", axis=1, tiled=True),
            lax.all_gather(w_down, "fs", axis=1, tiled=True),
        )
        (
            qkv_weight,
            out_weight,
            router_weight,
            cproj_weight,
            cvec_weight,
            attn_gain,
            moe_gain,
            gate_weight,
            up_weight,
            down_weight,
        ) = gathered
        gate_weight = gate_weight[0]
        up_weight = up_weight[0]
        down_weight = down_weight[0]
        attn_gain = attn_gain.astype(jnp.float32)
        moe_gain = moe_gain.astype(jnp.float32)
        router_float = router_weight.astype(jnp.float32)
        cproj_float = cproj_weight.astype(jnp.float32)
        cvec_float = cvec_weight.astype(jnp.float32)
        token_rows = tokens[step_index].astype(jnp.float32)
        seg_all = segments[step_index]
        seg_mine = lax.dynamic_slice_in_dim(seg_all, my_index * row_count, row_count)
        allowed = (seg_mine[:, None] == seg_all[None, :]) & (pos_all[None, :] <= pos_mine[:, None])
        valid_rows = (seg_mine != SEGS - 1).astype(jnp.float32)[:, None]
        normed = rms_scale(token_rows, attn_gain).astype(jnp.bfloat16)
        qkv_rows = jnp.dot(normed, qkv_weight, preferred_element_type=jnp.float32).astype(
            jnp.bfloat16
        )
        queries = qkv_rows[:, :model_width].reshape(row_count, head_count, HEAD)
        keys_local = qkv_rows[:, model_width : 2 * model_width]
        values_local = qkv_rows[:, 2 * model_width :]
        keys_all, values_all = (
            lax.all_gather(keys_local, "ep", axis=0, tiled=True),
            lax.all_gather(values_local, "ep", axis=0, tiled=True),
        )
        key_heads = keys_all.reshape(seq_length, head_count, HEAD)
        value_heads = values_all.reshape(seq_length, head_count, HEAD)
        scores = (
            jnp.einsum("qhd,khd->hqk", queries, key_heads, preferred_element_type=jnp.float32)
            * 0.125
        )
        scores = jnp.where(allowed[None], scores, MASK_FILL)
        largest = jnp.max(scores, axis=-1, keepdims=True)
        powers = jnp.exp(scores - largest)
        row_total = jnp.sum(powers, axis=-1, keepdims=True)
        log_total = largest + jnp.log(row_total)
        attn_probs = powers / row_total
        attended = jnp.einsum(
            "hqk,khd->qhd",
            attn_probs.astype(jnp.bfloat16),
            value_heads,
            preferred_element_type=jnp.float32,
        ).reshape(row_count, model_width)
        attended = (attended * valid_rows).astype(jnp.bfloat16)
        residual = token_rows + jnp.dot(attended, out_weight, preferred_element_type=jnp.float32)
        mixed = rms_scale(residual, moe_gain).astype(jnp.bfloat16)
        mixed_float = mixed.astype(jnp.float32)
        logits = (
            jnp.dot(mixed, router_weight, preferred_element_type=jnp.float32)
            + prev_logits[step_index]
        )
        router_probs = small_softmax(logits)
        route_rows = routes[step_index]
        choose = (route_rows[:, :, None] == route_ids[None, None, :]).astype(jnp.float32)
        gate_values = jnp.sum(choose * router_probs[:, None, :], axis=-1)
        const_logits = jnp.dot(mixed, cproj_weight, preferred_element_type=jnp.float32)
        mixings = []
        const_outs = []
        for const_index in range(2):
            mixing = small_softmax(const_logits[:, 2 * const_index : 2 * const_index + 2])
            mixings.append(mixing)
            const_outs.append(
                mixing[:, :1] * mixed_float + mixing[:, 1:] * cvec_float[:, const_index][None, :]
            )
        pair_route = route_rows.reshape(-1)
        expert_hit = (pair_route[:, None] == expert_ids[None, :]).astype(jnp.int32)
        slot_index = jnp.sum((jnp.cumsum(expert_hit, axis=0) - expert_hit) * expert_hit, axis=1)
        slot_cell = jnp.sum(expert_hit * expert_ids[None, :], axis=1) * capacity + slot_index
        slot_place = jnp.where(jnp.sum(expert_hit, axis=1) > 0, slot_cell, -1)
        slot_table = (slot_ids[:, None] == slot_place[None, :]).astype(jnp.bfloat16)
        pair_rows = jnp.repeat(mixed, 2, axis=0)
        packed = jnp.einsum(
            "sp,pd->sd", slot_table, pair_rows, preferred_element_type=jnp.float32
        ).astype(jnp.bfloat16)
        outgoing = jnp.broadcast_to(
            packed.reshape(expert_count, 1, capacity, model_width),
            (expert_count, half_count, capacity, model_width),
        ).reshape(peer_count, capacity, model_width)
        received = lax.all_to_all(outgoing, "ep", split_axis=0, concat_axis=0, tiled=True)
        flat_rows = received.reshape(-1, model_width)
        gate_part = jnp.dot(flat_rows, gate_weight, preferred_element_type=jnp.float32)
        up_part = jnp.dot(flat_rows, up_weight, preferred_element_type=jnp.float32)
        hidden = (jax.nn.silu(gate_part) * up_part).astype(jnp.bfloat16)
        part_out = (
            jnp.dot(hidden, down_weight, preferred_element_type=jnp.float32)
            .astype(jnp.bfloat16)
            .reshape(received.shape)
        )
        returned_rows = lax.all_to_all(part_out, "ep", split_axis=0, concat_axis=0, tiled=True)
        returned_rows, kept_rows = (returned_rows, received)
        halves = returned_rows.reshape(expert_count, half_count, capacity, model_width)
        pair_ffn = jnp.zeros((2 * row_count, model_width), jnp.float32)
        for half_index in range(half_count):
            pair_ffn = pair_ffn + jnp.einsum(
                "sp,sd->pd",
                slot_table,
                halves[:, half_index].reshape(slot_count, model_width),
                preferred_element_type=jnp.float32,
            )
        expert_out = pair_ffn.reshape(row_count, 2, model_width)
        expert_out = (
            expert_out + choose[:, :, expert_count + 1 : expert_count + 2] * mixed_float[:, None, :]
        )
        for const_index in range(2):
            column = expert_count + 2 + const_index
            expert_out = (
                expert_out + choose[:, :, column : column + 1] * const_outs[const_index][:, None, :]
            )
        result_rows = residual + jnp.sum(gate_values[:, :, None] * expert_out, axis=1)
        layer_outputs.append(result_rows.astype(jnp.bfloat16))
        grad_rows = cotangent[step_index].astype(jnp.float32)
        d_gates = jnp.sum(expert_out * grad_rows[:, None, :], axis=-1)
        d_probs = jnp.sum(choose * d_gates[:, :, None], axis=1)
        d_logits = router_probs * (
            d_probs - jnp.sum(router_probs * d_probs, axis=-1, keepdims=True)
        )
        prev_grads.append(d_logits)
        grad_router = jnp.dot(mixed_float.T, d_logits, precision=HIGHEST)
        d_mixed = jnp.dot(d_logits, router_float.T, precision=HIGHEST)
        weighted = gate_values[:, :, None] * grad_rows[:, None, :]
        d_mixed = d_mixed + jnp.sum(
            choose[:, :, expert_count + 1 : expert_count + 2] * weighted, axis=1
        )
        cproj_grads = []
        cvec_grads = []
        for const_index in range(2):
            column = expert_count + 2 + const_index
            mixing = mixings[const_index]
            d_const = jnp.sum(choose[:, :, column : column + 1] * weighted, axis=1)
            d_mix = jnp.stack(
                [
                    jnp.sum(d_const * mixed_float, axis=-1),
                    jnp.sum(d_const * cvec_float[:, const_index][None, :], axis=-1),
                ],
                axis=-1,
            )
            d_mixlog = mixing * (d_mix - jnp.sum(mixing * d_mix, axis=-1, keepdims=True))
            cproj_grads.append(jnp.dot(mixed_float.T, d_mixlog, precision=HIGHEST))
            cvec_grads.append(jnp.sum(mixing[:, 1:] * d_const, axis=0))
            d_mixed = (
                d_mixed
                + mixing[:, :1] * d_const
                + jnp.dot(
                    d_mixlog,
                    cproj_float[:, 2 * const_index : 2 * const_index + 2].T,
                    precision=HIGHEST,
                )
            )
        grad_cproj = jnp.concatenate(cproj_grads, axis=1)
        grad_cvec = jnp.stack(cvec_grads, axis=1)
        d_pairs = weighted.reshape(2 * row_count, model_width).astype(jnp.bfloat16)
        d_packed = jnp.einsum(
            "sp,pd->sd", slot_table, d_pairs, preferred_element_type=jnp.float32
        ).astype(jnp.bfloat16)
        d_outgoing = jnp.broadcast_to(
            d_packed.reshape(expert_count, 1, capacity, model_width),
            (expert_count, half_count, capacity, model_width),
        ).reshape(peer_count, capacity, model_width)
        d_received = lax.all_to_all(d_outgoing, "ep", split_axis=0, concat_axis=0, tiled=True)
        flat_rows = kept_rows.reshape(-1, model_width)
        flat_grads = d_received.reshape(-1, model_width)
        gate_part = jnp.dot(flat_rows, gate_weight, preferred_element_type=jnp.float32)
        up_part = jnp.dot(flat_rows, up_weight, preferred_element_type=jnp.float32)
        activated = jax.nn.silu(gate_part)
        hidden = (activated * up_part).astype(jnp.bfloat16)
        grad_down = jnp.einsum("rf,rd->fd", hidden, flat_grads, preferred_element_type=jnp.float32)
        d_hidden = jnp.einsum(
            "rd,fd->rf", flat_grads, down_weight, preferred_element_type=jnp.float32
        )
        sigmoid_gate = jax.nn.sigmoid(gate_part)
        d_gate_part = (
            d_hidden * up_part * sigmoid_gate * (1.0 + gate_part * (1.0 - sigmoid_gate))
        ).astype(jnp.bfloat16)
        d_up_part = (d_hidden * activated).astype(jnp.bfloat16)
        grad_gate = jnp.einsum(
            "rd,rf->df", flat_rows, d_gate_part, preferred_element_type=jnp.float32
        )
        grad_up = jnp.einsum("rd,rf->df", flat_rows, d_up_part, preferred_element_type=jnp.float32)
        d_inputs = jnp.einsum(
            "rf,df->rd", d_gate_part, gate_weight, preferred_element_type=jnp.float32
        )
        d_inputs = d_inputs + jnp.einsum(
            "rf,df->rd", d_up_part, up_weight, preferred_element_type=jnp.float32
        )
        d_inputs = d_inputs.astype(jnp.bfloat16).reshape(peer_count, capacity, model_width)
        d_returned = lax.all_to_all(d_inputs, "ep", split_axis=0, concat_axis=0, tiled=True)
        d_halves = d_returned.reshape(expert_count, half_count, capacity, model_width)
        for half_index in range(half_count):
            d_pair_in = jnp.einsum(
                "sp,sd->pd",
                slot_table,
                d_halves[:, half_index].reshape(slot_count, model_width),
                preferred_element_type=jnp.float32,
            )
            d_mixed = d_mixed + jnp.sum(d_pair_in.reshape(row_count, 2, model_width), axis=1)
        expert_acc = add_tuple(expert_acc, (grad_gate, grad_up, grad_down))
        moe_vjp = jax.vjp(rms_scale, residual, moe_gain)[1]
        d_residual_norm, grad_moe_gain = moe_vjp(d_mixed)
        d_residual = grad_rows + d_residual_norm
        d_branch = d_residual.astype(jnp.bfloat16)
        grad_out = jnp.einsum("rd,re->de", attended, d_branch, preferred_element_type=jnp.float32)
        d_attended = (
            jnp.einsum("re,de->rd", d_branch, out_weight, preferred_element_type=jnp.float32)
            * valid_rows
        ).astype(jnp.bfloat16)
        d_heads = d_attended.reshape(row_count, head_count, HEAD)
        scores = (
            jnp.einsum("qhd,khd->hqk", queries, key_heads, preferred_element_type=jnp.float32)
            * 0.125
        )
        scores = jnp.where(allowed[None], scores, MASK_FILL)
        attn_probs = jnp.exp(scores - log_total)
        d_weights = jnp.einsum(
            "qhd,khd->hqk", d_heads, value_heads, preferred_element_type=jnp.float32
        )
        delta_rows = jnp.sum(attn_probs * d_weights, axis=-1, keepdims=True)
        d_scores = (attn_probs * (d_weights - delta_rows)).astype(jnp.bfloat16)
        d_queries = (
            jnp.einsum(
                "hqk,khd->qhd", d_scores, key_heads, preferred_element_type=jnp.float32
            ).reshape(row_count, model_width)
            * 0.125
        )
        d_values = jnp.einsum(
            "hqk,qhd->khd",
            attn_probs.astype(jnp.bfloat16),
            d_heads,
            preferred_element_type=jnp.float32,
        ).reshape(seq_length, model_width)
        d_keys = (
            jnp.einsum(
                "hqk,qhd->khd", d_scores, queries, preferred_element_type=jnp.float32
            ).reshape(seq_length, model_width)
            * 0.125
        )
        d_keys_mine, d_values_mine = (
            lax.psum_scatter(
                d_keys.astype(jnp.bfloat16), "ep", scatter_dimension=0, tiled=True
            ).astype(jnp.float32),
            lax.psum_scatter(
                d_values.astype(jnp.bfloat16), "ep", scatter_dimension=0, tiled=True
            ).astype(jnp.float32),
        )
        d_qkv = jnp.concatenate([d_queries, d_keys_mine, d_values_mine], axis=1).astype(
            jnp.bfloat16
        )
        grad_qkv = jnp.einsum("rd,re->de", normed, d_qkv, preferred_element_type=jnp.float32)
        d_normed = jnp.einsum("re,de->rd", d_qkv, qkv_weight, preferred_element_type=jnp.float32)
        attn_vjp = jax.vjp(rms_scale, token_rows, attn_gain)[1]
        d_tokens_norm, grad_attn_gain = attn_vjp(d_normed)
        input_grads.append(d_residual + d_tokens_norm)
        dense_terms = (
            grad_attn_gain,
            grad_qkv,
            grad_out,
            grad_moe_gain,
            grad_router,
            grad_cproj,
            grad_cvec,
        )
        dense_shares = (
            lax.psum_scatter(dense_terms[0], ("ep", "dp", "fs"), scatter_dimension=0, tiled=True),
            lax.psum_scatter(dense_terms[1], ("ep", "dp", "fs"), scatter_dimension=0, tiled=True),
            lax.psum_scatter(dense_terms[2], ("ep", "dp", "fs"), scatter_dimension=0, tiled=True),
            lax.psum_scatter(dense_terms[3], ("ep", "dp", "fs"), scatter_dimension=0, tiled=True),
            lax.psum_scatter(dense_terms[4], ("ep", "dp", "fs"), scatter_dimension=0, tiled=True),
            lax.psum_scatter(dense_terms[5], ("ep", "dp", "fs"), scatter_dimension=0, tiled=True),
            lax.psum_scatter(dense_terms[6], ("ep", "dp", "fs"), scatter_dimension=0, tiled=True),
        )
        dense_acc = add_tuple(dense_acc, dense_shares)
    expert_shares = (
        lax.psum_scatter(
            expert_acc[0][None].astype(jnp.bfloat16), ("dp", "fs"), scatter_dimension=1, tiled=True
        ).astype(jnp.float32),
        lax.psum_scatter(
            expert_acc[1][None].astype(jnp.bfloat16), ("dp", "fs"), scatter_dimension=1, tiled=True
        ).astype(jnp.float32),
        lax.psum_scatter(
            expert_acc[2][None].astype(jnp.bfloat16), ("dp", "fs"), scatter_dimension=1, tiled=True
        ).astype(jnp.float32),
    )
    return (
        jnp.stack(layer_outputs),
        jnp.stack(input_grads),
        jnp.stack(prev_grads),
        dense_acc[0],
        dense_acc[1],
        dense_acc[2],
        dense_acc[3],
        dense_acc[4],
        dense_acc[5],
        dense_acc[6],
        expert_shares[0],
        expert_shares[1],
        expert_shares[2],
    )


NEG = -1e30
KINDS = 2
SMALL = 16
LANES = 128
F32 = jnp.float32
BF16 = jnp.bfloat16


def dot(lhs, rhs, dims=((1,), (0,)), precision=None):
    return lax.dot_general(
        lhs, rhs, (dims, ((), ())), precision=precision, preferred_element_type=F32
    )


def norm_qkv_kernel(x_ref, gain_ref, w_ref, normed_ref, qkv_ref):
    rows = x_ref[...].astype(F32)
    inverse = lax.rsqrt(jnp.mean(rows * rows, axis=-1, keepdims=True) + NORM_EPS)
    normed = (rows * inverse * gain_ref[...]).astype(BF16)
    normed_ref[...] = normed
    qkv_ref[...] = dot(normed, w_ref[...]).astype(BF16)


def key_span(block, rows, reach):
    start = max(0, block * rows - reach)
    return start, (block + 1) * rows - start


def attend_kernel(rows, reach, q_ref, k_ref, v_ref, segc_ref, segr_ref, att_ref, lse_ref):
    length = q_ref.shape[0]
    for block in range(length // rows):
        start, width = key_span(block, rows, reach)
        queries = q_ref[block * rows : (block + 1) * rows, :]
        keys = k_ref[start : start + width, :]
        values = v_ref[start : start + width, :]
        seg_q = segc_ref[block * rows : (block + 1) * rows, :]
        seg_k = segr_ref[:, start : start + width]
        row_pos = block * rows + lax.broadcasted_iota(jnp.int32, (rows, width), 0)
        col_pos = start + lax.broadcasted_iota(jnp.int32, (rows, width), 1)
        allowed = (seg_q == seg_k) & (col_pos <= row_pos)
        lane = lax.broadcasted_iota(jnp.int32, (rows, LANES), 1)
        outs = []
        logs = []
        for head in range(2):
            mine = (lane // HEAD) == head
            scores = dot(jnp.where(mine, queries, 0), keys, ((1,), (1,))) * 0.125
            scores = jnp.where(allowed, scores, NEG)
            largest = jnp.max(scores, axis=-1, keepdims=True)
            powers = jnp.exp(scores - largest)
            total = jnp.sum(powers, axis=-1, keepdims=True)
            outs.append(dot(powers.astype(BF16), values) / total)
            logs.append(largest + jnp.log(total))
        valid = (seg_q != SEGS - 1).astype(F32)
        att = jnp.where(lane < HEAD, outs[0], outs[1]) * valid
        att_ref[block * rows : (block + 1) * rows, :] = att.astype(BF16)
        both = jnp.where(lane < HEAD, logs[0], logs[1]).T
        lse_ref[0, 0:1, block * rows : (block + 1) * rows] = both[0:1, :]
        lse_ref[0, 1:2, block * rows : (block + 1) * rows] = both[HEAD : HEAD + 1, :]


def attend_back_kernel(
    rows, reach, q_ref, k_ref, v_ref, do_ref, segc_ref, segr_ref, lse_ref,
    dq_ref, dk_ref, dv_ref, dk_sum, dv_sum,
):
    length = q_ref.shape[0]
    dk_sum[...] = jnp.zeros_like(dk_sum)
    dv_sum[...] = jnp.zeros_like(dv_sum)
    keys_turned = k_ref[...].T
    for block in range(length // rows):
        start, width = key_span(block, rows, reach)
        queries = q_ref[block * rows : (block + 1) * rows, :]
        grads = do_ref[block * rows : (block + 1) * rows, :]
        keys = k_ref[start : start + width, :]
        values = v_ref[start : start + width, :]
        seg_k = segc_ref[start : start + width, :]
        seg_q = segr_ref[:, block * rows : (block + 1) * rows]
        key_pos = start + lax.broadcasted_iota(jnp.int32, (width, rows), 0)
        query_pos = block * rows + lax.broadcasted_iota(jnp.int32, (width, rows), 1)
        allowed = (seg_q == seg_k) & (key_pos <= query_pos)
        lane = lax.broadcasted_iota(jnp.int32, (rows, LANES), 1)
        dq_parts = []
        for head in range(2):
            mine = (lane // HEAD) == head
            head_q = jnp.where(mine, queries, 0)
            head_g = jnp.where(mine, grads, 0)
            log_total = lse_ref[0, head : head + 1, block * rows : (block + 1) * rows]
            scores = dot(keys, head_q, ((1,), (1,))) * 0.125
            probs = jnp.exp(jnp.where(allowed, scores, NEG) - log_total)
            d_probs = dot(values, head_g, ((1,), (1,)))
            delta = jnp.sum(probs * d_probs, axis=0, keepdims=True)
            d_scores = (probs * (d_probs - delta)).astype(BF16)
            dv_sum[start : start + width, :] += dot(probs.astype(BF16), head_g)
            dk_sum[start : start + width, :] += dot(d_scores, head_q)
            turned = keys_turned[head * HEAD : (head + 1) * HEAD, start : start + width]
            dq_parts.append(dot(turned, d_scores))
        dq = jnp.concatenate(dq_parts, axis=0).T * 0.125
        dq_ref[block * rows : (block + 1) * rows, :] = dq.astype(BF16)
    dk_ref[...] = (dk_sum[...] * 0.125).astype(BF16)
    dv_ref[...] = dv_sum[...].astype(BF16)


def column(rows, index):
    return rows[:, index : index + 1]


def chosen_of(ctl):
    lane = lax.broadcasted_iota(jnp.int32, ctl.shape, 1).astype(F32)
    return ((lane == column(ctl, 8)) | (lane == column(ctl, 9))).astype(F32)


def spread_kernel(
    experts, routes, att_own_ref, att_sib_ref, x_ref, g_ref, ctl_ref, w_own_ref, w_sib_ref,
    gain_ref, wsm_ref, residual_ref, mixed_ref, pm_ref, place_ref, send_ref,
):
    rows = x_ref.shape[0]
    residual = x_ref[...].astype(F32) + (
        dot(att_own_ref[...], w_own_ref[...]) + dot(att_sib_ref[...], w_sib_ref[...])
    )
    residual_ref[...] = residual
    inverse = lax.rsqrt(jnp.mean(residual * residual, axis=-1, keepdims=True) + NORM_EPS)
    mixed = (residual * inverse * gain_ref[...]).astype(BF16)
    mixed_ref[...] = mixed
    logits = dot(mixed, wsm_ref[...])
    ctl = ctl_ref[...]
    lane = lax.broadcasted_iota(jnp.int32, (rows, LANES), 1)
    is_route = lane < routes
    router = jnp.where(is_route, logits + ctl, NEG)
    powers = jnp.exp(router - jnp.max(router, axis=-1, keepdims=True))
    probs = powers / jnp.sum(powers, axis=-1, keepdims=True)
    probs = jnp.where(is_route, probs, 0.0)
    pm = probs
    for const_index in range(2):
        first = column(logits, 8 + 2 * const_index)
        second = column(logits, 9 + 2 * const_index)
        largest = jnp.maximum(first, second)
        first = jnp.exp(first - largest)
        second = jnp.exp(second - largest)
        total = first + second
        pm = jnp.where(lane == 8 + 2 * const_index, first / total, pm)
        pm = jnp.where(lane == 9 + 2 * const_index, second / total, pm)
    pm_ref[...] = pm
    chosen = chosen_of(ctl)
    gated = chosen * probs
    earlier = lax.broadcasted_iota(jnp.int32, (rows, rows), 1) < lax.broadcasted_iota(
        jnp.int32, (rows, rows), 0
    )
    rank = dot(earlier.astype(BF16), chosen.astype(BF16))
    lane_f = lane.astype(F32)
    halves = send_ref.shape[0] // experts
    for expert in range(experts):
        place = jnp.where(
            (lane_f == column(rank, expert)) & (column(chosen, expert) > 0.0), 1.0, 0.0
        )
        place_ref[:, expert * LANES : (expert + 1) * LANES] = place.astype(BF16)
        pick = place.T.astype(BF16)
        d_part = (column(gated, expert) * g_ref[...].astype(F32)).astype(BF16)
        packed = dot(pick, mixed).astype(BF16)
        d_packed = dot(pick, d_part).astype(BF16)
        for half in range(halves):
            send_ref[expert * halves + half, 0, 0] = packed
            send_ref[expert * halves + half, 1, 0] = d_packed


def expert_kernel(in_ref, gate_ref, up_ref, down_ref, out_ref, hidden_ref, dgate_ref, dup_ref):
    size = in_ref.shape[2] * in_ref.shape[3]
    width = in_ref.shape[4]
    rows = in_ref[0, 0].reshape(size, width)
    d_rows = in_ref[0, 1].reshape(size, width)
    gate = dot(rows, gate_ref[...])
    up = dot(rows, up_ref[...])
    sig = jax.nn.sigmoid(gate)
    active = gate * sig
    hidden = (active * up).astype(BF16)
    hidden_ref[...] = hidden
    part = dot(hidden, down_ref[...]).astype(BF16)
    out_ref[0, 0] = part.reshape(in_ref.shape[2:])
    d_hidden = dot(d_rows, down_ref[...], ((1,), (1,)))
    d_gate = (d_hidden * up * sig * (1.0 + gate * (1.0 - sig))).astype(BF16)
    d_up = (d_hidden * active).astype(BF16)
    dgate_ref[...] = d_gate
    dup_ref[...] = d_up
    d_in = dot(d_gate, gate_ref[...], ((1,), (1,))) + dot(d_up, up_ref[...], ((1,), (1,)))
    out_ref[0, 1] = d_in.astype(BF16).reshape(in_ref.shape[2:])


def combine_kernel(
    experts, routes, residual_ref, mixed_ref, pm_ref, ctl_ref, place_ref, back_ref, g_ref,
    gain_ref, turned_ref, cvec_ref, out_ref, prev_ref, dres_ref, branch_ref, small_ref,
):
    halves = back_ref.shape[0] // experts
    rows = g_ref.shape[0]
    grads = g_ref[...].astype(F32)
    mixed = mixed_ref[...].astype(F32)
    residual = residual_ref[...]
    pm = pm_ref[...]
    lane = lax.broadcasted_iota(jnp.int32, (rows, LANES), 1)
    chosen = chosen_of(ctl_ref[...])
    probs = jnp.where(lane < routes, pm, 0.0)
    gated = chosen * probs
    d_probs = jnp.zeros((rows, LANES), F32)
    result = residual
    d_mixed = None
    for expert in range(experts):
        place = place_ref[:, expert * LANES : (expert + 1) * LANES]
        expert_out = None
        for half in range(halves):
            owner = expert * halves + half
            term = dot(place, back_ref[owner, 0, 0])
            expert_out = term if expert_out is None else expert_out + term
            term = dot(place, back_ref[owner, 1, 0])
            d_mixed = term if d_mixed is None else d_mixed + term
        result = result + column(gated, expert) * expert_out
        d_gate = jnp.sum(expert_out * grads, axis=-1, keepdims=True)
        d_probs = jnp.where(lane == expert, d_gate, d_probs)
    turned = turned_ref[...]
    g_mixed = jnp.sum(grads * mixed, axis=-1, keepdims=True)
    g_const = dot(g_ref[...], cvec_ref[...], ((1,), (1,)))
    copy = experts + 1
    d_probs = jnp.where(lane == copy, g_mixed, d_probs)
    mixed_weight = column(gated, copy)
    grad_weight = column(gated, copy)
    d_small = jnp.zeros((rows, LANES), F32)
    for const_index in range(2):
        route = copy + 1 + const_index
        first = column(pm, 8 + 2 * const_index)
        second = column(pm, 9 + 2 * const_index)
        gate = column(gated, route)
        g_vec = column(g_const, const_index)
        d_probs = jnp.where(lane == route, first * g_mixed + second * g_vec, d_probs)
        mixed_weight = mixed_weight + gate * first
        grad_weight = grad_weight + gate * first
        vec = cvec_ref[const_index : const_index + 1, :].astype(F32)
        result = result + (gate * second) * vec
        d_first = gate * g_mixed
        d_second = gate * g_vec
        mean = first * d_first + second * d_second
        d_small = jnp.where(lane == 8 + 2 * const_index, first * (d_first - mean), d_small)
        d_small = jnp.where(lane == 9 + 2 * const_index, second * (d_second - mean), d_small)
        d_small = jnp.where(lane == 12 + const_index, gate * second, d_small)
    result = result + mixed_weight * mixed
    out_ref[...] = result.astype(BF16)
    d_probs = d_probs * chosen
    d_logits = probs * (d_probs - jnp.sum(probs * d_probs, axis=-1, keepdims=True))
    prev_ref[...] = d_logits
    d_small = jnp.where(lane < routes, d_logits, d_small)
    d_mixed = d_mixed + grad_weight * grads
    d_mixed = d_mixed + dot(
        jnp.where(lane < 12, d_small, 0.0), turned, precision=HIGHEST
    )
    inverse = lax.rsqrt(jnp.mean(residual * residual, axis=-1, keepdims=True) + NORM_EPS)
    scaled = d_mixed * gain_ref[...]
    mean = jnp.mean(scaled * residual, axis=-1, keepdims=True)
    d_residual = grads + inverse * scaled - residual * (inverse * inverse * inverse * mean)
    dres_ref[...] = d_residual
    branch_ref[...] = d_residual.astype(BF16)
    d_turned = d_small.T[:SMALL, :]
    sub = lax.broadcasted_iota(jnp.int32, (SMALL, rows), 0)
    small = dot(jnp.where(sub < 12, d_turned, 0.0), mixed, precision=HIGHEST)
    small = small + dot(
        jnp.where((sub >= 12) & (sub < 14), d_turned, 0.0), grads, precision=HIGHEST
    )
    d_gain = jnp.sum(d_mixed * residual * inverse, axis=0, keepdims=True)
    which = lax.broadcasted_iota(jnp.int32, small.shape, 0)
    small = jnp.where(which == 14, d_gain, small)

    @pl.when(pl.program_id(0) == 0)
    def _():
        small_ref[...] = jnp.zeros_like(small_ref)

    small_ref[...] += small


def finish_kernel(x_ref, own_ref, sib_ref, dres_ref, gain_ref, out_ref, gain_out_ref):
    rows = x_ref[...].astype(F32)
    d_normed = own_ref[...].astype(F32) + sib_ref[...].astype(F32)
    inverse = lax.rsqrt(jnp.mean(rows * rows, axis=-1, keepdims=True) + NORM_EPS)
    scaled = d_normed * gain_ref[...]
    mean = jnp.mean(scaled * rows, axis=-1, keepdims=True)
    out = dres_ref[...] + inverse * scaled - rows * (inverse * inverse * inverse * mean)
    out_ref[...] = out.astype(out_ref.dtype)

    @pl.when(pl.program_id(0) == 0)
    def _():
        gain_out_ref[...] = jnp.zeros_like(gain_out_ref)

    gain_out_ref[0:1, :] += jnp.sum(d_normed * rows * inverse, axis=0, keepdims=True)


def shape(dims, dtype):
    return jax.ShapeDtypeStruct(dims, dtype)


def whole(dims):
    return pl.BlockSpec(dims, lambda *_: (0,) * len(dims))


def per_row(rows, width):
    return pl.BlockSpec((rows, width), lambda i: (i, 0))


def params():
    return pltpu.CompilerParams(vmem_limit_bytes=56 * 1024 * 1024)


def cost(flops, moved):
    return pl.CostEstimate(flops=int(flops), bytes_accessed=int(moved), transcendentals=0)


def one_chip(
    tokens,
    prev_logits,
    segments,
    routes,
    cotangent,
    gain_attn,
    w_qkv,
    w_out,
    gain_moe,
    w_router,
    const_proj,
    const_vec,
    w_gate,
    w_up,
    w_down,
):
    rows, width = tokens.shape[1:]
    peers = lax.axis_size("ep")
    place = lax.axis_index("ep")
    core = lax.axis_index("fs")
    cross = place % 2
    route_count = w_router.shape[1]
    experts = route_count - 4
    capacity = LANES
    length = rows * peers
    mine = length // 2
    span = width // 2
    hidden_width = w_gate.shape[2]
    pairs = [[], []]
    for flip in range(2):
        for source in range(peers):
            for side in range(2):
                target = side * 2 + ((source % 2) ^ flip)
                pairs[flip].append((source * 2 + side, target * 2 + source // 2))

    def swap(array):
        return lax.ppermute(array, "fs", [(0, 1), (1, 0)])

    def by_core(own, other, axis=0):
        return jnp.where(
            core == 0,
            jnp.concatenate([own, other], axis=axis),
            jnp.concatenate([other, own], axis=axis),
        )

    def to_chip(array):
        near = lax.ppermute(
            lax.dynamic_index_in_dim(array, cross, 0, False), ("ep", "fs"), pairs[0]
        )
        far = lax.ppermute(
            lax.dynamic_index_in_dim(array, 1 - cross, 0, False), ("ep", "fs"), pairs[1]
        )
        return jnp.where(
            cross == 0, jnp.concatenate([near, far]), jnp.concatenate([far, near])
        )

    def from_chip(array):
        split = array.reshape((2, rows) + array.shape[1:])
        near = lax.ppermute(
            lax.dynamic_index_in_dim(split, cross, 0, False), ("ep", "fs"), pairs[0]
        )
        far = lax.ppermute(
            lax.dynamic_index_in_dim(split, 1 - cross, 0, False), ("ep", "fs"), pairs[1]
        )
        return jnp.where(cross == 0, jnp.stack([near, far]), jnp.stack([far, near]))

    x_own = to_chip(tokens)
    x_sib = swap(x_own)
    qkv_split = w_qkv.reshape(span, 3, 2, span)
    qkv_mine = lax.dynamic_index_in_dim(qkv_split, core, 2, False).reshape(span, 3 * span)
    qkv_sent = lax.dynamic_index_in_dim(qkv_split, 1 - core, 2, False).reshape(span, 3 * span)
    qkv_weight = by_core(qkv_mine, swap(qkv_sent))
    out_sib = swap(w_out)
    pad = jnp.zeros((span, 8 - route_count), BF16)
    small_own = jnp.concatenate(
        [w_router, pad, const_proj, const_vec, gain_attn[:, None], gain_moe[:, None]], axis=1
    )
    small_all = by_core(small_own, swap(small_own))
    small_turned = small_all.T.astype(F32)
    attn_gain = small_turned[14:15]
    moe_gain = small_turned[15:16]
    wsm = jnp.pad(small_all[:, :12], ((0, 0), (0, LANES - 12)))
    turned = jnp.pad(small_turned[:12], ((0, LANES - 12), (0, 0)))
    cvec_turned = jnp.pad(small_all[:, 12:14].T, ((0, LANES - 2), (0, 0)))
    gate_weight = by_core(w_gate[0], swap(w_gate[0]))
    up_weight = by_core(w_up[0], swap(w_up[0]))
    down_weight = by_core(w_down[0], swap(w_down[0]))
    seg_sib = swap(segments)
    seg_pair = by_core(segments[None], seg_sib[None])
    seg_row = seg_pair.reshape(4, length)[place][None, :]
    seg_col = seg_row.reshape(length, 1)

    x_all = by_core(x_own, x_sib)
    normed, qkv = pl.pallas_call(
        norm_qkv_kernel,
        grid=(length // rows,),
        in_specs=[per_row(rows, width), whole((1, width)), whole((width, 3 * span))],
        out_specs=[per_row(rows, width), per_row(rows, 3 * span)],
        out_shape=[shape((length, width), BF16), shape((length, 3 * span), BF16)],
        compiler_params=params(),
        cost_estimate=cost(2 * length * width * 3 * span, 6e6),
        name="norm_qkv",
    )(x_all, attn_gain, qkv_weight)

    head_pairs = span // LANES
    reach = length // 2

    def heads_at(offset):
        return pl.BlockSpec((length, LANES), lambda p: (0, offset + p))

    lse_spec = pl.BlockSpec((1, 8, length), lambda p: (p, 0, 0))
    attended, lse = pl.pallas_call(
        functools.partial(attend_kernel, rows, reach),
        grid=(head_pairs,),
        in_specs=[
            heads_at(0), heads_at(head_pairs), heads_at(2 * head_pairs),
            whole((length, 1)), whole((1, length)),
        ],
        out_specs=[heads_at(0), lse_spec],
        out_shape=[shape((length, span), BF16), shape((head_pairs, 8, length), F32)],
        compiler_params=params(),
        cost_estimate=cost(12e9, 4e6),
        name="attend",
    )(qkv, qkv, qkv, seg_col, seg_row)

    att_own = lax.dynamic_slice_in_dim(attended, core * mine, mine)
    att_sib = swap(lax.dynamic_slice_in_dim(attended, (1 - core) * mine, mine))
    cot_own = to_chip(cotangent)
    ctl = jnp.concatenate(
        [
            prev_logits,
            jnp.zeros(prev_logits.shape[:2] + (8 - route_count,), F32),
            routes.astype(F32),
        ],
        axis=2,
    )
    ctl = jnp.pad(to_chip(ctl), ((0, 0), (0, LANES - 10)))
    blocks = mine // rows
    send_dims = (peers, KINDS, blocks, capacity, width)
    send_spec = pl.BlockSpec(
        (peers, KINDS, 1, capacity, width), lambda b: (0, 0, b, 0, 0)
    )
    residual, mixed, pm, places, sent = pl.pallas_call(
        functools.partial(spread_kernel, experts, route_count),
        grid=(blocks,),
        in_specs=[
            per_row(rows, span), per_row(rows, span), per_row(rows, width),
            per_row(rows, width), per_row(rows, LANES), whole((span, width)),
            whole((span, width)), whole((1, width)), whole((width, LANES)),
        ],
        out_specs=[
            per_row(rows, width), per_row(rows, width), per_row(rows, LANES),
            per_row(rows, experts * LANES), send_spec,
        ],
        out_shape=[
            shape((mine, width), F32), shape((mine, width), BF16), shape((mine, LANES), F32),
            shape((mine, experts * LANES), BF16), shape(send_dims, BF16),
        ],
        compiler_params=params(),
        cost_estimate=cost(2e9, 8e6),
        name="spread",
    )(att_own, att_sib, x_own, cot_own, ctl, w_out, out_sib, moe_gain, wsm)

    received = lax.all_to_all(sent, "ep", split_axis=0, concat_axis=0, tiled=True)
    group = blocks * capacity
    item_spec = pl.BlockSpec(
        (1, KINDS, blocks, capacity, width), lambda s: (s, 0, 0, 0, 0)
    )
    results, hidden, d_gate, d_up = pl.pallas_call(
        expert_kernel,
        grid=(peers,),
        in_specs=[
            item_spec, whole((width, hidden_width)), whole((width, hidden_width)),
            whole((hidden_width, width)),
        ],
        out_specs=[item_spec] + [per_row(group, hidden_width)] * 3,
        out_shape=[shape(send_dims, BF16)] + [shape((peers * group, hidden_width), BF16)] * 3,
        compiler_params=params(),
        cost_estimate=cost(10e9, 15e6),
        name="experts",
    )(received, gate_weight, up_weight, down_weight)
    returned = lax.all_to_all(results, "ep", split_axis=0, concat_axis=0, tiled=True)
    flat_rows = received[:, 0].reshape(peers * group, width)
    flat_grads = received[:, 1].reshape(peers * group, width)
    grad_gate = dot(flat_rows, d_gate, ((0,), (0,))).astype(BF16)
    grad_up = dot(flat_rows, d_up, ((0,), (0,))).astype(BF16)
    grad_down = dot(hidden, flat_grads, ((0,), (0,))).astype(BF16)

    block_out, d_prev, d_residual, d_branch, small = pl.pallas_call(
        functools.partial(combine_kernel, experts, route_count),
        grid=(blocks,),
        in_specs=[
            per_row(rows, width), per_row(rows, width), per_row(rows, LANES),
            per_row(rows, LANES), per_row(rows, experts * LANES), send_spec,
            per_row(rows, width), whole((1, width)), whole((LANES, width)),
            whole((LANES, width)),
        ],
        out_specs=[
            per_row(rows, width), per_row(rows, LANES), per_row(rows, width),
            per_row(rows, width), whole((SMALL, width)),
        ],
        out_shape=[
            shape((mine, width), BF16), shape((mine, LANES), F32), shape((mine, width), F32),
            shape((mine, width), BF16), shape((SMALL, width), F32),
        ],
        compiler_params=params(),
        cost_estimate=cost(3e9, 10e6),
        name="combine",
    )(
        residual, mixed, pm, ctl, places, returned, cot_own, moe_gain, turned, cvec_turned,
    )

    branch_all = by_core(d_branch, swap(d_branch))
    valid = (seg_col != SEGS - 1).astype(F32)
    d_att = (dot(branch_all, w_out, ((1,), (1,))) * valid).astype(BF16)
    grad_out = dot(attended, branch_all, ((0,), (0,))).astype(BF16)
    d_queries, d_keys, d_values = pl.pallas_call(
        functools.partial(attend_back_kernel, rows, reach),
        grid=(head_pairs,),
        in_specs=[
            heads_at(0), heads_at(head_pairs), heads_at(2 * head_pairs), heads_at(0),
            whole((length, 1)), whole((1, length)), lse_spec,
        ],
        out_specs=[heads_at(0)] * 3,
        out_shape=[shape((length, span), BF16)] * 3,
        scratch_shapes=[pltpu.VMEM((length, LANES), F32)] * 2,
        compiler_params=params(),
        cost_estimate=cost(30e9, 5e6),
        name="attend_back",
    )(qkv, qkv, qkv, d_att, seg_col, seg_row, lse)
    d_qkv = jnp.concatenate([d_queries, d_keys, d_values], axis=1)
    d_normed = dot(d_qkv, qkv_weight, ((1,), (1,)))
    d_normed_own = lax.dynamic_slice_in_dim(d_normed, core * mine, mine)
    d_normed_sib = swap(
        lax.dynamic_slice_in_dim(d_normed, (1 - core) * mine, mine).astype(BF16)
    )
    grad_qkv = dot(normed, d_qkv, ((0,), (0,))).astype(BF16)
    d_tokens, gain_rows = pl.pallas_call(
        finish_kernel,
        grid=(blocks,),
        in_specs=[per_row(rows, width)] * 4 + [whole((1, width))],
        out_specs=[per_row(rows, width), whole((8, width))],
        out_shape=[shape((mine, width), BF16), shape((8, width), F32)],
        compiler_params=params(),
        cost_estimate=cost(1e8, 6e6),
        name="finish",
    )(x_own, d_normed_own, d_normed_sib, d_residual, attn_gain)

    out_mine = lax.dynamic_slice_in_dim(grad_out, core * span, span, axis=1)
    out_sent = lax.dynamic_slice_in_dim(grad_out, (1 - core) * span, span, axis=1)
    out_cols = by_core(out_mine, swap(out_sent))
    small = jnp.concatenate([small[: SMALL - 1], gain_rows[:1]]).T.astype(BF16)
    dense = jnp.concatenate(
        [grad_qkv, out_cols, jnp.pad(small, ((0, 0), (0, LANES - SMALL)))], axis=1
    )
    dense = lax.psum_scatter(dense, ("ep", "dp"), scatter_dimension=0, tiled=True)
    final = dense.shape[0] // 2
    dense_own = lax.dynamic_slice_in_dim(dense, core * final, final)
    dense_sib = swap(lax.dynamic_slice_in_dim(dense, (1 - core) * final, final))
    pieces = (dense_own.astype(F32), dense_sib.astype(F32))

    def columns_of(start):
        own, other = (piece[:, start : start + span] for piece in pieces)
        return by_core(own, other, axis=1)

    share_qkv = jnp.concatenate([columns_of(k * span) for k in range(3)], axis=1)
    share_out = columns_of(3 * span)
    share_small = sum(piece[:, 4 * span : 4 * span + SMALL] for piece in pieces)
    expert_shares = tuple(
        lax.psum_scatter(grad[None], ("dp", "fs"), scatter_dimension=1, tiled=True).astype(F32)
        for grad in (grad_gate, grad_up, grad_down)
    )
    prev_cols = d_prev[:, :route_count]
    return (
        from_chip(block_out),
        from_chip(d_tokens).astype(F32),
        from_chip(prev_cols),
        share_small[:, 15],
        share_qkv,
        share_out,
        share_small[:, 14],
        share_small[:, :route_count],
        share_small[:, 8:12],
        share_small[:, 12:14],
    ) + expert_shares


def suits(mesh, tokens, w_router, w_gate):
    peers = mesh.shape["ep"]
    rows = tokens.shape[1] // peers
    micro = tokens.shape[0] // (mesh.shape["dp"] * mesh.shape["fs"])
    routes = w_router.shape[1]
    return (
        peers == 4
        and mesh.shape["fs"] == 2
        and micro == 2
        and (routes - 4) * 2 == peers
        and 3 * rows // routes == LANES
        and tokens.shape[2] % (2 * LANES) == 0
    )


def solution(mesh):
    placed = (
        P(("dp", "fs"), "ep", None),
        P(("dp", "fs"), "ep", None),
        P(("dp", "fs"), None),
        P(("dp", "fs"), "ep", None),
        P(("dp", "fs"), "ep", None),
        P("fs"),
        P("fs", None),
        P("fs", None),
        P("fs"),
        P("fs", None),
        P("fs", None),
        P("fs", None),
        P("ep", "fs", None),
        P("ep", "fs", None),
        P("ep", "fs", None),
    )
    def layer(*arrays):
        fits = suits(mesh, arrays[0], arrays[9], arrays[12])
        return mapped(one_chip if fits else shards)(*arrays)

    def mapped(body):
        return jax.shard_map(
            body,
            mesh=mesh,
            in_specs=placed,
            out_specs=(
                P(("dp", "fs"), "ep", None),
                P(("dp", "fs"), "ep", None),
                P(("dp", "fs"), "ep", None),
                P(("ep", "dp", "fs")),
                P(("ep", "dp", "fs"), None),
                P(("ep", "dp", "fs"), None),
                P(("ep", "dp", "fs")),
                P(("ep", "dp", "fs"), None),
                P(("ep", "dp", "fs"), None),
                P(("ep", "dp", "fs"), None),
                P("ep", ("dp", "fs"), None),
                P("ep", ("dp", "fs"), None),
                P("ep", ("dp", "fs"), None),
            ),
            check_vma=False,
        )

    return layer
```

```python
import functools

import jax
import jax.numpy as jnp
from jax import lax
from jax.experimental import pallas as pl
from jax.experimental.pallas import tpu as pltpu
from jax.sharding import PartitionSpec as P

HEAD = 64
SEGS = 4


NORM_EPS = 1e-06
MASK_FILL = -1e30
HIGHEST = lax.Precision.HIGHEST


def rms_scale(values, gains):
    inverse = lax.rsqrt(jnp.mean(values * values, axis=-1, keepdims=True) + NORM_EPS)
    return values * inverse * gains


def small_softmax(logit_rows):
    largest = jnp.max(logit_rows, axis=-1, keepdims=True)
    powers = jnp.exp(logit_rows - largest)
    return powers / jnp.sum(powers, axis=-1, keepdims=True)


def add_tuple(first_tuple, second_tuple):
    if first_tuple is None:
        return second_tuple
    return tuple(
        (first_term + second_term for first_term, second_term in zip(first_tuple, second_tuple))
    )


def shards(
    tokens,
    prev_logits,
    segments,
    routes,
    cotangent,
    gain_attn,
    w_qkv,
    w_out,
    gain_moe,
    w_router,
    const_proj,
    const_vec,
    w_gate,
    w_up,
    w_down,
):
    micro_count, row_count, model_width = tokens.shape
    head_count = model_width // HEAD
    peer_count = lax.axis_size("ep")
    my_index = lax.axis_index("ep")
    route_count = w_router.shape[1]
    expert_count = route_count - 4
    half_count = peer_count // expert_count
    capacity = (3 * row_count // route_count + 7) // 8 * 8
    seq_length = row_count * peer_count
    slot_count = expert_count * capacity
    pos_all = jnp.arange(seq_length, dtype=jnp.int32)
    pos_mine = my_index * row_count + jnp.arange(row_count, dtype=jnp.int32)
    expert_ids = jnp.arange(expert_count, dtype=jnp.int32)
    slot_ids = jnp.arange(slot_count, dtype=jnp.int32)
    route_ids = jnp.arange(route_count, dtype=jnp.int32)
    layer_outputs = []
    input_grads = []
    prev_grads = []
    dense_acc = None
    expert_acc = None
    for step_index in range(micro_count):
        gathered = (
            lax.all_gather(w_qkv, "fs", axis=0, tiled=True),
            lax.all_gather(w_out, "fs", axis=0, tiled=True),
            lax.all_gather(w_router, "fs", axis=0, tiled=True),
            lax.all_gather(const_proj, "fs", axis=0, tiled=True),
            lax.all_gather(const_vec, "fs", axis=0, tiled=True),
            lax.all_gather(gain_attn, "fs", axis=0, tiled=True),
            lax.all_gather(gain_moe, "fs", axis=0, tiled=True),
            lax.all_gather(w_gate, "fs", axis=1, tiled=True),
            lax.all_gather(w_up, "fs", axis=1, tiled=True),
            lax.all_gather(w_down, "fs", axis=1, tiled=True),
        )
        (
            qkv_weight,
            out_weight,
            router_weight,
            cproj_weight,
            cvec_weight,
            attn_gain,
            moe_gain,
            gate_weight,
            up_weight,
            down_weight,
        ) = gathered
        gate_weight = gate_weight[0]
        up_weight = up_weight[0]
        down_weight = down_weight[0]
        attn_gain = attn_gain.astype(jnp.float32)
        moe_gain = moe_gain.astype(jnp.float32)
        router_float = router_weight.astype(jnp.float32)
        cproj_float = cproj_weight.astype(jnp.float32)
        cvec_float = cvec_weight.astype(jnp.float32)
        token_rows = tokens[step_index].astype(jnp.float32)
        seg_all = segments[step_index]
        seg_mine = lax.dynamic_slice_in_dim(seg_all, my_index * row_count, row_count)
        allowed = (seg_mine[:, None] == seg_all[None, :]) & (pos_all[None, :] <= pos_mine[:, None])
        valid_rows = (seg_mine != SEGS - 1).astype(jnp.float32)[:, None]
        normed = rms_scale(token_rows, attn_gain).astype(jnp.bfloat16)
        qkv_rows = jnp.dot(normed, qkv_weight, preferred_element_type=jnp.float32).astype(
            jnp.bfloat16
        )
        queries = qkv_rows[:, :model_width].reshape(row_count, head_count, HEAD)
        keys_local = qkv_rows[:, model_width : 2 * model_width]
        values_local = qkv_rows[:, 2 * model_width :]
        keys_all, values_all = (
            lax.all_gather(keys_local, "ep", axis=0, tiled=True),
            lax.all_gather(values_local, "ep", axis=0, tiled=True),
        )
        key_heads = keys_all.reshape(seq_length, head_count, HEAD)
        value_heads = values_all.reshape(seq_length, head_count, HEAD)
        scores = (
            jnp.einsum("qhd,khd->hqk", queries, key_heads, preferred_element_type=jnp.float32)
            * 0.125
        )
        scores = jnp.where(allowed[None], scores, MASK_FILL)
        largest = jnp.max(scores, axis=-1, keepdims=True)
        powers = jnp.exp(scores - largest)
        row_total = jnp.sum(powers, axis=-1, keepdims=True)
        log_total = largest + jnp.log(row_total)
        attn_probs = powers / row_total
        attended = jnp.einsum(
            "hqk,khd->qhd",
            attn_probs.astype(jnp.bfloat16),
            value_heads,
            preferred_element_type=jnp.float32,
        ).reshape(row_count, model_width)
        attended = (attended * valid_rows).astype(jnp.bfloat16)
        residual = token_rows + jnp.dot(attended, out_weight, preferred_element_type=jnp.float32)
        mixed = rms_scale(residual, moe_gain).astype(jnp.bfloat16)
        mixed_float = mixed.astype(jnp.float32)
        logits = (
            jnp.dot(mixed, router_weight, preferred_element_type=jnp.float32)
            + prev_logits[step_index]
        )
        router_probs = small_softmax(logits)
        route_rows = routes[step_index]
        choose = (route_rows[:, :, None] == route_ids[None, None, :]).astype(jnp.float32)
        gate_values = jnp.sum(choose * router_probs[:, None, :], axis=-1)
        const_logits = jnp.dot(mixed, cproj_weight, preferred_element_type=jnp.float32)
        mixings = []
        const_outs = []
        for const_index in range(2):
            mixing = small_softmax(const_logits[:, 2 * const_index : 2 * const_index + 2])
            mixings.append(mixing)
            const_outs.append(
                mixing[:, :1] * mixed_float + mixing[:, 1:] * cvec_float[:, const_index][None, :]
            )
        pair_route = route_rows.reshape(-1)
        expert_hit = (pair_route[:, None] == expert_ids[None, :]).astype(jnp.int32)
        slot_index = jnp.sum((jnp.cumsum(expert_hit, axis=0) - expert_hit) * expert_hit, axis=1)
        slot_cell = jnp.sum(expert_hit * expert_ids[None, :], axis=1) * capacity + slot_index
        slot_place = jnp.where(jnp.sum(expert_hit, axis=1) > 0, slot_cell, -1)
        slot_table = (slot_ids[:, None] == slot_place[None, :]).astype(jnp.bfloat16)
        pair_rows = jnp.repeat(mixed, 2, axis=0)
        packed = jnp.einsum(
            "sp,pd->sd", slot_table, pair_rows, preferred_element_type=jnp.float32
        ).astype(jnp.bfloat16)
        outgoing = jnp.broadcast_to(
            packed.reshape(expert_count, 1, capacity, model_width),
            (expert_count, half_count, capacity, model_width),
        ).reshape(peer_count, capacity, model_width)
        received = lax.all_to_all(outgoing, "ep", split_axis=0, concat_axis=0, tiled=True)
        flat_rows = received.reshape(-1, model_width)
        gate_part = jnp.dot(flat_rows, gate_weight, preferred_element_type=jnp.float32)
        up_part = jnp.dot(flat_rows, up_weight, preferred_element_type=jnp.float32)
        hidden = (jax.nn.silu(gate_part) * up_part).astype(jnp.bfloat16)
        part_out = (
            jnp.dot(hidden, down_weight, preferred_element_type=jnp.float32)
            .astype(jnp.bfloat16)
            .reshape(received.shape)
        )
        returned_rows = lax.all_to_all(part_out, "ep", split_axis=0, concat_axis=0, tiled=True)
        returned_rows, kept_rows = (returned_rows, received)
        halves = returned_rows.reshape(expert_count, half_count, capacity, model_width)
        pair_ffn = jnp.zeros((2 * row_count, model_width), jnp.float32)
        for half_index in range(half_count):
            pair_ffn = pair_ffn + jnp.einsum(
                "sp,sd->pd",
                slot_table,
                halves[:, half_index].reshape(slot_count, model_width),
                preferred_element_type=jnp.float32,
            )
        expert_out = pair_ffn.reshape(row_count, 2, model_width)
        expert_out = (
            expert_out + choose[:, :, expert_count + 1 : expert_count + 2] * mixed_float[:, None, :]
        )
        for const_index in range(2):
            column = expert_count + 2 + const_index
            expert_out = (
                expert_out + choose[:, :, column : column + 1] * const_outs[const_index][:, None, :]
            )
        result_rows = residual + jnp.sum(gate_values[:, :, None] * expert_out, axis=1)
        layer_outputs.append(result_rows.astype(jnp.bfloat16))
        grad_rows = cotangent[step_index].astype(jnp.float32)
        d_gates = jnp.sum(expert_out * grad_rows[:, None, :], axis=-1)
        d_probs = jnp.sum(choose * d_gates[:, :, None], axis=1)
        d_logits = router_probs * (
            d_probs - jnp.sum(router_probs * d_probs, axis=-1, keepdims=True)
        )
        prev_grads.append(d_logits)
        grad_router = jnp.dot(mixed_float.T, d_logits, precision=HIGHEST)
        d_mixed = jnp.dot(d_logits, router_float.T, precision=HIGHEST)
        weighted = gate_values[:, :, None] * grad_rows[:, None, :]
        d_mixed = d_mixed + jnp.sum(
            choose[:, :, expert_count + 1 : expert_count + 2] * weighted, axis=1
        )
        cproj_grads = []
        cvec_grads = []
        for const_index in range(2):
            column = expert_count + 2 + const_index
            mixing = mixings[const_index]
            d_const = jnp.sum(choose[:, :, column : column + 1] * weighted, axis=1)
            d_mix = jnp.stack(
                [
                    jnp.sum(d_const * mixed_float, axis=-1),
                    jnp.sum(d_const * cvec_float[:, const_index][None, :], axis=-1),
                ],
                axis=-1,
            )
            d_mixlog = mixing * (d_mix - jnp.sum(mixing * d_mix, axis=-1, keepdims=True))
            cproj_grads.append(jnp.dot(mixed_float.T, d_mixlog, precision=HIGHEST))
            cvec_grads.append(jnp.sum(mixing[:, 1:] * d_const, axis=0))
            d_mixed = (
                d_mixed
                + mixing[:, :1] * d_const
                + jnp.dot(
                    d_mixlog,
                    cproj_float[:, 2 * const_index : 2 * const_index + 2].T,
                    precision=HIGHEST,
                )
            )
        grad_cproj = jnp.concatenate(cproj_grads, axis=1)
        grad_cvec = jnp.stack(cvec_grads, axis=1)
        d_pairs = weighted.reshape(2 * row_count, model_width).astype(jnp.bfloat16)
        d_packed = jnp.einsum(
            "sp,pd->sd", slot_table, d_pairs, preferred_element_type=jnp.float32
        ).astype(jnp.bfloat16)
        d_outgoing = jnp.broadcast_to(
            d_packed.reshape(expert_count, 1, capacity, model_width),
            (expert_count, half_count, capacity, model_width),
        ).reshape(peer_count, capacity, model_width)
        d_received = lax.all_to_all(d_outgoing, "ep", split_axis=0, concat_axis=0, tiled=True)
        flat_rows = kept_rows.reshape(-1, model_width)
        flat_grads = d_received.reshape(-1, model_width)
        gate_part = jnp.dot(flat_rows, gate_weight, preferred_element_type=jnp.float32)
        up_part = jnp.dot(flat_rows, up_weight, preferred_element_type=jnp.float32)
        activated = jax.nn.silu(gate_part)
        hidden = (activated * up_part).astype(jnp.bfloat16)
        grad_down = jnp.einsum("rf,rd->fd", hidden, flat_grads, preferred_element_type=jnp.float32)
        d_hidden = jnp.einsum(
            "rd,fd->rf", flat_grads, down_weight, preferred_element_type=jnp.float32
        )
        sigmoid_gate = jax.nn.sigmoid(gate_part)
        d_gate_part = (
            d_hidden * up_part * sigmoid_gate * (1.0 + gate_part * (1.0 - sigmoid_gate))
        ).astype(jnp.bfloat16)
        d_up_part = (d_hidden * activated).astype(jnp.bfloat16)
        grad_gate = jnp.einsum(
            "rd,rf->df", flat_rows, d_gate_part, preferred_element_type=jnp.float32
        )
        grad_up = jnp.einsum("rd,rf->df", flat_rows, d_up_part, preferred_element_type=jnp.float32)
        d_inputs = jnp.einsum(
            "rf,df->rd", d_gate_part, gate_weight, preferred_element_type=jnp.float32
        )
        d_inputs = d_inputs + jnp.einsum(
            "rf,df->rd", d_up_part, up_weight, preferred_element_type=jnp.float32
        )
        d_inputs = d_inputs.astype(jnp.bfloat16).reshape(peer_count, capacity, model_width)
        d_returned = lax.all_to_all(d_inputs, "ep", split_axis=0, concat_axis=0, tiled=True)
        d_halves = d_returned.reshape(expert_count, half_count, capacity, model_width)
        for half_index in range(half_count):
            d_pair_in = jnp.einsum(
                "sp,sd->pd",
                slot_table,
                d_halves[:, half_index].reshape(slot_count, model_width),
                preferred_element_type=jnp.float32,
            )
            d_mixed = d_mixed + jnp.sum(d_pair_in.reshape(row_count, 2, model_width), axis=1)
        expert_acc = add_tuple(expert_acc, (grad_gate, grad_up, grad_down))
        moe_vjp = jax.vjp(rms_scale, residual, moe_gain)[1]
        d_residual_norm, grad_moe_gain = moe_vjp(d_mixed)
        d_residual = grad_rows + d_residual_norm
        d_branch = d_residual.astype(jnp.bfloat16)
        grad_out = jnp.einsum("rd,re->de", attended, d_branch, preferred_element_type=jnp.float32)
        d_attended = (
            jnp.einsum("re,de->rd", d_branch, out_weight, preferred_element_type=jnp.float32)
            * valid_rows
        ).astype(jnp.bfloat16)
        d_heads = d_attended.reshape(row_count, head_count, HEAD)
        scores = (
            jnp.einsum("qhd,khd->hqk", queries, key_heads, preferred_element_type=jnp.float32)
            * 0.125
        )
        scores = jnp.where(allowed[None], scores, MASK_FILL)
        attn_probs = jnp.exp(scores - log_total)
        d_weights = jnp.einsum(
            "qhd,khd->hqk", d_heads, value_heads, preferred_element_type=jnp.float32
        )
        delta_rows = jnp.sum(attn_probs * d_weights, axis=-1, keepdims=True)
        d_scores = (attn_probs * (d_weights - delta_rows)).astype(jnp.bfloat16)
        d_queries = (
            jnp.einsum(
                "hqk,khd->qhd", d_scores, key_heads, preferred_element_type=jnp.float32
            ).reshape(row_count, model_width)
            * 0.125
        )
        d_values = jnp.einsum(
            "hqk,qhd->khd",
            attn_probs.astype(jnp.bfloat16),
            d_heads,
            preferred_element_type=jnp.float32,
        ).reshape(seq_length, model_width)
        d_keys = (
            jnp.einsum(
                "hqk,qhd->khd", d_scores, queries, preferred_element_type=jnp.float32
            ).reshape(seq_length, model_width)
            * 0.125
        )
        d_keys_mine, d_values_mine = (
            lax.psum_scatter(
                d_keys.astype(jnp.bfloat16), "ep", scatter_dimension=0, tiled=True
            ).astype(jnp.float32),
            lax.psum_scatter(
                d_values.astype(jnp.bfloat16), "ep", scatter_dimension=0, tiled=True
            ).astype(jnp.float32),
        )
        d_qkv = jnp.concatenate([d_queries, d_keys_mine, d_values_mine], axis=1).astype(
            jnp.bfloat16
        )
        grad_qkv = jnp.einsum("rd,re->de", normed, d_qkv, preferred_element_type=jnp.float32)
        d_normed = jnp.einsum("re,de->rd", d_qkv, qkv_weight, preferred_element_type=jnp.float32)
        attn_vjp = jax.vjp(rms_scale, token_rows, attn_gain)[1]
        d_tokens_norm, grad_attn_gain = attn_vjp(d_normed)
        input_grads.append(d_residual + d_tokens_norm)
        dense_terms = (
            grad_attn_gain,
            grad_qkv,
            grad_out,
            grad_moe_gain,
            grad_router,
            grad_cproj,
            grad_cvec,
        )
        dense_shares = (
            lax.psum_scatter(dense_terms[0], ("ep", "dp", "fs"), scatter_dimension=0, tiled=True),
            lax.psum_scatter(dense_terms[1], ("ep", "dp", "fs"), scatter_dimension=0, tiled=True),
            lax.psum_scatter(dense_terms[2], ("ep", "dp", "fs"), scatter_dimension=0, tiled=True),
            lax.psum_scatter(dense_terms[3], ("ep", "dp", "fs"), scatter_dimension=0, tiled=True),
            lax.psum_scatter(dense_terms[4], ("ep", "dp", "fs"), scatter_dimension=0, tiled=True),
            lax.psum_scatter(dense_terms[5], ("ep", "dp", "fs"), scatter_dimension=0, tiled=True),
            lax.psum_scatter(dense_terms[6], ("ep", "dp", "fs"), scatter_dimension=0, tiled=True),
        )
        dense_acc = add_tuple(dense_acc, dense_shares)
    expert_shares = (
        lax.psum_scatter(
            expert_acc[0][None].astype(jnp.bfloat16), ("dp", "fs"), scatter_dimension=1, tiled=True
        ).astype(jnp.float32),
        lax.psum_scatter(
            expert_acc[1][None].astype(jnp.bfloat16), ("dp", "fs"), scatter_dimension=1, tiled=True
        ).astype(jnp.float32),
        lax.psum_scatter(
            expert_acc[2][None].astype(jnp.bfloat16), ("dp", "fs"), scatter_dimension=1, tiled=True
        ).astype(jnp.float32),
    )
    return (
        jnp.stack(layer_outputs),
        jnp.stack(input_grads),
        jnp.stack(prev_grads),
        dense_acc[0],
        dense_acc[1],
        dense_acc[2],
        dense_acc[3],
        dense_acc[4],
        dense_acc[5],
        dense_acc[6],
        expert_shares[0],
        expert_shares[1],
        expert_shares[2],
    )


NEG = -1e30
KINDS = 2
SMALL = 16
LANES = 128
F32 = jnp.float32
BF16 = jnp.bfloat16


def dot(lhs, rhs, dims=((1,), (0,)), precision=None):
    return lax.dot_general(
        lhs, rhs, (dims, ((), ())), precision=precision, preferred_element_type=F32
    )


def norm_qkv_kernel(x_ref, gain_ref, w_ref, normed_ref, qkv_ref):
    rows = x_ref[...].astype(F32)
    inverse = lax.rsqrt(jnp.mean(rows * rows, axis=-1, keepdims=True) + NORM_EPS)
    normed = (rows * inverse * gain_ref[...]).astype(BF16)
    normed_ref[...] = normed
    qkv_ref[...] = dot(normed, w_ref[...]).astype(BF16)


def key_span(block, rows, reach):
    start = max(0, block * rows - reach)
    return start, (block + 1) * rows - start


def attend_kernel(rows, reach, q_ref, k_ref, v_ref, segc_ref, segr_ref, att_ref, lse_ref):
    length = q_ref.shape[0]
    for block in range(length // rows):
        start, width = key_span(block, rows, reach)
        queries = q_ref[block * rows : (block + 1) * rows, :]
        keys = k_ref[start : start + width, :]
        values = v_ref[start : start + width, :]
        seg_q = segc_ref[block * rows : (block + 1) * rows, :]
        seg_k = segr_ref[:, start : start + width]
        row_pos = block * rows + lax.broadcasted_iota(jnp.int32, (rows, width), 0)
        col_pos = start + lax.broadcasted_iota(jnp.int32, (rows, width), 1)
        allowed = (seg_q == seg_k) & (col_pos <= row_pos)
        lane = lax.broadcasted_iota(jnp.int32, (rows, LANES), 1)
        outs = []
        logs = []
        for head in range(2):
            mine = (lane // HEAD) == head
            scores = dot(jnp.where(mine, queries, 0), keys, ((1,), (1,))) * 0.125
            scores = jnp.where(allowed, scores, NEG)
            largest = jnp.max(scores, axis=-1, keepdims=True)
            powers = jnp.exp(scores - largest)
            total = jnp.sum(powers, axis=-1, keepdims=True)
            outs.append(dot(powers.astype(BF16), values) / total)
            logs.append(largest + jnp.log(total))
        valid = (seg_q != SEGS - 1).astype(F32)
        att = jnp.where(lane < HEAD, outs[0], outs[1]) * valid
        att_ref[block * rows : (block + 1) * rows, :] = att.astype(BF16)
        both = jnp.where(lane < HEAD, logs[0], logs[1]).T
        lse_ref[0, 0:1, block * rows : (block + 1) * rows] = both[0:1, :]
        lse_ref[0, 1:2, block * rows : (block + 1) * rows] = both[HEAD : HEAD + 1, :]


def attend_back_kernel(
    rows, reach, q_ref, k_ref, v_ref, do_ref, segc_ref, segr_ref, lse_ref,
    dq_ref, dk_ref, dv_ref, dk_sum, dv_sum,
):
    length = q_ref.shape[0]
    dk_sum[...] = jnp.zeros_like(dk_sum)
    dv_sum[...] = jnp.zeros_like(dv_sum)
    keys_turned = k_ref[...].T
    for block in range(length // rows):
        start, width = key_span(block, rows, reach)
        queries = q_ref[block * rows : (block + 1) * rows, :]
        grads = do_ref[block * rows : (block + 1) * rows, :]
        keys = k_ref[start : start + width, :]
        values = v_ref[start : start + width, :]
        seg_k = segc_ref[start : start + width, :]
        seg_q = segr_ref[:, block * rows : (block + 1) * rows]
        key_pos = start + lax.broadcasted_iota(jnp.int32, (width, rows), 0)
        query_pos = block * rows + lax.broadcasted_iota(jnp.int32, (width, rows), 1)
        allowed = (seg_q == seg_k) & (key_pos <= query_pos)
        lane = lax.broadcasted_iota(jnp.int32, (rows, LANES), 1)
        dq_parts = []
        for head in range(2):
            mine = (lane // HEAD) == head
            head_q = jnp.where(mine, queries, 0)
            head_g = jnp.where(mine, grads, 0)
            log_total = lse_ref[0, head : head + 1, block * rows : (block + 1) * rows]
            scores = dot(keys, head_q, ((1,), (1,))) * 0.125
            probs = jnp.exp(jnp.where(allowed, scores, NEG) - log_total)
            d_probs = dot(values, head_g, ((1,), (1,)))
            delta = jnp.sum(probs * d_probs, axis=0, keepdims=True)
            d_scores = (probs * (d_probs - delta)).astype(BF16)
            dv_sum[start : start + width, :] += dot(probs.astype(BF16), head_g)
            dk_sum[start : start + width, :] += dot(d_scores, head_q)
            turned = keys_turned[head * HEAD : (head + 1) * HEAD, start : start + width]
            dq_parts.append(dot(turned, d_scores))
        dq = jnp.concatenate(dq_parts, axis=0).T * 0.125
        dq_ref[block * rows : (block + 1) * rows, :] = dq.astype(BF16)
    dk_ref[...] = (dk_sum[...] * 0.125).astype(BF16)
    dv_ref[...] = dv_sum[...].astype(BF16)


def column(rows, index):
    return rows[:, index : index + 1]


def chosen_of(ctl):
    lane = lax.broadcasted_iota(jnp.int32, ctl.shape, 1).astype(F32)
    return ((lane == column(ctl, 8)) | (lane == column(ctl, 9))).astype(F32)


def spread_kernel(
    experts, routes, att_own_ref, att_sib_ref, x_ref, g_ref, ctl_ref, w_own_ref, w_sib_ref,
    gain_ref, wsm_ref, residual_ref, mixed_ref, pm_ref, place_ref, send_ref,
):
    rows = x_ref.shape[0]
    residual = x_ref[...].astype(F32) + (
        dot(att_own_ref[...], w_own_ref[...]) + dot(att_sib_ref[...], w_sib_ref[...])
    )
    residual_ref[...] = residual
    inverse = lax.rsqrt(jnp.mean(residual * residual, axis=-1, keepdims=True) + NORM_EPS)
    mixed = (residual * inverse * gain_ref[...]).astype(BF16)
    mixed_ref[...] = mixed
    logits = dot(mixed, wsm_ref[...])
    ctl = ctl_ref[...]
    lane = lax.broadcasted_iota(jnp.int32, (rows, LANES), 1)
    is_route = lane < routes
    router = jnp.where(is_route, logits + ctl, NEG)
    powers = jnp.exp(router - jnp.max(router, axis=-1, keepdims=True))
    probs = powers / jnp.sum(powers, axis=-1, keepdims=True)
    probs = jnp.where(is_route, probs, 0.0)
    pm = probs
    for const_index in range(2):
        first = column(logits, 8 + 2 * const_index)
        second = column(logits, 9 + 2 * const_index)
        largest = jnp.maximum(first, second)
        first = jnp.exp(first - largest)
        second = jnp.exp(second - largest)
        total = first + second
        pm = jnp.where(lane == 8 + 2 * const_index, first / total, pm)
        pm = jnp.where(lane == 9 + 2 * const_index, second / total, pm)
    pm_ref[...] = pm
    chosen = chosen_of(ctl)
    gated = chosen * probs
    earlier = lax.broadcasted_iota(jnp.int32, (rows, rows), 1) < lax.broadcasted_iota(
        jnp.int32, (rows, rows), 0
    )
    rank = dot(earlier.astype(BF16), chosen.astype(BF16))
    lane_f = lane.astype(F32)
    halves = send_ref.shape[0] // experts
    for expert in range(experts):
        place = jnp.where(
            (lane_f == column(rank, expert)) & (column(chosen, expert) > 0.0), 1.0, 0.0
        )
        place_ref[:, expert * LANES : (expert + 1) * LANES] = place.astype(BF16)
        pick = place.T.astype(BF16)
        d_part = (column(gated, expert) * g_ref[...].astype(F32)).astype(BF16)
        packed = dot(pick, mixed).astype(BF16)
        d_packed = dot(pick, d_part).astype(BF16)
        for half in range(halves):
            send_ref[expert * halves + half, 0, 0] = packed
            send_ref[expert * halves + half, 1, 0] = d_packed


def expert_kernel(in_ref, gate_ref, up_ref, down_ref, out_ref, hidden_ref, dgate_ref, dup_ref):
    size = in_ref.shape[2] * in_ref.shape[3]
    width = in_ref.shape[4]
    rows = in_ref[0, 0].reshape(size, width)
    d_rows = in_ref[0, 1].reshape(size, width)
    gate = dot(rows, gate_ref[...])
    up = dot(rows, up_ref[...])
    sig = jax.nn.sigmoid(gate)
    active = gate * sig
    hidden = (active * up).astype(BF16)
    hidden_ref[...] = hidden
    part = dot(hidden, down_ref[...]).astype(BF16)
    out_ref[0, 0] = part.reshape(in_ref.shape[2:])
    d_hidden = dot(d_rows, down_ref[...], ((1,), (1,)))
    d_gate = (d_hidden * up * sig * (1.0 + gate * (1.0 - sig))).astype(BF16)
    d_up = (d_hidden * active).astype(BF16)
    dgate_ref[...] = d_gate
    dup_ref[...] = d_up
    d_in = dot(d_gate, gate_ref[...], ((1,), (1,))) + dot(d_up, up_ref[...], ((1,), (1,)))
    out_ref[0, 1] = d_in.astype(BF16).reshape(in_ref.shape[2:])


def combine_kernel(
    experts, routes, residual_ref, mixed_ref, pm_ref, ctl_ref, place_ref, back_ref, g_ref,
    gain_ref, turned_ref, cvec_ref, out_ref, prev_ref, dres_ref, branch_ref, small_ref,
):
    halves = back_ref.shape[0] // experts
    rows = g_ref.shape[0]
    grads = g_ref[...].astype(F32)
    mixed = mixed_ref[...].astype(F32)
    residual = residual_ref[...]
    pm = pm_ref[...]
    lane = lax.broadcasted_iota(jnp.int32, (rows, LANES), 1)
    chosen = chosen_of(ctl_ref[...])
    probs = jnp.where(lane < routes, pm, 0.0)
    gated = chosen * probs
    d_probs = jnp.zeros((rows, LANES), F32)
    result = residual
    d_mixed = None
    for expert in range(experts):
        place = place_ref[:, expert * LANES : (expert + 1) * LANES]
        expert_out = None
        for half in range(halves):
            owner = expert * halves + half
            term = dot(place, back_ref[owner, 0, 0])
            expert_out = term if expert_out is None else expert_out + term
            term = dot(place, back_ref[owner, 1, 0])
            d_mixed = term if d_mixed is None else d_mixed + term
        result = result + column(gated, expert) * expert_out
        d_gate = jnp.sum(expert_out * grads, axis=-1, keepdims=True)
        d_probs = jnp.where(lane == expert, d_gate, d_probs)
    turned = turned_ref[...]
    g_mixed = jnp.sum(grads * mixed, axis=-1, keepdims=True)
    g_const = dot(g_ref[...], cvec_ref[...], ((1,), (1,)))
    copy = experts + 1
    d_probs = jnp.where(lane == copy, g_mixed, d_probs)
    mixed_weight = column(gated, copy)
    grad_weight = column(gated, copy)
    d_small = jnp.zeros((rows, LANES), F32)
    for const_index in range(2):
        route = copy + 1 + const_index
        first = column(pm, 8 + 2 * const_index)
        second = column(pm, 9 + 2 * const_index)
        gate = column(gated, route)
        g_vec = column(g_const, const_index)
        d_probs = jnp.where(lane == route, first * g_mixed + second * g_vec, d_probs)
        mixed_weight = mixed_weight + gate * first
        grad_weight = grad_weight + gate * first
        vec = cvec_ref[const_index : const_index + 1, :].astype(F32)
        result = result + (gate * second) * vec
        d_first = gate * g_mixed
        d_second = gate * g_vec
        mean = first * d_first + second * d_second
        d_small = jnp.where(lane == 8 + 2 * const_index, first * (d_first - mean), d_small)
        d_small = jnp.where(lane == 9 + 2 * const_index, second * (d_second - mean), d_small)
        d_small = jnp.where(lane == 12 + const_index, gate * second, d_small)
    result = result + mixed_weight * mixed
    out_ref[...] = result.astype(BF16)
    d_probs = d_probs * chosen
    d_logits = probs * (d_probs - jnp.sum(probs * d_probs, axis=-1, keepdims=True))
    d_small = jnp.where(lane < routes, d_logits, d_small)
    d_mixed = d_mixed + grad_weight * grads
    d_mixed = d_mixed + dot(
        jnp.where(lane < 12, d_small, 0.0), turned, precision=HIGHEST
    )
    inverse = lax.rsqrt(jnp.mean(residual * residual, axis=-1, keepdims=True) + NORM_EPS)
    scaled = d_mixed * gain_ref[...]
    mean = jnp.mean(scaled * residual, axis=-1, keepdims=True)
    d_residual = grads + inverse * scaled - residual * (inverse * inverse * inverse * mean)
    dres_ref[...] = d_residual
    branch_ref[...] = d_residual.astype(BF16)
    d_turned = d_small.T[:SMALL, :]
    prev_ref[0] = d_turned[:8, :]
    sub = lax.broadcasted_iota(jnp.int32, (SMALL, rows), 0)
    small = dot(jnp.where(sub < 12, d_turned, 0.0), mixed, precision=HIGHEST)
    small = small + dot(
        jnp.where((sub >= 12) & (sub < 14), d_turned, 0.0), grads, precision=HIGHEST
    )
    d_gain = jnp.sum(d_mixed * residual * inverse, axis=0, keepdims=True)
    which = lax.broadcasted_iota(jnp.int32, small.shape, 0)
    small = jnp.where(which == 14, d_gain, small)

    @pl.when(pl.program_id(0) == 0)
    def _():
        small_ref[...] = jnp.zeros_like(small_ref)

    small_ref[...] += small


def finish_kernel(x_ref, own_ref, sib_ref, dres_ref, gain_ref, out_ref, gain_out_ref):
    rows = x_ref[...].astype(F32)
    d_normed = own_ref[...].astype(F32) + sib_ref[...].astype(F32)
    inverse = lax.rsqrt(jnp.mean(rows * rows, axis=-1, keepdims=True) + NORM_EPS)
    scaled = d_normed * gain_ref[...]
    mean = jnp.mean(scaled * rows, axis=-1, keepdims=True)
    out = dres_ref[...] + inverse * scaled - rows * (inverse * inverse * inverse * mean)
    out_ref[...] = out.astype(out_ref.dtype)

    @pl.when(pl.program_id(0) == 0)
    def _():
        gain_out_ref[...] = jnp.zeros_like(gain_out_ref)

    gain_out_ref[0:1, :] += jnp.sum(d_normed * rows * inverse, axis=0, keepdims=True)


def shape(dims, dtype):
    return jax.ShapeDtypeStruct(dims, dtype)


def whole(dims):
    return pl.BlockSpec(dims, lambda *_: (0,) * len(dims))


def per_row(rows, width):
    return pl.BlockSpec((rows, width), lambda i: (i, 0))


def params():
    return pltpu.CompilerParams(vmem_limit_bytes=56 * 1024 * 1024)


def cost(flops, moved):
    return pl.CostEstimate(flops=int(flops), bytes_accessed=int(moved), transcendentals=0)


class Mail:
    def __init__(self, send_sems, recv_sems):
        self.send_sems = send_sems
        self.recv_sems = recv_sems
        self.used = 0

    def copy(self, source, target, device):
        slot = self.used
        self.used = slot + 1
        return pltpu.make_async_remote_copy(
            src_ref=source,
            dst_ref=target,
            send_sem=self.send_sems.at[slot],
            recv_sem=self.recv_sems.at[slot],
            device_id=device,
            device_id_type=pl.DeviceIdType.MESH,
        )


def position():
    place = lax.axis_index("ep")
    return place // 2, place % 2, lax.axis_index("dp"), lax.axis_index("fs")


def greet(devices):
    barrier = pltpu.get_barrier_semaphore()
    total = 0
    for device, present in devices:
        if present is True:
            pl.semaphore_signal(
                barrier, inc=1, device_id=device, device_id_type=pl.DeviceIdType.MESH
            )
            total = total + 1
        else:

            @pl.when(present)
            def _():
                pl.semaphore_signal(
                    barrier, inc=1, device_id=device, device_id_type=pl.DeviceIdType.MESH
                )

            total = total + jnp.where(present, 1, 0)
    pl.semaphore_wait(barrier, total)


class Line:
    def __init__(self, mail, depth, slots):
        self.depth = depth
        self.slots = slots
        self.place = lax.axis_index("dp")
        y, x, z, core = position()
        self.copies = {}
        for way in range(2):
            step_to = 1 if way == 0 else -1
            device = (y * 2 + x, z + step_to, core)
            for step in range(depth - 1):
                for item, (acc, landing) in enumerate(slots):
                    shard = self.shard(way, step)
                    safe = jnp.clip(shard, 0, depth - 1)
                    self.copies[way, step, item] = mail.copy(
                        acc.at[safe], landing.at[way, step], device
                    )

    def shard(self, way, step):
        if way == 0:
            return self.place + self.depth - 1 - step
        return self.place - (self.depth - 1 - step)

    def sends(self, way, step):
        shard = self.shard(way, step)
        if way == 0:
            return (shard <= self.depth - 1) & (self.place < self.depth - 1)
        return (shard >= 0) & (self.place > 0)

    def gets(self, way, step):
        if way == 0:
            return (self.place > 0) & (self.shard(way, step + 1) <= self.depth - 1)
        return (self.place < self.depth - 1) & (self.shard(way, step + 1) >= 0)

    def send(self, step, item):
        for way in range(2):

            @pl.when(self.sends(way, step))
            def _():
                self.copies[way, step, item].start()

    def take(self, step, item):
        acc, landing = self.slots[item]
        for way in range(2):
            shard = jnp.clip(self.shard(way, step + 1), 0, self.depth - 1)

            @pl.when(self.gets(way, step))
            def _():
                self.copies[way, step, item].wait_recv()
                acc[shard] = (
                    acc[shard].astype(F32) + landing[way, step].astype(F32)
                ).astype(BF16)

    def finish(self, item, store):
        acc, landing = self.slots[item]
        store(acc[self.place].astype(F32))
        for way in range(2):

            @pl.when(self.gets(way, self.depth - 2))
            def _():
                self.copies[way, self.depth - 2, item].wait_recv()
                store(landing[way, self.depth - 2].astype(F32), True)

    def close(self):
        for (way, step, item), copy in self.copies.items():

            @pl.when(self.sends(way, step))
            def _():
                copy.wait_send()


def reduce_kernel(
    depth, cut,
    gate_ref, up_ref, down_ref, dense_ref, out_ref, dtok_ref, prev_ref,
    gate_out, up_out, down_out, own_out, sib_out, out_home, dtok_home, prev_home,
    gate_land, up_land, down_land, gate_acc, up_acc, down_acc,
    gate_line, up_line, down_line,
    y1_land, x1_land, y1_acc, x1_acc, x2_land, y2_land, dense_acc, dense_line, dense_sum,
    send_sems, recv_sems, local_sems,
):
    y, x, z, core = position()
    sibling = (y * 2 + x, z, 1 - core)
    across = (y * 2 + 1 - x, z, core)
    along = ((1 - y) * 2 + x, z, core)
    moved = y != core
    near = ((1 - y) * 2 + x, z, 1 - core)
    far = (core * 2 + 1 - x, z, y)
    greet(
        [
            (sibling, True), (across, True), (along, True),
            (near, moved), (far, moved),
            ((y * 2 + x, z + 1, core), z < depth - 1), ((y * 2 + x, z - 1, core), z > 0),
        ]
    )
    mail = Mail(send_sems, recv_sems)
    experts = [
        (gate_ref, gate_land, gate_acc, gate_line, gate_out),
        (up_ref, up_land, up_acc, up_line, up_out),
        (down_ref, down_land, down_acc, down_line, down_out),
    ]
    halves = [
        mail.copy(source.at[:, 1 - core], land, sibling)
        for source, land, _, _, _ in experts
    ]
    line = Line(mail, depth, [(acc, landing) for _, _, acc, landing, _ in experts])
    rest = dense_ref.shape[3] - cut
    left = pl.ds(0, cut)
    right = pl.ds(cut, rest)
    first_y = mail.copy(dense_ref.at[1 - y, :, :, left], y1_land, along)
    first_x = mail.copy(dense_ref.at[:, 1 - x, :, right], x1_land, across)
    second_x = mail.copy(y1_acc.at[1 - x], x2_land, across)
    second_y = mail.copy(x1_acc.at[1 - y], y2_land, along)
    dense = Line(mail, depth, [(dense_acc, dense_line)])
    homes = [(out_ref, out_home), (dtok_ref, dtok_home), (prev_ref, prev_home)]
    nears = [mail.copy(a.at[x], b.at[x], near) for a, b in homes]
    fars = [mail.copy(a.at[1 - x], b.at[x], far) for a, b in homes]
    stays = [
        pltpu.make_async_copy(a.at[x], b.at[x], local_sems.at[k])
        for k, (a, b) in enumerate(homes)
    ]

    for copy in halves:
        copy.start()
    first_y.start()
    first_x.start()
    for item, (source, land, acc, _, _) in enumerate(experts):
        halves[item].wait_recv()
        for shard in range(depth):
            acc[shard] = (source[shard, core].astype(F32) + land[shard].astype(F32)).astype(BF16)
        line.send(0, item)
    first_y.wait_recv()
    for k in range(2):
        y1_acc[k] = (dense_ref[y, k, :, left].astype(F32) + y1_land[k].astype(F32)).astype(BF16)
    second_x.start()
    first_x.wait_recv()
    for k in range(2):
        x1_acc[k] = (dense_ref[k, x, :, right].astype(F32) + x1_land[k].astype(F32)).astype(BF16)
    second_y.start()
    for copy in fars:
        copy.start()

    @pl.when(moved)
    def _():
        for copy in nears:
            copy.start()

    @pl.when(jnp.logical_not(moved))
    def _():
        for copy in stays:
            copy.start()

    for item in range(3):
        line.take(0, item)
        line.send(1, item)
    size = dense_acc.shape[1]
    second_x.wait_recv()
    second_y.wait_recv()
    for shard in range(depth):
        part = pl.ds(shard * size, size)
        dense_acc[shard, :, left] = (
            y1_acc[x, part].astype(F32) + x2_land[part].astype(F32)
        ).astype(BF16)
        dense_acc[shard, :, right] = (
            x1_acc[y, part].astype(F32) + y2_land[part].astype(F32)
        ).astype(BF16)
    dense.send(0, 0)
    for item in range(3):
        line.take(1, item)
        line.send(2, item)
    dense.take(0, 0)
    dense.send(1, 0)
    for item, (_, _, _, _, result) in enumerate(experts):

        def store(value, add=False):
            result[0] = result[0] + value if add else value

        line.finish(item, store)
    dense.take(1, 0)
    dense.send(2, 0)

    def store_dense(value, add=False):
        dense_sum[...] = dense_sum[...] + value if add else value

    dense.finish(0, store_dense)
    half = size // 2
    last = mail.copy(
        dense_sum.at[pl.ds(pl.multiple_of((1 - core) * half, 8), half)], sib_out, sibling
    )
    last.start()
    own_out[...] = dense_sum[pl.ds(pl.multiple_of(core * half, 8), half), :]
    last.wait()
    for copy in halves + [first_y, first_x, second_x, second_y]:
        copy.wait_send()
    line.close()
    dense.close()
    for copy in fars:
        copy.wait()

    @pl.when(moved)
    def _():
        for copy in nears:
            copy.wait()

    @pl.when(jnp.logical_not(moved))
    def _():
        for copy in stays:
            copy.wait()


def reduce_all(grad_gate, grad_up, grad_down, dense, block_out, d_tokens, d_prev):
    depth = lax.axis_size("dp")
    rows, width = block_out.shape
    experts = [
        grad.reshape(depth, 2, grad.shape[0] // (2 * depth), grad.shape[1])
        for grad in (grad_gate, grad_up, grad_down)
    ]
    quarter = dense.shape[0] // 4
    columns = dense.shape[1]
    cut = (columns // LANES + 1) // 2 * LANES
    dense = dense.reshape(2, 2, quarter, columns)
    homes = [
        block_out.reshape(2, rows // 2, width),
        d_tokens.reshape(2, rows // 2, width),
        d_prev,
    ]
    size = quarter // depth
    parts = [grad.shape[2:] for grad in experts]
    vmem = pl.BlockSpec(memory_space=pltpu.VMEM)
    copies = 3 + 2 * (depth - 1) * 4 + 4 + 6 + 1
    outs = pl.pallas_call(
        functools.partial(reduce_kernel, depth, cut),
        in_specs=[vmem] * 7,
        out_specs=[vmem] * 8,
        out_shape=[shape((1,) + part, F32) for part in parts]
        + [shape((size // 2, columns), F32)] * 2
        + [shape(home.shape, home.dtype) for home in homes],
        scratch_shapes=[pltpu.VMEM((depth,) + part, BF16) for part in parts] * 2
        + [pltpu.VMEM((2, depth - 1) + part, BF16) for part in parts]
        + [
            pltpu.VMEM((2, quarter, cut), BF16),
            pltpu.VMEM((2, quarter, columns - cut), BF16),
            pltpu.VMEM((2, quarter, cut), BF16),
            pltpu.VMEM((2, quarter, columns - cut), BF16),
            pltpu.VMEM((quarter, cut), BF16),
            pltpu.VMEM((quarter, columns - cut), BF16),
            pltpu.VMEM((depth, size, columns), BF16),
            pltpu.VMEM((2, depth - 1, size, columns), BF16),
            pltpu.VMEM((size, columns), F32),
            pltpu.SemaphoreType.DMA((copies,)),
            pltpu.SemaphoreType.DMA((copies,)),
            pltpu.SemaphoreType.DMA((3,)),
        ],
        compiler_params=pltpu.CompilerParams(
            collective_id=1, has_side_effects=True, vmem_limit_bytes=60 * 1024 * 1024
        ),
        name="reduce_all",
    )(*experts, dense, *homes)
    return outs


def one_chip(
    tokens,
    prev_logits,
    segments,
    routes,
    cotangent,
    gain_attn,
    w_qkv,
    w_out,
    gain_moe,
    w_router,
    const_proj,
    const_vec,
    w_gate,
    w_up,
    w_down,
):
    rows, width = tokens.shape[1:]
    peers = lax.axis_size("ep")
    place = lax.axis_index("ep")
    core = lax.axis_index("fs")
    cross = place % 2
    route_count = w_router.shape[1]
    experts = route_count - 4
    capacity = LANES
    length = rows * peers
    mine = length // 2
    span = width // 2
    hidden_width = w_gate.shape[2]
    pairs = [[], []]
    for flip in range(2):
        for source in range(peers):
            for side in range(2):
                target = side * 2 + ((source % 2) ^ flip)
                pairs[flip].append((source * 2 + side, target * 2 + source // 2))

    def swap(array):
        return lax.ppermute(array, "fs", [(0, 1), (1, 0)])

    def by_core(own, other, axis=0):
        return jnp.where(
            core == 0,
            jnp.concatenate([own, other], axis=axis),
            jnp.concatenate([other, own], axis=axis),
        )

    def to_chip(array):
        near = lax.ppermute(
            lax.dynamic_index_in_dim(array, cross, 0, False), ("ep", "fs"), pairs[0]
        )
        far = lax.ppermute(
            lax.dynamic_index_in_dim(array, 1 - cross, 0, False), ("ep", "fs"), pairs[1]
        )
        return jnp.where(
            cross == 0, jnp.concatenate([near, far]), jnp.concatenate([far, near])
        )

    x_own = to_chip(tokens)
    x_sib = swap(x_own)
    qkv_split = w_qkv.reshape(span, 3, 2, span)
    qkv_mine = lax.dynamic_index_in_dim(qkv_split, core, 2, False).reshape(span, 3 * span)
    qkv_sent = lax.dynamic_index_in_dim(qkv_split, 1 - core, 2, False).reshape(span, 3 * span)
    qkv_weight = by_core(qkv_mine, swap(qkv_sent))
    out_sib = swap(w_out)
    pad = jnp.zeros((span, 8 - route_count), BF16)
    small_own = jnp.concatenate(
        [w_router, pad, const_proj, const_vec, gain_attn[:, None], gain_moe[:, None]], axis=1
    )
    small_all = by_core(small_own, swap(small_own))
    small_turned = small_all.T.astype(F32)
    attn_gain = small_turned[14:15]
    moe_gain = small_turned[15:16]
    wsm = jnp.pad(small_all[:, :12], ((0, 0), (0, LANES - 12)))
    turned = jnp.pad(small_turned[:12], ((0, LANES - 12), (0, 0)))
    cvec_turned = jnp.pad(small_all[:, 12:14].T, ((0, LANES - 2), (0, 0)))
    gate_weight = by_core(w_gate[0], swap(w_gate[0]))
    up_weight = by_core(w_up[0], swap(w_up[0]))
    down_weight = by_core(w_down[0], swap(w_down[0]))
    seg_sib = swap(segments)
    seg_pair = by_core(segments[None], seg_sib[None])
    seg_row = seg_pair.reshape(4, length)[place][None, :]
    seg_col = seg_row.reshape(length, 1)

    x_all = by_core(x_own, x_sib)
    normed, qkv = pl.pallas_call(
        norm_qkv_kernel,
        grid=(length // rows,),
        in_specs=[per_row(rows, width), whole((1, width)), whole((width, 3 * span))],
        out_specs=[per_row(rows, width), per_row(rows, 3 * span)],
        out_shape=[shape((length, width), BF16), shape((length, 3 * span), BF16)],
        compiler_params=params(),
        cost_estimate=cost(2 * length * width * 3 * span, 6e6),
        name="norm_qkv",
    )(x_all, attn_gain, qkv_weight)

    head_pairs = span // LANES
    reach = length // 2

    def heads_at(offset):
        return pl.BlockSpec((length, LANES), lambda p: (0, offset + p))

    lse_spec = pl.BlockSpec((1, 8, length), lambda p: (p, 0, 0))
    attended, lse = pl.pallas_call(
        functools.partial(attend_kernel, rows, reach),
        grid=(head_pairs,),
        in_specs=[
            heads_at(0), heads_at(head_pairs), heads_at(2 * head_pairs),
            whole((length, 1)), whole((1, length)),
        ],
        out_specs=[heads_at(0), lse_spec],
        out_shape=[shape((length, span), BF16), shape((head_pairs, 8, length), F32)],
        compiler_params=params(),
        cost_estimate=cost(12e9, 4e6),
        name="attend",
    )(qkv, qkv, qkv, seg_col, seg_row)

    att_own = lax.dynamic_slice_in_dim(attended, core * mine, mine)
    att_sib = swap(lax.dynamic_slice_in_dim(attended, (1 - core) * mine, mine))
    cot_own = to_chip(cotangent)
    ctl = jnp.concatenate(
        [
            prev_logits,
            jnp.zeros(prev_logits.shape[:2] + (8 - route_count,), F32),
            routes.astype(F32),
        ],
        axis=2,
    )
    ctl = jnp.pad(to_chip(ctl), ((0, 0), (0, LANES - 10)))
    blocks = mine // rows
    send_dims = (peers, KINDS, blocks, capacity, width)
    send_spec = pl.BlockSpec(
        (peers, KINDS, 1, capacity, width), lambda b: (0, 0, b, 0, 0)
    )
    residual, mixed, pm, places, sent = pl.pallas_call(
        functools.partial(spread_kernel, experts, route_count),
        grid=(blocks,),
        in_specs=[
            per_row(rows, span), per_row(rows, span), per_row(rows, width),
            per_row(rows, width), per_row(rows, LANES), whole((span, width)),
            whole((span, width)), whole((1, width)), whole((width, LANES)),
        ],
        out_specs=[
            per_row(rows, width), per_row(rows, width), per_row(rows, LANES),
            per_row(rows, experts * LANES), send_spec,
        ],
        out_shape=[
            shape((mine, width), F32), shape((mine, width), BF16), shape((mine, LANES), F32),
            shape((mine, experts * LANES), BF16), shape(send_dims, BF16),
        ],
        compiler_params=params(),
        cost_estimate=cost(2e9, 8e6),
        name="spread",
    )(att_own, att_sib, x_own, cot_own, ctl, w_out, out_sib, moe_gain, wsm)

    received = lax.all_to_all(sent, "ep", split_axis=0, concat_axis=0, tiled=True)
    group = blocks * capacity
    item_spec = pl.BlockSpec(
        (1, KINDS, blocks, capacity, width), lambda s: (s, 0, 0, 0, 0)
    )
    results, hidden, d_gate, d_up = pl.pallas_call(
        expert_kernel,
        grid=(peers,),
        in_specs=[
            item_spec, whole((width, hidden_width)), whole((width, hidden_width)),
            whole((hidden_width, width)),
        ],
        out_specs=[item_spec] + [per_row(group, hidden_width)] * 3,
        out_shape=[shape(send_dims, BF16)] + [shape((peers * group, hidden_width), BF16)] * 3,
        compiler_params=params(),
        cost_estimate=cost(10e9, 15e6),
        name="experts",
    )(received, gate_weight, up_weight, down_weight)
    returned = lax.all_to_all(results, "ep", split_axis=0, concat_axis=0, tiled=True)
    flat_rows = received[:, 0].reshape(peers * group, width)
    flat_grads = received[:, 1].reshape(peers * group, width)
    grad_gate = dot(flat_rows, d_gate, ((0,), (0,))).astype(BF16)
    grad_up = dot(flat_rows, d_up, ((0,), (0,))).astype(BF16)
    grad_down = dot(hidden, flat_grads, ((0,), (0,))).astype(BF16)

    block_out, d_prev, d_residual, d_branch, small = pl.pallas_call(
        functools.partial(combine_kernel, experts, route_count),
        grid=(blocks,),
        in_specs=[
            per_row(rows, width), per_row(rows, width), per_row(rows, LANES),
            per_row(rows, LANES), per_row(rows, experts * LANES), send_spec,
            per_row(rows, width), whole((1, width)), whole((LANES, width)),
            whole((LANES, width)),
        ],
        out_specs=[
            per_row(rows, width), pl.BlockSpec((1, 8, rows), lambda b: (b, 0, 0)),
            per_row(rows, width), per_row(rows, width), whole((SMALL, width)),
        ],
        out_shape=[
            shape((mine, width), BF16), shape((blocks, 8, rows), F32),
            shape((mine, width), F32), shape((mine, width), BF16), shape((SMALL, width), F32),
        ],
        compiler_params=params(),
        cost_estimate=cost(3e9, 10e6),
        name="combine",
    )(
        residual, mixed, pm, ctl, places, returned, cot_own, moe_gain, turned, cvec_turned,
    )

    branch_all = by_core(d_branch, swap(d_branch))
    valid = (seg_col != SEGS - 1).astype(F32)
    d_att = (dot(branch_all, w_out, ((1,), (1,))) * valid).astype(BF16)
    grad_out = dot(attended, branch_all, ((0,), (0,))).astype(BF16)
    d_queries, d_keys, d_values = pl.pallas_call(
        functools.partial(attend_back_kernel, rows, reach),
        grid=(head_pairs,),
        in_specs=[
            heads_at(0), heads_at(head_pairs), heads_at(2 * head_pairs), heads_at(0),
            whole((length, 1)), whole((1, length)), lse_spec,
        ],
        out_specs=[heads_at(0)] * 3,
        out_shape=[shape((length, span), BF16)] * 3,
        scratch_shapes=[pltpu.VMEM((length, LANES), F32)] * 2,
        compiler_params=params(),
        cost_estimate=cost(30e9, 5e6),
        name="attend_back",
    )(qkv, qkv, qkv, d_att, seg_col, seg_row, lse)
    d_qkv = jnp.concatenate([d_queries, d_keys, d_values], axis=1)
    d_normed = dot(d_qkv, qkv_weight, ((1,), (1,)))
    d_normed_own = lax.dynamic_slice_in_dim(d_normed, core * mine, mine)
    d_normed_sib = swap(
        lax.dynamic_slice_in_dim(d_normed, (1 - core) * mine, mine).astype(BF16)
    )
    grad_qkv = dot(normed, d_qkv, ((0,), (0,))).astype(BF16)
    d_tokens, gain_rows = pl.pallas_call(
        finish_kernel,
        grid=(blocks,),
        in_specs=[per_row(rows, width)] * 4 + [whole((1, width))],
        out_specs=[per_row(rows, width), whole((8, width))],
        out_shape=[shape((mine, width), BF16), shape((8, width), F32)],
        compiler_params=params(),
        cost_estimate=cost(1e8, 6e6),
        name="finish",
    )(x_own, d_normed_own, d_normed_sib, d_residual, attn_gain)

    out_mine = lax.dynamic_slice_in_dim(grad_out, core * span, span, axis=1)
    out_sent = lax.dynamic_slice_in_dim(grad_out, (1 - core) * span, span, axis=1)
    out_cols = by_core(out_mine, swap(out_sent))
    small = jnp.concatenate([small[: SMALL - 1], gain_rows[:1]]).T.astype(BF16)
    dense = jnp.concatenate(
        [grad_qkv, out_cols, jnp.pad(small, ((0, 0), (0, LANES - SMALL)))], axis=1
    )
    shares = reduce_all(
        grad_gate, grad_up, grad_down, dense, block_out, d_tokens, d_prev
    )
    pieces = shares[3:5]
    out_home, dtok_home, prev_home = shares[5:]

    def columns_of(start):
        own, other = (piece[:, start : start + span] for piece in pieces)
        return by_core(own, other, axis=1)

    share_qkv = jnp.concatenate([columns_of(k * span) for k in range(3)], axis=1)
    share_out = columns_of(3 * span)
    share_small = sum(piece[:, 4 * span : 4 * span + SMALL] for piece in pieces)
    return (
        out_home,
        dtok_home.astype(F32),
        jnp.swapaxes(prev_home, 1, 2)[:, :, :route_count],
        share_small[:, 15],
        share_qkv,
        share_out,
        share_small[:, 14],
        share_small[:, :route_count],
        share_small[:, 8:12],
        share_small[:, 12:14],
    ) + tuple(shares[:3])


def suits(mesh, tokens, w_router, w_gate):
    peers = mesh.shape["ep"]
    rows = tokens.shape[1] // peers
    micro = tokens.shape[0] // (mesh.shape["dp"] * mesh.shape["fs"])
    routes = w_router.shape[1]
    return (
        peers == 4
        and mesh.shape["fs"] == 2
        and micro == 2
        and (routes - 4) * 2 == peers
        and 3 * rows // routes == LANES
        and tokens.shape[2] % (2 * LANES) == 0
    )


def solution(mesh):
    placed = (
        P(("dp", "fs"), "ep", None),
        P(("dp", "fs"), "ep", None),
        P(("dp", "fs"), None),
        P(("dp", "fs"), "ep", None),
        P(("dp", "fs"), "ep", None),
        P("fs"),
        P("fs", None),
        P("fs", None),
        P("fs"),
        P("fs", None),
        P("fs", None),
        P("fs", None),
        P("ep", "fs", None),
        P("ep", "fs", None),
        P("ep", "fs", None),
    )
    def layer(*arrays):
        fits = suits(mesh, arrays[0], arrays[9], arrays[12])
        return mapped(one_chip if fits else shards)(*arrays)

    def mapped(body):
        return jax.shard_map(
            body,
            mesh=mesh,
            in_specs=placed,
            out_specs=(
                P(("dp", "fs"), "ep", None),
                P(("dp", "fs"), "ep", None),
                P(("dp", "fs"), "ep", None),
                P(("ep", "dp", "fs")),
                P(("ep", "dp", "fs"), None),
                P(("ep", "dp", "fs"), None),
                P(("ep", "dp", "fs")),
                P(("ep", "dp", "fs"), None),
                P(("ep", "dp", "fs"), None),
                P(("ep", "dp", "fs"), None),
                P("ep", ("dp", "fs"), None),
                P("ep", ("dp", "fs"), None),
                P("ep", ("dp", "fs"), None),
            ),
            check_vma=False,
        )

    return layer
```

```python
import functools

import jax
import jax.numpy as jnp
from jax import lax
from jax.experimental import pallas as pl
from jax.experimental.pallas import tpu as pltpu
from jax.sharding import PartitionSpec as P

HEAD = 64
SEGS = 4


NORM_EPS = 1e-06
MASK_FILL = -1e30
HIGHEST = lax.Precision.HIGHEST


def rms_scale(values, gains):
    inverse = lax.rsqrt(jnp.mean(values * values, axis=-1, keepdims=True) + NORM_EPS)
    return values * inverse * gains


def small_softmax(logit_rows):
    largest = jnp.max(logit_rows, axis=-1, keepdims=True)
    powers = jnp.exp(logit_rows - largest)
    return powers / jnp.sum(powers, axis=-1, keepdims=True)


def add_tuple(first_tuple, second_tuple):
    if first_tuple is None:
        return second_tuple
    return tuple(
        (first_term + second_term for first_term, second_term in zip(first_tuple, second_tuple))
    )


def shards(
    tokens,
    prev_logits,
    segments,
    routes,
    cotangent,
    gain_attn,
    w_qkv,
    w_out,
    gain_moe,
    w_router,
    const_proj,
    const_vec,
    w_gate,
    w_up,
    w_down,
):
    micro_count, row_count, model_width = tokens.shape
    head_count = model_width // HEAD
    peer_count = lax.axis_size("ep")
    my_index = lax.axis_index("ep")
    route_count = w_router.shape[1]
    expert_count = route_count - 4
    half_count = peer_count // expert_count
    capacity = (3 * row_count // route_count + 7) // 8 * 8
    seq_length = row_count * peer_count
    slot_count = expert_count * capacity
    pos_all = jnp.arange(seq_length, dtype=jnp.int32)
    pos_mine = my_index * row_count + jnp.arange(row_count, dtype=jnp.int32)
    expert_ids = jnp.arange(expert_count, dtype=jnp.int32)
    slot_ids = jnp.arange(slot_count, dtype=jnp.int32)
    route_ids = jnp.arange(route_count, dtype=jnp.int32)
    layer_outputs = []
    input_grads = []
    prev_grads = []
    dense_acc = None
    expert_acc = None
    for step_index in range(micro_count):
        gathered = (
            lax.all_gather(w_qkv, "fs", axis=0, tiled=True),
            lax.all_gather(w_out, "fs", axis=0, tiled=True),
            lax.all_gather(w_router, "fs", axis=0, tiled=True),
            lax.all_gather(const_proj, "fs", axis=0, tiled=True),
            lax.all_gather(const_vec, "fs", axis=0, tiled=True),
            lax.all_gather(gain_attn, "fs", axis=0, tiled=True),
            lax.all_gather(gain_moe, "fs", axis=0, tiled=True),
            lax.all_gather(w_gate, "fs", axis=1, tiled=True),
            lax.all_gather(w_up, "fs", axis=1, tiled=True),
            lax.all_gather(w_down, "fs", axis=1, tiled=True),
        )
        (
            qkv_weight,
            out_weight,
            router_weight,
            cproj_weight,
            cvec_weight,
            attn_gain,
            moe_gain,
            gate_weight,
            up_weight,
            down_weight,
        ) = gathered
        gate_weight = gate_weight[0]
        up_weight = up_weight[0]
        down_weight = down_weight[0]
        attn_gain = attn_gain.astype(jnp.float32)
        moe_gain = moe_gain.astype(jnp.float32)
        router_float = router_weight.astype(jnp.float32)
        cproj_float = cproj_weight.astype(jnp.float32)
        cvec_float = cvec_weight.astype(jnp.float32)
        token_rows = tokens[step_index].astype(jnp.float32)
        seg_all = segments[step_index]
        seg_mine = lax.dynamic_slice_in_dim(seg_all, my_index * row_count, row_count)
        allowed = (seg_mine[:, None] == seg_all[None, :]) & (pos_all[None, :] <= pos_mine[:, None])
        valid_rows = (seg_mine != SEGS - 1).astype(jnp.float32)[:, None]
        normed = rms_scale(token_rows, attn_gain).astype(jnp.bfloat16)
        qkv_rows = jnp.dot(normed, qkv_weight, preferred_element_type=jnp.float32).astype(
            jnp.bfloat16
        )
        queries = qkv_rows[:, :model_width].reshape(row_count, head_count, HEAD)
        keys_local = qkv_rows[:, model_width : 2 * model_width]
        values_local = qkv_rows[:, 2 * model_width :]
        keys_all, values_all = (
            lax.all_gather(keys_local, "ep", axis=0, tiled=True),
            lax.all_gather(values_local, "ep", axis=0, tiled=True),
        )
        key_heads = keys_all.reshape(seq_length, head_count, HEAD)
        value_heads = values_all.reshape(seq_length, head_count, HEAD)
        scores = (
            jnp.einsum("qhd,khd->hqk", queries, key_heads, preferred_element_type=jnp.float32)
            * 0.125
        )
        scores = jnp.where(allowed[None], scores, MASK_FILL)
        largest = jnp.max(scores, axis=-1, keepdims=True)
        powers = jnp.exp(scores - largest)
        row_total = jnp.sum(powers, axis=-1, keepdims=True)
        log_total = largest + jnp.log(row_total)
        attn_probs = powers / row_total
        attended = jnp.einsum(
            "hqk,khd->qhd",
            attn_probs.astype(jnp.bfloat16),
            value_heads,
            preferred_element_type=jnp.float32,
        ).reshape(row_count, model_width)
        attended = (attended * valid_rows).astype(jnp.bfloat16)
        residual = token_rows + jnp.dot(attended, out_weight, preferred_element_type=jnp.float32)
        mixed = rms_scale(residual, moe_gain).astype(jnp.bfloat16)
        mixed_float = mixed.astype(jnp.float32)
        logits = (
            jnp.dot(mixed, router_weight, preferred_element_type=jnp.float32)
            + prev_logits[step_index]
        )
        router_probs = small_softmax(logits)
        route_rows = routes[step_index]
        choose = (route_rows[:, :, None] == route_ids[None, None, :]).astype(jnp.float32)
        gate_values = jnp.sum(choose * router_probs[:, None, :], axis=-1)
        const_logits = jnp.dot(mixed, cproj_weight, preferred_element_type=jnp.float32)
        mixings = []
        const_outs = []
        for const_index in range(2):
            mixing = small_softmax(const_logits[:, 2 * const_index : 2 * const_index + 2])
            mixings.append(mixing)
            const_outs.append(
                mixing[:, :1] * mixed_float + mixing[:, 1:] * cvec_float[:, const_index][None, :]
            )
        pair_route = route_rows.reshape(-1)
        expert_hit = (pair_route[:, None] == expert_ids[None, :]).astype(jnp.int32)
        slot_index = jnp.sum((jnp.cumsum(expert_hit, axis=0) - expert_hit) * expert_hit, axis=1)
        slot_cell = jnp.sum(expert_hit * expert_ids[None, :], axis=1) * capacity + slot_index
        slot_place = jnp.where(jnp.sum(expert_hit, axis=1) > 0, slot_cell, -1)
        slot_table = (slot_ids[:, None] == slot_place[None, :]).astype(jnp.bfloat16)
        pair_rows = jnp.repeat(mixed, 2, axis=0)
        packed = jnp.einsum(
            "sp,pd->sd", slot_table, pair_rows, preferred_element_type=jnp.float32
        ).astype(jnp.bfloat16)
        outgoing = jnp.broadcast_to(
            packed.reshape(expert_count, 1, capacity, model_width),
            (expert_count, half_count, capacity, model_width),
        ).reshape(peer_count, capacity, model_width)
        received = lax.all_to_all(outgoing, "ep", split_axis=0, concat_axis=0, tiled=True)
        flat_rows = received.reshape(-1, model_width)
        gate_part = jnp.dot(flat_rows, gate_weight, preferred_element_type=jnp.float32)
        up_part = jnp.dot(flat_rows, up_weight, preferred_element_type=jnp.float32)
        hidden = (jax.nn.silu(gate_part) * up_part).astype(jnp.bfloat16)
        part_out = (
            jnp.dot(hidden, down_weight, preferred_element_type=jnp.float32)
            .astype(jnp.bfloat16)
            .reshape(received.shape)
        )
        returned_rows = lax.all_to_all(part_out, "ep", split_axis=0, concat_axis=0, tiled=True)
        returned_rows, kept_rows = (returned_rows, received)
        halves = returned_rows.reshape(expert_count, half_count, capacity, model_width)
        pair_ffn = jnp.zeros((2 * row_count, model_width), jnp.float32)
        for half_index in range(half_count):
            pair_ffn = pair_ffn + jnp.einsum(
                "sp,sd->pd",
                slot_table,
                halves[:, half_index].reshape(slot_count, model_width),
                preferred_element_type=jnp.float32,
            )
        expert_out = pair_ffn.reshape(row_count, 2, model_width)
        expert_out = (
            expert_out + choose[:, :, expert_count + 1 : expert_count + 2] * mixed_float[:, None, :]
        )
        for const_index in range(2):
            column = expert_count + 2 + const_index
            expert_out = (
                expert_out + choose[:, :, column : column + 1] * const_outs[const_index][:, None, :]
            )
        result_rows = residual + jnp.sum(gate_values[:, :, None] * expert_out, axis=1)
        layer_outputs.append(result_rows.astype(jnp.bfloat16))
        grad_rows = cotangent[step_index].astype(jnp.float32)
        d_gates = jnp.sum(expert_out * grad_rows[:, None, :], axis=-1)
        d_probs = jnp.sum(choose * d_gates[:, :, None], axis=1)
        d_logits = router_probs * (
            d_probs - jnp.sum(router_probs * d_probs, axis=-1, keepdims=True)
        )
        prev_grads.append(d_logits)
        grad_router = jnp.dot(mixed_float.T, d_logits, precision=HIGHEST)
        d_mixed = jnp.dot(d_logits, router_float.T, precision=HIGHEST)
        weighted = gate_values[:, :, None] * grad_rows[:, None, :]
        d_mixed = d_mixed + jnp.sum(
            choose[:, :, expert_count + 1 : expert_count + 2] * weighted, axis=1
        )
        cproj_grads = []
        cvec_grads = []
        for const_index in range(2):
            column = expert_count + 2 + const_index
            mixing = mixings[const_index]
            d_const = jnp.sum(choose[:, :, column : column + 1] * weighted, axis=1)
            d_mix = jnp.stack(
                [
                    jnp.sum(d_const * mixed_float, axis=-1),
                    jnp.sum(d_const * cvec_float[:, const_index][None, :], axis=-1),
                ],
                axis=-1,
            )
            d_mixlog = mixing * (d_mix - jnp.sum(mixing * d_mix, axis=-1, keepdims=True))
            cproj_grads.append(jnp.dot(mixed_float.T, d_mixlog, precision=HIGHEST))
            cvec_grads.append(jnp.sum(mixing[:, 1:] * d_const, axis=0))
            d_mixed = (
                d_mixed
                + mixing[:, :1] * d_const
                + jnp.dot(
                    d_mixlog,
                    cproj_float[:, 2 * const_index : 2 * const_index + 2].T,
                    precision=HIGHEST,
                )
            )
        grad_cproj = jnp.concatenate(cproj_grads, axis=1)
        grad_cvec = jnp.stack(cvec_grads, axis=1)
        d_pairs = weighted.reshape(2 * row_count, model_width).astype(jnp.bfloat16)
        d_packed = jnp.einsum(
            "sp,pd->sd", slot_table, d_pairs, preferred_element_type=jnp.float32
        ).astype(jnp.bfloat16)
        d_outgoing = jnp.broadcast_to(
            d_packed.reshape(expert_count, 1, capacity, model_width),
            (expert_count, half_count, capacity, model_width),
        ).reshape(peer_count, capacity, model_width)
        d_received = lax.all_to_all(d_outgoing, "ep", split_axis=0, concat_axis=0, tiled=True)
        flat_rows = kept_rows.reshape(-1, model_width)
        flat_grads = d_received.reshape(-1, model_width)
        gate_part = jnp.dot(flat_rows, gate_weight, preferred_element_type=jnp.float32)
        up_part = jnp.dot(flat_rows, up_weight, preferred_element_type=jnp.float32)
        activated = jax.nn.silu(gate_part)
        hidden = (activated * up_part).astype(jnp.bfloat16)
        grad_down = jnp.einsum("rf,rd->fd", hidden, flat_grads, preferred_element_type=jnp.float32)
        d_hidden = jnp.einsum(
            "rd,fd->rf", flat_grads, down_weight, preferred_element_type=jnp.float32
        )
        sigmoid_gate = jax.nn.sigmoid(gate_part)
        d_gate_part = (
            d_hidden * up_part * sigmoid_gate * (1.0 + gate_part * (1.0 - sigmoid_gate))
        ).astype(jnp.bfloat16)
        d_up_part = (d_hidden * activated).astype(jnp.bfloat16)
        grad_gate = jnp.einsum(
            "rd,rf->df", flat_rows, d_gate_part, preferred_element_type=jnp.float32
        )
        grad_up = jnp.einsum("rd,rf->df", flat_rows, d_up_part, preferred_element_type=jnp.float32)
        d_inputs = jnp.einsum(
            "rf,df->rd", d_gate_part, gate_weight, preferred_element_type=jnp.float32
        )
        d_inputs = d_inputs + jnp.einsum(
            "rf,df->rd", d_up_part, up_weight, preferred_element_type=jnp.float32
        )
        d_inputs = d_inputs.astype(jnp.bfloat16).reshape(peer_count, capacity, model_width)
        d_returned = lax.all_to_all(d_inputs, "ep", split_axis=0, concat_axis=0, tiled=True)
        d_halves = d_returned.reshape(expert_count, half_count, capacity, model_width)
        for half_index in range(half_count):
            d_pair_in = jnp.einsum(
                "sp,sd->pd",
                slot_table,
                d_halves[:, half_index].reshape(slot_count, model_width),
                preferred_element_type=jnp.float32,
            )
            d_mixed = d_mixed + jnp.sum(d_pair_in.reshape(row_count, 2, model_width), axis=1)
        expert_acc = add_tuple(expert_acc, (grad_gate, grad_up, grad_down))
        moe_vjp = jax.vjp(rms_scale, residual, moe_gain)[1]
        d_residual_norm, grad_moe_gain = moe_vjp(d_mixed)
        d_residual = grad_rows + d_residual_norm
        d_branch = d_residual.astype(jnp.bfloat16)
        grad_out = jnp.einsum("rd,re->de", attended, d_branch, preferred_element_type=jnp.float32)
        d_attended = (
            jnp.einsum("re,de->rd", d_branch, out_weight, preferred_element_type=jnp.float32)
            * valid_rows
        ).astype(jnp.bfloat16)
        d_heads = d_attended.reshape(row_count, head_count, HEAD)
        scores = (
            jnp.einsum("qhd,khd->hqk", queries, key_heads, preferred_element_type=jnp.float32)
            * 0.125
        )
        scores = jnp.where(allowed[None], scores, MASK_FILL)
        attn_probs = jnp.exp(scores - log_total)
        d_weights = jnp.einsum(
            "qhd,khd->hqk", d_heads, value_heads, preferred_element_type=jnp.float32
        )
        delta_rows = jnp.sum(attn_probs * d_weights, axis=-1, keepdims=True)
        d_scores = (attn_probs * (d_weights - delta_rows)).astype(jnp.bfloat16)
        d_queries = (
            jnp.einsum(
                "hqk,khd->qhd", d_scores, key_heads, preferred_element_type=jnp.float32
            ).reshape(row_count, model_width)
            * 0.125
        )
        d_values = jnp.einsum(
            "hqk,qhd->khd",
            attn_probs.astype(jnp.bfloat16),
            d_heads,
            preferred_element_type=jnp.float32,
        ).reshape(seq_length, model_width)
        d_keys = (
            jnp.einsum(
                "hqk,qhd->khd", d_scores, queries, preferred_element_type=jnp.float32
            ).reshape(seq_length, model_width)
            * 0.125
        )
        d_keys_mine, d_values_mine = (
            lax.psum_scatter(
                d_keys.astype(jnp.bfloat16), "ep", scatter_dimension=0, tiled=True
            ).astype(jnp.float32),
            lax.psum_scatter(
                d_values.astype(jnp.bfloat16), "ep", scatter_dimension=0, tiled=True
            ).astype(jnp.float32),
        )
        d_qkv = jnp.concatenate([d_queries, d_keys_mine, d_values_mine], axis=1).astype(
            jnp.bfloat16
        )
        grad_qkv = jnp.einsum("rd,re->de", normed, d_qkv, preferred_element_type=jnp.float32)
        d_normed = jnp.einsum("re,de->rd", d_qkv, qkv_weight, preferred_element_type=jnp.float32)
        attn_vjp = jax.vjp(rms_scale, token_rows, attn_gain)[1]
        d_tokens_norm, grad_attn_gain = attn_vjp(d_normed)
        input_grads.append(d_residual + d_tokens_norm)
        dense_terms = (
            grad_attn_gain,
            grad_qkv,
            grad_out,
            grad_moe_gain,
            grad_router,
            grad_cproj,
            grad_cvec,
        )
        dense_shares = (
            lax.psum_scatter(dense_terms[0], ("ep", "dp", "fs"), scatter_dimension=0, tiled=True),
            lax.psum_scatter(dense_terms[1], ("ep", "dp", "fs"), scatter_dimension=0, tiled=True),
            lax.psum_scatter(dense_terms[2], ("ep", "dp", "fs"), scatter_dimension=0, tiled=True),
            lax.psum_scatter(dense_terms[3], ("ep", "dp", "fs"), scatter_dimension=0, tiled=True),
            lax.psum_scatter(dense_terms[4], ("ep", "dp", "fs"), scatter_dimension=0, tiled=True),
            lax.psum_scatter(dense_terms[5], ("ep", "dp", "fs"), scatter_dimension=0, tiled=True),
            lax.psum_scatter(dense_terms[6], ("ep", "dp", "fs"), scatter_dimension=0, tiled=True),
        )
        dense_acc = add_tuple(dense_acc, dense_shares)
    expert_shares = (
        lax.psum_scatter(
            expert_acc[0][None].astype(jnp.bfloat16), ("dp", "fs"), scatter_dimension=1, tiled=True
        ).astype(jnp.float32),
        lax.psum_scatter(
            expert_acc[1][None].astype(jnp.bfloat16), ("dp", "fs"), scatter_dimension=1, tiled=True
        ).astype(jnp.float32),
        lax.psum_scatter(
            expert_acc[2][None].astype(jnp.bfloat16), ("dp", "fs"), scatter_dimension=1, tiled=True
        ).astype(jnp.float32),
    )
    return (
        jnp.stack(layer_outputs),
        jnp.stack(input_grads),
        jnp.stack(prev_grads),
        dense_acc[0],
        dense_acc[1],
        dense_acc[2],
        dense_acc[3],
        dense_acc[4],
        dense_acc[5],
        dense_acc[6],
        expert_shares[0],
        expert_shares[1],
        expert_shares[2],
    )


NEG = -1e30
KINDS = 2
SMALL = 16
LANES = 128
F32 = jnp.float32
BF16 = jnp.bfloat16


def dot(lhs, rhs, dims=((1,), (0,)), precision=None):
    return lax.dot_general(
        lhs, rhs, (dims, ((), ())), precision=precision, preferred_element_type=F32
    )


def norm_qkv_kernel(x_ref, gain_ref, w_ref, normed_ref, qkv_ref):
    rows = x_ref[...].astype(F32)
    inverse = lax.rsqrt(jnp.mean(rows * rows, axis=-1, keepdims=True) + NORM_EPS)
    normed = (rows * inverse * gain_ref[...]).astype(BF16)
    normed_ref[...] = normed
    qkv_ref[...] = dot(normed, w_ref[...]).astype(BF16)


def key_span(block, rows, reach):
    start = max(0, block * rows - reach)
    return start, (block + 1) * rows - start


def attend_kernel(rows, reach, q_ref, k_ref, v_ref, segc_ref, segr_ref, att_ref, lse_ref):
    length = q_ref.shape[0]
    for block in range(length // rows):
        start, width = key_span(block, rows, reach)
        queries = q_ref[block * rows : (block + 1) * rows, :]
        keys = k_ref[start : start + width, :]
        values = v_ref[start : start + width, :]
        seg_q = segc_ref[block * rows : (block + 1) * rows, :]
        seg_k = segr_ref[:, start : start + width]
        row_pos = block * rows + lax.broadcasted_iota(jnp.int32, (rows, width), 0)
        col_pos = start + lax.broadcasted_iota(jnp.int32, (rows, width), 1)
        allowed = (seg_q == seg_k) & (col_pos <= row_pos)
        lane = lax.broadcasted_iota(jnp.int32, (rows, LANES), 1)
        outs = []
        logs = []
        for head in range(2):
            mine = (lane // HEAD) == head
            scores = dot(jnp.where(mine, queries, 0), keys, ((1,), (1,))) * 0.125
            scores = jnp.where(allowed, scores, NEG)
            largest = jnp.max(scores, axis=-1, keepdims=True)
            powers = jnp.exp(scores - largest)
            total = jnp.sum(powers, axis=-1, keepdims=True)
            outs.append(dot(powers.astype(BF16), values) / total)
            logs.append(largest + jnp.log(total))
        valid = (seg_q != SEGS - 1).astype(F32)
        att = jnp.where(lane < HEAD, outs[0], outs[1]) * valid
        att_ref[block * rows : (block + 1) * rows, :] = att.astype(BF16)
        both = jnp.where(lane < HEAD, logs[0], logs[1]).T
        lse_ref[0, 0:1, block * rows : (block + 1) * rows] = both[0:1, :]
        lse_ref[0, 1:2, block * rows : (block + 1) * rows] = both[HEAD : HEAD + 1, :]


def attend_back_kernel(
    rows, reach, q_ref, k_ref, v_ref, do_ref, segc_ref, segr_ref, lse_ref,
    dq_ref, dk_ref, dv_ref, dk_sum, dv_sum,
):
    length = q_ref.shape[0]
    dk_sum[...] = jnp.zeros_like(dk_sum)
    dv_sum[...] = jnp.zeros_like(dv_sum)
    keys_turned = k_ref[...].T
    for block in range(length // rows):
        start, width = key_span(block, rows, reach)
        queries = q_ref[block * rows : (block + 1) * rows, :]
        grads = do_ref[block * rows : (block + 1) * rows, :]
        keys = k_ref[start : start + width, :]
        values = v_ref[start : start + width, :]
        seg_k = segc_ref[start : start + width, :]
        seg_q = segr_ref[:, block * rows : (block + 1) * rows]
        key_pos = start + lax.broadcasted_iota(jnp.int32, (width, rows), 0)
        query_pos = block * rows + lax.broadcasted_iota(jnp.int32, (width, rows), 1)
        allowed = (seg_q == seg_k) & (key_pos <= query_pos)
        lane = lax.broadcasted_iota(jnp.int32, (rows, LANES), 1)
        dq_parts = []
        for head in range(2):
            mine = (lane // HEAD) == head
            head_q = jnp.where(mine, queries, 0)
            head_g = jnp.where(mine, grads, 0)
            log_total = lse_ref[0, head : head + 1, block * rows : (block + 1) * rows]
            scores = dot(keys, head_q, ((1,), (1,))) * 0.125
            probs = jnp.exp(jnp.where(allowed, scores, NEG) - log_total)
            d_probs = dot(values, head_g, ((1,), (1,)))
            delta = jnp.sum(probs * d_probs, axis=0, keepdims=True)
            d_scores = (probs * (d_probs - delta)).astype(BF16)
            dv_sum[start : start + width, :] += dot(probs.astype(BF16), head_g)
            dk_sum[start : start + width, :] += dot(d_scores, head_q)
            turned = keys_turned[head * HEAD : (head + 1) * HEAD, start : start + width]
            dq_parts.append(dot(turned, d_scores))
        dq = jnp.concatenate(dq_parts, axis=0).T * 0.125
        dq_ref[block * rows : (block + 1) * rows, :] = dq.astype(BF16)
    dk_ref[...] = (dk_sum[...] * 0.125).astype(BF16)
    dv_ref[...] = dv_sum[...].astype(BF16)


def column(rows, index):
    return rows[:, index : index + 1]


def chosen_of(ctl):
    lane = lax.broadcasted_iota(jnp.int32, ctl.shape, 1).astype(F32)
    return ((lane == column(ctl, 8)) | (lane == column(ctl, 9))).astype(F32)


def finish_kernel(x_ref, own_ref, sib_ref, dres_ref, gain_ref, out_ref, gain_out_ref):
    rows = x_ref[...].astype(F32)
    d_normed = own_ref[...].astype(F32) + sib_ref[...].astype(F32)
    inverse = lax.rsqrt(jnp.mean(rows * rows, axis=-1, keepdims=True) + NORM_EPS)
    scaled = d_normed * gain_ref[...]
    mean = jnp.mean(scaled * rows, axis=-1, keepdims=True)
    out = dres_ref[...] + inverse * scaled - rows * (inverse * inverse * inverse * mean)
    out_ref[...] = out.astype(out_ref.dtype)

    @pl.when(pl.program_id(0) == 0)
    def _():
        gain_out_ref[...] = jnp.zeros_like(gain_out_ref)

    gain_out_ref[0:1, :] += jnp.sum(d_normed * rows * inverse, axis=0, keepdims=True)


def shape(dims, dtype):
    return jax.ShapeDtypeStruct(dims, dtype)


def whole(dims):
    return pl.BlockSpec(dims, lambda *_: (0,) * len(dims))


def per_row(rows, width):
    return pl.BlockSpec((rows, width), lambda i: (i, 0))


def params():
    return pltpu.CompilerParams(vmem_limit_bytes=56 * 1024 * 1024)


def cost(flops, moved):
    return pl.CostEstimate(flops=int(flops), bytes_accessed=int(moved), transcendentals=0)


class Mail:
    def __init__(self, send_sems, recv_sems):
        self.send_sems = send_sems
        self.recv_sems = recv_sems
        self.used = 0

    def copy(self, source, target, device):
        slot = self.used
        self.used = slot + 1
        return pltpu.make_async_remote_copy(
            src_ref=source,
            dst_ref=target,
            send_sem=self.send_sems.at[slot],
            recv_sem=self.recv_sems.at[slot],
            device_id=device,
            device_id_type=pl.DeviceIdType.MESH,
        )


def position():
    place = lax.axis_index("ep")
    return place // 2, place % 2, lax.axis_index("dp"), lax.axis_index("fs")


def greet(devices):
    barrier = pltpu.get_barrier_semaphore()
    total = 0
    for device, present in devices:
        if present is True:
            pl.semaphore_signal(
                barrier, inc=1, device_id=device, device_id_type=pl.DeviceIdType.MESH
            )
            total = total + 1
        else:

            @pl.when(present)
            def _():
                pl.semaphore_signal(
                    barrier, inc=1, device_id=device, device_id_type=pl.DeviceIdType.MESH
                )

            total = total + jnp.where(present, 1, 0)
    pl.semaphore_wait(barrier, total)


class Line:
    def __init__(self, mail, depth, slots):
        self.depth = depth
        self.slots = slots
        self.place = lax.axis_index("dp")
        y, x, z, core = position()
        self.copies = {}
        for way in range(2):
            step_to = 1 if way == 0 else -1
            device = (y * 2 + x, z + step_to, core)
            for step in range(depth - 1):
                for item, (acc, landing) in enumerate(slots):
                    shard = self.shard(way, step)
                    safe = jnp.clip(shard, 0, depth - 1)
                    self.copies[way, step, item] = mail.copy(
                        acc.at[safe], landing.at[way, step], device
                    )

    def shard(self, way, step):
        if way == 0:
            return self.place + self.depth - 1 - step
        return self.place - (self.depth - 1 - step)

    def sends(self, way, step):
        shard = self.shard(way, step)
        if way == 0:
            return (shard <= self.depth - 1) & (self.place < self.depth - 1)
        return (shard >= 0) & (self.place > 0)

    def gets(self, way, step):
        if way == 0:
            return (self.place > 0) & (self.shard(way, step + 1) <= self.depth - 1)
        return (self.place < self.depth - 1) & (self.shard(way, step + 1) >= 0)

    def send(self, step, item):
        for way in range(2):

            @pl.when(self.sends(way, step))
            def _():
                self.copies[way, step, item].start()

    def take(self, step, item):
        acc, landing = self.slots[item]
        for way in range(2):
            shard = jnp.clip(self.shard(way, step + 1), 0, self.depth - 1)

            @pl.when(self.gets(way, step))
            def _():
                self.copies[way, step, item].wait_recv()
                acc[shard] = (
                    acc[shard].astype(F32) + landing[way, step].astype(F32)
                ).astype(BF16)

    def finish(self, item, store):
        acc, landing = self.slots[item]
        store(acc[self.place].astype(F32))
        for way in range(2):

            @pl.when(self.gets(way, self.depth - 2))
            def _():
                self.copies[way, self.depth - 2, item].wait_recv()
                store(landing[way, self.depth - 2].astype(F32), True)

    def close(self):
        for (way, step, item), copy in self.copies.items():

            @pl.when(self.sends(way, step))
            def _():
                copy.wait_send()


def reduce_kernel(
    depth, cut,
    gate_ref, up_ref, down_ref, dense_ref, out_ref, dtok_ref, prev_ref,
    gate_out, up_out, down_out, own_out, sib_out, out_home, dtok_home, prev_home,
    gate_land, up_land, down_land, gate_acc, up_acc, down_acc,
    gate_line, up_line, down_line,
    y1_land, x1_land, y1_acc, x1_acc, x2_land, y2_land, dense_acc, dense_line, dense_sum,
    send_sems, recv_sems, local_sems,
):
    y, x, z, core = position()
    sibling = (y * 2 + x, z, 1 - core)
    across = (y * 2 + 1 - x, z, core)
    along = ((1 - y) * 2 + x, z, core)
    moved = y != core
    near = ((1 - y) * 2 + x, z, 1 - core)
    far = (core * 2 + 1 - x, z, y)
    greet(
        [
            (sibling, True), (across, True), (along, True),
            (near, moved), (far, moved),
            ((y * 2 + x, z + 1, core), z < depth - 1), ((y * 2 + x, z - 1, core), z > 0),
        ]
    )
    mail = Mail(send_sems, recv_sems)
    experts = [
        (gate_ref, gate_land, gate_acc, gate_line, gate_out),
        (up_ref, up_land, up_acc, up_line, up_out),
        (down_ref, down_land, down_acc, down_line, down_out),
    ]
    halves = [
        mail.copy(source.at[:, 1 - core], land, sibling)
        for source, land, _, _, _ in experts
    ]
    line = Line(mail, depth, [(acc, landing) for _, _, acc, landing, _ in experts])
    rest = dense_ref.shape[3] - cut
    left = pl.ds(0, cut)
    right = pl.ds(cut, rest)
    first_y = mail.copy(dense_ref.at[1 - y, :, :, left], y1_land, along)
    first_x = mail.copy(dense_ref.at[:, 1 - x, :, right], x1_land, across)
    second_x = mail.copy(y1_acc.at[1 - x], x2_land, across)
    second_y = mail.copy(x1_acc.at[1 - y], y2_land, along)
    dense = Line(mail, depth, [(dense_acc, dense_line)])
    homes = [(out_ref, out_home), (dtok_ref, dtok_home), (prev_ref, prev_home)]
    nears = [mail.copy(a.at[x], b.at[x], near) for a, b in homes]
    fars = [mail.copy(a.at[1 - x], b.at[x], far) for a, b in homes]
    stays = [
        pltpu.make_async_copy(a.at[x], b.at[x], local_sems.at[k])
        for k, (a, b) in enumerate(homes)
    ]

    for copy in halves:
        copy.start()
    first_y.start()
    first_x.start()
    for item, (source, land, acc, _, _) in enumerate(experts):
        halves[item].wait_recv()
        for shard in range(depth):
            acc[shard] = (source[shard, core].astype(F32) + land[shard].astype(F32)).astype(BF16)
        line.send(0, item)
    first_y.wait_recv()
    for k in range(2):
        y1_acc[k] = (dense_ref[y, k, :, left].astype(F32) + y1_land[k].astype(F32)).astype(BF16)
    second_x.start()
    first_x.wait_recv()
    for k in range(2):
        x1_acc[k] = (dense_ref[k, x, :, right].astype(F32) + x1_land[k].astype(F32)).astype(BF16)
    second_y.start()
    for copy in fars:
        copy.start()

    @pl.when(moved)
    def _():
        for copy in nears:
            copy.start()

    @pl.when(jnp.logical_not(moved))
    def _():
        for copy in stays:
            copy.start()

    for item in range(3):
        line.take(0, item)
        line.send(1, item)
    size = dense_acc.shape[1]
    second_x.wait_recv()
    second_y.wait_recv()
    for shard in range(depth):
        part = pl.ds(shard * size, size)
        dense_acc[shard, :, left] = (
            y1_acc[x, part].astype(F32) + x2_land[part].astype(F32)
        ).astype(BF16)
        dense_acc[shard, :, right] = (
            x1_acc[y, part].astype(F32) + y2_land[part].astype(F32)
        ).astype(BF16)
    dense.send(0, 0)
    for item in range(3):
        line.take(1, item)
        line.send(2, item)
    dense.take(0, 0)
    dense.send(1, 0)
    for item, (_, _, _, _, result) in enumerate(experts):

        def store(value, add=False):
            result[0] = result[0] + value if add else value

        line.finish(item, store)
    dense.take(1, 0)
    dense.send(2, 0)

    def store_dense(value, add=False):
        dense_sum[...] = dense_sum[...] + value if add else value

    dense.finish(0, store_dense)
    half = size // 2
    last = mail.copy(
        dense_sum.at[pl.ds(pl.multiple_of((1 - core) * half, 8), half)], sib_out, sibling
    )
    last.start()
    own_out[...] = dense_sum[pl.ds(pl.multiple_of(core * half, 8), half), :]
    last.wait()
    for copy in halves + [first_y, first_x, second_x, second_y]:
        copy.wait_send()
    line.close()
    dense.close()
    for copy in fars:
        copy.wait()

    @pl.when(moved)
    def _():
        for copy in nears:
            copy.wait()

    @pl.when(jnp.logical_not(moved))
    def _():
        for copy in stays:
            copy.wait()


def reduce_all(grad_gate, grad_up, grad_down, dense, block_out, d_tokens, d_prev):
    depth = lax.axis_size("dp")
    experts = [
        grad.reshape(depth, 2, grad.shape[0] // (2 * depth), grad.shape[1])
        for grad in (grad_gate, grad_up, grad_down)
    ]
    quarter = dense.shape[0] // 4
    columns = dense.shape[1]
    cut = (columns // LANES + 1) // 2 * LANES
    dense = dense.reshape(2, 2, quarter, columns)
    homes = [
        block_out,
        d_tokens.reshape(block_out.shape),
        d_prev,
    ]
    size = quarter // depth
    parts = [grad.shape[2:] for grad in experts]
    vmem = pl.BlockSpec(memory_space=pltpu.VMEM)
    copies = 3 + 2 * (depth - 1) * 4 + 4 + 6 + 1
    outs = pl.pallas_call(
        functools.partial(reduce_kernel, depth, cut),
        in_specs=[vmem] * 7,
        out_specs=[vmem] * 8,
        out_shape=[shape((1,) + part, F32) for part in parts]
        + [shape((size // 2, columns), F32)] * 2
        + [shape(home.shape, home.dtype) for home in homes],
        scratch_shapes=[pltpu.VMEM((depth,) + part, BF16) for part in parts] * 2
        + [pltpu.VMEM((2, depth - 1) + part, BF16) for part in parts]
        + [
            pltpu.VMEM((2, quarter, cut), BF16),
            pltpu.VMEM((2, quarter, columns - cut), BF16),
            pltpu.VMEM((2, quarter, cut), BF16),
            pltpu.VMEM((2, quarter, columns - cut), BF16),
            pltpu.VMEM((quarter, cut), BF16),
            pltpu.VMEM((quarter, columns - cut), BF16),
            pltpu.VMEM((depth, size, columns), BF16),
            pltpu.VMEM((2, depth - 1, size, columns), BF16),
            pltpu.VMEM((size, columns), F32),
            pltpu.SemaphoreType.DMA((copies,)),
            pltpu.SemaphoreType.DMA((copies,)),
            pltpu.SemaphoreType.DMA((3,)),
        ],
        compiler_params=pltpu.CompilerParams(
            collective_id=1, has_side_effects=True, vmem_limit_bytes=60 * 1024 * 1024
        ),
        name="reduce_all",
    )(*experts, dense, *homes)
    return outs


def spread_block(experts, routes, rows, block, refs, send_ref, recv_ref, keep):
    (att_own, att_sib, x_ref, g_ref, ctl_ref, w_own, w_sib, gain_ref, wsm_ref) = refs
    residual_ref, mixed_ref, pm_ref, place_ref = keep
    y, x, z, core = position()
    here = pl.ds(pl.multiple_of(block * rows, rows), rows)
    residual = x_ref[here, :].astype(F32) + (
        dot(att_own[here, :], w_own[...]) + dot(att_sib[here, :], w_sib[...])
    )
    residual_ref[here, :] = residual
    inverse = lax.rsqrt(jnp.mean(residual * residual, axis=-1, keepdims=True) + NORM_EPS)
    mixed = (residual * inverse * gain_ref[...]).astype(BF16)
    mixed_ref[here, :] = mixed
    logits = dot(mixed, wsm_ref[...])
    ctl = ctl_ref[here, :]
    lane = lax.broadcasted_iota(jnp.int32, (rows, LANES), 1)
    is_route = lane < routes
    router = jnp.where(is_route, logits + ctl, NEG)
    powers = jnp.exp(router - jnp.max(router, axis=-1, keepdims=True))
    probs = powers / jnp.sum(powers, axis=-1, keepdims=True)
    probs = jnp.where(is_route, probs, 0.0)
    pm = probs
    for const_index in range(2):
        first = column(logits, 8 + 2 * const_index)
        second = column(logits, 9 + 2 * const_index)
        largest = jnp.maximum(first, second)
        first = jnp.exp(first - largest)
        second = jnp.exp(second - largest)
        total = first + second
        pm = jnp.where(lane == 8 + 2 * const_index, first / total, pm)
        pm = jnp.where(lane == 9 + 2 * const_index, second / total, pm)
    pm_ref[here, :] = pm
    chosen = chosen_of(ctl)
    gated = chosen * probs
    earlier = lax.broadcasted_iota(jnp.int32, (rows, rows), 1) < lax.broadcasted_iota(
        jnp.int32, (rows, rows), 0
    )
    rank = dot(earlier.astype(BF16), chosen.astype(BF16))
    lane_f = lane.astype(F32)
    grads = g_ref[here, :].astype(F32)
    for expert in range(experts):
        place = jnp.where(
            (lane_f == column(rank, expert)) & (column(chosen, expert) > 0.0), 1.0, 0.0
        )
        place_ref[here, expert * LANES : (expert + 1) * LANES] = place.astype(BF16)
        pick = place.T.astype(BF16)
        d_part = (column(gated, expert) * grads).astype(BF16)
        send_ref[block, expert, 0] = dot(pick, mixed).astype(BF16)
        send_ref[block, expert, 1] = dot(pick, d_part).astype(BF16)
    recv_ref[block, y * 2 + x] = send_ref[block, y]


def expert_block(block, recv_ref, result_ref, back_ref, weights, keep):
    gate_w, up_w, down_w = weights
    hidden_ref, d_gate_ref, d_up_ref = keep
    y, x, z, core = position()
    peers, _, capacity, width = recv_ref.shape[1:]
    size = peers * capacity
    here = pl.ds(pl.multiple_of(block * size, size), size)
    rows = recv_ref[block, :, 0].reshape(size, width)
    d_rows = recv_ref[block, :, 1].reshape(size, width)
    gate = dot(rows, gate_w[...])
    up = dot(rows, up_w[...])
    sig = jax.nn.sigmoid(gate)
    active = gate * sig
    hidden = (active * up).astype(BF16)
    hidden_ref[here, :] = hidden
    part = dot(hidden, down_w[...]).astype(BF16)
    result_ref[block, :, 0] = part.reshape(peers, capacity, width)
    d_hidden = dot(d_rows, down_w[...], ((1,), (1,)))
    d_gate = (d_hidden * up * sig * (1.0 + gate * (1.0 - sig))).astype(BF16)
    d_up = (d_hidden * active).astype(BF16)
    d_gate_ref[here, :] = d_gate
    d_up_ref[here, :] = d_up
    d_in = dot(d_gate, gate_w[...], ((1,), (1,))) + dot(d_up, up_w[...], ((1,), (1,)))
    result_ref[block, :, 1] = d_in.astype(BF16).reshape(peers, capacity, width)
    back_ref[block, y * 2 + x] = result_ref[block, y * 2 + x]


def combine_block(experts, routes, rows, block, refs, keep, back_ref, outs, small_ref):
    g_ref, ctl_ref, gain_ref, turned_ref, cvec_ref = refs
    residual_ref, mixed_ref, pm_ref, place_ref = keep
    out_ref, prev_ref, dres_ref, branch_ref = outs
    halves = back_ref.shape[1] // experts
    here = pl.ds(pl.multiple_of(block * rows, rows), rows)
    g_low = g_ref[here, :]
    grads = g_low.astype(F32)
    mixed = mixed_ref[here, :].astype(F32)
    residual = residual_ref[here, :]
    pm = pm_ref[here, :]
    lane = lax.broadcasted_iota(jnp.int32, (rows, LANES), 1)
    chosen = chosen_of(ctl_ref[here, :])
    probs = jnp.where(lane < routes, pm, 0.0)
    gated = chosen * probs
    d_probs = jnp.zeros((rows, LANES), F32)
    result = residual
    d_mixed = None
    for expert in range(experts):
        place = place_ref[here, expert * LANES : (expert + 1) * LANES]
        expert_out = None
        for half in range(halves):
            owner = expert * halves + half
            term = dot(place, back_ref[block, owner, 0])
            expert_out = term if expert_out is None else expert_out + term
            term = dot(place, back_ref[block, owner, 1])
            d_mixed = term if d_mixed is None else d_mixed + term
        result = result + column(gated, expert) * expert_out
        d_gate = jnp.sum(expert_out * grads, axis=-1, keepdims=True)
        d_probs = jnp.where(lane == expert, d_gate, d_probs)
    g_mixed = jnp.sum(grads * mixed, axis=-1, keepdims=True)
    g_const = dot(g_low, cvec_ref[...], ((1,), (1,)))
    copy = experts + 1
    d_probs = jnp.where(lane == copy, g_mixed, d_probs)
    weight = column(gated, copy)
    d_small = jnp.zeros((rows, LANES), F32)
    for const_index in range(2):
        route = copy + 1 + const_index
        first = column(pm, 8 + 2 * const_index)
        second = column(pm, 9 + 2 * const_index)
        gate = column(gated, route)
        g_vec = column(g_const, const_index)
        d_probs = jnp.where(lane == route, first * g_mixed + second * g_vec, d_probs)
        weight = weight + gate * first
        vec = cvec_ref[const_index : const_index + 1, :].astype(F32)
        result = result + (gate * second) * vec
        d_first = gate * g_mixed
        d_second = gate * g_vec
        mean = first * d_first + second * d_second
        d_small = jnp.where(lane == 8 + 2 * const_index, first * (d_first - mean), d_small)
        d_small = jnp.where(lane == 9 + 2 * const_index, second * (d_second - mean), d_small)
        d_small = jnp.where(lane == 12 + const_index, gate * second, d_small)
    result = result + weight * mixed
    out_ref[block] = result.astype(BF16)
    d_probs = d_probs * chosen
    d_logits = probs * (d_probs - jnp.sum(probs * d_probs, axis=-1, keepdims=True))
    d_small = jnp.where(lane < routes, d_logits, d_small)
    d_mixed = d_mixed + weight * grads
    d_mixed = d_mixed + dot(
        jnp.where(lane < 12, d_small, 0.0), turned_ref[...], precision=HIGHEST
    )
    inverse = lax.rsqrt(jnp.mean(residual * residual, axis=-1, keepdims=True) + NORM_EPS)
    scaled = d_mixed * gain_ref[...]
    mean = jnp.mean(scaled * residual, axis=-1, keepdims=True)
    d_residual = grads + inverse * scaled - residual * (inverse * inverse * inverse * mean)
    dres_ref[here, :] = d_residual
    branch_ref[here, :] = d_residual.astype(BF16)
    d_turned = d_small.T[:SMALL, :]
    prev_ref[block] = d_turned[:8, :]
    sub = lax.broadcasted_iota(jnp.int32, (SMALL, rows), 0)
    small = dot(jnp.where(sub < 12, d_turned, 0.0), mixed, precision=HIGHEST)
    small = small + dot(
        jnp.where((sub >= 12) & (sub < 14), d_turned, 0.0), grads, precision=HIGHEST
    )
    d_gain = jnp.sum(d_mixed * residual * inverse, axis=0, keepdims=True)
    which = lax.broadcasted_iota(jnp.int32, small.shape, 0)
    small_ref[...] += jnp.where(which == 14, d_gain, small)


def layer_kernel(
    experts, routes, rows, blocks,
    att_ref, x_ref, g_ref, ctl_ref, w_own, w_sib, gain_ref, wsm_ref, turned_ref, cvec_ref,
    gate_ref, up_ref, down_ref,
    out_ref, prev_ref, dres_ref, branch_ref, small_ref, dgate_out, dup_out, ddown_out,
    att_own, att_sib, gate_w, up_w, down_w, residual_ref, mixed_ref, pm_ref, place_ref,
    send_ref, recv_ref, result_ref, back_ref, hidden_ref, d_gate_ref, d_up_ref,
    head_send, head_recv, local_sems, send_sems, recv_sems, back_send, back_recv,
):
    y, x, z, core = position()
    me = y * 2 + x
    sibling = (me, z, 1 - core)
    partners = [(1 - y) * 2 + 1 - x, y * 2 + 1 - x, (1 - y) * 2 + x]
    wanted = [1 - y, y, 1 - y]
    greet([(sibling, True)] + [((place, z, core), True) for place in partners])
    mine = rows * blocks
    mail = Mail(head_send, head_recv)
    pairs = [(gate_ref, gate_w), (up_ref, up_w), (down_ref, down_w)]
    heads = [mail.copy(att_ref.at[1 - core], att_sib, sibling)]
    locals_ = [pltpu.make_async_copy(att_ref.at[core], att_own, local_sems.at[3])]
    for k, (source, target) in enumerate(pairs):
        size = source.shape[0]
        spot = target.at[pl.ds(pl.multiple_of(core * size, size), size)]
        heads.append(mail.copy(source, spot, sibling))
        locals_.append(pltpu.make_async_copy(source, spot, local_sems.at[k]))
    for copy in heads + locals_:
        copy.start()

    def dispatch(block, k):
        return pltpu.make_async_remote_copy(
            src_ref=send_ref.at[block, wanted[k]],
            dst_ref=recv_ref.at[block, me],
            send_sem=send_sems.at[block, k],
            recv_sem=recv_sems.at[block, k],
            device_id=(partners[k], z, core),
            device_id_type=pl.DeviceIdType.MESH,
        )

    def giveback(block, k):
        return pltpu.make_async_remote_copy(
            src_ref=result_ref.at[block, partners[k]],
            dst_ref=back_ref.at[block, me],
            send_sem=back_send.at[block, k],
            recv_sem=back_recv.at[block, k],
            device_id=(partners[k], z, core),
            device_id_type=pl.DeviceIdType.MESH,
        )

    small_ref[...] = jnp.zeros_like(small_ref)
    heads[0].wait_recv()
    locals_[0].wait()
    keep = (residual_ref, mixed_ref, pm_ref, place_ref)
    spread_refs = (
        att_own, att_sib, x_ref, g_ref, ctl_ref, w_own, w_sib, gain_ref, wsm_ref
    )

    @pl.loop(0, blocks)
    def _(block):
        spread_block(experts, routes, rows, block, spread_refs, send_ref, recv_ref, keep)
        for k in range(3):
            dispatch(block, k).start()

    for copy in heads[1:]:
        copy.wait_recv()
    for copy in locals_[1:]:
        copy.wait()

    @pl.loop(0, blocks)
    def _(block):
        for k in range(3):
            dispatch(block, k).wait_recv()
        expert_block(
            block, recv_ref, result_ref, back_ref, (gate_w, up_w, down_w),
            (hidden_ref, d_gate_ref, d_up_ref),
        )
        for k in range(3):
            giveback(block, k).start()

    peers, _, capacity, width = recv_ref.shape[1:]
    total = blocks * peers * capacity
    step = 2 * LANES

    @pl.loop(0, width // step)
    def _(chunk):
        span = pl.ds(pl.multiple_of(chunk * step, step), step)
        lhs = recv_ref[:, :, 0, :, span].reshape(total, step).T
        dgate_out[span, :] = dot(lhs, d_gate_ref[...]).astype(BF16)
        dup_out[span, :] = dot(lhs, d_up_ref[...]).astype(BF16)

    @pl.loop(0, hidden_ref.shape[1] // step)
    def _(chunk):
        span = pl.ds(pl.multiple_of(chunk * step, step), step)
        lhs = hidden_ref[:, span].T
        rhs = recv_ref[:, :, 1].reshape(total, width)
        ddown_out[span, :] = dot(lhs, rhs).astype(BF16)

    @pl.loop(0, blocks)
    def _(block):
        for k in range(3):
            giveback(block, k).wait_recv()
        combine_block(
            experts, routes, rows, block, (g_ref, ctl_ref, gain_ref, turned_ref, cvec_ref),
            keep, back_ref, (out_ref, prev_ref, dres_ref, branch_ref), small_ref,
        )

    for copy in heads:
        copy.wait_send()
    for block in range(blocks):
        for k in range(3):
            dispatch(block, k).wait_send()
            giveback(block, k).wait_send()


def expert_layer(
    experts, routes, rows, attended, x_own, cot_own, ctl, w_own, w_sib, gain, wsm, turned,
    cvec, w_gate, w_up, w_down,
):
    mine, width = x_own.shape
    blocks = mine // rows
    peers = lax.axis_size("ep")
    span = attended.shape[1]
    hidden = w_gate.shape[1]
    vmem = pl.BlockSpec(memory_space=pltpu.VMEM)
    total = blocks * peers * LANES
    grads = [(2 * w.shape[0], w.shape[1]) for w in (w_gate, w_up, w_down)]
    return pl.pallas_call(
        functools.partial(layer_kernel, experts, routes, rows, blocks),
        in_specs=[vmem] * 13,
        out_specs=[vmem] * 8,
        out_shape=[
            shape((blocks, rows, width), BF16), shape((blocks, 8, rows), F32),
            shape((mine, width), F32), shape((mine, width), BF16), shape((SMALL, width), F32),
        ]
        + [shape(dims, BF16) for dims in grads],
        scratch_shapes=[pltpu.VMEM((mine, span), BF16)] * 2
        + [pltpu.VMEM(dims, BF16) for dims in grads]
        + [
            pltpu.VMEM((mine, width), F32), pltpu.VMEM((mine, width), BF16),
            pltpu.VMEM((mine, LANES), F32), pltpu.VMEM((mine, experts * LANES), BF16),
            pltpu.VMEM((blocks, experts, KINDS, LANES, width), BF16),
        ]
        + [pltpu.VMEM((blocks, peers, KINDS, LANES, width), BF16)] * 3
        + [pltpu.VMEM((total, hidden), BF16)] * 3
        + [
            pltpu.SemaphoreType.DMA((4,)), pltpu.SemaphoreType.DMA((4,)),
            pltpu.SemaphoreType.DMA((4,)),
        ]
        + [pltpu.SemaphoreType.DMA((blocks, 3))] * 4,
        compiler_params=pltpu.CompilerParams(
            collective_id=2, has_side_effects=True, vmem_limit_bytes=62 * 1024 * 1024
        ),
        name="expert_layer",
    )(
        attended.reshape(2, mine, span), x_own, cot_own, ctl, w_own, w_sib, gain, wsm,
        turned, cvec, w_gate, w_up, w_down,
    )


def one_chip(
    tokens,
    prev_logits,
    segments,
    routes,
    cotangent,
    gain_attn,
    w_qkv,
    w_out,
    gain_moe,
    w_router,
    const_proj,
    const_vec,
    w_gate,
    w_up,
    w_down,
):
    rows, width = tokens.shape[1:]
    peers = lax.axis_size("ep")
    place = lax.axis_index("ep")
    core = lax.axis_index("fs")
    cross = place % 2
    route_count = w_router.shape[1]
    experts = route_count - 4
    capacity = LANES
    length = rows * peers
    mine = length // 2
    span = width // 2
    hidden_width = w_gate.shape[2]
    pairs = [[], []]
    for flip in range(2):
        for source in range(peers):
            for side in range(2):
                target = side * 2 + ((source % 2) ^ flip)
                pairs[flip].append((source * 2 + side, target * 2 + source // 2))

    def swap(array):
        return lax.ppermute(array, "fs", [(0, 1), (1, 0)])

    def by_core(own, other, axis=0):
        return jnp.where(
            core == 0,
            jnp.concatenate([own, other], axis=axis),
            jnp.concatenate([other, own], axis=axis),
        )

    def to_chip(array):
        near = lax.ppermute(
            lax.dynamic_index_in_dim(array, cross, 0, False), ("ep", "fs"), pairs[0]
        )
        far = lax.ppermute(
            lax.dynamic_index_in_dim(array, 1 - cross, 0, False), ("ep", "fs"), pairs[1]
        )
        return jnp.where(
            cross == 0, jnp.concatenate([near, far]), jnp.concatenate([far, near])
        )

    x_own = to_chip(tokens)
    x_sib = swap(x_own)
    qkv_split = w_qkv.reshape(span, 3, 2, span)
    qkv_mine = lax.dynamic_index_in_dim(qkv_split, core, 2, False).reshape(span, 3 * span)
    qkv_sent = lax.dynamic_index_in_dim(qkv_split, 1 - core, 2, False).reshape(span, 3 * span)
    qkv_weight = by_core(qkv_mine, swap(qkv_sent))
    out_sib = swap(w_out)
    pad = jnp.zeros((span, 8 - route_count), BF16)
    small_own = jnp.concatenate(
        [w_router, pad, const_proj, const_vec, gain_attn[:, None], gain_moe[:, None]], axis=1
    )
    small_all = by_core(small_own, swap(small_own))
    small_turned = small_all.T.astype(F32)
    attn_gain = small_turned[14:15]
    moe_gain = small_turned[15:16]
    wsm = jnp.pad(small_all[:, :12], ((0, 0), (0, LANES - 12)))
    turned = jnp.pad(small_turned[:12], ((0, LANES - 12), (0, 0)))
    cvec_turned = jnp.pad(small_all[:, 12:14].T, ((0, LANES - 2), (0, 0)))
    seg_sib = swap(segments)
    seg_pair = by_core(segments[None], seg_sib[None])
    seg_row = seg_pair.reshape(4, length)[place][None, :]
    seg_col = seg_row.reshape(length, 1)

    x_all = by_core(x_own, x_sib)
    normed, qkv = pl.pallas_call(
        norm_qkv_kernel,
        grid=(length // rows,),
        in_specs=[per_row(rows, width), whole((1, width)), whole((width, 3 * span))],
        out_specs=[per_row(rows, width), per_row(rows, 3 * span)],
        out_shape=[shape((length, width), BF16), shape((length, 3 * span), BF16)],
        compiler_params=params(),
        cost_estimate=cost(2 * length * width * 3 * span, 6e6),
        name="norm_qkv",
    )(x_all, attn_gain, qkv_weight)

    head_pairs = span // LANES
    reach = length // 2

    def heads_at(offset):
        return pl.BlockSpec((length, LANES), lambda p: (0, offset + p))

    lse_spec = pl.BlockSpec((1, 8, length), lambda p: (p, 0, 0))
    attended, lse = pl.pallas_call(
        functools.partial(attend_kernel, rows, reach),
        grid=(head_pairs,),
        in_specs=[
            heads_at(0), heads_at(head_pairs), heads_at(2 * head_pairs),
            whole((length, 1)), whole((1, length)),
        ],
        out_specs=[heads_at(0), lse_spec],
        out_shape=[shape((length, span), BF16), shape((head_pairs, 8, length), F32)],
        compiler_params=params(),
        cost_estimate=cost(12e9, 4e6),
        name="attend",
    )(qkv, qkv, qkv, seg_col, seg_row)

    cot_own = to_chip(cotangent)
    ctl = jnp.concatenate(
        [
            prev_logits,
            jnp.zeros(prev_logits.shape[:2] + (8 - route_count,), F32),
            routes.astype(F32),
        ],
        axis=2,
    )
    ctl = jnp.pad(to_chip(ctl), ((0, 0), (0, LANES - 10)))
    blocks = mine // rows
    (
        block_out, d_prev, d_residual, d_branch, small, grad_gate, grad_up, grad_down,
    ) = expert_layer(
        experts, route_count, rows, attended, x_own, cot_own, ctl, w_out, out_sib, moe_gain,
        wsm, turned, cvec_turned, w_gate[0], w_up[0], w_down[0],
    )

    branch_all = by_core(d_branch, swap(d_branch))
    valid = (seg_col != SEGS - 1).astype(F32)
    d_att = (dot(branch_all, w_out, ((1,), (1,))) * valid).astype(BF16)
    grad_out = dot(attended, branch_all, ((0,), (0,))).astype(BF16)
    d_queries, d_keys, d_values = pl.pallas_call(
        functools.partial(attend_back_kernel, rows, reach),
        grid=(head_pairs,),
        in_specs=[
            heads_at(0), heads_at(head_pairs), heads_at(2 * head_pairs), heads_at(0),
            whole((length, 1)), whole((1, length)), lse_spec,
        ],
        out_specs=[heads_at(0)] * 3,
        out_shape=[shape((length, span), BF16)] * 3,
        scratch_shapes=[pltpu.VMEM((length, LANES), F32)] * 2,
        compiler_params=params(),
        cost_estimate=cost(30e9, 5e6),
        name="attend_back",
    )(qkv, qkv, qkv, d_att, seg_col, seg_row, lse)
    d_qkv = jnp.concatenate([d_queries, d_keys, d_values], axis=1)
    d_normed = dot(d_qkv, qkv_weight, ((1,), (1,)))
    d_normed_own = lax.dynamic_slice_in_dim(d_normed, core * mine, mine)
    d_normed_sib = swap(
        lax.dynamic_slice_in_dim(d_normed, (1 - core) * mine, mine).astype(BF16)
    )
    grad_qkv = dot(normed, d_qkv, ((0,), (0,))).astype(BF16)
    d_tokens, gain_rows = pl.pallas_call(
        finish_kernel,
        grid=(blocks,),
        in_specs=[per_row(rows, width)] * 4 + [whole((1, width))],
        out_specs=[per_row(rows, width), whole((8, width))],
        out_shape=[shape((mine, width), BF16), shape((8, width), F32)],
        compiler_params=params(),
        cost_estimate=cost(1e8, 6e6),
        name="finish",
    )(x_own, d_normed_own, d_normed_sib, d_residual, attn_gain)

    out_mine = lax.dynamic_slice_in_dim(grad_out, core * span, span, axis=1)
    out_sent = lax.dynamic_slice_in_dim(grad_out, (1 - core) * span, span, axis=1)
    out_cols = by_core(out_mine, swap(out_sent))
    small = jnp.concatenate([small[: SMALL - 1], gain_rows[:1]]).T.astype(BF16)
    dense = jnp.concatenate(
        [grad_qkv, out_cols, jnp.pad(small, ((0, 0), (0, LANES - SMALL)))], axis=1
    )
    shares = reduce_all(
        grad_gate, grad_up, grad_down, dense, block_out, d_tokens, d_prev
    )
    pieces = shares[3:5]
    out_home, dtok_home, prev_home = shares[5:]

    def columns_of(start):
        own, other = (piece[:, start : start + span] for piece in pieces)
        return by_core(own, other, axis=1)

    share_qkv = jnp.concatenate([columns_of(k * span) for k in range(3)], axis=1)
    share_out = columns_of(3 * span)
    share_small = sum(piece[:, 4 * span : 4 * span + SMALL] for piece in pieces)
    return (
        out_home,
        dtok_home.astype(F32),
        jnp.swapaxes(prev_home, 1, 2)[:, :, :route_count],
        share_small[:, 15],
        share_qkv,
        share_out,
        share_small[:, 14],
        share_small[:, :route_count],
        share_small[:, 8:12],
        share_small[:, 12:14],
    ) + tuple(shares[:3])


def suits(mesh, tokens, w_router, w_gate):
    peers = mesh.shape["ep"]
    rows = tokens.shape[1] // peers
    micro = tokens.shape[0] // (mesh.shape["dp"] * mesh.shape["fs"])
    routes = w_router.shape[1]
    return (
        peers == 4
        and mesh.shape["fs"] == 2
        and micro == 2
        and (routes - 4) * 2 == peers
        and 3 * rows // routes == LANES
        and tokens.shape[2] % (2 * LANES) == 0
    )


def solution(mesh):
    placed = (
        P(("dp", "fs"), "ep", None),
        P(("dp", "fs"), "ep", None),
        P(("dp", "fs"), None),
        P(("dp", "fs"), "ep", None),
        P(("dp", "fs"), "ep", None),
        P("fs"),
        P("fs", None),
        P("fs", None),
        P("fs"),
        P("fs", None),
        P("fs", None),
        P("fs", None),
        P("ep", "fs", None),
        P("ep", "fs", None),
        P("ep", "fs", None),
    )
    def layer(*arrays):
        fits = suits(mesh, arrays[0], arrays[9], arrays[12])
        return mapped(one_chip if fits else shards)(*arrays)

    def mapped(body):
        return jax.shard_map(
            body,
            mesh=mesh,
            in_specs=placed,
            out_specs=(
                P(("dp", "fs"), "ep", None),
                P(("dp", "fs"), "ep", None),
                P(("dp", "fs"), "ep", None),
                P(("ep", "dp", "fs")),
                P(("ep", "dp", "fs"), None),
                P(("ep", "dp", "fs"), None),
                P(("ep", "dp", "fs")),
                P(("ep", "dp", "fs"), None),
                P(("ep", "dp", "fs"), None),
                P(("ep", "dp", "fs"), None),
                P("ep", ("dp", "fs"), None),
                P("ep", ("dp", "fs"), None),
                P("ep", ("dp", "fs"), None),
            ),
            check_vma=False,
        )

    return layer
```

```python
import functools

import jax
import jax.numpy as jnp
from jax import lax
from jax.experimental import pallas as pl
from jax.experimental.pallas import tpu as pltpu
from jax.sharding import PartitionSpec as P

HEAD = 64
SEGS = 4


NORM_EPS = 1e-06
MASK_FILL = -1e30
HIGHEST = lax.Precision.HIGHEST


def rms_scale(values, gains):
    inverse = lax.rsqrt(jnp.mean(values * values, axis=-1, keepdims=True) + NORM_EPS)
    return values * inverse * gains


def small_softmax(logit_rows):
    largest = jnp.max(logit_rows, axis=-1, keepdims=True)
    powers = jnp.exp(logit_rows - largest)
    return powers / jnp.sum(powers, axis=-1, keepdims=True)


def add_tuple(first_tuple, second_tuple):
    if first_tuple is None:
        return second_tuple
    return tuple(
        (first_term + second_term for first_term, second_term in zip(first_tuple, second_tuple))
    )


def shards(
    tokens,
    prev_logits,
    segments,
    routes,
    cotangent,
    gain_attn,
    w_qkv,
    w_out,
    gain_moe,
    w_router,
    const_proj,
    const_vec,
    w_gate,
    w_up,
    w_down,
):
    micro_count, row_count, model_width = tokens.shape
    head_count = model_width // HEAD
    peer_count = lax.axis_size("ep")
    my_index = lax.axis_index("ep")
    route_count = w_router.shape[1]
    expert_count = route_count - 4
    half_count = peer_count // expert_count
    capacity = (3 * row_count // route_count + 7) // 8 * 8
    seq_length = row_count * peer_count
    slot_count = expert_count * capacity
    pos_all = jnp.arange(seq_length, dtype=jnp.int32)
    pos_mine = my_index * row_count + jnp.arange(row_count, dtype=jnp.int32)
    expert_ids = jnp.arange(expert_count, dtype=jnp.int32)
    slot_ids = jnp.arange(slot_count, dtype=jnp.int32)
    route_ids = jnp.arange(route_count, dtype=jnp.int32)
    layer_outputs = []
    input_grads = []
    prev_grads = []
    dense_acc = None
    expert_acc = None
    for step_index in range(micro_count):
        gathered = (
            lax.all_gather(w_qkv, "fs", axis=0, tiled=True),
            lax.all_gather(w_out, "fs", axis=0, tiled=True),
            lax.all_gather(w_router, "fs", axis=0, tiled=True),
            lax.all_gather(const_proj, "fs", axis=0, tiled=True),
            lax.all_gather(const_vec, "fs", axis=0, tiled=True),
            lax.all_gather(gain_attn, "fs", axis=0, tiled=True),
            lax.all_gather(gain_moe, "fs", axis=0, tiled=True),
            lax.all_gather(w_gate, "fs", axis=1, tiled=True),
            lax.all_gather(w_up, "fs", axis=1, tiled=True),
            lax.all_gather(w_down, "fs", axis=1, tiled=True),
        )
        (
            qkv_weight,
            out_weight,
            router_weight,
            cproj_weight,
            cvec_weight,
            attn_gain,
            moe_gain,
            gate_weight,
            up_weight,
            down_weight,
        ) = gathered
        gate_weight = gate_weight[0]
        up_weight = up_weight[0]
        down_weight = down_weight[0]
        attn_gain = attn_gain.astype(jnp.float32)
        moe_gain = moe_gain.astype(jnp.float32)
        router_float = router_weight.astype(jnp.float32)
        cproj_float = cproj_weight.astype(jnp.float32)
        cvec_float = cvec_weight.astype(jnp.float32)
        token_rows = tokens[step_index].astype(jnp.float32)
        seg_all = segments[step_index]
        seg_mine = lax.dynamic_slice_in_dim(seg_all, my_index * row_count, row_count)
        allowed = (seg_mine[:, None] == seg_all[None, :]) & (pos_all[None, :] <= pos_mine[:, None])
        valid_rows = (seg_mine != SEGS - 1).astype(jnp.float32)[:, None]
        normed = rms_scale(token_rows, attn_gain).astype(jnp.bfloat16)
        qkv_rows = jnp.dot(normed, qkv_weight, preferred_element_type=jnp.float32).astype(
            jnp.bfloat16
        )
        queries = qkv_rows[:, :model_width].reshape(row_count, head_count, HEAD)
        keys_local = qkv_rows[:, model_width : 2 * model_width]
        values_local = qkv_rows[:, 2 * model_width :]
        keys_all, values_all = (
            lax.all_gather(keys_local, "ep", axis=0, tiled=True),
            lax.all_gather(values_local, "ep", axis=0, tiled=True),
        )
        key_heads = keys_all.reshape(seq_length, head_count, HEAD)
        value_heads = values_all.reshape(seq_length, head_count, HEAD)
        scores = (
            jnp.einsum("qhd,khd->hqk", queries, key_heads, preferred_element_type=jnp.float32)
            * 0.125
        )
        scores = jnp.where(allowed[None], scores, MASK_FILL)
        largest = jnp.max(scores, axis=-1, keepdims=True)
        powers = jnp.exp(scores - largest)
        row_total = jnp.sum(powers, axis=-1, keepdims=True)
        log_total = largest + jnp.log(row_total)
        attn_probs = powers / row_total
        attended = jnp.einsum(
            "hqk,khd->qhd",
            attn_probs.astype(jnp.bfloat16),
            value_heads,
            preferred_element_type=jnp.float32,
        ).reshape(row_count, model_width)
        attended = (attended * valid_rows).astype(jnp.bfloat16)
        residual = token_rows + jnp.dot(attended, out_weight, preferred_element_type=jnp.float32)
        mixed = rms_scale(residual, moe_gain).astype(jnp.bfloat16)
        mixed_float = mixed.astype(jnp.float32)
        logits = (
            jnp.dot(mixed, router_weight, preferred_element_type=jnp.float32)
            + prev_logits[step_index]
        )
        router_probs = small_softmax(logits)
        route_rows = routes[step_index]
        choose = (route_rows[:, :, None] == route_ids[None, None, :]).astype(jnp.float32)
        gate_values = jnp.sum(choose * router_probs[:, None, :], axis=-1)
        const_logits = jnp.dot(mixed, cproj_weight, preferred_element_type=jnp.float32)
        mixings = []
        const_outs = []
        for const_index in range(2):
            mixing = small_softmax(const_logits[:, 2 * const_index : 2 * const_index + 2])
            mixings.append(mixing)
            const_outs.append(
                mixing[:, :1] * mixed_float + mixing[:, 1:] * cvec_float[:, const_index][None, :]
            )
        pair_route = route_rows.reshape(-1)
        expert_hit = (pair_route[:, None] == expert_ids[None, :]).astype(jnp.int32)
        slot_index = jnp.sum((jnp.cumsum(expert_hit, axis=0) - expert_hit) * expert_hit, axis=1)
        slot_cell = jnp.sum(expert_hit * expert_ids[None, :], axis=1) * capacity + slot_index
        slot_place = jnp.where(jnp.sum(expert_hit, axis=1) > 0, slot_cell, -1)
        slot_table = (slot_ids[:, None] == slot_place[None, :]).astype(jnp.bfloat16)
        pair_rows = jnp.repeat(mixed, 2, axis=0)
        packed = jnp.einsum(
            "sp,pd->sd", slot_table, pair_rows, preferred_element_type=jnp.float32
        ).astype(jnp.bfloat16)
        outgoing = jnp.broadcast_to(
            packed.reshape(expert_count, 1, capacity, model_width),
            (expert_count, half_count, capacity, model_width),
        ).reshape(peer_count, capacity, model_width)
        received = lax.all_to_all(outgoing, "ep", split_axis=0, concat_axis=0, tiled=True)
        flat_rows = received.reshape(-1, model_width)
        gate_part = jnp.dot(flat_rows, gate_weight, preferred_element_type=jnp.float32)
        up_part = jnp.dot(flat_rows, up_weight, preferred_element_type=jnp.float32)
        hidden = (jax.nn.silu(gate_part) * up_part).astype(jnp.bfloat16)
        part_out = (
            jnp.dot(hidden, down_weight, preferred_element_type=jnp.float32)
            .astype(jnp.bfloat16)
            .reshape(received.shape)
        )
        returned_rows = lax.all_to_all(part_out, "ep", split_axis=0, concat_axis=0, tiled=True)
        returned_rows, kept_rows = (returned_rows, received)
        halves = returned_rows.reshape(expert_count, half_count, capacity, model_width)
        pair_ffn = jnp.zeros((2 * row_count, model_width), jnp.float32)
        for half_index in range(half_count):
            pair_ffn = pair_ffn + jnp.einsum(
                "sp,sd->pd",
                slot_table,
                halves[:, half_index].reshape(slot_count, model_width),
                preferred_element_type=jnp.float32,
            )
        expert_out = pair_ffn.reshape(row_count, 2, model_width)
        expert_out = (
            expert_out + choose[:, :, expert_count + 1 : expert_count + 2] * mixed_float[:, None, :]
        )
        for const_index in range(2):
            column = expert_count + 2 + const_index
            expert_out = (
                expert_out + choose[:, :, column : column + 1] * const_outs[const_index][:, None, :]
            )
        result_rows = residual + jnp.sum(gate_values[:, :, None] * expert_out, axis=1)
        layer_outputs.append(result_rows.astype(jnp.bfloat16))
        grad_rows = cotangent[step_index].astype(jnp.float32)
        d_gates = jnp.sum(expert_out * grad_rows[:, None, :], axis=-1)
        d_probs = jnp.sum(choose * d_gates[:, :, None], axis=1)
        d_logits = router_probs * (
            d_probs - jnp.sum(router_probs * d_probs, axis=-1, keepdims=True)
        )
        prev_grads.append(d_logits)
        grad_router = jnp.dot(mixed_float.T, d_logits, precision=HIGHEST)
        d_mixed = jnp.dot(d_logits, router_float.T, precision=HIGHEST)
        weighted = gate_values[:, :, None] * grad_rows[:, None, :]
        d_mixed = d_mixed + jnp.sum(
            choose[:, :, expert_count + 1 : expert_count + 2] * weighted, axis=1
        )
        cproj_grads = []
        cvec_grads = []
        for const_index in range(2):
            column = expert_count + 2 + const_index
            mixing = mixings[const_index]
            d_const = jnp.sum(choose[:, :, column : column + 1] * weighted, axis=1)
            d_mix = jnp.stack(
                [
                    jnp.sum(d_const * mixed_float, axis=-1),
                    jnp.sum(d_const * cvec_float[:, const_index][None, :], axis=-1),
                ],
                axis=-1,
            )
            d_mixlog = mixing * (d_mix - jnp.sum(mixing * d_mix, axis=-1, keepdims=True))
            cproj_grads.append(jnp.dot(mixed_float.T, d_mixlog, precision=HIGHEST))
            cvec_grads.append(jnp.sum(mixing[:, 1:] * d_const, axis=0))
            d_mixed = (
                d_mixed
                + mixing[:, :1] * d_const
                + jnp.dot(
                    d_mixlog,
                    cproj_float[:, 2 * const_index : 2 * const_index + 2].T,
                    precision=HIGHEST,
                )
            )
        grad_cproj = jnp.concatenate(cproj_grads, axis=1)
        grad_cvec = jnp.stack(cvec_grads, axis=1)
        d_pairs = weighted.reshape(2 * row_count, model_width).astype(jnp.bfloat16)
        d_packed = jnp.einsum(
            "sp,pd->sd", slot_table, d_pairs, preferred_element_type=jnp.float32
        ).astype(jnp.bfloat16)
        d_outgoing = jnp.broadcast_to(
            d_packed.reshape(expert_count, 1, capacity, model_width),
            (expert_count, half_count, capacity, model_width),
        ).reshape(peer_count, capacity, model_width)
        d_received = lax.all_to_all(d_outgoing, "ep", split_axis=0, concat_axis=0, tiled=True)
        flat_rows = kept_rows.reshape(-1, model_width)
        flat_grads = d_received.reshape(-1, model_width)
        gate_part = jnp.dot(flat_rows, gate_weight, preferred_element_type=jnp.float32)
        up_part = jnp.dot(flat_rows, up_weight, preferred_element_type=jnp.float32)
        activated = jax.nn.silu(gate_part)
        hidden = (activated * up_part).astype(jnp.bfloat16)
        grad_down = jnp.einsum("rf,rd->fd", hidden, flat_grads, preferred_element_type=jnp.float32)
        d_hidden = jnp.einsum(
            "rd,fd->rf", flat_grads, down_weight, preferred_element_type=jnp.float32
        )
        sigmoid_gate = jax.nn.sigmoid(gate_part)
        d_gate_part = (
            d_hidden * up_part * sigmoid_gate * (1.0 + gate_part * (1.0 - sigmoid_gate))
        ).astype(jnp.bfloat16)
        d_up_part = (d_hidden * activated).astype(jnp.bfloat16)
        grad_gate = jnp.einsum(
            "rd,rf->df", flat_rows, d_gate_part, preferred_element_type=jnp.float32
        )
        grad_up = jnp.einsum("rd,rf->df", flat_rows, d_up_part, preferred_element_type=jnp.float32)
        d_inputs = jnp.einsum(
            "rf,df->rd", d_gate_part, gate_weight, preferred_element_type=jnp.float32
        )
        d_inputs = d_inputs + jnp.einsum(
            "rf,df->rd", d_up_part, up_weight, preferred_element_type=jnp.float32
        )
        d_inputs = d_inputs.astype(jnp.bfloat16).reshape(peer_count, capacity, model_width)
        d_returned = lax.all_to_all(d_inputs, "ep", split_axis=0, concat_axis=0, tiled=True)
        d_halves = d_returned.reshape(expert_count, half_count, capacity, model_width)
        for half_index in range(half_count):
            d_pair_in = jnp.einsum(
                "sp,sd->pd",
                slot_table,
                d_halves[:, half_index].reshape(slot_count, model_width),
                preferred_element_type=jnp.float32,
            )
            d_mixed = d_mixed + jnp.sum(d_pair_in.reshape(row_count, 2, model_width), axis=1)
        expert_acc = add_tuple(expert_acc, (grad_gate, grad_up, grad_down))
        moe_vjp = jax.vjp(rms_scale, residual, moe_gain)[1]
        d_residual_norm, grad_moe_gain = moe_vjp(d_mixed)
        d_residual = grad_rows + d_residual_norm
        d_branch = d_residual.astype(jnp.bfloat16)
        grad_out = jnp.einsum("rd,re->de", attended, d_branch, preferred_element_type=jnp.float32)
        d_attended = (
            jnp.einsum("re,de->rd", d_branch, out_weight, preferred_element_type=jnp.float32)
            * valid_rows
        ).astype(jnp.bfloat16)
        d_heads = d_attended.reshape(row_count, head_count, HEAD)
        scores = (
            jnp.einsum("qhd,khd->hqk", queries, key_heads, preferred_element_type=jnp.float32)
            * 0.125
        )
        scores = jnp.where(allowed[None], scores, MASK_FILL)
        attn_probs = jnp.exp(scores - log_total)
        d_weights = jnp.einsum(
            "qhd,khd->hqk", d_heads, value_heads, preferred_element_type=jnp.float32
        )
        delta_rows = jnp.sum(attn_probs * d_weights, axis=-1, keepdims=True)
        d_scores = (attn_probs * (d_weights - delta_rows)).astype(jnp.bfloat16)
        d_queries = (
            jnp.einsum(
                "hqk,khd->qhd", d_scores, key_heads, preferred_element_type=jnp.float32
            ).reshape(row_count, model_width)
            * 0.125
        )
        d_values = jnp.einsum(
            "hqk,qhd->khd",
            attn_probs.astype(jnp.bfloat16),
            d_heads,
            preferred_element_type=jnp.float32,
        ).reshape(seq_length, model_width)
        d_keys = (
            jnp.einsum(
                "hqk,qhd->khd", d_scores, queries, preferred_element_type=jnp.float32
            ).reshape(seq_length, model_width)
            * 0.125
        )
        d_keys_mine, d_values_mine = (
            lax.psum_scatter(
                d_keys.astype(jnp.bfloat16), "ep", scatter_dimension=0, tiled=True
            ).astype(jnp.float32),
            lax.psum_scatter(
                d_values.astype(jnp.bfloat16), "ep", scatter_dimension=0, tiled=True
            ).astype(jnp.float32),
        )
        d_qkv = jnp.concatenate([d_queries, d_keys_mine, d_values_mine], axis=1).astype(
            jnp.bfloat16
        )
        grad_qkv = jnp.einsum("rd,re->de", normed, d_qkv, preferred_element_type=jnp.float32)
        d_normed = jnp.einsum("re,de->rd", d_qkv, qkv_weight, preferred_element_type=jnp.float32)
        attn_vjp = jax.vjp(rms_scale, token_rows, attn_gain)[1]
        d_tokens_norm, grad_attn_gain = attn_vjp(d_normed)
        input_grads.append(d_residual + d_tokens_norm)
        dense_terms = (
            grad_attn_gain,
            grad_qkv,
            grad_out,
            grad_moe_gain,
            grad_router,
            grad_cproj,
            grad_cvec,
        )
        dense_shares = (
            lax.psum_scatter(dense_terms[0], ("ep", "dp", "fs"), scatter_dimension=0, tiled=True),
            lax.psum_scatter(dense_terms[1], ("ep", "dp", "fs"), scatter_dimension=0, tiled=True),
            lax.psum_scatter(dense_terms[2], ("ep", "dp", "fs"), scatter_dimension=0, tiled=True),
            lax.psum_scatter(dense_terms[3], ("ep", "dp", "fs"), scatter_dimension=0, tiled=True),
            lax.psum_scatter(dense_terms[4], ("ep", "dp", "fs"), scatter_dimension=0, tiled=True),
            lax.psum_scatter(dense_terms[5], ("ep", "dp", "fs"), scatter_dimension=0, tiled=True),
            lax.psum_scatter(dense_terms[6], ("ep", "dp", "fs"), scatter_dimension=0, tiled=True),
        )
        dense_acc = add_tuple(dense_acc, dense_shares)
    expert_shares = (
        lax.psum_scatter(
            expert_acc[0][None].astype(jnp.bfloat16), ("dp", "fs"), scatter_dimension=1, tiled=True
        ).astype(jnp.float32),
        lax.psum_scatter(
            expert_acc[1][None].astype(jnp.bfloat16), ("dp", "fs"), scatter_dimension=1, tiled=True
        ).astype(jnp.float32),
        lax.psum_scatter(
            expert_acc[2][None].astype(jnp.bfloat16), ("dp", "fs"), scatter_dimension=1, tiled=True
        ).astype(jnp.float32),
    )
    return (
        jnp.stack(layer_outputs),
        jnp.stack(input_grads),
        jnp.stack(prev_grads),
        dense_acc[0],
        dense_acc[1],
        dense_acc[2],
        dense_acc[3],
        dense_acc[4],
        dense_acc[5],
        dense_acc[6],
        expert_shares[0],
        expert_shares[1],
        expert_shares[2],
    )


NEG = -1e30
KINDS = 2
SMALL = 16
LANES = 128
F32 = jnp.float32
BF16 = jnp.bfloat16


def dot(lhs, rhs, dims=((1,), (0,)), precision=None):
    return lax.dot_general(
        lhs, rhs, (dims, ((), ())), precision=precision, preferred_element_type=F32
    )


def key_span(block, rows, reach):
    start = max(0, block * rows - reach)
    return start, (block + 1) * rows - start


def attend_back_kernel(
    rows, reach, q_ref, k_ref, v_ref, do_ref, segc_ref, segr_ref, lse_ref,
    dq_ref, dk_ref, dv_ref, dk_sum, dv_sum,
):
    length = q_ref.shape[0]
    dk_sum[...] = jnp.zeros_like(dk_sum)
    dv_sum[...] = jnp.zeros_like(dv_sum)
    keys_turned = k_ref[...].T
    for block in range(length // rows):
        start, width = key_span(block, rows, reach)
        queries = q_ref[block * rows : (block + 1) * rows, :]
        grads = do_ref[block * rows : (block + 1) * rows, :]
        keys = k_ref[start : start + width, :]
        values = v_ref[start : start + width, :]
        seg_k = segc_ref[start : start + width, 0:1]
        seg_q = segr_ref[0:1, block * rows : (block + 1) * rows]
        key_pos = start + lax.broadcasted_iota(jnp.int32, (width, rows), 0)
        query_pos = block * rows + lax.broadcasted_iota(jnp.int32, (width, rows), 1)
        allowed = (seg_q == seg_k) & (key_pos <= query_pos)
        lane = lax.broadcasted_iota(jnp.int32, (rows, LANES), 1)
        dq_parts = []
        for head in range(2):
            mine = (lane // HEAD) == head
            head_q = jnp.where(mine, queries, 0)
            head_g = jnp.where(mine, grads, 0)
            log_total = lse_ref[0, head : head + 1, block * rows : (block + 1) * rows]
            scores = dot(keys, head_q, ((1,), (1,))) * 0.125
            probs = jnp.exp(jnp.where(allowed, scores, NEG) - log_total)
            d_probs = dot(values, head_g, ((1,), (1,)))
            delta = jnp.sum(probs * d_probs, axis=0, keepdims=True)
            d_scores = (probs * (d_probs - delta)).astype(BF16)
            dv_sum[start : start + width, :] += dot(probs.astype(BF16), head_g)
            dk_sum[start : start + width, :] += dot(d_scores, head_q)
            turned = keys_turned[head * HEAD : (head + 1) * HEAD, start : start + width]
            dq_parts.append(dot(turned, d_scores))
        dq = jnp.concatenate(dq_parts, axis=0).T * 0.125
        dq_ref[block * rows : (block + 1) * rows, :] = dq.astype(BF16)
    dk_ref[...] = (dk_sum[...] * 0.125).astype(BF16)
    dv_ref[...] = dv_sum[...].astype(BF16)


def column(rows, index):
    return rows[:, index : index + 1]


def chosen_of(ctl):
    lane = lax.broadcasted_iota(jnp.int32, ctl.shape, 1).astype(F32)
    return ((lane == column(ctl, 8)) | (lane == column(ctl, 9))).astype(F32)


def finish_kernel(x_ref, own_ref, sib_ref, dres_ref, gain_ref, out_ref, gain_out_ref):
    rows = x_ref[...].astype(F32)
    d_normed = own_ref[...].astype(F32) + sib_ref[...].astype(F32)
    inverse = lax.rsqrt(jnp.mean(rows * rows, axis=-1, keepdims=True) + NORM_EPS)
    scaled = d_normed * gain_ref[...]
    mean = jnp.mean(scaled * rows, axis=-1, keepdims=True)
    out = dres_ref[...] + inverse * scaled - rows * (inverse * inverse * inverse * mean)
    out_ref[...] = out.astype(out_ref.dtype)

    @pl.when(pl.program_id(0) == 0)
    def _():
        gain_out_ref[...] = jnp.zeros_like(gain_out_ref)

    gain_out_ref[0:1, :] += jnp.sum(d_normed * rows * inverse, axis=0, keepdims=True)


def shape(dims, dtype):
    return jax.ShapeDtypeStruct(dims, dtype)


def whole(dims):
    return pl.BlockSpec(dims, lambda *_: (0,) * len(dims))


def per_row(rows, width):
    return pl.BlockSpec((rows, width), lambda i: (i, 0))


def params():
    return pltpu.CompilerParams(vmem_limit_bytes=56 * 1024 * 1024)


def cost(flops, moved):
    return pl.CostEstimate(flops=int(flops), bytes_accessed=int(moved), transcendentals=0)


class Mail:
    def __init__(self, send_sems, recv_sems):
        self.send_sems = send_sems
        self.recv_sems = recv_sems
        self.used = 0

    def copy(self, source, target, device):
        slot = self.used
        self.used = slot + 1
        return pltpu.make_async_remote_copy(
            src_ref=source,
            dst_ref=target,
            send_sem=self.send_sems.at[slot],
            recv_sem=self.recv_sems.at[slot],
            device_id=device,
            device_id_type=pl.DeviceIdType.MESH,
        )


def position():
    place = lax.axis_index("ep")
    return place // 2, place % 2, lax.axis_index("dp"), lax.axis_index("fs")


def greet(devices):
    barrier = pltpu.get_barrier_semaphore()
    total = 0
    for device, present in devices:
        if present is True:
            pl.semaphore_signal(
                barrier, inc=1, device_id=device, device_id_type=pl.DeviceIdType.MESH
            )
            total = total + 1
        else:

            @pl.when(present)
            def _():
                pl.semaphore_signal(
                    barrier, inc=1, device_id=device, device_id_type=pl.DeviceIdType.MESH
                )

            total = total + jnp.where(present, 1, 0)
    pl.semaphore_wait(barrier, total)


class Line:
    def __init__(self, mail, depth, slots):
        self.depth = depth
        self.slots = slots
        self.place = lax.axis_index("dp")
        y, x, z, core = position()
        self.copies = {}
        for way in range(2):
            step_to = 1 if way == 0 else -1
            device = (y * 2 + x, z + step_to, core)
            for step in range(depth - 1):
                for item, (acc, landing) in enumerate(slots):
                    shard = self.shard(way, step)
                    safe = jnp.clip(shard, 0, depth - 1)
                    self.copies[way, step, item] = mail.copy(
                        acc.at[safe], landing.at[way, step], device
                    )

    def shard(self, way, step):
        if way == 0:
            return self.place + self.depth - 1 - step
        return self.place - (self.depth - 1 - step)

    def sends(self, way, step):
        shard = self.shard(way, step)
        if way == 0:
            return (shard <= self.depth - 1) & (self.place < self.depth - 1)
        return (shard >= 0) & (self.place > 0)

    def gets(self, way, step):
        if way == 0:
            return (self.place > 0) & (self.shard(way, step + 1) <= self.depth - 1)
        return (self.place < self.depth - 1) & (self.shard(way, step + 1) >= 0)

    def send(self, step, item):
        for way in range(2):

            @pl.when(self.sends(way, step))
            def _():
                self.copies[way, step, item].start()

    def take(self, step, item):
        acc, landing = self.slots[item]
        for way in range(2):
            shard = jnp.clip(self.shard(way, step + 1), 0, self.depth - 1)

            @pl.when(self.gets(way, step))
            def _():
                self.copies[way, step, item].wait_recv()
                acc[shard] = (
                    acc[shard].astype(F32) + landing[way, step].astype(F32)
                ).astype(BF16)

    def finish(self, item, store):
        acc, landing = self.slots[item]
        store(acc[self.place].astype(F32))
        for way in range(2):

            @pl.when(self.gets(way, self.depth - 2))
            def _():
                self.copies[way, self.depth - 2, item].wait_recv()
                store(landing[way, self.depth - 2].astype(F32), True)

    def close(self):
        for (way, step, item), copy in self.copies.items():

            @pl.when(self.sends(way, step))
            def _():
                copy.wait_send()


def reduce_kernel(
    depth, cut,
    gate_ref, up_ref, down_ref, dense_ref, out_ref, dtok_ref, prev_ref,
    gate_out, up_out, down_out, own_out, sib_out, out_home, dtok_home, prev_home,
    gate_land, up_land, down_land, gate_acc, up_acc, down_acc,
    gate_line, up_line, down_line,
    y1_land, x1_land, y1_acc, x1_acc, x2_land, y2_land, dense_acc, dense_line, dense_sum,
    send_sems, recv_sems, local_sems,
):
    y, x, z, core = position()
    sibling = (y * 2 + x, z, 1 - core)
    across = (y * 2 + 1 - x, z, core)
    along = ((1 - y) * 2 + x, z, core)
    moved = y != core
    near = ((1 - y) * 2 + x, z, 1 - core)
    far = (core * 2 + 1 - x, z, y)
    greet(
        [
            (sibling, True), (across, True), (along, True),
            (near, moved), (far, moved),
            ((y * 2 + x, z + 1, core), z < depth - 1), ((y * 2 + x, z - 1, core), z > 0),
        ]
    )
    mail = Mail(send_sems, recv_sems)
    experts = [
        (gate_ref, gate_land, gate_acc, gate_line, gate_out),
        (up_ref, up_land, up_acc, up_line, up_out),
        (down_ref, down_land, down_acc, down_line, down_out),
    ]
    halves = [
        mail.copy(source.at[:, 1 - core], land, sibling)
        for source, land, _, _, _ in experts
    ]
    line = Line(mail, depth, [(acc, landing) for _, _, acc, landing, _ in experts])
    rest = dense_ref.shape[3] - cut
    left = pl.ds(0, cut)
    right = pl.ds(cut, rest)
    first_y = mail.copy(dense_ref.at[1 - y, :, :, left], y1_land, along)
    first_x = mail.copy(dense_ref.at[:, 1 - x, :, right], x1_land, across)
    second_x = mail.copy(y1_acc.at[1 - x], x2_land, across)
    second_y = mail.copy(x1_acc.at[1 - y], y2_land, along)
    dense = Line(mail, depth, [(dense_acc, dense_line)])
    homes = [(out_ref, out_home), (dtok_ref, dtok_home), (prev_ref, prev_home)]
    nears = [mail.copy(a.at[x], b.at[x], near) for a, b in homes]
    fars = [mail.copy(a.at[1 - x], b.at[x], far) for a, b in homes]
    stays = [
        pltpu.make_async_copy(a.at[x], b.at[x], local_sems.at[k])
        for k, (a, b) in enumerate(homes)
    ]

    for copy in halves:
        copy.start()
    first_y.start()
    first_x.start()
    for item, (source, land, acc, _, _) in enumerate(experts):
        halves[item].wait_recv()
        for shard in range(depth):
            acc[shard] = (source[shard, core].astype(F32) + land[shard].astype(F32)).astype(BF16)
        line.send(0, item)
    first_y.wait_recv()
    for k in range(2):
        y1_acc[k] = (dense_ref[y, k, :, left].astype(F32) + y1_land[k].astype(F32)).astype(BF16)
    second_x.start()
    first_x.wait_recv()
    for k in range(2):
        x1_acc[k] = (dense_ref[k, x, :, right].astype(F32) + x1_land[k].astype(F32)).astype(BF16)
    second_y.start()
    for copy in fars:
        copy.start()

    @pl.when(moved)
    def _():
        for copy in nears:
            copy.start()

    @pl.when(jnp.logical_not(moved))
    def _():
        for copy in stays:
            copy.start()

    for item in range(3):
        line.take(0, item)
        line.send(1, item)
    size = dense_acc.shape[1]
    second_x.wait_recv()
    second_y.wait_recv()
    for shard in range(depth):
        part = pl.ds(shard * size, size)
        dense_acc[shard, :, left] = (
            y1_acc[x, part].astype(F32) + x2_land[part].astype(F32)
        ).astype(BF16)
        dense_acc[shard, :, right] = (
            x1_acc[y, part].astype(F32) + y2_land[part].astype(F32)
        ).astype(BF16)
    dense.send(0, 0)
    for item in range(3):
        line.take(1, item)
        line.send(2, item)
    dense.take(0, 0)
    dense.send(1, 0)
    for item, (_, _, _, _, result) in enumerate(experts):

        def store(value, add=False):
            result[0] = result[0] + value if add else value

        line.finish(item, store)
    dense.take(1, 0)
    dense.send(2, 0)

    def store_dense(value, add=False):
        dense_sum[...] = dense_sum[...] + value if add else value

    dense.finish(0, store_dense)
    half = size // 2
    last = mail.copy(
        dense_sum.at[pl.ds(pl.multiple_of((1 - core) * half, 8), half)], sib_out, sibling
    )
    last.start()
    own_out[...] = dense_sum[pl.ds(pl.multiple_of(core * half, 8), half), :]
    last.wait()
    for copy in halves + [first_y, first_x, second_x, second_y]:
        copy.wait_send()
    line.close()
    dense.close()
    for copy in fars:
        copy.wait()

    @pl.when(moved)
    def _():
        for copy in nears:
            copy.wait()

    @pl.when(jnp.logical_not(moved))
    def _():
        for copy in stays:
            copy.wait()


def reduce_all(grad_gate, grad_up, grad_down, dense, block_out, d_tokens, d_prev):
    depth = lax.axis_size("dp")
    experts = [
        grad.reshape(depth, 2, grad.shape[0] // (2 * depth), grad.shape[1])
        for grad in (grad_gate, grad_up, grad_down)
    ]
    quarter = dense.shape[0] // 4
    columns = dense.shape[1]
    cut = (columns // LANES + 1) // 2 * LANES
    dense = dense.reshape(2, 2, quarter, columns)
    homes = [
        block_out,
        d_tokens.reshape(block_out.shape),
        d_prev,
    ]
    size = quarter // depth
    parts = [grad.shape[2:] for grad in experts]
    vmem = pl.BlockSpec(memory_space=pltpu.VMEM)
    copies = 3 + 2 * (depth - 1) * 4 + 4 + 6 + 1
    outs = pl.pallas_call(
        functools.partial(reduce_kernel, depth, cut),
        in_specs=[vmem] * 7,
        out_specs=[vmem] * 8,
        out_shape=[shape((1,) + part, F32) for part in parts]
        + [shape((size // 2, columns), F32)] * 2
        + [shape(home.shape, home.dtype) for home in homes],
        scratch_shapes=[pltpu.VMEM((depth,) + part, BF16) for part in parts] * 2
        + [pltpu.VMEM((2, depth - 1) + part, BF16) for part in parts]
        + [
            pltpu.VMEM((2, quarter, cut), BF16),
            pltpu.VMEM((2, quarter, columns - cut), BF16),
            pltpu.VMEM((2, quarter, cut), BF16),
            pltpu.VMEM((2, quarter, columns - cut), BF16),
            pltpu.VMEM((quarter, cut), BF16),
            pltpu.VMEM((quarter, columns - cut), BF16),
            pltpu.VMEM((depth, size, columns), BF16),
            pltpu.VMEM((2, depth - 1, size, columns), BF16),
            pltpu.VMEM((size, columns), F32),
            pltpu.SemaphoreType.DMA((copies,)),
            pltpu.SemaphoreType.DMA((copies,)),
            pltpu.SemaphoreType.DMA((3,)),
        ],
        compiler_params=pltpu.CompilerParams(
            collective_id=1, has_side_effects=True, vmem_limit_bytes=60 * 1024 * 1024
        ),
        name="reduce_all",
    )(*experts, dense, *homes)
    return outs


def attend_pair(pair, rows, reach, span, qkv_ref, segc_ref, segr_ref, att_ref, lse_ref):
    length = qkv_ref.shape[0]
    at_q, at_k, at_v = (
        pl.ds(pl.multiple_of(part * span + pair * LANES, LANES), LANES) for part in range(3)
    )
    for block in range(length // rows):
        start, width = key_span(block, rows, reach)
        here = pl.ds(block * rows, rows)
        there = pl.ds(start, width)
        queries = qkv_ref[here, at_q]
        keys = qkv_ref[there, at_k]
        values = qkv_ref[there, at_v]
        seg_q = segc_ref[here, 0:1]
        seg_k = segr_ref[0:1, there]
        row_pos = block * rows + lax.broadcasted_iota(jnp.int32, (rows, width), 0)
        col_pos = start + lax.broadcasted_iota(jnp.int32, (rows, width), 1)
        allowed = (seg_q == seg_k) & (col_pos <= row_pos)
        lane = lax.broadcasted_iota(jnp.int32, (rows, LANES), 1)
        outs = []
        logs = []
        for head in range(2):
            mine = (lane // HEAD) == head
            scores = dot(jnp.where(mine, queries, 0), keys, ((1,), (1,))) * 0.125
            scores = jnp.where(allowed, scores, NEG)
            largest = jnp.max(scores, axis=-1, keepdims=True)
            powers = jnp.exp(scores - largest)
            total = jnp.sum(powers, axis=-1, keepdims=True)
            outs.append(dot(powers.astype(BF16), values) / total)
            logs.append(largest + jnp.log(total))
        valid = (seg_q != SEGS - 1.0).astype(F32)
        att = jnp.where(lane < HEAD, outs[0], outs[1]) * valid
        att_ref[here, at_q] = att.astype(BF16)
        both = jnp.where(lane < HEAD, logs[0], logs[1]).T
        lse_ref[pair, 0:1, here] = both[0:1, :]
        lse_ref[pair, 1:2, here] = both[HEAD : HEAD + 1, :]


def gather_kernel(
    rows, reach, routes,
    tok_ref, cot_ref, wqkv_ref, wout_ref, prev_ref, route_ref, seg_ref, router_ref, cproj_ref,
    cvec_ref, gain_a_ref, gain_m_ref,
    x_all, cot_own, ctl_own, normed_ref, qkv_ref, att_ref, lse_ref, small_all, wqkv_all,
    wout_sib, segc_ref, segr_ref,
    ctl_wide, ctl_send, small_wide, small_send, seg_all,
    near_send, near_recv, far_send, far_recv, core_send, core_recv, local_sems,
):
    y, x, z, core = position()
    me = y * 2 + x
    sibling = (me, z, 1 - core)
    moved = y != core
    near = ((1 - y) * 2 + x, z, 1 - core)
    far = (core * 2 + 1 - x, z, y)
    greet([(sibling, True), (far, True), (near, moved)])
    span = wqkv_ref.shape[0]

    def block_of(index):
        return pl.ds(pl.multiple_of(index * rows, rows), rows)

    within = block_of(x)
    homes = [
        (tok_ref, x_all.at[block_of(me)]),
        (cot_ref, cot_own.at[within]),
        (ctl_send, ctl_own.at[x]),
    ]
    nears = Mail(near_send, near_recv)
    fars = Mail(far_send, far_recv)
    near_copies = [nears.copy(a.at[x], b, near) for a, b in homes]
    far_copies = [fars.copy(a.at[1 - x], b, far) for a, b in homes]
    stay_copies = [
        pltpu.make_async_copy(a.at[x], b, local_sems.at[k]) for k, (a, b) in enumerate(homes)
    ]

    def send(k):
        far_copies[k].start()

        @pl.when(moved)
        def _():
            near_copies[k].start()

        @pl.when(jnp.logical_not(moved))
        def _():
            stay_copies[k].start()

    def take_near(k):
        @pl.when(moved)
        def _():
            near_copies[k].wait_recv()

        @pl.when(jnp.logical_not(moved))
        def _():
            stay_copies[k].wait()

    send(0)
    inner = Mail(core_send, core_recv)
    weight_copies = []
    own_copies = []
    band = pl.ds(pl.multiple_of(core * span, span), span)
    for part in range(3):
        columns = pl.ds(part * span, span)
        for side, copies in ((1 - core, weight_copies), (core, own_copies)):
            source = wqkv_ref.at[
                :, pl.ds(pl.multiple_of(part * 2 * span + side * span, LANES), span)
            ]
            target = wqkv_all.at[band, columns]
            if copies is weight_copies:
                copies.append(inner.copy(source, target, sibling))
            else:
                copies.append(
                    pltpu.make_async_copy(source, target, local_sems.at[3 + part])
                )
    out_copy = inner.copy(wout_ref, wout_sib, sibling)
    seg_copy = inner.copy(seg_ref, seg_all.at[core], sibling)
    seg_own = pltpu.make_async_copy(seg_ref, seg_all.at[core], local_sems.at[6])
    small_copy = inner.copy(small_send, small_all.at[:, band], sibling)
    seg_copy.start()
    seg_own.start()
    for copy in weight_copies + own_copies:
        copy.start()

    small_wide[...] = jnp.zeros_like(small_wide)
    small_wide[:, 0:routes] = router_ref[...].astype(F32)
    small_wide[:, 8:12] = cproj_ref[...].astype(F32)
    small_wide[:, 12:14] = cvec_ref[...].astype(F32)
    turned = small_wide[...].T[:SMALL, :]
    which = lax.broadcasted_iota(jnp.int32, (SMALL, span), 0)
    turned = jnp.where(which == 14, gain_a_ref[...].astype(F32), turned)
    turned = jnp.where(which == 15, gain_m_ref[...].astype(F32), turned)
    small_send[...] = turned.astype(BF16)
    small_all[:, band] = turned.astype(BF16)
    small_copy.start()
    out_copy.start()
    for m in range(2):
        ctl_wide[...] = jnp.zeros_like(ctl_wide)
        ctl_wide[:, 0:routes] = prev_ref[m]
        ctl_wide[:, 8:10] = route_ref[m].astype(F32)
        ctl_send[m] = ctl_wide[...].T[:SMALL, :]
    send(2)
    seg_copy.wait_recv()
    seg_own.wait()
    seg_row = seg_all[y, pl.ds(x, 1), :].astype(F32)
    length = seg_row.shape[1]
    segr_ref[...] = jnp.broadcast_to(seg_row, segr_ref.shape)
    segc_ref[...] = jnp.broadcast_to(seg_row, (LANES, length)).T
    small_copy.wait_recv()
    for copy in weight_copies:
        copy.wait_recv()
    for copy in own_copies:
        copy.wait()
    gain = small_all[14:15, :].astype(F32)

    def project(index):
        here = block_of(index)
        values = x_all[here, :].astype(F32)
        inverse = lax.rsqrt(jnp.mean(values * values, axis=-1, keepdims=True) + NORM_EPS)
        normed = (values * inverse * gain).astype(BF16)
        normed_ref[here, :] = normed
        qkv_ref[here, :] = dot(normed, wqkv_all[...]).astype(BF16)

    forward = []
    for step in range(2):
        spot = x_all.at[block_of(core * 2 + (x if step == 0 else 1 - x))]
        forward.append(inner.copy(spot, spot, sibling))
    take_near(0)
    forward[0].start()
    project(core * 2 + x)
    far_copies[0].wait_recv()
    forward[1].start()
    send(1)
    project(core * 2 + 1 - x)
    forward[0].wait_recv()
    project((1 - core) * 2 + x)
    forward[1].wait_recv()
    project((1 - core) * 2 + 1 - x)

    @pl.loop(0, span // LANES)
    def _(pair):
        attend_pair(pair, rows, reach, span, qkv_ref, segc_ref, segr_ref, att_ref, lse_ref)

    for k in (1, 2):
        take_near(k)
        far_copies[k].wait_recv()
    out_copy.wait_recv()
    for copy in far_copies + weight_copies + forward + [out_copy, seg_copy, small_copy]:
        copy.wait_send()

    @pl.when(moved)
    def _():
        for copy in near_copies:
            copy.wait_send()


def gather_all(
    tokens, cotangent, w_qkv, w_out, prev_logits, routes, segments, w_router, const_proj,
    const_vec, gain_attn, gain_moe,
):
    rows, width = tokens.shape[1:]
    length = segments.shape[1]
    mine = length // 2
    span = width // 2
    vmem = pl.BlockSpec(memory_space=pltpu.VMEM)
    anywhere = pl.BlockSpec(memory_space=pl.ANY)
    return pl.pallas_call(
        functools.partial(gather_kernel, rows, length // 2, w_router.shape[1]),
        in_specs=[anywhere] * 4 + [vmem] * 8,
        out_specs=[vmem] * 12,
        out_shape=[
            shape((length, width), BF16), shape((mine, width), BF16),
            shape((2, SMALL, rows), F32), shape((length, width), BF16),
            shape((length, 3 * span), BF16), shape((length, span), BF16),
            shape((span // LANES, 8, length), F32), shape((SMALL, width), BF16),
            shape((width, 3 * span), BF16), shape((span, width), BF16),
            shape((length, LANES), F32), shape((8, length), F32),
        ],
        scratch_shapes=[
            pltpu.VMEM((rows, LANES), F32), pltpu.VMEM((2, SMALL, rows), F32),
            pltpu.VMEM((span, LANES), F32), pltpu.VMEM((SMALL, span), BF16),
            pltpu.VMEM((2, 2, length), jnp.int32),
        ]
        + [pltpu.SemaphoreType.DMA((3,))] * 4
        + [pltpu.SemaphoreType.DMA((8,))] * 2
        + [pltpu.SemaphoreType.DMA((7,))],
        compiler_params=pltpu.CompilerParams(
            collective_id=3, has_side_effects=True, vmem_limit_bytes=60 * 1024 * 1024
        ),
        name="gather_all",
    )(
        tokens, cotangent, w_qkv, w_out, prev_logits, routes, segments, w_router, const_proj,
        const_vec, gain_attn[None], gain_moe[None],
    )


def widen(turned):
    pad = jnp.zeros((LANES - turned.shape[0], turned.shape[1]), turned.dtype)
    return jnp.concatenate([turned, pad], axis=0).T


def spread_block(experts, routes, rows, block, refs, send_ref, recv_ref, keep):
    att_own, att_sib, x_ref, g_ref, ctl_ref, w_own, w_sib, small_rows, wide_rows = refs
    residual_ref, mixed_ref, pm_ref, place_ref = keep
    y, x, z, core = position()
    here = pl.ds(pl.multiple_of(block * rows, rows), rows)
    tokens = x_ref[pl.ds(pl.multiple_of((core * 2 + block) * rows, rows), rows), :]
    residual = tokens.astype(F32) + (
        dot(att_own[here, :], w_own[...]) + dot(att_sib[here, :], w_sib[...])
    )
    residual_ref[here, :] = residual
    inverse = lax.rsqrt(jnp.mean(residual * residual, axis=-1, keepdims=True) + NORM_EPS)
    mixed = (residual * inverse * small_rows[15:16, :].astype(F32)).astype(BF16)
    mixed_ref[here, :] = mixed
    logits = dot(mixed, wide_rows[...], ((1,), (1,)))
    ctl = widen(ctl_ref[block])
    lane = lax.broadcasted_iota(jnp.int32, (rows, LANES), 1)
    is_route = lane < routes
    router = jnp.where(is_route, logits + ctl, NEG)
    powers = jnp.exp(router - jnp.max(router, axis=-1, keepdims=True))
    probs = powers / jnp.sum(powers, axis=-1, keepdims=True)
    probs = jnp.where(is_route, probs, 0.0)
    pm = probs
    for const_index in range(2):
        first = column(logits, 8 + 2 * const_index)
        second = column(logits, 9 + 2 * const_index)
        largest = jnp.maximum(first, second)
        first = jnp.exp(first - largest)
        second = jnp.exp(second - largest)
        total = first + second
        pm = jnp.where(lane == 8 + 2 * const_index, first / total, pm)
        pm = jnp.where(lane == 9 + 2 * const_index, second / total, pm)
    pm_ref[here, :] = pm
    chosen = chosen_of(ctl)
    gated = chosen * probs
    earlier = lax.broadcasted_iota(jnp.int32, (rows, rows), 1) < lax.broadcasted_iota(
        jnp.int32, (rows, rows), 0
    )
    rank = dot(earlier.astype(BF16), chosen.astype(BF16))
    lane_f = lane.astype(F32)
    grads = g_ref[here, :].astype(F32)
    for expert in range(experts):
        place = jnp.where(
            (lane_f == column(rank, expert)) & (column(chosen, expert) > 0.0), 1.0, 0.0
        )
        place_ref[here, expert * LANES : (expert + 1) * LANES] = place.astype(BF16)
        pick = place.T.astype(BF16)
        d_part = (column(gated, expert) * grads).astype(BF16)
        send_ref[block, expert, 0] = dot(pick, mixed).astype(BF16)
        send_ref[block, expert, 1] = dot(pick, d_part).astype(BF16)
    recv_ref[block, y * 2 + x] = send_ref[block, y]


def expert_block(block, recv_ref, result_ref, back_ref, weights, keep):
    gate_w, up_w, down_w = weights
    hidden_ref, d_gate_ref, d_up_ref = keep
    y, x, z, core = position()
    peers, _, capacity, width = recv_ref.shape[1:]
    size = peers * capacity
    here = pl.ds(pl.multiple_of(block * size, size), size)
    rows = recv_ref[block, :, 0].reshape(size, width)
    d_rows = recv_ref[block, :, 1].reshape(size, width)
    gate = dot(rows, gate_w[...])
    up = dot(rows, up_w[...])
    sig = jax.nn.sigmoid(gate)
    active = gate * sig
    hidden = (active * up).astype(BF16)
    hidden_ref[here, :] = hidden
    part = dot(hidden, down_w[...]).astype(BF16)
    result_ref[block, :, 0] = part.reshape(peers, capacity, width)
    d_hidden = dot(d_rows, down_w[...], ((1,), (1,)))
    d_gate = (d_hidden * up * sig * (1.0 + gate * (1.0 - sig))).astype(BF16)
    d_up = (d_hidden * active).astype(BF16)
    d_gate_ref[here, :] = d_gate
    d_up_ref[here, :] = d_up
    d_in = dot(d_gate, gate_w[...], ((1,), (1,))) + dot(d_up, up_w[...], ((1,), (1,)))
    result_ref[block, :, 1] = d_in.astype(BF16).reshape(peers, capacity, width)
    back_ref[block, y * 2 + x] = result_ref[block, y * 2 + x]


def combine_block(experts, routes, rows, block, refs, keep, back_ref, outs, small_ref):
    g_ref, ctl_ref, small_rows, wide_rows = refs
    residual_ref, mixed_ref, pm_ref, place_ref = keep
    out_ref, prev_ref, dres_ref, branch_ref = outs
    halves = back_ref.shape[1] // experts
    here = pl.ds(pl.multiple_of(block * rows, rows), rows)
    g_low = g_ref[here, :]
    grads = g_low.astype(F32)
    mixed = mixed_ref[here, :].astype(F32)
    residual = residual_ref[here, :]
    pm = pm_ref[here, :]
    lane = lax.broadcasted_iota(jnp.int32, (rows, LANES), 1)
    chosen = chosen_of(widen(ctl_ref[block]))
    probs = jnp.where(lane < routes, pm, 0.0)
    gated = chosen * probs
    d_probs = jnp.zeros((rows, LANES), F32)
    result = residual
    d_mixed = None
    for expert in range(experts):
        place = place_ref[here, expert * LANES : (expert + 1) * LANES]
        expert_out = None
        for half in range(halves):
            owner = expert * halves + half
            term = dot(place, back_ref[block, owner, 0])
            expert_out = term if expert_out is None else expert_out + term
            term = dot(place, back_ref[block, owner, 1])
            d_mixed = term if d_mixed is None else d_mixed + term
        result = result + column(gated, expert) * expert_out
        d_gate = jnp.sum(expert_out * grads, axis=-1, keepdims=True)
        d_probs = jnp.where(lane == expert, d_gate, d_probs)
    g_mixed = jnp.sum(grads * mixed, axis=-1, keepdims=True)
    g_const = dot(g_low, wide_rows[...], ((1,), (1,)))
    copy = experts + 1
    d_probs = jnp.where(lane == copy, g_mixed, d_probs)
    weight = column(gated, copy)
    d_small = jnp.zeros((rows, LANES), F32)
    for const_index in range(2):
        route = copy + 1 + const_index
        first = column(pm, 8 + 2 * const_index)
        second = column(pm, 9 + 2 * const_index)
        gate = column(gated, route)
        g_vec = column(g_const, 12 + const_index)
        d_probs = jnp.where(lane == route, first * g_mixed + second * g_vec, d_probs)
        weight = weight + gate * first
        vec = small_rows[12 + const_index : 13 + const_index, :].astype(F32)
        result = result + (gate * second) * vec
        d_first = gate * g_mixed
        d_second = gate * g_vec
        mean = first * d_first + second * d_second
        d_small = jnp.where(lane == 8 + 2 * const_index, first * (d_first - mean), d_small)
        d_small = jnp.where(lane == 9 + 2 * const_index, second * (d_second - mean), d_small)
        d_small = jnp.where(lane == 12 + const_index, gate * second, d_small)
    result = result + weight * mixed
    out_ref[block] = result.astype(BF16)
    d_probs = d_probs * chosen
    d_logits = probs * (d_probs - jnp.sum(probs * d_probs, axis=-1, keepdims=True))
    d_small = jnp.where(lane < routes, d_logits, d_small)
    d_mixed = d_mixed + weight * grads
    d_mixed = d_mixed + dot(
        jnp.where(lane < 12, d_small, 0.0), wide_rows[...].astype(F32), precision=HIGHEST
    )
    inverse = lax.rsqrt(jnp.mean(residual * residual, axis=-1, keepdims=True) + NORM_EPS)
    scaled = d_mixed * small_rows[15:16, :].astype(F32)
    mean = jnp.mean(scaled * residual, axis=-1, keepdims=True)
    d_residual = grads + inverse * scaled - residual * (inverse * inverse * inverse * mean)
    dres_ref[here, :] = d_residual
    branch_ref[here, :] = d_residual.astype(BF16)
    d_turned = d_small.T[:SMALL, :]
    prev_ref[block] = d_turned[:8, :]
    sub = lax.broadcasted_iota(jnp.int32, (SMALL, rows), 0)
    small = dot(jnp.where(sub < 12, d_turned, 0.0), mixed, precision=HIGHEST)
    small = small + dot(
        jnp.where((sub >= 12) & (sub < 14), d_turned, 0.0), grads, precision=HIGHEST
    )
    d_gain = jnp.sum(d_mixed * residual * inverse, axis=0, keepdims=True)
    which = lax.broadcasted_iota(jnp.int32, small.shape, 0)
    small_ref[...] += jnp.where(which == 14, d_gain, small)


def layer_kernel(
    experts, routes, rows, blocks,
    att_ref, x_ref, g_ref, ctl_ref, w_own, w_sib, small_rows, gate_ref, up_ref, down_ref,
    out_ref, prev_ref, dres_ref, branch_ref, small_ref, dgate_out, dup_out, ddown_out,
    wide_rows, att_own, att_sib, gate_w, up_w, down_w, residual_ref, mixed_ref, pm_ref, place_ref,
    send_ref, recv_ref, result_ref, back_ref, hidden_ref, d_gate_ref, d_up_ref,
    head_send, head_recv, local_sems, send_sems, recv_sems, back_send, back_recv,
):
    y, x, z, core = position()
    me = y * 2 + x
    sibling = (me, z, 1 - core)
    partners = [(1 - y) * 2 + 1 - x, y * 2 + 1 - x, (1 - y) * 2 + x]
    wanted = [1 - y, y, 1 - y]
    greet([(sibling, True)] + [((place, z, core), True) for place in partners])
    mine = rows * blocks
    mail = Mail(head_send, head_recv)
    pairs = [(gate_ref, gate_w), (up_ref, up_w), (down_ref, down_w)]
    heads = [mail.copy(att_ref.at[1 - core], att_sib, sibling)]
    locals_ = [pltpu.make_async_copy(att_ref.at[core], att_own, local_sems.at[3])]
    for k, (source, target) in enumerate(pairs):
        size = source.shape[0]
        spot = target.at[pl.ds(pl.multiple_of(core * size, size), size)]
        heads.append(mail.copy(source, spot, sibling))
        locals_.append(pltpu.make_async_copy(source, spot, local_sems.at[k]))
    for copy in heads + locals_:
        copy.start()

    def dispatch(block, k):
        return pltpu.make_async_remote_copy(
            src_ref=send_ref.at[block, wanted[k]],
            dst_ref=recv_ref.at[block, me],
            send_sem=send_sems.at[block, k],
            recv_sem=recv_sems.at[block, k],
            device_id=(partners[k], z, core),
            device_id_type=pl.DeviceIdType.MESH,
        )

    def giveback(block, k):
        return pltpu.make_async_remote_copy(
            src_ref=result_ref.at[block, partners[k]],
            dst_ref=back_ref.at[block, me],
            send_sem=back_send.at[block, k],
            recv_sem=back_recv.at[block, k],
            device_id=(partners[k], z, core),
            device_id_type=pl.DeviceIdType.MESH,
        )

    small_ref[...] = jnp.zeros_like(small_ref)
    wide_rows[...] = jnp.zeros_like(wide_rows)
    wide_rows[0:SMALL, :] = small_rows[...]
    heads[0].wait_recv()
    locals_[0].wait()
    keep = (residual_ref, mixed_ref, pm_ref, place_ref)
    spread_refs = (
        att_own, att_sib, x_ref, g_ref, ctl_ref, w_own, w_sib, small_rows, wide_rows
    )

    @pl.loop(0, blocks)
    def _(block):
        spread_block(experts, routes, rows, block, spread_refs, send_ref, recv_ref, keep)
        for k in range(3):
            dispatch(block, k).start()

    for copy in heads[1:]:
        copy.wait_recv()
    for copy in locals_[1:]:
        copy.wait()

    @pl.loop(0, blocks)
    def _(block):
        for k in range(3):
            dispatch(block, k).wait_recv()
        expert_block(
            block, recv_ref, result_ref, back_ref, (gate_w, up_w, down_w),
            (hidden_ref, d_gate_ref, d_up_ref),
        )
        for k in range(3):
            giveback(block, k).start()

    peers, _, capacity, width = recv_ref.shape[1:]
    total = blocks * peers * capacity
    step = 2 * LANES

    @pl.loop(0, width // step)
    def _(chunk):
        span = pl.ds(pl.multiple_of(chunk * step, step), step)
        lhs = recv_ref[:, :, 0, :, span].reshape(total, step).T
        dgate_out[span, :] = dot(lhs, d_gate_ref[...]).astype(BF16)
        dup_out[span, :] = dot(lhs, d_up_ref[...]).astype(BF16)

    @pl.loop(0, hidden_ref.shape[1] // step)
    def _(chunk):
        span = pl.ds(pl.multiple_of(chunk * step, step), step)
        lhs = hidden_ref[:, span].T
        rhs = recv_ref[:, :, 1].reshape(total, width)
        ddown_out[span, :] = dot(lhs, rhs).astype(BF16)

    @pl.loop(0, blocks)
    def _(block):
        for k in range(3):
            giveback(block, k).wait_recv()
        combine_block(
            experts, routes, rows, block, (g_ref, ctl_ref, small_rows, wide_rows),
            keep, back_ref, (out_ref, prev_ref, dres_ref, branch_ref), small_ref,
        )

    for copy in heads:
        copy.wait_send()
    for block in range(blocks):
        for k in range(3):
            dispatch(block, k).wait_send()
            giveback(block, k).wait_send()


def expert_layer(
    experts, routes, rows, attended, x_all, cot_own, ctl, w_own, w_sib, small_all, w_gate,
    w_up, w_down,
):
    mine, width = cot_own.shape
    blocks = mine // rows
    peers = lax.axis_size("ep")
    span = attended.shape[1]
    hidden = w_gate.shape[1]
    vmem = pl.BlockSpec(memory_space=pltpu.VMEM)
    total = blocks * peers * LANES
    grads = [(2 * w.shape[0], w.shape[1]) for w in (w_gate, w_up, w_down)]
    return pl.pallas_call(
        functools.partial(layer_kernel, experts, routes, rows, blocks),
        in_specs=[vmem] * 10,
        out_specs=[vmem] * 8,
        out_shape=[
            shape((blocks, rows, width), BF16), shape((blocks, 8, rows), F32),
            shape((mine, width), F32), shape((mine, width), BF16), shape((SMALL, width), F32),
        ]
        + [shape(dims, BF16) for dims in grads],
        scratch_shapes=[pltpu.VMEM((LANES, width), BF16)]
        + [pltpu.VMEM((mine, span), BF16)] * 2
        + [pltpu.VMEM(dims, BF16) for dims in grads]
        + [
            pltpu.VMEM((mine, width), F32), pltpu.VMEM((mine, width), BF16),
            pltpu.VMEM((mine, LANES), F32), pltpu.VMEM((mine, experts * LANES), BF16),
            pltpu.VMEM((blocks, experts, KINDS, LANES, width), BF16),
        ]
        + [pltpu.VMEM((blocks, peers, KINDS, LANES, width), BF16)] * 3
        + [pltpu.VMEM((total, hidden), BF16)] * 3
        + [
            pltpu.SemaphoreType.DMA((4,)), pltpu.SemaphoreType.DMA((4,)),
            pltpu.SemaphoreType.DMA((4,)),
        ]
        + [pltpu.SemaphoreType.DMA((blocks, 3))] * 4,
        compiler_params=pltpu.CompilerParams(
            collective_id=2, has_side_effects=True, vmem_limit_bytes=62 * 1024 * 1024
        ),
        name="expert_layer",
    )(
        attended.reshape(2, mine, span), x_all, cot_own, ctl, w_own, w_sib, small_all,
        w_gate, w_up, w_down,
    )


def one_chip(
    tokens,
    prev_logits,
    segments,
    routes,
    cotangent,
    gain_attn,
    w_qkv,
    w_out,
    gain_moe,
    w_router,
    const_proj,
    const_vec,
    w_gate,
    w_up,
    w_down,
):
    rows, width = tokens.shape[1:]
    core = lax.axis_index("fs")
    route_count = w_router.shape[1]
    experts = route_count - 4
    length = segments.shape[1]
    mine = length // 2
    span = width // 2
    blocks = mine // rows

    def swap(array):
        return lax.ppermute(array, "fs", [(0, 1), (1, 0)])

    def by_core(own, other, axis=0):
        return jnp.where(
            core == 0,
            jnp.concatenate([own, other], axis=axis),
            jnp.concatenate([other, own], axis=axis),
        )

    (
        x_all, cot_own, ctl, normed, qkv, attended, lse, small_all, qkv_weight, out_sib,
        seg_col, seg_row,
    ) = gather_all(
        tokens, cotangent, w_qkv, w_out, prev_logits, routes, segments, w_router, const_proj,
        const_vec, gain_attn, gain_moe,
    )
    head_pairs = span // LANES
    reach = length // 2

    def heads_at(offset):
        return pl.BlockSpec((length, LANES), lambda p: (0, offset + p))

    lse_spec = pl.BlockSpec((1, 8, length), lambda p: (p, 0, 0))
    attn_gain = small_all[14:15].astype(F32)
    x_own = lax.dynamic_slice_in_dim(x_all, core * mine, mine)
    (
        block_out, d_prev, d_residual, d_branch, small, grad_gate, grad_up, grad_down,
    ) = expert_layer(
        experts, route_count, rows, attended, x_all, cot_own, ctl, w_out, out_sib, small_all,
        w_gate[0], w_up[0], w_down[0],
    )

    branch_all = by_core(d_branch, swap(d_branch))
    valid = (seg_col[:, :1] != SEGS - 1.0).astype(F32)
    d_att = (dot(branch_all, w_out, ((1,), (1,))) * valid).astype(BF16)
    grad_out = dot(attended, branch_all, ((0,), (0,))).astype(BF16)
    d_queries, d_keys, d_values = pl.pallas_call(
        functools.partial(attend_back_kernel, rows, reach),
        grid=(head_pairs,),
        in_specs=[
            heads_at(0), heads_at(head_pairs), heads_at(2 * head_pairs), heads_at(0),
            whole((length, LANES)), whole((8, length)), lse_spec,
        ],
        out_specs=[heads_at(0)] * 3,
        out_shape=[shape((length, span), BF16)] * 3,
        scratch_shapes=[pltpu.VMEM((length, LANES), F32)] * 2,
        compiler_params=params(),
        cost_estimate=cost(30e9, 5e6),
        name="attend_back",
    )(qkv, qkv, qkv, d_att, seg_col, seg_row, lse)
    d_qkv = jnp.concatenate([d_queries, d_keys, d_values], axis=1)
    d_normed = dot(d_qkv, qkv_weight, ((1,), (1,)))
    d_normed_own = lax.dynamic_slice_in_dim(d_normed, core * mine, mine)
    d_normed_sib = swap(
        lax.dynamic_slice_in_dim(d_normed, (1 - core) * mine, mine).astype(BF16)
    )
    grad_qkv = dot(normed, d_qkv, ((0,), (0,))).astype(BF16)
    d_tokens, gain_rows = pl.pallas_call(
        finish_kernel,
        grid=(blocks,),
        in_specs=[per_row(rows, width)] * 4 + [whole((1, width))],
        out_specs=[per_row(rows, width), whole((8, width))],
        out_shape=[shape((mine, width), BF16), shape((8, width), F32)],
        compiler_params=params(),
        cost_estimate=cost(1e8, 6e6),
        name="finish",
    )(x_own, d_normed_own, d_normed_sib, d_residual, attn_gain)

    out_mine = lax.dynamic_slice_in_dim(grad_out, core * span, span, axis=1)
    out_sent = lax.dynamic_slice_in_dim(grad_out, (1 - core) * span, span, axis=1)
    out_cols = by_core(out_mine, swap(out_sent))
    small = jnp.concatenate([small[: SMALL - 1], gain_rows[:1]]).T.astype(BF16)
    dense = jnp.concatenate(
        [grad_qkv, out_cols, jnp.pad(small, ((0, 0), (0, LANES - SMALL)))], axis=1
    )
    shares = reduce_all(
        grad_gate, grad_up, grad_down, dense, block_out, d_tokens, d_prev
    )
    pieces = shares[3:5]
    out_home, dtok_home, prev_home = shares[5:]

    def columns_of(start):
        own, other = (piece[:, start : start + span] for piece in pieces)
        return by_core(own, other, axis=1)

    share_qkv = jnp.concatenate([columns_of(k * span) for k in range(3)], axis=1)
    share_out = columns_of(3 * span)
    share_small = sum(piece[:, 4 * span : 4 * span + SMALL] for piece in pieces)
    return (
        out_home,
        dtok_home.astype(F32),
        jnp.swapaxes(prev_home, 1, 2)[:, :, :route_count],
        share_small[:, 15],
        share_qkv,
        share_out,
        share_small[:, 14],
        share_small[:, :route_count],
        share_small[:, 8:12],
        share_small[:, 12:14],
    ) + tuple(shares[:3])


def suits(mesh, tokens, w_router, w_gate):
    peers = mesh.shape["ep"]
    rows = tokens.shape[1] // peers
    micro = tokens.shape[0] // (mesh.shape["dp"] * mesh.shape["fs"])
    routes = w_router.shape[1]
    return (
        peers == 4
        and mesh.shape["fs"] == 2
        and micro == 2
        and (routes - 4) * 2 == peers
        and 3 * rows // routes == LANES
        and tokens.shape[2] % (2 * LANES) == 0
    )


def solution(mesh):
    placed = (
        P(("dp", "fs"), "ep", None),
        P(("dp", "fs"), "ep", None),
        P(("dp", "fs"), None),
        P(("dp", "fs"), "ep", None),
        P(("dp", "fs"), "ep", None),
        P("fs"),
        P("fs", None),
        P("fs", None),
        P("fs"),
        P("fs", None),
        P("fs", None),
        P("fs", None),
        P("ep", "fs", None),
        P("ep", "fs", None),
        P("ep", "fs", None),
    )
    def layer(*arrays):
        fits = suits(mesh, arrays[0], arrays[9], arrays[12])
        return mapped(one_chip if fits else shards)(*arrays)

    def mapped(body):
        return jax.shard_map(
            body,
            mesh=mesh,
            in_specs=placed,
            out_specs=(
                P(("dp", "fs"), "ep", None),
                P(("dp", "fs"), "ep", None),
                P(("dp", "fs"), "ep", None),
                P(("ep", "dp", "fs")),
                P(("ep", "dp", "fs"), None),
                P(("ep", "dp", "fs"), None),
                P(("ep", "dp", "fs")),
                P(("ep", "dp", "fs"), None),
                P(("ep", "dp", "fs"), None),
                P(("ep", "dp", "fs"), None),
                P("ep", ("dp", "fs"), None),
                P("ep", ("dp", "fs"), None),
                P("ep", ("dp", "fs"), None),
            ),
            check_vma=False,
        )

    return layer
```

```python
import functools

import jax
import jax.numpy as jnp
from jax import lax
from jax.experimental import pallas as pl
from jax.experimental.pallas import tpu as pltpu
from jax.sharding import PartitionSpec as P

HEAD = 64
SEGS = 4


NORM_EPS = 1e-06
MASK_FILL = -1e30
HIGHEST = lax.Precision.HIGHEST


def rms_scale(values, gains):
    inverse = lax.rsqrt(jnp.mean(values * values, axis=-1, keepdims=True) + NORM_EPS)
    return values * inverse * gains


def small_softmax(logit_rows):
    largest = jnp.max(logit_rows, axis=-1, keepdims=True)
    powers = jnp.exp(logit_rows - largest)
    return powers / jnp.sum(powers, axis=-1, keepdims=True)


def add_tuple(first_tuple, second_tuple):
    if first_tuple is None:
        return second_tuple
    return tuple(
        (first_term + second_term for first_term, second_term in zip(first_tuple, second_tuple))
    )


def shards(
    tokens,
    prev_logits,
    segments,
    routes,
    cotangent,
    gain_attn,
    w_qkv,
    w_out,
    gain_moe,
    w_router,
    const_proj,
    const_vec,
    w_gate,
    w_up,
    w_down,
):
    micro_count, row_count, model_width = tokens.shape
    head_count = model_width // HEAD
    peer_count = lax.axis_size("ep")
    my_index = lax.axis_index("ep")
    route_count = w_router.shape[1]
    expert_count = route_count - 4
    half_count = peer_count // expert_count
    capacity = (3 * row_count // route_count + 7) // 8 * 8
    seq_length = row_count * peer_count
    slot_count = expert_count * capacity
    pos_all = jnp.arange(seq_length, dtype=jnp.int32)
    pos_mine = my_index * row_count + jnp.arange(row_count, dtype=jnp.int32)
    expert_ids = jnp.arange(expert_count, dtype=jnp.int32)
    slot_ids = jnp.arange(slot_count, dtype=jnp.int32)
    route_ids = jnp.arange(route_count, dtype=jnp.int32)
    layer_outputs = []
    input_grads = []
    prev_grads = []
    dense_acc = None
    expert_acc = None
    for step_index in range(micro_count):
        gathered = (
            lax.all_gather(w_qkv, "fs", axis=0, tiled=True),
            lax.all_gather(w_out, "fs", axis=0, tiled=True),
            lax.all_gather(w_router, "fs", axis=0, tiled=True),
            lax.all_gather(const_proj, "fs", axis=0, tiled=True),
            lax.all_gather(const_vec, "fs", axis=0, tiled=True),
            lax.all_gather(gain_attn, "fs", axis=0, tiled=True),
            lax.all_gather(gain_moe, "fs", axis=0, tiled=True),
            lax.all_gather(w_gate, "fs", axis=1, tiled=True),
            lax.all_gather(w_up, "fs", axis=1, tiled=True),
            lax.all_gather(w_down, "fs", axis=1, tiled=True),
        )
        (
            qkv_weight,
            out_weight,
            router_weight,
            cproj_weight,
            cvec_weight,
            attn_gain,
            moe_gain,
            gate_weight,
            up_weight,
            down_weight,
        ) = gathered
        gate_weight = gate_weight[0]
        up_weight = up_weight[0]
        down_weight = down_weight[0]
        attn_gain = attn_gain.astype(jnp.float32)
        moe_gain = moe_gain.astype(jnp.float32)
        router_float = router_weight.astype(jnp.float32)
        cproj_float = cproj_weight.astype(jnp.float32)
        cvec_float = cvec_weight.astype(jnp.float32)
        token_rows = tokens[step_index].astype(jnp.float32)
        seg_all = segments[step_index]
        seg_mine = lax.dynamic_slice_in_dim(seg_all, my_index * row_count, row_count)
        allowed = (seg_mine[:, None] == seg_all[None, :]) & (pos_all[None, :] <= pos_mine[:, None])
        valid_rows = (seg_mine != SEGS - 1).astype(jnp.float32)[:, None]
        normed = rms_scale(token_rows, attn_gain).astype(jnp.bfloat16)
        qkv_rows = jnp.dot(normed, qkv_weight, preferred_element_type=jnp.float32).astype(
            jnp.bfloat16
        )
        queries = qkv_rows[:, :model_width].reshape(row_count, head_count, HEAD)
        keys_local = qkv_rows[:, model_width : 2 * model_width]
        values_local = qkv_rows[:, 2 * model_width :]
        keys_all, values_all = (
            lax.all_gather(keys_local, "ep", axis=0, tiled=True),
            lax.all_gather(values_local, "ep", axis=0, tiled=True),
        )
        key_heads = keys_all.reshape(seq_length, head_count, HEAD)
        value_heads = values_all.reshape(seq_length, head_count, HEAD)
        scores = (
            jnp.einsum("qhd,khd->hqk", queries, key_heads, preferred_element_type=jnp.float32)
            * 0.125
        )
        scores = jnp.where(allowed[None], scores, MASK_FILL)
        largest = jnp.max(scores, axis=-1, keepdims=True)
        powers = jnp.exp(scores - largest)
        row_total = jnp.sum(powers, axis=-1, keepdims=True)
        log_total = largest + jnp.log(row_total)
        attn_probs = powers / row_total
        attended = jnp.einsum(
            "hqk,khd->qhd",
            attn_probs.astype(jnp.bfloat16),
            value_heads,
            preferred_element_type=jnp.float32,
        ).reshape(row_count, model_width)
        attended = (attended * valid_rows).astype(jnp.bfloat16)
        residual = token_rows + jnp.dot(attended, out_weight, preferred_element_type=jnp.float32)
        mixed = rms_scale(residual, moe_gain).astype(jnp.bfloat16)
        mixed_float = mixed.astype(jnp.float32)
        logits = (
            jnp.dot(mixed, router_weight, preferred_element_type=jnp.float32)
            + prev_logits[step_index]
        )
        router_probs = small_softmax(logits)
        route_rows = routes[step_index]
        choose = (route_rows[:, :, None] == route_ids[None, None, :]).astype(jnp.float32)
        gate_values = jnp.sum(choose * router_probs[:, None, :], axis=-1)
        const_logits = jnp.dot(mixed, cproj_weight, preferred_element_type=jnp.float32)
        mixings = []
        const_outs = []
        for const_index in range(2):
            mixing = small_softmax(const_logits[:, 2 * const_index : 2 * const_index + 2])
            mixings.append(mixing)
            const_outs.append(
                mixing[:, :1] * mixed_float + mixing[:, 1:] * cvec_float[:, const_index][None, :]
            )
        pair_route = route_rows.reshape(-1)
        expert_hit = (pair_route[:, None] == expert_ids[None, :]).astype(jnp.int32)
        slot_index = jnp.sum((jnp.cumsum(expert_hit, axis=0) - expert_hit) * expert_hit, axis=1)
        slot_cell = jnp.sum(expert_hit * expert_ids[None, :], axis=1) * capacity + slot_index
        slot_place = jnp.where(jnp.sum(expert_hit, axis=1) > 0, slot_cell, -1)
        slot_table = (slot_ids[:, None] == slot_place[None, :]).astype(jnp.bfloat16)
        pair_rows = jnp.repeat(mixed, 2, axis=0)
        packed = jnp.einsum(
            "sp,pd->sd", slot_table, pair_rows, preferred_element_type=jnp.float32
        ).astype(jnp.bfloat16)
        outgoing = jnp.broadcast_to(
            packed.reshape(expert_count, 1, capacity, model_width),
            (expert_count, half_count, capacity, model_width),
        ).reshape(peer_count, capacity, model_width)
        received = lax.all_to_all(outgoing, "ep", split_axis=0, concat_axis=0, tiled=True)
        flat_rows = received.reshape(-1, model_width)
        gate_part = jnp.dot(flat_rows, gate_weight, preferred_element_type=jnp.float32)
        up_part = jnp.dot(flat_rows, up_weight, preferred_element_type=jnp.float32)
        hidden = (jax.nn.silu(gate_part) * up_part).astype(jnp.bfloat16)
        part_out = (
            jnp.dot(hidden, down_weight, preferred_element_type=jnp.float32)
            .astype(jnp.bfloat16)
            .reshape(received.shape)
        )
        returned_rows = lax.all_to_all(part_out, "ep", split_axis=0, concat_axis=0, tiled=True)
        returned_rows, kept_rows = (returned_rows, received)
        halves = returned_rows.reshape(expert_count, half_count, capacity, model_width)
        pair_ffn = jnp.zeros((2 * row_count, model_width), jnp.float32)
        for half_index in range(half_count):
            pair_ffn = pair_ffn + jnp.einsum(
                "sp,sd->pd",
                slot_table,
                halves[:, half_index].reshape(slot_count, model_width),
                preferred_element_type=jnp.float32,
            )
        expert_out = pair_ffn.reshape(row_count, 2, model_width)
        expert_out = (
            expert_out + choose[:, :, expert_count + 1 : expert_count + 2] * mixed_float[:, None, :]
        )
        for const_index in range(2):
            column = expert_count + 2 + const_index
            expert_out = (
                expert_out + choose[:, :, column : column + 1] * const_outs[const_index][:, None, :]
            )
        result_rows = residual + jnp.sum(gate_values[:, :, None] * expert_out, axis=1)
        layer_outputs.append(result_rows.astype(jnp.bfloat16))
        grad_rows = cotangent[step_index].astype(jnp.float32)
        d_gates = jnp.sum(expert_out * grad_rows[:, None, :], axis=-1)
        d_probs = jnp.sum(choose * d_gates[:, :, None], axis=1)
        d_logits = router_probs * (
            d_probs - jnp.sum(router_probs * d_probs, axis=-1, keepdims=True)
        )
        prev_grads.append(d_logits)
        grad_router = jnp.dot(mixed_float.T, d_logits, precision=HIGHEST)
        d_mixed = jnp.dot(d_logits, router_float.T, precision=HIGHEST)
        weighted = gate_values[:, :, None] * grad_rows[:, None, :]
        d_mixed = d_mixed + jnp.sum(
            choose[:, :, expert_count + 1 : expert_count + 2] * weighted, axis=1
        )
        cproj_grads = []
        cvec_grads = []
        for const_index in range(2):
            column = expert_count + 2 + const_index
            mixing = mixings[const_index]
            d_const = jnp.sum(choose[:, :, column : column + 1] * weighted, axis=1)
            d_mix = jnp.stack(
                [
                    jnp.sum(d_const * mixed_float, axis=-1),
                    jnp.sum(d_const * cvec_float[:, const_index][None, :], axis=-1),
                ],
                axis=-1,
            )
            d_mixlog = mixing * (d_mix - jnp.sum(mixing * d_mix, axis=-1, keepdims=True))
            cproj_grads.append(jnp.dot(mixed_float.T, d_mixlog, precision=HIGHEST))
            cvec_grads.append(jnp.sum(mixing[:, 1:] * d_const, axis=0))
            d_mixed = (
                d_mixed
                + mixing[:, :1] * d_const
                + jnp.dot(
                    d_mixlog,
                    cproj_float[:, 2 * const_index : 2 * const_index + 2].T,
                    precision=HIGHEST,
                )
            )
        grad_cproj = jnp.concatenate(cproj_grads, axis=1)
        grad_cvec = jnp.stack(cvec_grads, axis=1)
        d_pairs = weighted.reshape(2 * row_count, model_width).astype(jnp.bfloat16)
        d_packed = jnp.einsum(
            "sp,pd->sd", slot_table, d_pairs, preferred_element_type=jnp.float32
        ).astype(jnp.bfloat16)
        d_outgoing = jnp.broadcast_to(
            d_packed.reshape(expert_count, 1, capacity, model_width),
            (expert_count, half_count, capacity, model_width),
        ).reshape(peer_count, capacity, model_width)
        d_received = lax.all_to_all(d_outgoing, "ep", split_axis=0, concat_axis=0, tiled=True)
        flat_rows = kept_rows.reshape(-1, model_width)
        flat_grads = d_received.reshape(-1, model_width)
        gate_part = jnp.dot(flat_rows, gate_weight, preferred_element_type=jnp.float32)
        up_part = jnp.dot(flat_rows, up_weight, preferred_element_type=jnp.float32)
        activated = jax.nn.silu(gate_part)
        hidden = (activated * up_part).astype(jnp.bfloat16)
        grad_down = jnp.einsum("rf,rd->fd", hidden, flat_grads, preferred_element_type=jnp.float32)
        d_hidden = jnp.einsum(
            "rd,fd->rf", flat_grads, down_weight, preferred_element_type=jnp.float32
        )
        sigmoid_gate = jax.nn.sigmoid(gate_part)
        d_gate_part = (
            d_hidden * up_part * sigmoid_gate * (1.0 + gate_part * (1.0 - sigmoid_gate))
        ).astype(jnp.bfloat16)
        d_up_part = (d_hidden * activated).astype(jnp.bfloat16)
        grad_gate = jnp.einsum(
            "rd,rf->df", flat_rows, d_gate_part, preferred_element_type=jnp.float32
        )
        grad_up = jnp.einsum("rd,rf->df", flat_rows, d_up_part, preferred_element_type=jnp.float32)
        d_inputs = jnp.einsum(
            "rf,df->rd", d_gate_part, gate_weight, preferred_element_type=jnp.float32
        )
        d_inputs = d_inputs + jnp.einsum(
            "rf,df->rd", d_up_part, up_weight, preferred_element_type=jnp.float32
        )
        d_inputs = d_inputs.astype(jnp.bfloat16).reshape(peer_count, capacity, model_width)
        d_returned = lax.all_to_all(d_inputs, "ep", split_axis=0, concat_axis=0, tiled=True)
        d_halves = d_returned.reshape(expert_count, half_count, capacity, model_width)
        for half_index in range(half_count):
            d_pair_in = jnp.einsum(
                "sp,sd->pd",
                slot_table,
                d_halves[:, half_index].reshape(slot_count, model_width),
                preferred_element_type=jnp.float32,
            )
            d_mixed = d_mixed + jnp.sum(d_pair_in.reshape(row_count, 2, model_width), axis=1)
        expert_acc = add_tuple(expert_acc, (grad_gate, grad_up, grad_down))
        moe_vjp = jax.vjp(rms_scale, residual, moe_gain)[1]
        d_residual_norm, grad_moe_gain = moe_vjp(d_mixed)
        d_residual = grad_rows + d_residual_norm
        d_branch = d_residual.astype(jnp.bfloat16)
        grad_out = jnp.einsum("rd,re->de", attended, d_branch, preferred_element_type=jnp.float32)
        d_attended = (
            jnp.einsum("re,de->rd", d_branch, out_weight, preferred_element_type=jnp.float32)
            * valid_rows
        ).astype(jnp.bfloat16)
        d_heads = d_attended.reshape(row_count, head_count, HEAD)
        scores = (
            jnp.einsum("qhd,khd->hqk", queries, key_heads, preferred_element_type=jnp.float32)
            * 0.125
        )
        scores = jnp.where(allowed[None], scores, MASK_FILL)
        attn_probs = jnp.exp(scores - log_total)
        d_weights = jnp.einsum(
            "qhd,khd->hqk", d_heads, value_heads, preferred_element_type=jnp.float32
        )
        delta_rows = jnp.sum(attn_probs * d_weights, axis=-1, keepdims=True)
        d_scores = (attn_probs * (d_weights - delta_rows)).astype(jnp.bfloat16)
        d_queries = (
            jnp.einsum(
                "hqk,khd->qhd", d_scores, key_heads, preferred_element_type=jnp.float32
            ).reshape(row_count, model_width)
            * 0.125
        )
        d_values = jnp.einsum(
            "hqk,qhd->khd",
            attn_probs.astype(jnp.bfloat16),
            d_heads,
            preferred_element_type=jnp.float32,
        ).reshape(seq_length, model_width)
        d_keys = (
            jnp.einsum(
                "hqk,qhd->khd", d_scores, queries, preferred_element_type=jnp.float32
            ).reshape(seq_length, model_width)
            * 0.125
        )
        d_keys_mine, d_values_mine = (
            lax.psum_scatter(
                d_keys.astype(jnp.bfloat16), "ep", scatter_dimension=0, tiled=True
            ).astype(jnp.float32),
            lax.psum_scatter(
                d_values.astype(jnp.bfloat16), "ep", scatter_dimension=0, tiled=True
            ).astype(jnp.float32),
        )
        d_qkv = jnp.concatenate([d_queries, d_keys_mine, d_values_mine], axis=1).astype(
            jnp.bfloat16
        )
        grad_qkv = jnp.einsum("rd,re->de", normed, d_qkv, preferred_element_type=jnp.float32)
        d_normed = jnp.einsum("re,de->rd", d_qkv, qkv_weight, preferred_element_type=jnp.float32)
        attn_vjp = jax.vjp(rms_scale, token_rows, attn_gain)[1]
        d_tokens_norm, grad_attn_gain = attn_vjp(d_normed)
        input_grads.append(d_residual + d_tokens_norm)
        dense_terms = (
            grad_attn_gain,
            grad_qkv,
            grad_out,
            grad_moe_gain,
            grad_router,
            grad_cproj,
            grad_cvec,
        )
        dense_shares = (
            lax.psum_scatter(dense_terms[0], ("ep", "dp", "fs"), scatter_dimension=0, tiled=True),
            lax.psum_scatter(dense_terms[1], ("ep", "dp", "fs"), scatter_dimension=0, tiled=True),
            lax.psum_scatter(dense_terms[2], ("ep", "dp", "fs"), scatter_dimension=0, tiled=True),
            lax.psum_scatter(dense_terms[3], ("ep", "dp", "fs"), scatter_dimension=0, tiled=True),
            lax.psum_scatter(dense_terms[4], ("ep", "dp", "fs"), scatter_dimension=0, tiled=True),
            lax.psum_scatter(dense_terms[5], ("ep", "dp", "fs"), scatter_dimension=0, tiled=True),
            lax.psum_scatter(dense_terms[6], ("ep", "dp", "fs"), scatter_dimension=0, tiled=True),
        )
        dense_acc = add_tuple(dense_acc, dense_shares)
    expert_shares = (
        lax.psum_scatter(
            expert_acc[0][None].astype(jnp.bfloat16), ("dp", "fs"), scatter_dimension=1, tiled=True
        ).astype(jnp.float32),
        lax.psum_scatter(
            expert_acc[1][None].astype(jnp.bfloat16), ("dp", "fs"), scatter_dimension=1, tiled=True
        ).astype(jnp.float32),
        lax.psum_scatter(
            expert_acc[2][None].astype(jnp.bfloat16), ("dp", "fs"), scatter_dimension=1, tiled=True
        ).astype(jnp.float32),
    )
    return (
        jnp.stack(layer_outputs),
        jnp.stack(input_grads),
        jnp.stack(prev_grads),
        dense_acc[0],
        dense_acc[1],
        dense_acc[2],
        dense_acc[3],
        dense_acc[4],
        dense_acc[5],
        dense_acc[6],
        expert_shares[0],
        expert_shares[1],
        expert_shares[2],
    )


NEG = -1e30
KINDS = 2
SMALL = 16
LANES = 128
F32 = jnp.float32
BF16 = jnp.bfloat16


def dot(lhs, rhs, dims=((1,), (0,)), precision=None):
    return lax.dot_general(
        lhs, rhs, (dims, ((), ())), precision=precision, preferred_element_type=F32
    )


def key_span(block, rows, reach):
    start = max(0, block * rows - reach)
    return start, (block + 1) * rows - start


def column(rows, index):
    return rows[:, index : index + 1]


def chosen_of(ctl):
    lane = lax.broadcasted_iota(jnp.int32, ctl.shape, 1).astype(F32)
    return ((lane == column(ctl, 8)) | (lane == column(ctl, 9))).astype(F32)


def shape(dims, dtype):
    return jax.ShapeDtypeStruct(dims, dtype)


def whole(dims):
    return pl.BlockSpec(dims, lambda *_: (0,) * len(dims))


def per_row(rows, width):
    return pl.BlockSpec((rows, width), lambda i: (i, 0))


def params():
    return pltpu.CompilerParams(vmem_limit_bytes=56 * 1024 * 1024)


def cost(flops, moved):
    return pl.CostEstimate(flops=int(flops), bytes_accessed=int(moved), transcendentals=0)


class Mail:
    def __init__(self, send_sems, recv_sems):
        self.send_sems = send_sems
        self.recv_sems = recv_sems
        self.used = 0

    def copy(self, source, target, device):
        slot = self.used
        self.used = slot + 1
        return pltpu.make_async_remote_copy(
            src_ref=source,
            dst_ref=target,
            send_sem=self.send_sems.at[slot],
            recv_sem=self.recv_sems.at[slot],
            device_id=device,
            device_id_type=pl.DeviceIdType.MESH,
        )


def position():
    place = lax.axis_index("ep")
    return place // 2, place % 2, lax.axis_index("dp"), lax.axis_index("fs")


def greet(devices):
    barrier = pltpu.get_barrier_semaphore()
    total = 0
    for device, present in devices:
        if present is True:
            pl.semaphore_signal(
                barrier, inc=1, device_id=device, device_id_type=pl.DeviceIdType.MESH
            )
            total = total + 1
        else:

            @pl.when(present)
            def _():
                pl.semaphore_signal(
                    barrier, inc=1, device_id=device, device_id_type=pl.DeviceIdType.MESH
                )

            total = total + jnp.where(present, 1, 0)
    pl.semaphore_wait(barrier, total)


def attend_pair(pair, rows, reach, span, qkv_ref, segc_ref, segr_ref, att_ref, lse_ref):
    length = qkv_ref.shape[0]
    at_q, at_k, at_v = (
        pl.ds(pl.multiple_of(part * span + pair * LANES, LANES), LANES) for part in range(3)
    )
    for block in range(length // rows):
        start, width = key_span(block, rows, reach)
        here = pl.ds(block * rows, rows)
        there = pl.ds(start, width)
        queries = qkv_ref[here, at_q]
        keys = qkv_ref[there, at_k]
        values = qkv_ref[there, at_v]
        seg_q = segc_ref[here, 0:1]
        seg_k = segr_ref[0:1, there]
        row_pos = block * rows + lax.broadcasted_iota(jnp.int32, (rows, width), 0)
        col_pos = start + lax.broadcasted_iota(jnp.int32, (rows, width), 1)
        allowed = (seg_q == seg_k) & (col_pos <= row_pos)
        lane = lax.broadcasted_iota(jnp.int32, (rows, LANES), 1)
        outs = []
        logs = []
        for head in range(2):
            mine = (lane // HEAD) == head
            scores = dot(jnp.where(mine, queries, 0), keys, ((1,), (1,))) * 0.125
            scores = jnp.where(allowed, scores, NEG)
            largest = jnp.max(scores, axis=-1, keepdims=True)
            powers = jnp.exp(scores - largest)
            total = jnp.sum(powers, axis=-1, keepdims=True)
            outs.append(dot(powers.astype(BF16), values) / total)
            logs.append(largest + jnp.log(total))
        valid = (seg_q != SEGS - 1.0).astype(F32)
        att = jnp.where(lane < HEAD, outs[0], outs[1]) * valid
        att_ref[here, at_q] = att.astype(BF16)
        both = jnp.where(lane < HEAD, logs[0], logs[1]).T
        lse_ref[pair, 0:1, here] = both[0:1, :]
        lse_ref[pair, 1:2, here] = both[HEAD : HEAD + 1, :]


def gather_kernel(
    rows, reach, routes,
    tok_ref, cot_ref, wqkv_ref, wout_ref, prev_ref, route_ref, seg_ref, router_ref, cproj_ref,
    cvec_ref, gain_a_ref, gain_m_ref,
    x_all, cot_own, ctl_own, normed_ref, qkv_ref, att_ref, lse_ref, small_all, wqkv_all,
    wout_sib, segc_ref, segr_ref,
    ctl_wide, ctl_send, small_wide, small_send, seg_all,
    near_send, near_recv, far_send, far_recv, core_send, core_recv, local_sems,
):
    y, x, z, core = position()
    me = y * 2 + x
    sibling = (me, z, 1 - core)
    moved = y != core
    near = ((1 - y) * 2 + x, z, 1 - core)
    far = (core * 2 + 1 - x, z, y)
    greet([(sibling, True), (far, True), (near, moved)])
    span = wqkv_ref.shape[0]

    def block_of(index):
        return pl.ds(pl.multiple_of(index * rows, rows), rows)

    within = block_of(x)
    homes = [
        (tok_ref, x_all.at[block_of(me)]),
        (cot_ref, cot_own.at[within]),
        (ctl_send, ctl_own.at[x]),
    ]
    nears = Mail(near_send, near_recv)
    fars = Mail(far_send, far_recv)
    near_copies = [nears.copy(a.at[x], b, near) for a, b in homes]
    far_copies = [fars.copy(a.at[1 - x], b, far) for a, b in homes]
    stay_copies = [
        pltpu.make_async_copy(a.at[x], b, local_sems.at[k]) for k, (a, b) in enumerate(homes)
    ]

    def send(k):
        far_copies[k].start()

        @pl.when(moved)
        def _():
            near_copies[k].start()

        @pl.when(jnp.logical_not(moved))
        def _():
            stay_copies[k].start()

    def take_near(k):
        @pl.when(moved)
        def _():
            near_copies[k].wait_recv()

        @pl.when(jnp.logical_not(moved))
        def _():
            stay_copies[k].wait()

    send(0)
    inner = Mail(core_send, core_recv)
    weight_copies = []
    own_copies = []
    band = pl.ds(pl.multiple_of(core * span, span), span)
    for part in range(3):
        columns = pl.ds(part * span, span)
        for side, copies in ((1 - core, weight_copies), (core, own_copies)):
            source = wqkv_ref.at[
                :, pl.ds(pl.multiple_of(part * 2 * span + side * span, LANES), span)
            ]
            target = wqkv_all.at[band, columns]
            if copies is weight_copies:
                copies.append(inner.copy(source, target, sibling))
            else:
                copies.append(
                    pltpu.make_async_copy(source, target, local_sems.at[3 + part])
                )
    out_copy = inner.copy(wout_ref, wout_sib, sibling)
    seg_copy = inner.copy(seg_ref, seg_all.at[core], sibling)
    seg_own = pltpu.make_async_copy(seg_ref, seg_all.at[core], local_sems.at[6])
    small_copy = inner.copy(small_send, small_all.at[:, band], sibling)
    seg_copy.start()
    seg_own.start()
    for copy in weight_copies + own_copies:
        copy.start()

    small_wide[...] = jnp.zeros_like(small_wide)
    small_wide[:, 0:routes] = router_ref[...].astype(F32)
    small_wide[:, 8:12] = cproj_ref[...].astype(F32)
    small_wide[:, 12:14] = cvec_ref[...].astype(F32)
    turned = small_wide[...].T[:SMALL, :]
    which = lax.broadcasted_iota(jnp.int32, (SMALL, span), 0)
    turned = jnp.where(which == 14, gain_a_ref[...].astype(F32), turned)
    turned = jnp.where(which == 15, gain_m_ref[...].astype(F32), turned)
    small_send[...] = turned.astype(BF16)
    small_all[:, band] = turned.astype(BF16)
    small_copy.start()
    out_copy.start()
    for m in range(2):
        ctl_wide[...] = jnp.zeros_like(ctl_wide)
        ctl_wide[:, 0:routes] = prev_ref[m]
        ctl_wide[:, 8:10] = route_ref[m].astype(F32)
        ctl_send[m] = ctl_wide[...].T[:SMALL, :]
    send(2)
    seg_copy.wait_recv()
    seg_own.wait()
    seg_row = seg_all[y, pl.ds(x, 1), :].astype(F32)
    length = seg_row.shape[1]
    segr_ref[...] = jnp.broadcast_to(seg_row, segr_ref.shape)
    segc_ref[...] = jnp.broadcast_to(seg_row, (LANES, length)).T
    small_copy.wait_recv()
    for copy in weight_copies:
        copy.wait_recv()
    for copy in own_copies:
        copy.wait()
    gain = small_all[14:15, :].astype(F32)

    def project(index):
        here = block_of(index)
        values = x_all[here, :].astype(F32)
        inverse = lax.rsqrt(jnp.mean(values * values, axis=-1, keepdims=True) + NORM_EPS)
        normed = (values * inverse * gain).astype(BF16)
        normed_ref[here, :] = normed
        qkv_ref[here, :] = dot(normed, wqkv_all[...]).astype(BF16)

    forward = []
    for step in range(2):
        spot = x_all.at[block_of(core * 2 + (x if step == 0 else 1 - x))]
        forward.append(inner.copy(spot, spot, sibling))
    take_near(0)
    forward[0].start()
    project(core * 2 + x)
    far_copies[0].wait_recv()
    forward[1].start()
    send(1)
    project(core * 2 + 1 - x)
    forward[0].wait_recv()
    project((1 - core) * 2 + x)
    forward[1].wait_recv()
    project((1 - core) * 2 + 1 - x)

    @pl.loop(0, span // LANES)
    def _(pair):
        attend_pair(pair, rows, reach, span, qkv_ref, segc_ref, segr_ref, att_ref, lse_ref)

    for k in (1, 2):
        take_near(k)
        far_copies[k].wait_recv()
    out_copy.wait_recv()
    for copy in far_copies + weight_copies + forward + [out_copy, seg_copy, small_copy]:
        copy.wait_send()

    @pl.when(moved)
    def _():
        for copy in near_copies:
            copy.wait_send()


def gather_all(
    tokens, cotangent, w_qkv, w_out, prev_logits, routes, segments, w_router, const_proj,
    const_vec, gain_attn, gain_moe,
):
    rows, width = tokens.shape[1:]
    length = segments.shape[1]
    mine = length // 2
    span = width // 2
    vmem = pl.BlockSpec(memory_space=pltpu.VMEM)
    anywhere = pl.BlockSpec(memory_space=pl.ANY)
    return pl.pallas_call(
        functools.partial(gather_kernel, rows, length // 2, w_router.shape[1]),
        in_specs=[anywhere] * 4 + [vmem] * 8,
        out_specs=[vmem] * 12,
        out_shape=[
            shape((length, width), BF16), shape((mine, width), BF16),
            shape((2, SMALL, rows), F32), shape((length, width), BF16),
            shape((length, 3 * span), BF16), shape((length, span), BF16),
            shape((span // LANES, 8, length), F32), shape((SMALL, width), BF16),
            shape((width, 3 * span), BF16), shape((span, width), BF16),
            shape((length, LANES), F32), shape((8, length), F32),
        ],
        scratch_shapes=[
            pltpu.VMEM((rows, LANES), F32), pltpu.VMEM((2, SMALL, rows), F32),
            pltpu.VMEM((span, LANES), F32), pltpu.VMEM((SMALL, span), BF16),
            pltpu.VMEM((2, 2, length), jnp.int32),
        ]
        + [pltpu.SemaphoreType.DMA((3,))] * 4
        + [pltpu.SemaphoreType.DMA((8,))] * 2
        + [pltpu.SemaphoreType.DMA((7,))],
        compiler_params=pltpu.CompilerParams(
            collective_id=3, has_side_effects=True, vmem_limit_bytes=60 * 1024 * 1024
        ),
        name="gather_all",
    )(
        tokens, cotangent, w_qkv, w_out, prev_logits, routes, segments, w_router, const_proj,
        const_vec, gain_attn[None], gain_moe[None],
    )


def widen(turned):
    pad = jnp.zeros((LANES - turned.shape[0], turned.shape[1]), turned.dtype)
    return jnp.concatenate([turned, pad], axis=0).T


def spread_block(experts, routes, rows, block, refs, send_ref, recv_ref, keep):
    att_own, att_sib, x_ref, g_ref, ctl_ref, w_own, w_sib, small_rows, wide_rows = refs
    residual_ref, mixed_ref, pm_ref, place_ref = keep
    y, x, z, core = position()
    here = pl.ds(pl.multiple_of(block * rows, rows), rows)
    tokens = x_ref[pl.ds(pl.multiple_of((core * 2 + block) * rows, rows), rows), :]
    residual = tokens.astype(F32) + (
        dot(att_own[here, :], w_own[...]) + dot(att_sib[here, :], w_sib[...])
    )
    residual_ref[here, :] = residual
    inverse = lax.rsqrt(jnp.mean(residual * residual, axis=-1, keepdims=True) + NORM_EPS)
    mixed = (residual * inverse * small_rows[15:16, :].astype(F32)).astype(BF16)
    mixed_ref[here, :] = mixed
    logits = dot(mixed, wide_rows[...], ((1,), (1,)))
    ctl = widen(ctl_ref[block])
    lane = lax.broadcasted_iota(jnp.int32, (rows, LANES), 1)
    is_route = lane < routes
    router = jnp.where(is_route, logits + ctl, NEG)
    powers = jnp.exp(router - jnp.max(router, axis=-1, keepdims=True))
    probs = powers / jnp.sum(powers, axis=-1, keepdims=True)
    probs = jnp.where(is_route, probs, 0.0)
    pm = probs
    for const_index in range(2):
        first = column(logits, 8 + 2 * const_index)
        second = column(logits, 9 + 2 * const_index)
        largest = jnp.maximum(first, second)
        first = jnp.exp(first - largest)
        second = jnp.exp(second - largest)
        total = first + second
        pm = jnp.where(lane == 8 + 2 * const_index, first / total, pm)
        pm = jnp.where(lane == 9 + 2 * const_index, second / total, pm)
    pm_ref[here, :] = pm
    chosen = chosen_of(ctl)
    gated = chosen * probs
    earlier = lax.broadcasted_iota(jnp.int32, (rows, rows), 1) < lax.broadcasted_iota(
        jnp.int32, (rows, rows), 0
    )
    rank = dot(earlier.astype(BF16), chosen.astype(BF16))
    lane_f = lane.astype(F32)
    grads = g_ref[here, :].astype(F32)
    for expert in range(experts):
        place = jnp.where(
            (lane_f == column(rank, expert)) & (column(chosen, expert) > 0.0), 1.0, 0.0
        )
        place_ref[here, expert * LANES : (expert + 1) * LANES] = place.astype(BF16)
        pick = place.T.astype(BF16)
        d_part = (column(gated, expert) * grads).astype(BF16)
        send_ref[block, expert, 0] = dot(pick, mixed).astype(BF16)
        send_ref[block, expert, 1] = dot(pick, d_part).astype(BF16)
    recv_ref[block, y * 2 + x] = send_ref[block, y]


def expert_block(block, recv_ref, result_ref, back_ref, weights, keep):
    gate_w, up_w, down_w = weights
    hidden_ref, d_gate_ref, d_up_ref = keep
    y, x, z, core = position()
    peers, _, capacity, width = recv_ref.shape[1:]
    size = peers * capacity
    here = pl.ds(pl.multiple_of(block * size, size), size)
    rows = recv_ref[block, :, 0].reshape(size, width)
    d_rows = recv_ref[block, :, 1].reshape(size, width)
    gate = dot(rows, gate_w[...])
    up = dot(rows, up_w[...])
    sig = jax.nn.sigmoid(gate)
    active = gate * sig
    hidden = (active * up).astype(BF16)
    hidden_ref[here, :] = hidden
    part = dot(hidden, down_w[...]).astype(BF16)
    result_ref[block, :, 0] = part.reshape(peers, capacity, width)
    d_hidden = dot(d_rows, down_w[...], ((1,), (1,)))
    d_gate = (d_hidden * up * sig * (1.0 + gate * (1.0 - sig))).astype(BF16)
    d_up = (d_hidden * active).astype(BF16)
    d_gate_ref[here, :] = d_gate
    d_up_ref[here, :] = d_up
    d_in = dot(d_gate, gate_w[...], ((1,), (1,))) + dot(d_up, up_w[...], ((1,), (1,)))
    result_ref[block, :, 1] = d_in.astype(BF16).reshape(peers, capacity, width)
    back_ref[block, y * 2 + x] = result_ref[block, y * 2 + x]


def combine_block(experts, routes, rows, block, refs, keep, back_ref, outs, small_ref):
    g_ref, ctl_ref, small_rows, wide_rows = refs
    residual_ref, mixed_ref, pm_ref, place_ref = keep
    out_ref, prev_ref, dres_ref, branch_ref = outs
    halves = back_ref.shape[1] // experts
    here = pl.ds(pl.multiple_of(block * rows, rows), rows)
    g_low = g_ref[here, :]
    grads = g_low.astype(F32)
    mixed = mixed_ref[here, :].astype(F32)
    residual = residual_ref[here, :]
    pm = pm_ref[here, :]
    lane = lax.broadcasted_iota(jnp.int32, (rows, LANES), 1)
    chosen = chosen_of(widen(ctl_ref[block]))
    probs = jnp.where(lane < routes, pm, 0.0)
    gated = chosen * probs
    d_probs = jnp.zeros((rows, LANES), F32)
    result = residual
    d_mixed = None
    for expert in range(experts):
        place = place_ref[here, expert * LANES : (expert + 1) * LANES]
        expert_out = None
        for half in range(halves):
            owner = expert * halves + half
            term = dot(place, back_ref[block, owner, 0])
            expert_out = term if expert_out is None else expert_out + term
            term = dot(place, back_ref[block, owner, 1])
            d_mixed = term if d_mixed is None else d_mixed + term
        result = result + column(gated, expert) * expert_out
        d_gate = jnp.sum(expert_out * grads, axis=-1, keepdims=True)
        d_probs = jnp.where(lane == expert, d_gate, d_probs)
    g_mixed = jnp.sum(grads * mixed, axis=-1, keepdims=True)
    g_const = dot(g_low, wide_rows[...], ((1,), (1,)))
    copy = experts + 1
    d_probs = jnp.where(lane == copy, g_mixed, d_probs)
    weight = column(gated, copy)
    d_small = jnp.zeros((rows, LANES), F32)
    for const_index in range(2):
        route = copy + 1 + const_index
        first = column(pm, 8 + 2 * const_index)
        second = column(pm, 9 + 2 * const_index)
        gate = column(gated, route)
        g_vec = column(g_const, 12 + const_index)
        d_probs = jnp.where(lane == route, first * g_mixed + second * g_vec, d_probs)
        weight = weight + gate * first
        vec = small_rows[12 + const_index : 13 + const_index, :].astype(F32)
        result = result + (gate * second) * vec
        d_first = gate * g_mixed
        d_second = gate * g_vec
        mean = first * d_first + second * d_second
        d_small = jnp.where(lane == 8 + 2 * const_index, first * (d_first - mean), d_small)
        d_small = jnp.where(lane == 9 + 2 * const_index, second * (d_second - mean), d_small)
        d_small = jnp.where(lane == 12 + const_index, gate * second, d_small)
    result = result + weight * mixed
    out_ref[block] = result.astype(BF16)
    d_probs = d_probs * chosen
    d_logits = probs * (d_probs - jnp.sum(probs * d_probs, axis=-1, keepdims=True))
    d_small = jnp.where(lane < routes, d_logits, d_small)
    d_mixed = d_mixed + weight * grads
    d_mixed = d_mixed + dot(
        jnp.where(lane < 12, d_small, 0.0), wide_rows[...].astype(F32), precision=HIGHEST
    )
    inverse = lax.rsqrt(jnp.mean(residual * residual, axis=-1, keepdims=True) + NORM_EPS)
    scaled = d_mixed * small_rows[15:16, :].astype(F32)
    mean = jnp.mean(scaled * residual, axis=-1, keepdims=True)
    d_residual = grads + inverse * scaled - residual * (inverse * inverse * inverse * mean)
    dres_ref[here, :] = d_residual
    branch_ref[here, :] = d_residual.astype(BF16)
    d_turned = d_small.T[:SMALL, :]
    prev_ref[block] = d_turned[:8, :]
    sub = lax.broadcasted_iota(jnp.int32, (SMALL, rows), 0)
    small = dot(jnp.where(sub < 12, d_turned, 0.0), mixed, precision=HIGHEST)
    small = small + dot(
        jnp.where((sub >= 12) & (sub < 14), d_turned, 0.0), grads, precision=HIGHEST
    )
    d_gain = jnp.sum(d_mixed * residual * inverse, axis=0, keepdims=True)
    which = lax.broadcasted_iota(jnp.int32, small.shape, 0)
    small_ref[...] += jnp.where(which == 14, d_gain, small)


def layer_kernel(
    experts, routes, rows, blocks,
    att_ref, x_ref, g_ref, ctl_ref, w_own, w_sib, small_rows, gate_ref, up_ref, down_ref,
    out_ref, prev_ref, dres_ref, branch_ref, small_ref, dgate_out, dup_out, ddown_out,
    wide_rows, att_own, att_sib, gate_w, up_w, down_w, residual_ref, mixed_ref, pm_ref, place_ref,
    send_ref, recv_ref, result_ref, back_ref, hidden_ref, d_gate_ref, d_up_ref,
    head_send, head_recv, local_sems, send_sems, recv_sems, back_send, back_recv,
):
    y, x, z, core = position()
    me = y * 2 + x
    sibling = (me, z, 1 - core)
    partners = [(1 - y) * 2 + 1 - x, y * 2 + 1 - x, (1 - y) * 2 + x]
    wanted = [1 - y, y, 1 - y]
    greet([(sibling, True)] + [((place, z, core), True) for place in partners])
    mine = rows * blocks
    mail = Mail(head_send, head_recv)
    pairs = [(gate_ref, gate_w), (up_ref, up_w), (down_ref, down_w)]
    heads = [mail.copy(att_ref.at[1 - core], att_sib, sibling)]
    locals_ = [pltpu.make_async_copy(att_ref.at[core], att_own, local_sems.at[3])]
    for k, (source, target) in enumerate(pairs):
        size = source.shape[0]
        spot = target.at[pl.ds(pl.multiple_of(core * size, size), size)]
        heads.append(mail.copy(source, spot, sibling))
        locals_.append(pltpu.make_async_copy(source, spot, local_sems.at[k]))
    for copy in heads + locals_:
        copy.start()

    def dispatch(block, k):
        return pltpu.make_async_remote_copy(
            src_ref=send_ref.at[block, wanted[k]],
            dst_ref=recv_ref.at[block, me],
            send_sem=send_sems.at[block, k],
            recv_sem=recv_sems.at[block, k],
            device_id=(partners[k], z, core),
            device_id_type=pl.DeviceIdType.MESH,
        )

    def giveback(block, k):
        return pltpu.make_async_remote_copy(
            src_ref=result_ref.at[block, partners[k]],
            dst_ref=back_ref.at[block, me],
            send_sem=back_send.at[block, k],
            recv_sem=back_recv.at[block, k],
            device_id=(partners[k], z, core),
            device_id_type=pl.DeviceIdType.MESH,
        )

    small_ref[...] = jnp.zeros_like(small_ref)
    wide_rows[...] = jnp.zeros_like(wide_rows)
    wide_rows[0:SMALL, :] = small_rows[...]
    heads[0].wait_recv()
    locals_[0].wait()
    keep = (residual_ref, mixed_ref, pm_ref, place_ref)
    spread_refs = (
        att_own, att_sib, x_ref, g_ref, ctl_ref, w_own, w_sib, small_rows, wide_rows
    )

    @pl.loop(0, blocks)
    def _(block):
        spread_block(experts, routes, rows, block, spread_refs, send_ref, recv_ref, keep)
        for k in range(3):
            dispatch(block, k).start()

    for copy in heads[1:]:
        copy.wait_recv()
    for copy in locals_[1:]:
        copy.wait()

    @pl.loop(0, blocks)
    def _(block):
        for k in range(3):
            dispatch(block, k).wait_recv()
        expert_block(
            block, recv_ref, result_ref, back_ref, (gate_w, up_w, down_w),
            (hidden_ref, d_gate_ref, d_up_ref),
        )
        for k in range(3):
            giveback(block, k).start()

    peers, _, capacity, width = recv_ref.shape[1:]
    total = blocks * peers * capacity
    step = 2 * LANES

    @pl.loop(0, width // step)
    def _(chunk):
        span = pl.ds(pl.multiple_of(chunk * step, step), step)
        lhs = recv_ref[:, :, 0, :, span].reshape(total, step).T
        dgate_out[span, :] = dot(lhs, d_gate_ref[...]).astype(BF16)
        dup_out[span, :] = dot(lhs, d_up_ref[...]).astype(BF16)

    @pl.loop(0, hidden_ref.shape[1] // step)
    def _(chunk):
        span = pl.ds(pl.multiple_of(chunk * step, step), step)
        lhs = hidden_ref[:, span].T
        rhs = recv_ref[:, :, 1].reshape(total, width)
        ddown_out[span, :] = dot(lhs, rhs).astype(BF16)

    @pl.loop(0, blocks)
    def _(block):
        for k in range(3):
            giveback(block, k).wait_recv()
        combine_block(
            experts, routes, rows, block, (g_ref, ctl_ref, small_rows, wide_rows),
            keep, back_ref, (out_ref, prev_ref, dres_ref, branch_ref), small_ref,
        )

    for copy in heads:
        copy.wait_send()
    for block in range(blocks):
        for k in range(3):
            dispatch(block, k).wait_send()
            giveback(block, k).wait_send()


def expert_layer(
    experts, routes, rows, attended, x_all, cot_own, ctl, w_own, w_sib, small_all, w_gate,
    w_up, w_down,
):
    mine, width = cot_own.shape
    blocks = mine // rows
    peers = lax.axis_size("ep")
    span = attended.shape[1]
    hidden = w_gate.shape[1]
    vmem = pl.BlockSpec(memory_space=pltpu.VMEM)
    total = blocks * peers * LANES
    grads = [(2 * w.shape[0], w.shape[1]) for w in (w_gate, w_up, w_down)]
    return pl.pallas_call(
        functools.partial(layer_kernel, experts, routes, rows, blocks),
        in_specs=[vmem] * 10,
        out_specs=[vmem] * 8,
        out_shape=[
            shape((blocks, rows, width), BF16), shape((blocks, 8, rows), F32),
            shape((mine, width), F32), shape((mine, width), BF16), shape((SMALL, width), F32),
        ]
        + [shape(dims, BF16) for dims in grads],
        scratch_shapes=[pltpu.VMEM((LANES, width), BF16)]
        + [pltpu.VMEM((mine, span), BF16)] * 2
        + [pltpu.VMEM(dims, BF16) for dims in grads]
        + [
            pltpu.VMEM((mine, width), F32), pltpu.VMEM((mine, width), BF16),
            pltpu.VMEM((mine, LANES), F32), pltpu.VMEM((mine, experts * LANES), BF16),
            pltpu.VMEM((blocks, experts, KINDS, LANES, width), BF16),
        ]
        + [pltpu.VMEM((blocks, peers, KINDS, LANES, width), BF16)] * 3
        + [pltpu.VMEM((total, hidden), BF16)] * 3
        + [
            pltpu.SemaphoreType.DMA((4,)), pltpu.SemaphoreType.DMA((4,)),
            pltpu.SemaphoreType.DMA((4,)),
        ]
        + [pltpu.SemaphoreType.DMA((blocks, 3))] * 4,
        compiler_params=pltpu.CompilerParams(
            collective_id=2, has_side_effects=True, vmem_limit_bytes=62 * 1024 * 1024
        ),
        name="expert_layer",
    )(
        attended.reshape(2, mine, span), x_all, cot_own, ctl, w_own, w_sib, small_all,
        w_gate, w_up, w_down,
    )


class Line:
    def __init__(self, mail, depth, slots):
        self.depth = depth
        self.slots = slots
        self.place = lax.axis_index("dp")
        y, x, z, core = position()
        self.copies = {}
        for way in range(2):
            step_to = 1 if way == 0 else -1
            device = (y * 2 + x, z + step_to, core)
            for step in range(depth - 1):
                for item, (acc, landing) in enumerate(slots):
                    shard = self.shard(way, step)
                    safe = jnp.clip(shard, 0, depth - 1)
                    self.copies[way, step, item] = mail.copy(
                        acc.at[safe], landing.at[way, step], device
                    )

    def shard(self, way, step):
        if way == 0:
            return self.place + self.depth - 1 - step
        return self.place - (self.depth - 1 - step)

    def edge(self, way):
        return self.place == (0 if way == 0 else self.depth - 1)

    def sends(self, way, step):
        shard = self.shard(way, step)
        if way == 0:
            return (shard <= self.depth - 1) & (self.place < self.depth - 1)
        return (shard >= 0) & (self.place > 0)

    def gets(self, way, step):
        if way == 0:
            return (self.place > 0) & (self.shard(way, step + 1) <= self.depth - 1)
        return (self.place < self.depth - 1) & (self.shard(way, step + 1) >= 0)

    def send(self, step, item):
        for way in range(2):
            wanted = self.sends(way, step)
            if step > 0:
                wanted = wanted & jnp.logical_not(self.edge(way))

            @pl.when(wanted)
            def _():
                self.copies[way, step, item].start()

    def send_edge(self, step, item):
        for way in range(2):

            @pl.when(self.sends(way, step) & self.edge(way))
            def _():
                self.copies[way, step, item].start()

    def take(self, step, item):
        acc, landing = self.slots[item]
        for way in range(2):
            shard = jnp.clip(self.shard(way, step + 1), 0, self.depth - 1)

            @pl.when(self.gets(way, step))
            def _():
                self.copies[way, step, item].wait_recv()
                acc[shard] = (
                    acc[shard].astype(F32) + landing[way, step].astype(F32)
                ).astype(BF16)

    def finish(self, item, store):
        acc, landing = self.slots[item]
        store(acc[self.place].astype(F32))
        for way in range(2):

            @pl.when(self.gets(way, self.depth - 2))
            def _():
                self.copies[way, self.depth - 2, item].wait_recv()
                store(landing[way, self.depth - 2].astype(F32), True)

    def close(self):
        for (way, step, item), copy in self.copies.items():

            @pl.when(self.sends(way, step))
            def _():
                copy.wait_send()


class Plane:
    def __init__(self, mail, source, buffers, total):
        y, x, z, core = position()
        self.place = y, x
        self.source = source
        self.buffers = buffers
        self.total = total
        y1_land, x1_land, y1_acc, x1_acc, x2_land, y2_land = buffers
        half = x2_land.shape[0]
        self.low = pl.ds(0, half)
        self.high = pl.ds(half, half)
        across = (y * 2 + 1 - x, z, core)
        along = ((1 - y) * 2 + x, z, core)
        self.first = [
            mail.copy(source.at[1 - y, :, self.low], y1_land, along),
            mail.copy(source.at[:, 1 - x, self.high], x1_land, across),
        ]
        self.second = [
            mail.copy(y1_acc.at[1 - x], x2_land, across),
            mail.copy(x1_acc.at[1 - y], y2_land, along),
        ]

    def start(self):
        for copy in self.first:
            copy.start()

    def middle(self):
        y, x = self.place
        y1_land, x1_land, y1_acc, x1_acc, _, _ = self.buffers
        self.first[0].wait_recv()
        for k in range(2):
            y1_acc[k] = (
                self.source[y, k, self.low].astype(F32) + y1_land[k].astype(F32)
            ).astype(BF16)
        self.second[0].start()
        self.first[1].wait_recv()
        for k in range(2):
            x1_acc[k] = (
                self.source[k, x, self.high].astype(F32) + x1_land[k].astype(F32)
            ).astype(BF16)
        self.second[1].start()

    def end(self):
        y, x = self.place
        _, _, y1_acc, x1_acc, x2_land, y2_land = self.buffers
        shards, size = self.total.shape[0] // 2, self.total.shape[1]
        self.second[0].wait_recv()
        for shard in range(shards):
            part = pl.ds(shard * size, size)
            self.total[shard] = (
                y1_acc[x, part].astype(F32) + x2_land[part].astype(F32)
            ).astype(BF16)
        self.second[1].wait_recv()
        for shard in range(shards):
            part = pl.ds(shard * size, size)
            self.total[shards + shard] = (
                x1_acc[y, part].astype(F32) + y2_land[part].astype(F32)
            ).astype(BF16)

    def close(self):
        for copy in self.first + self.second:
            copy.wait_send()


def back_pair(
    pair, rows, reach, span, qkv_ref, datt_ref, segc_ref, segr_ref, lse_ref, dqkv_ref,
    dk_sum, dv_sum,
):
    length = qkv_ref.shape[0]
    at_q, at_k, at_v = (
        pl.ds(pl.multiple_of(part * span + pair * LANES, LANES), LANES) for part in range(3)
    )
    dk_sum[...] = jnp.zeros_like(dk_sum)
    dv_sum[...] = jnp.zeros_like(dv_sum)
    keys_turned = qkv_ref[:, at_k].T
    for block in range(length // rows):
        start, width = key_span(block, rows, reach)
        here = pl.ds(block * rows, rows)
        there = pl.ds(start, width)
        queries = qkv_ref[here, at_q]
        grads = datt_ref[here, at_q]
        keys = qkv_ref[there, at_k]
        values = qkv_ref[there, at_v]
        seg_k = segc_ref[there, 0:1]
        seg_q = segr_ref[0:1, here]
        key_pos = start + lax.broadcasted_iota(jnp.int32, (width, rows), 0)
        query_pos = block * rows + lax.broadcasted_iota(jnp.int32, (width, rows), 1)
        allowed = (seg_q == seg_k) & (key_pos <= query_pos)
        lane = lax.broadcasted_iota(jnp.int32, (rows, LANES), 1)
        dq_parts = []
        for head in range(2):
            mine = (lane // HEAD) == head
            head_q = jnp.where(mine, queries, 0)
            head_g = jnp.where(mine, grads, 0)
            log_total = lse_ref[pair, head : head + 1, here]
            scores = dot(keys, head_q, ((1,), (1,))) * 0.125
            probs = jnp.exp(jnp.where(allowed, scores, NEG) - log_total)
            d_probs = dot(values, head_g, ((1,), (1,)))
            delta = jnp.sum(probs * d_probs, axis=0, keepdims=True)
            d_scores = (probs * (d_probs - delta)).astype(BF16)
            dv_sum[there, :] += dot(probs.astype(BF16), head_g)
            dk_sum[there, :] += dot(d_scores, head_q)
            turned = keys_turned[head * HEAD : (head + 1) * HEAD, start : start + width]
            dq_parts.append(dot(turned, d_scores))
        dq = jnp.concatenate(dq_parts, axis=0).T * 0.125
        dqkv_ref[here, at_q] = dq.astype(BF16)
    dqkv_ref[:, at_k] = (dk_sum[...] * 0.125).astype(BF16)
    dqkv_ref[:, at_v] = dv_sum[...].astype(BF16)


def back_kernel(depth, rows, reach, *refs):
    (
        gate_any, up_any, down_any, branch_any, wout_any, att_any, qkv_any, segc_any, normed_any,
        wqkv_any, x_any, dres_any, out_ref, prev_ref, lse_ref, segr_ref, small_ref, small_rows,
        gate_out, up_out, down_out, qkv_out, wout_out, small_out, out_home, dtok_home, prev_home,
        gate_land, up_land, down_land, gate_acc, up_acc, down_acc, gate_line, up_line, down_line,
        branch_ref, wout_ref, att_ref, qkv_ref, segc_ref, normed_ref, wqkv_ref, x_ref, dres_ref,
        normed_turned, datt_ref, turned_ref, dqkv_ref, dk_sum, dv_sum, dn_send, dn_recv, dtok_ref,
        dense_ref, y1_land, x1_land, y1_acc, x1_acc, x2_land, y2_land, dense_acc, dense_line,
        tail_ref, ty1_land, tx1_land, ty1_acc, tx1_acc, tx2_land, ty2_land, tail_acc, tail_line,
        dense_sum, dense_sib, tail_sum, tail_sib, small_wide,
        send_sems, recv_sems, local_sems,
    ) = refs
    y, x, z, core = position()
    sibling = (y * 2 + x, z, 1 - core)
    across = (y * 2 + 1 - x, z, core)
    along = ((1 - y) * 2 + x, z, core)
    moved = y != core
    near = ((1 - y) * 2 + x, z, 1 - core)
    far = (core * 2 + 1 - x, z, y)
    greet(
        [
            (sibling, True), (across, True), (along, True),
            (near, moved), (far, moved),
            ((y * 2 + x, z + 1, core), z < depth - 1), ((y * 2 + x, z - 1, core), z > 0),
        ]
    )
    mail = Mail(send_sems, recv_sems)
    length, width = normed_ref.shape
    mine = length // 2
    span = wout_ref.shape[0]
    pairs = span // LANES
    own_rows = pl.ds(pl.multiple_of(core * mine, mine), mine)
    experts = [
        (gate_any, gate_land, gate_acc, gate_line, gate_out),
        (up_any, up_land, up_acc, up_line, up_out),
        (down_any, down_land, down_acc, down_line, down_out),
    ]
    halves = [mail.copy(source.at[:, 1 - core], land, sibling) for source, land, _, _, _ in experts]
    line = Line(mail, depth, [(acc, landing) for _, _, acc, landing, _ in experts])
    branch_copy = mail.copy(branch_any, branch_ref.at[own_rows], sibling)
    loads = [
        pltpu.make_async_copy(source, target, local_sems.at[k])
        for k, (source, target) in enumerate(
            [
                (gate_any.at[:, core], gate_acc), (up_any.at[:, core], up_acc),
                (down_any.at[:, core], down_acc), (branch_any, branch_ref.at[own_rows]),
                (normed_any, normed_ref), (att_any, att_ref), (wout_any, wout_ref),
                (segc_any, segc_ref), (qkv_any, qkv_ref), (wqkv_any, wqkv_ref),
                (x_any.at[own_rows], x_ref), (dres_any, dres_ref),
            ]
        )
    ]
    homes = [(out_ref, out_home), (prev_ref, prev_home), (dtok_ref, dtok_home)]
    nears = [mail.copy(a.at[x], b.at[x], near) for a, b in homes]
    fars = [mail.copy(a.at[1 - x], b.at[x], far) for a, b in homes]
    stays = [
        pltpu.make_async_copy(a.at[x], b.at[x], local_sems.at[len(loads) + k])
        for k, (a, b) in enumerate(homes)
    ]

    def go_near(k):
        @pl.when(moved)
        def _():
            nears[k].start()

        @pl.when(jnp.logical_not(moved))
        def _():
            stays[k].start()

    half_copy = mail.copy(turned_ref.at[1 - core], dense_ref.at[0, core], sibling)
    planes = [
        Plane(
            mail, dense_ref.at[c],
            [b.at[c] for b in (y1_land, x1_land, y1_acc, x1_acc, x2_land, y2_land)],
            dense_acc.at[c],
        )
        for c in range(pairs + 1)
    ] + [
        Plane(
            mail, tail_ref, (ty1_land, tx1_land, ty1_acc, tx1_acc, tx2_land, ty2_land), tail_acc
        )
    ]
    dense = Line(
        mail, depth,
        [(dense_acc.at[c], dense_line.at[c]) for c in range(pairs + 1)] + [(tail_acc, tail_line)],
    )
    chunks = pairs + 2
    size = tail_sum.shape[0]
    half = size // 2
    other = pl.ds(pl.multiple_of((1 - core) * half, 8), half)
    ours = pl.ds(pl.multiple_of(core * half, 8), half)
    sums = [(dense_sum.at[c], dense_sib.at[c]) for c in range(pairs + 1)] + [(tail_sum, tail_sib)]
    lasts = [mail.copy(a.at[other], b, sibling) for a, b in sums]
    dn_copies = [mail.copy(dn_send.at[b], dn_recv.at[b], sibling) for b in range(2)]

    for copy in halves[:1] + [branch_copy] + halves[1:]:
        copy.start()
    for copy in loads:
        copy.start()
    fars[0].start()
    fars[1].start()
    go_near(0)
    go_near(1)

    loads[4].wait()
    normed_turned[...] = normed_ref[...].T
    for item, (_, land, acc, _, _) in enumerate(experts):
        loads[item].wait()
        halves[item].wait_recv()
        for shard in range(depth):
            acc[shard] = (acc[shard].astype(F32) + land[shard].astype(F32)).astype(BF16)
        line.send(0, item)
    for item in range(3):
        line.send_edge(1, item)
    for k in (3, 5, 6, 7):
        loads[k].wait()
    branch_copy.wait_recv()

    @pl.loop(0, length // rows)
    def _(block):
        here = pl.ds(pl.multiple_of(block * rows, rows), rows)
        valid = (segc_ref[here, 0:1] != SEGS - 1.0).astype(F32)
        datt_ref[here, :] = (
            dot(branch_ref[here, :], wout_ref[...], ((1,), (1,))) * valid
        ).astype(BF16)

    att_turned = att_ref[...].T
    for side in range(2):
        part = dot(att_turned, branch_ref[:, side * span : (side + 1) * span]).astype(BF16)
        turned_ref[side] = part.reshape(turned_ref.shape[1:])
    half_copy.start()
    dense_ref[0, core] = turned_ref[core]
    for k in (8, 9):
        loads[k].wait()
    small_wide[...] = jnp.zeros_like(small_wide)

    quarter = width // 4

    @pl.loop(0, pairs)
    def _(pair):
        back_pair(
            pair, rows, reach, span, qkv_ref, datt_ref, segc_ref, segr_ref, lse_ref, dqkv_ref,
            dk_sum, dv_sum,
        )
        columns = [
            pl.ds(pl.multiple_of(part * span + pair * LANES, LANES), LANES) for part in range(3)
        ]

        @pl.loop(0, 4)
        def _(fourth):
            here = pl.ds(pl.multiple_of(fourth * quarter, quarter), quarter)
            d_pair = jnp.concatenate([dqkv_ref[:, at] for at in columns], axis=1)
            weights = jnp.concatenate([wqkv_ref[here, at] for at in columns], axis=1)
            grads = dot(normed_turned[here, :], d_pair)
            dense_ref[1 + pair, fourth // 2, fourth % 2] = grads.astype(BF16)
            gain = jnp.sum(grads * weights.astype(F32), axis=1, keepdims=True)
            lane = lax.broadcasted_iota(jnp.int32, (quarter, LANES), 1)
            small_wide[here, :] += jnp.where(lane == SMALL - 1, gain, 0.0)

        for now in range(pairs):

            @pl.when(pair == now)
            def _():
                planes[now + 1].start()
                if now == 0:
                    half_copy.wait_recv()
                    planes[0].start()
                    for item in range(2):
                        line.take(0, item)
                        line.send(1, item)
                if now >= 1:
                    planes[now - 1].middle()
                if now >= 2:
                    planes[now - 2].end()
                    dense.send(0, now - 2)
                    for step in range(1, depth - 1):
                        dense.send_edge(step, now - 2)
                if now == 1:
                    line.take(0, 2)
                    line.send(1, 2)
                if now == 2:
                    for item in range(2):
                        line.take(1, item)
                        line.send(2, item)

    small_all = small_rows[...].astype(F32)
    gain_column = column(widen(small_all), SMALL - 2)
    lane = lax.broadcasted_iota(jnp.int32, (width, LANES), 1)
    small_grads = jnp.where(
        lane < SMALL - 1, widen(small_ref[...]), small_wide[...] / gain_column
    )
    tail_ref[...] = small_grads.astype(BF16).reshape(tail_ref.shape)
    planes[chunks - 1].start()

    def partial(start, step):
        b = 1 - x if step == 0 else x
        here = pl.ds(pl.multiple_of(start * mine + b * rows, rows), rows)
        return b, dot(dqkv_ref[here, :], wqkv_ref[...], ((1,), (1,)))

    def launch(c):
        planes[c].end()
        dense.send(0, c)
        for step in range(1, depth - 1):
            dense.send_edge(step, c)

    for step in range(2):
        b, value = partial(1 - core, step)
        dn_send[step] = value.astype(BF16)
        dn_copies[step].start()
    planes[pairs - 1].middle()
    launch(pairs - 2)
    for item in range(3):
        line.send_edge(2, item)
    planes[pairs].middle()
    launch(pairs - 1)
    planes[pairs + 1].middle()
    loads[10].wait()
    loads[11].wait()
    gain_row = small_all[SMALL - 2 : SMALL - 1, :]
    for step in range(2):
        b, value = partial(core, step)
        here = pl.ds(pl.multiple_of(b * rows, rows), rows)
        values = x_ref[here, :].astype(F32)
        dn_copies[step].wait_recv()
        d_normed = value + dn_recv[step].astype(F32)
        inverse = lax.rsqrt(jnp.mean(values * values, axis=-1, keepdims=True) + NORM_EPS)
        scaled = d_normed * gain_row
        mean = jnp.mean(scaled * values, axis=-1, keepdims=True)
        result = dres_ref[here, :] + inverse * scaled
        result = result - values * (inverse * inverse * inverse * mean)
        dtok_ref[b] = result.astype(BF16)
        if step == 0:
            fars[2].start()
            launch(pairs)
            launch(pairs + 1)
        else:
            go_near(2)
    line.take(1, 2)
    line.send(2, 2)
    for step in range(depth - 2):
        for c in range(chunks):
            dense.take(step, c)
            dense.send(step + 1, c)
    for item, (_, _, _, _, result) in enumerate(experts):

        def store(value, add=False):
            result[0] = result[0] + value if add else value

        line.finish(item, store)
    for c, (total, _) in enumerate(sums):

        def store(value, add=False):
            total[...] = total[...] + value if add else value

        dense.finish(c, store)
        lasts[c].start()
    for c, (total, land) in enumerate(sums):
        own = total[ours]
        lasts[c].wait_recv()
        theirs = land[...]
        if c == 0:
            for side, value in ((core, own), (1 - core, theirs)):
                wout_out[:, pl.ds(pl.multiple_of(side * span, LANES), span)] = value
        elif c <= pairs:
            for part in range(3):
                for side, value in ((core, own), (1 - core, theirs)):
                    at = part * 2 * span + side * span + (c - 1) * LANES
                    qkv_out[:, pl.ds(pl.multiple_of(at, LANES), LANES)] = value[
                        :, part * LANES : (part + 1) * LANES
                    ]
        else:
            small_out[...] = own + theirs
    for copy in halves + [branch_copy, half_copy] + lasts + dn_copies:
        copy.wait_send()
    for plane in planes:
        plane.close()
    line.close()
    dense.close()
    for copy in fars:
        copy.wait()

    @pl.when(moved)
    def _():
        for copy in nears:
            copy.wait()

    @pl.when(jnp.logical_not(moved))
    def _():
        for copy in stays:
            copy.wait()


def back_all(
    grad_gate, grad_up, grad_down, d_branch, w_out, attended, qkv, seg_col, normed, qkv_weight,
    x_all, d_residual, block_out, d_prev, lse, seg_row, small, small_all,
):
    depth = lax.axis_size("dp")
    experts = [
        grad.reshape(depth, 2, grad.shape[0] // (2 * depth), grad.shape[1])
        for grad in (grad_gate, grad_up, grad_down)
    ]
    length, width = x_all.shape
    mine = length // 2
    span = width // 2
    rows = block_out.shape[1]
    groups = span // LANES + 1
    wide = 3 * LANES
    quarter = width // 4
    size = quarter // depth
    parts = [grad.shape[2:] for grad in experts]
    vmem = pl.BlockSpec(memory_space=pltpu.VMEM)
    anywhere = pl.BlockSpec(memory_space=pl.ANY)
    homes = [block_out.shape, block_out.shape, d_prev.shape]
    kinds = [block_out.dtype, BF16, d_prev.dtype]
    steps = 2 * (depth - 1)
    copies = 3 + 3 * steps + 2 + 6 + (groups + 1) * (4 + steps + 1) + 2

    def plane_buffers(lead, columns):
        return [
            pltpu.VMEM(lead + dims + (columns,), BF16)
            for dims in (
                [(2, 2, quarter)] + [(2, quarter // 2)] * 4 + [(quarter // 2,)] * 2
                + [(depth, size), (2, depth - 1, size)]
            )
        ]

    return pl.pallas_call(
        functools.partial(back_kernel, depth, rows, length // 2),
        in_specs=[anywhere] * 12 + [vmem] * 6,
        out_specs=[vmem] * 6 + [anywhere] * 3,
        out_shape=[shape((1,) + part, F32) for part in parts]
        + [shape((size // 2, 6 * span), F32), shape((size // 2, width), F32)]
        + [shape((size // 2, LANES), F32)]
        + [shape(dims, kind) for dims, kind in zip(homes, kinds)],
        scratch_shapes=[pltpu.VMEM((depth,) + part, BF16) for part in parts] * 2
        + [pltpu.VMEM((2, depth - 1) + part, BF16) for part in parts]
        + [
            pltpu.VMEM((length, width), BF16), pltpu.VMEM((span, width), BF16),
            pltpu.VMEM((length, span), BF16), pltpu.VMEM((length, 3 * span), BF16),
            pltpu.VMEM((length, LANES), F32), pltpu.VMEM((length, width), BF16),
            pltpu.VMEM((width, 3 * span), BF16), pltpu.VMEM((mine, width), BF16),
            pltpu.VMEM((mine, width), F32), pltpu.VMEM((width, length), BF16),
            pltpu.VMEM((length, span), BF16), pltpu.VMEM((2, 2, quarter, span), BF16),
            pltpu.VMEM((length, 3 * span), BF16), pltpu.VMEM((length, LANES), F32),
            pltpu.VMEM((length, LANES), F32), pltpu.VMEM((2, rows, width), BF16),
            pltpu.VMEM((2, rows, width), BF16), pltpu.VMEM((2, rows, width), BF16),
        ]
        + plane_buffers((groups,), wide)
        + plane_buffers((), LANES)
        + [
            pltpu.VMEM((groups, size, wide), F32), pltpu.VMEM((groups, size // 2, wide), F32),
            pltpu.VMEM((size, LANES), F32), pltpu.VMEM((size // 2, LANES), F32),
            pltpu.VMEM((width, LANES), F32),
            pltpu.SemaphoreType.DMA((copies,)),
            pltpu.SemaphoreType.DMA((copies,)),
            pltpu.SemaphoreType.DMA((15,)),
        ],
        compiler_params=pltpu.CompilerParams(
            collective_id=1, has_side_effects=True, vmem_limit_bytes=62 * 1024 * 1024
        ),
        name="back_all",
    )(
        *experts, d_branch, w_out, attended, qkv, seg_col, normed, qkv_weight, x_all, d_residual,
        block_out, d_prev, lse, seg_row, small, small_all,
    )


def one_chip(
    tokens,
    prev_logits,
    segments,
    routes,
    cotangent,
    gain_attn,
    w_qkv,
    w_out,
    gain_moe,
    w_router,
    const_proj,
    const_vec,
    w_gate,
    w_up,
    w_down,
):
    rows = tokens.shape[1]
    route_count = w_router.shape[1]
    experts = route_count - 4
    (
        x_all, cot_own, ctl, normed, qkv, attended, lse, small_all, qkv_weight, out_sib,
        seg_col, seg_row,
    ) = gather_all(
        tokens, cotangent, w_qkv, w_out, prev_logits, routes, segments, w_router, const_proj,
        const_vec, gain_attn, gain_moe,
    )
    (
        block_out, d_prev, d_residual, d_branch, small, grad_gate, grad_up, grad_down,
    ) = expert_layer(
        experts, route_count, rows, attended, x_all, cot_own, ctl, w_out, out_sib, small_all,
        w_gate[0], w_up[0], w_down[0],
    )

    (
        share_gate, share_up, share_down, share_qkv, share_out, share_small, out_home, dtok_home,
        prev_home,
    ) = back_all(
        grad_gate, grad_up, grad_down, d_branch, w_out, attended, qkv, seg_col, normed,
        qkv_weight, x_all, d_residual, block_out, d_prev, lse, seg_row, small, small_all,
    )
    return (
        out_home,
        dtok_home.astype(F32),
        jnp.swapaxes(prev_home, 1, 2)[:, :, :route_count],
        share_small[:, 15],
        share_qkv,
        share_out,
        share_small[:, 14],
        share_small[:, :route_count],
        share_small[:, 8:12],
        share_small[:, 12:14],
        share_gate,
        share_up,
        share_down,
    )


def suits(mesh, tokens, w_router, w_gate):
    peers = mesh.shape["ep"]
    rows = tokens.shape[1] // peers
    micro = tokens.shape[0] // (mesh.shape["dp"] * mesh.shape["fs"])
    routes = w_router.shape[1]
    return (
        peers == 4
        and mesh.shape["fs"] == 2
        and micro == 2
        and mesh.shape["dp"] % 2 == 0
        and (routes - 4) * 2 == peers
        and 3 * rows // routes == LANES
        and tokens.shape[2] % (2 * LANES) == 0
    )


def solution(mesh):
    placed = (
        P(("dp", "fs"), "ep", None),
        P(("dp", "fs"), "ep", None),
        P(("dp", "fs"), None),
        P(("dp", "fs"), "ep", None),
        P(("dp", "fs"), "ep", None),
        P("fs"),
        P("fs", None),
        P("fs", None),
        P("fs"),
        P("fs", None),
        P("fs", None),
        P("fs", None),
        P("ep", "fs", None),
        P("ep", "fs", None),
        P("ep", "fs", None),
    )
    def layer(*arrays):
        fits = suits(mesh, arrays[0], arrays[9], arrays[12])
        return mapped(one_chip if fits else shards)(*arrays)

    def mapped(body):
        return jax.shard_map(
            body,
            mesh=mesh,
            in_specs=placed,
            out_specs=(
                P(("dp", "fs"), "ep", None),
                P(("dp", "fs"), "ep", None),
                P(("dp", "fs"), "ep", None),
                P(("ep", "dp", "fs")),
                P(("ep", "dp", "fs"), None),
                P(("ep", "dp", "fs"), None),
                P(("ep", "dp", "fs")),
                P(("ep", "dp", "fs"), None),
                P(("ep", "dp", "fs"), None),
                P(("ep", "dp", "fs"), None),
                P("ep", ("dp", "fs"), None),
                P("ep", ("dp", "fs"), None),
                P("ep", ("dp", "fs"), None),
            ),
            check_vma=False,
        )

    return layer
```

```python
import functools

import jax
import jax.numpy as jnp
from jax import lax
from jax.experimental import pallas as pl
from jax.experimental.pallas import tpu as pltpu
from jax.sharding import PartitionSpec as P

HEAD = 64
SEGS = 4


NORM_EPS = 1e-06
MASK_FILL = -1e30
HIGHEST = lax.Precision.HIGHEST


def rms_scale(values, gains):
    inverse = lax.rsqrt(jnp.mean(values * values, axis=-1, keepdims=True) + NORM_EPS)
    return values * inverse * gains


def small_softmax(logit_rows):
    largest = jnp.max(logit_rows, axis=-1, keepdims=True)
    powers = jnp.exp(logit_rows - largest)
    return powers / jnp.sum(powers, axis=-1, keepdims=True)


def add_tuple(first_tuple, second_tuple):
    if first_tuple is None:
        return second_tuple
    return tuple(
        (first_term + second_term for first_term, second_term in zip(first_tuple, second_tuple))
    )


def shards(
    tokens,
    prev_logits,
    segments,
    routes,
    cotangent,
    gain_attn,
    w_qkv,
    w_out,
    gain_moe,
    w_router,
    const_proj,
    const_vec,
    w_gate,
    w_up,
    w_down,
):
    micro_count, row_count, model_width = tokens.shape
    head_count = model_width // HEAD
    peer_count = lax.axis_size("ep")
    my_index = lax.axis_index("ep")
    route_count = w_router.shape[1]
    expert_count = route_count - 4
    half_count = peer_count // expert_count
    capacity = (3 * row_count // route_count + 7) // 8 * 8
    seq_length = row_count * peer_count
    slot_count = expert_count * capacity
    pos_all = jnp.arange(seq_length, dtype=jnp.int32)
    pos_mine = my_index * row_count + jnp.arange(row_count, dtype=jnp.int32)
    expert_ids = jnp.arange(expert_count, dtype=jnp.int32)
    slot_ids = jnp.arange(slot_count, dtype=jnp.int32)
    route_ids = jnp.arange(route_count, dtype=jnp.int32)
    layer_outputs = []
    input_grads = []
    prev_grads = []
    dense_acc = None
    expert_acc = None
    for step_index in range(micro_count):
        gathered = (
            lax.all_gather(w_qkv, "fs", axis=0, tiled=True),
            lax.all_gather(w_out, "fs", axis=0, tiled=True),
            lax.all_gather(w_router, "fs", axis=0, tiled=True),
            lax.all_gather(const_proj, "fs", axis=0, tiled=True),
            lax.all_gather(const_vec, "fs", axis=0, tiled=True),
            lax.all_gather(gain_attn, "fs", axis=0, tiled=True),
            lax.all_gather(gain_moe, "fs", axis=0, tiled=True),
            lax.all_gather(w_gate, "fs", axis=1, tiled=True),
            lax.all_gather(w_up, "fs", axis=1, tiled=True),
            lax.all_gather(w_down, "fs", axis=1, tiled=True),
        )
        (
            qkv_weight,
            out_weight,
            router_weight,
            cproj_weight,
            cvec_weight,
            attn_gain,
            moe_gain,
            gate_weight,
            up_weight,
            down_weight,
        ) = gathered
        gate_weight = gate_weight[0]
        up_weight = up_weight[0]
        down_weight = down_weight[0]
        attn_gain = attn_gain.astype(jnp.float32)
        moe_gain = moe_gain.astype(jnp.float32)
        router_float = router_weight.astype(jnp.float32)
        cproj_float = cproj_weight.astype(jnp.float32)
        cvec_float = cvec_weight.astype(jnp.float32)
        token_rows = tokens[step_index].astype(jnp.float32)
        seg_all = segments[step_index]
        seg_mine = lax.dynamic_slice_in_dim(seg_all, my_index * row_count, row_count)
        allowed = (seg_mine[:, None] == seg_all[None, :]) & (pos_all[None, :] <= pos_mine[:, None])
        valid_rows = (seg_mine != SEGS - 1).astype(jnp.float32)[:, None]
        normed = rms_scale(token_rows, attn_gain).astype(jnp.bfloat16)
        qkv_rows = jnp.dot(normed, qkv_weight, preferred_element_type=jnp.float32).astype(
            jnp.bfloat16
        )
        queries = qkv_rows[:, :model_width].reshape(row_count, head_count, HEAD)
        keys_local = qkv_rows[:, model_width : 2 * model_width]
        values_local = qkv_rows[:, 2 * model_width :]
        keys_all, values_all = (
            lax.all_gather(keys_local, "ep", axis=0, tiled=True),
            lax.all_gather(values_local, "ep", axis=0, tiled=True),
        )
        key_heads = keys_all.reshape(seq_length, head_count, HEAD)
        value_heads = values_all.reshape(seq_length, head_count, HEAD)
        scores = (
            jnp.einsum("qhd,khd->hqk", queries, key_heads, preferred_element_type=jnp.float32)
            * 0.125
        )
        scores = jnp.where(allowed[None], scores, MASK_FILL)
        largest = jnp.max(scores, axis=-1, keepdims=True)
        powers = jnp.exp(scores - largest)
        row_total = jnp.sum(powers, axis=-1, keepdims=True)
        log_total = largest + jnp.log(row_total)
        attn_probs = powers / row_total
        attended = jnp.einsum(
            "hqk,khd->qhd",
            attn_probs.astype(jnp.bfloat16),
            value_heads,
            preferred_element_type=jnp.float32,
        ).reshape(row_count, model_width)
        attended = (attended * valid_rows).astype(jnp.bfloat16)
        residual = token_rows + jnp.dot(attended, out_weight, preferred_element_type=jnp.float32)
        mixed = rms_scale(residual, moe_gain).astype(jnp.bfloat16)
        mixed_float = mixed.astype(jnp.float32)
        logits = (
            jnp.dot(mixed, router_weight, preferred_element_type=jnp.float32)
            + prev_logits[step_index]
        )
        router_probs = small_softmax(logits)
        route_rows = routes[step_index]
        choose = (route_rows[:, :, None] == route_ids[None, None, :]).astype(jnp.float32)
        gate_values = jnp.sum(choose * router_probs[:, None, :], axis=-1)
        const_logits = jnp.dot(mixed, cproj_weight, preferred_element_type=jnp.float32)
        mixings = []
        const_outs = []
        for const_index in range(2):
            mixing = small_softmax(const_logits[:, 2 * const_index : 2 * const_index + 2])
            mixings.append(mixing)
            const_outs.append(
                mixing[:, :1] * mixed_float + mixing[:, 1:] * cvec_float[:, const_index][None, :]
            )
        pair_route = route_rows.reshape(-1)
        expert_hit = (pair_route[:, None] == expert_ids[None, :]).astype(jnp.int32)
        slot_index = jnp.sum((jnp.cumsum(expert_hit, axis=0) - expert_hit) * expert_hit, axis=1)
        slot_cell = jnp.sum(expert_hit * expert_ids[None, :], axis=1) * capacity + slot_index
        slot_place = jnp.where(jnp.sum(expert_hit, axis=1) > 0, slot_cell, -1)
        slot_table = (slot_ids[:, None] == slot_place[None, :]).astype(jnp.bfloat16)
        pair_rows = jnp.repeat(mixed, 2, axis=0)
        packed = jnp.einsum(
            "sp,pd->sd", slot_table, pair_rows, preferred_element_type=jnp.float32
        ).astype(jnp.bfloat16)
        outgoing = jnp.broadcast_to(
            packed.reshape(expert_count, 1, capacity, model_width),
            (expert_count, half_count, capacity, model_width),
        ).reshape(peer_count, capacity, model_width)
        received = lax.all_to_all(outgoing, "ep", split_axis=0, concat_axis=0, tiled=True)
        flat_rows = received.reshape(-1, model_width)
        gate_part = jnp.dot(flat_rows, gate_weight, preferred_element_type=jnp.float32)
        up_part = jnp.dot(flat_rows, up_weight, preferred_element_type=jnp.float32)
        hidden = (jax.nn.silu(gate_part) * up_part).astype(jnp.bfloat16)
        part_out = (
            jnp.dot(hidden, down_weight, preferred_element_type=jnp.float32)
            .astype(jnp.bfloat16)
            .reshape(received.shape)
        )
        returned_rows = lax.all_to_all(part_out, "ep", split_axis=0, concat_axis=0, tiled=True)
        returned_rows, kept_rows = (returned_rows, received)
        halves = returned_rows.reshape(expert_count, half_count, capacity, model_width)
        pair_ffn = jnp.zeros((2 * row_count, model_width), jnp.float32)
        for half_index in range(half_count):
            pair_ffn = pair_ffn + jnp.einsum(
                "sp,sd->pd",
                slot_table,
                halves[:, half_index].reshape(slot_count, model_width),
                preferred_element_type=jnp.float32,
            )
        expert_out = pair_ffn.reshape(row_count, 2, model_width)
        expert_out = (
            expert_out + choose[:, :, expert_count + 1 : expert_count + 2] * mixed_float[:, None, :]
        )
        for const_index in range(2):
            column = expert_count + 2 + const_index
            expert_out = (
                expert_out + choose[:, :, column : column + 1] * const_outs[const_index][:, None, :]
            )
        result_rows = residual + jnp.sum(gate_values[:, :, None] * expert_out, axis=1)
        layer_outputs.append(result_rows.astype(jnp.bfloat16))
        grad_rows = cotangent[step_index].astype(jnp.float32)
        d_gates = jnp.sum(expert_out * grad_rows[:, None, :], axis=-1)
        d_probs = jnp.sum(choose * d_gates[:, :, None], axis=1)
        d_logits = router_probs * (
            d_probs - jnp.sum(router_probs * d_probs, axis=-1, keepdims=True)
        )
        prev_grads.append(d_logits)
        grad_router = jnp.dot(mixed_float.T, d_logits, precision=HIGHEST)
        d_mixed = jnp.dot(d_logits, router_float.T, precision=HIGHEST)
        weighted = gate_values[:, :, None] * grad_rows[:, None, :]
        d_mixed = d_mixed + jnp.sum(
            choose[:, :, expert_count + 1 : expert_count + 2] * weighted, axis=1
        )
        cproj_grads = []
        cvec_grads = []
        for const_index in range(2):
            column = expert_count + 2 + const_index
            mixing = mixings[const_index]
            d_const = jnp.sum(choose[:, :, column : column + 1] * weighted, axis=1)
            d_mix = jnp.stack(
                [
                    jnp.sum(d_const * mixed_float, axis=-1),
                    jnp.sum(d_const * cvec_float[:, const_index][None, :], axis=-1),
                ],
                axis=-1,
            )
            d_mixlog = mixing * (d_mix - jnp.sum(mixing * d_mix, axis=-1, keepdims=True))
            cproj_grads.append(jnp.dot(mixed_float.T, d_mixlog, precision=HIGHEST))
            cvec_grads.append(jnp.sum(mixing[:, 1:] * d_const, axis=0))
            d_mixed = (
                d_mixed
                + mixing[:, :1] * d_const
                + jnp.dot(
                    d_mixlog,
                    cproj_float[:, 2 * const_index : 2 * const_index + 2].T,
                    precision=HIGHEST,
                )
            )
        grad_cproj = jnp.concatenate(cproj_grads, axis=1)
        grad_cvec = jnp.stack(cvec_grads, axis=1)
        d_pairs = weighted.reshape(2 * row_count, model_width).astype(jnp.bfloat16)
        d_packed = jnp.einsum(
            "sp,pd->sd", slot_table, d_pairs, preferred_element_type=jnp.float32
        ).astype(jnp.bfloat16)
        d_outgoing = jnp.broadcast_to(
            d_packed.reshape(expert_count, 1, capacity, model_width),
            (expert_count, half_count, capacity, model_width),
        ).reshape(peer_count, capacity, model_width)
        d_received = lax.all_to_all(d_outgoing, "ep", split_axis=0, concat_axis=0, tiled=True)
        flat_rows = kept_rows.reshape(-1, model_width)
        flat_grads = d_received.reshape(-1, model_width)
        gate_part = jnp.dot(flat_rows, gate_weight, preferred_element_type=jnp.float32)
        up_part = jnp.dot(flat_rows, up_weight, preferred_element_type=jnp.float32)
        activated = jax.nn.silu(gate_part)
        hidden = (activated * up_part).astype(jnp.bfloat16)
        grad_down = jnp.einsum("rf,rd->fd", hidden, flat_grads, preferred_element_type=jnp.float32)
        d_hidden = jnp.einsum(
            "rd,fd->rf", flat_grads, down_weight, preferred_element_type=jnp.float32
        )
        sigmoid_gate = jax.nn.sigmoid(gate_part)
        d_gate_part = (
            d_hidden * up_part * sigmoid_gate * (1.0 + gate_part * (1.0 - sigmoid_gate))
        ).astype(jnp.bfloat16)
        d_up_part = (d_hidden * activated).astype(jnp.bfloat16)
        grad_gate = jnp.einsum(
            "rd,rf->df", flat_rows, d_gate_part, preferred_element_type=jnp.float32
        )
        grad_up = jnp.einsum("rd,rf->df", flat_rows, d_up_part, preferred_element_type=jnp.float32)
        d_inputs = jnp.einsum(
            "rf,df->rd", d_gate_part, gate_weight, preferred_element_type=jnp.float32
        )
        d_inputs = d_inputs + jnp.einsum(
            "rf,df->rd", d_up_part, up_weight, preferred_element_type=jnp.float32
        )
        d_inputs = d_inputs.astype(jnp.bfloat16).reshape(peer_count, capacity, model_width)
        d_returned = lax.all_to_all(d_inputs, "ep", split_axis=0, concat_axis=0, tiled=True)
        d_halves = d_returned.reshape(expert_count, half_count, capacity, model_width)
        for half_index in range(half_count):
            d_pair_in = jnp.einsum(
                "sp,sd->pd",
                slot_table,
                d_halves[:, half_index].reshape(slot_count, model_width),
                preferred_element_type=jnp.float32,
            )
            d_mixed = d_mixed + jnp.sum(d_pair_in.reshape(row_count, 2, model_width), axis=1)
        expert_acc = add_tuple(expert_acc, (grad_gate, grad_up, grad_down))
        moe_vjp = jax.vjp(rms_scale, residual, moe_gain)[1]
        d_residual_norm, grad_moe_gain = moe_vjp(d_mixed)
        d_residual = grad_rows + d_residual_norm
        d_branch = d_residual.astype(jnp.bfloat16)
        grad_out = jnp.einsum("rd,re->de", attended, d_branch, preferred_element_type=jnp.float32)
        d_attended = (
            jnp.einsum("re,de->rd", d_branch, out_weight, preferred_element_type=jnp.float32)
            * valid_rows
        ).astype(jnp.bfloat16)
        d_heads = d_attended.reshape(row_count, head_count, HEAD)
        scores = (
            jnp.einsum("qhd,khd->hqk", queries, key_heads, preferred_element_type=jnp.float32)
            * 0.125
        )
        scores = jnp.where(allowed[None], scores, MASK_FILL)
        attn_probs = jnp.exp(scores - log_total)
        d_weights = jnp.einsum(
            "qhd,khd->hqk", d_heads, value_heads, preferred_element_type=jnp.float32
        )
        delta_rows = jnp.sum(attn_probs * d_weights, axis=-1, keepdims=True)
        d_scores = (attn_probs * (d_weights - delta_rows)).astype(jnp.bfloat16)
        d_queries = (
            jnp.einsum(
                "hqk,khd->qhd", d_scores, key_heads, preferred_element_type=jnp.float32
            ).reshape(row_count, model_width)
            * 0.125
        )
        d_values = jnp.einsum(
            "hqk,qhd->khd",
            attn_probs.astype(jnp.bfloat16),
            d_heads,
            preferred_element_type=jnp.float32,
        ).reshape(seq_length, model_width)
        d_keys = (
            jnp.einsum(
                "hqk,qhd->khd", d_scores, queries, preferred_element_type=jnp.float32
            ).reshape(seq_length, model_width)
            * 0.125
        )
        d_keys_mine, d_values_mine = (
            lax.psum_scatter(
                d_keys.astype(jnp.bfloat16), "ep", scatter_dimension=0, tiled=True
            ).astype(jnp.float32),
            lax.psum_scatter(
                d_values.astype(jnp.bfloat16), "ep", scatter_dimension=0, tiled=True
            ).astype(jnp.float32),
        )
        d_qkv = jnp.concatenate([d_queries, d_keys_mine, d_values_mine], axis=1).astype(
            jnp.bfloat16
        )
        grad_qkv = jnp.einsum("rd,re->de", normed, d_qkv, preferred_element_type=jnp.float32)
        d_normed = jnp.einsum("re,de->rd", d_qkv, qkv_weight, preferred_element_type=jnp.float32)
        attn_vjp = jax.vjp(rms_scale, token_rows, attn_gain)[1]
        d_tokens_norm, grad_attn_gain = attn_vjp(d_normed)
        input_grads.append(d_residual + d_tokens_norm)
        dense_terms = (
            grad_attn_gain,
            grad_qkv,
            grad_out,
            grad_moe_gain,
            grad_router,
            grad_cproj,
            grad_cvec,
        )
        dense_shares = (
            lax.psum_scatter(dense_terms[0], ("ep", "dp", "fs"), scatter_dimension=0, tiled=True),
            lax.psum_scatter(dense_terms[1], ("ep", "dp", "fs"), scatter_dimension=0, tiled=True),
            lax.psum_scatter(dense_terms[2], ("ep", "dp", "fs"), scatter_dimension=0, tiled=True),
            lax.psum_scatter(dense_terms[3], ("ep", "dp", "fs"), scatter_dimension=0, tiled=True),
            lax.psum_scatter(dense_terms[4], ("ep", "dp", "fs"), scatter_dimension=0, tiled=True),
            lax.psum_scatter(dense_terms[5], ("ep", "dp", "fs"), scatter_dimension=0, tiled=True),
            lax.psum_scatter(dense_terms[6], ("ep", "dp", "fs"), scatter_dimension=0, tiled=True),
        )
        dense_acc = add_tuple(dense_acc, dense_shares)
    expert_shares = (
        lax.psum_scatter(
            expert_acc[0][None].astype(jnp.bfloat16), ("dp", "fs"), scatter_dimension=1, tiled=True
        ).astype(jnp.float32),
        lax.psum_scatter(
            expert_acc[1][None].astype(jnp.bfloat16), ("dp", "fs"), scatter_dimension=1, tiled=True
        ).astype(jnp.float32),
        lax.psum_scatter(
            expert_acc[2][None].astype(jnp.bfloat16), ("dp", "fs"), scatter_dimension=1, tiled=True
        ).astype(jnp.float32),
    )
    return (
        jnp.stack(layer_outputs),
        jnp.stack(input_grads),
        jnp.stack(prev_grads),
        dense_acc[0],
        dense_acc[1],
        dense_acc[2],
        dense_acc[3],
        dense_acc[4],
        dense_acc[5],
        dense_acc[6],
        expert_shares[0],
        expert_shares[1],
        expert_shares[2],
    )


NEG = -1e30
KINDS = 2
SMALL = 16
LANES = 128
F32 = jnp.float32
BF16 = jnp.bfloat16


def dot(lhs, rhs, dims=((1,), (0,)), precision=None):
    return lax.dot_general(
        lhs, rhs, (dims, ((), ())), precision=precision, preferred_element_type=F32
    )


def key_span(block, rows, reach):
    start = max(0, block * rows - reach)
    return start, (block + 1) * rows - start


def column(rows, index):
    return rows[:, index : index + 1]


def chosen_of(ctl):
    lane = lax.broadcasted_iota(jnp.int32, ctl.shape, 1).astype(F32)
    return ((lane == column(ctl, 8)) | (lane == column(ctl, 9))).astype(F32)


def shape(dims, dtype):
    return jax.ShapeDtypeStruct(dims, dtype)


def whole(dims):
    return pl.BlockSpec(dims, lambda *_: (0,) * len(dims))


def per_row(rows, width):
    return pl.BlockSpec((rows, width), lambda i: (i, 0))


def params():
    return pltpu.CompilerParams(vmem_limit_bytes=56 * 1024 * 1024)


def cost(flops, moved):
    return pl.CostEstimate(flops=int(flops), bytes_accessed=int(moved), transcendentals=0)


class Mail:
    def __init__(self, send_sems, recv_sems):
        self.send_sems = send_sems
        self.recv_sems = recv_sems
        self.used = 0

    def copy(self, source, target, device):
        slot = self.used
        self.used = slot + 1
        return pltpu.make_async_remote_copy(
            src_ref=source,
            dst_ref=target,
            send_sem=self.send_sems.at[slot],
            recv_sem=self.recv_sems.at[slot],
            device_id=device,
            device_id_type=pl.DeviceIdType.MESH,
        )


def position():
    place = lax.axis_index("ep")
    return place // 2, place % 2, lax.axis_index("dp"), lax.axis_index("fs")


def greet(devices):
    barrier = pltpu.get_barrier_semaphore()
    total = 0
    for device, present in devices:
        if present is True:
            pl.semaphore_signal(
                barrier, inc=1, device_id=device, device_id_type=pl.DeviceIdType.MESH
            )
            total = total + 1
        else:

            @pl.when(present)
            def _():
                pl.semaphore_signal(
                    barrier, inc=1, device_id=device, device_id_type=pl.DeviceIdType.MESH
                )

            total = total + jnp.where(present, 1, 0)
    pl.semaphore_wait(barrier, total)


def attend_pair(pair, rows, reach, span, qkv_ref, segc_ref, segr_ref, att_ref, lse_ref):
    length = qkv_ref.shape[0]
    at_q, at_k, at_v = (
        pl.ds(pl.multiple_of(part * span + pair * LANES, LANES), LANES) for part in range(3)
    )
    for block in range(length // rows):
        start, width = key_span(block, rows, reach)
        here = pl.ds(block * rows, rows)
        there = pl.ds(start, width)
        queries = qkv_ref[here, at_q]
        keys = qkv_ref[there, at_k]
        values = qkv_ref[there, at_v]
        seg_q = segc_ref[here, 0:1]
        seg_k = segr_ref[0:1, there]
        row_pos = block * rows + lax.broadcasted_iota(jnp.int32, (rows, width), 0)
        col_pos = start + lax.broadcasted_iota(jnp.int32, (rows, width), 1)
        allowed = (seg_q == seg_k) & (col_pos <= row_pos)
        lane = lax.broadcasted_iota(jnp.int32, (rows, LANES), 1)
        outs = []
        logs = []
        for head in range(2):
            mine = (lane // HEAD) == head
            scores = dot(jnp.where(mine, queries, 0), keys, ((1,), (1,))) * 0.125
            scores = jnp.where(allowed, scores, NEG)
            largest = jnp.max(scores, axis=-1, keepdims=True)
            powers = jnp.exp(scores - largest)
            total = jnp.sum(powers, axis=-1, keepdims=True)
            outs.append(dot(powers.astype(BF16), values) / total)
            logs.append(largest + jnp.log(total))
        valid = (seg_q != SEGS - 1.0).astype(F32)
        att = jnp.where(lane < HEAD, outs[0], outs[1]) * valid
        att_ref[here, at_q] = att.astype(BF16)
        both = jnp.where(lane < HEAD, logs[0], logs[1]).T
        lse_ref[pair, 0:1, here] = both[0:1, :]
        lse_ref[pair, 1:2, here] = both[HEAD : HEAD + 1, :]


def gather_kernel(
    rows, reach, routes,
    tok_ref, cot_ref, wqkv_ref, wout_ref, prev_ref, route_ref, seg_ref, router_ref, cproj_ref,
    cvec_ref, gain_a_ref, gain_m_ref,
    x_all, cot_own, ctl_own, normed_ref, qkv_ref, att_ref, lse_ref, small_all, wqkv_all,
    wout_sib, segc_ref, segr_ref,
    ctl_send, small_wide, small_send, seg_all,
    near_send, near_recv, far_send, far_recv, core_send, core_recv, local_sems,
):
    y, x, z, core = position()
    me = y * 2 + x
    sibling = (me, z, 1 - core)
    moved = y != core
    near = ((1 - y) * 2 + x, z, 1 - core)
    far = (core * 2 + 1 - x, z, y)
    greet([(sibling, True), (far, True), (near, moved)])
    span = wqkv_ref.shape[0]

    def block_of(index):
        return pl.ds(pl.multiple_of(index * rows, rows), rows)

    within = block_of(x)
    homes = [
        (tok_ref, x_all.at[block_of(me)]),
        (cot_ref, cot_own.at[within]),
        (ctl_send, ctl_own.at[x]),
    ]
    nears = Mail(near_send, near_recv)
    fars = Mail(far_send, far_recv)
    near_copies = [nears.copy(a.at[x], b, near) for a, b in homes]
    far_copies = [fars.copy(a.at[1 - x], b, far) for a, b in homes]
    stay_copies = [
        pltpu.make_async_copy(a.at[x], b, local_sems.at[k]) for k, (a, b) in enumerate(homes)
    ]

    def send(k):
        far_copies[k].start()

        @pl.when(moved)
        def _():
            near_copies[k].start()

        @pl.when(jnp.logical_not(moved))
        def _():
            stay_copies[k].start()

    def take_near(k):
        @pl.when(moved)
        def _():
            near_copies[k].wait_recv()

        @pl.when(jnp.logical_not(moved))
        def _():
            stay_copies[k].wait()

    send(0)
    inner = Mail(core_send, core_recv)
    weight_copies = []
    own_copies = []
    band = pl.ds(pl.multiple_of(core * span, span), span)
    for part in range(3):
        columns = pl.ds(part * span, span)
        for side, copies in ((1 - core, weight_copies), (core, own_copies)):
            source = wqkv_ref.at[
                :, pl.ds(pl.multiple_of(part * 2 * span + side * span, LANES), span)
            ]
            target = wqkv_all.at[band, columns]
            if copies is weight_copies:
                copies.append(inner.copy(source, target, sibling))
            else:
                copies.append(
                    pltpu.make_async_copy(source, target, local_sems.at[3 + part])
                )
    out_copy = inner.copy(wout_ref, wout_sib, sibling)
    seg_copy = inner.copy(seg_ref, seg_all.at[core], sibling)
    seg_own = pltpu.make_async_copy(seg_ref, seg_all.at[core], local_sems.at[6])
    small_copy = inner.copy(small_send, small_all.at[:, band], sibling)
    seg_copy.start()
    seg_own.start()
    for copy in weight_copies + own_copies:
        copy.start()

    small_wide[...] = jnp.zeros_like(small_wide)
    small_wide[0:routes, :] = router_ref[...].astype(F32)
    small_wide[8:12, :] = cproj_ref[...].astype(F32)
    small_wide[12:14, :] = cvec_ref[...].astype(F32)
    small_wide[14:15, :] = gain_a_ref[...].astype(F32).reshape(1, span)
    small_wide[15:16, :] = gain_m_ref[...].astype(F32).reshape(1, span)
    turned = small_wide[...]
    small_send[...] = turned.astype(BF16)
    small_all[:, band] = turned.astype(BF16)
    small_copy.start()
    out_copy.start()
    ctl_send[...] = jnp.zeros_like(ctl_send)
    for m in range(2):
        for route in range(routes):
            ctl_send[m, route : route + 1, :] = prev_ref[route, m : m + 1, :]
        ctl_send[m, 8:10, :] = route_ref[m].astype(F32)
    send(2)
    seg_copy.wait_recv()
    seg_own.wait()
    seg_row = seg_all[y, pl.ds(x, 1), :].astype(F32)
    length = seg_row.shape[1]
    segr_ref[...] = jnp.broadcast_to(seg_row, segr_ref.shape)
    segc_ref[...] = jnp.broadcast_to(seg_row, (LANES, length)).T
    small_copy.wait_recv()
    for copy in weight_copies:
        copy.wait_recv()
    for copy in own_copies:
        copy.wait()
    gain = small_all[14:15, :].astype(F32)

    def project(index):
        here = block_of(index)
        values = x_all[here, :].astype(F32)
        inverse = lax.rsqrt(jnp.mean(values * values, axis=-1, keepdims=True) + NORM_EPS)
        normed = (values * inverse * gain).astype(BF16)
        normed_ref[here, :] = normed
        qkv_ref[here, :] = dot(normed, wqkv_all[...]).astype(BF16)

    forward = []
    for step in range(2):
        spot = x_all.at[block_of(core * 2 + (x if step == 0 else 1 - x))]
        forward.append(inner.copy(spot, spot, sibling))
    take_near(0)
    forward[0].start()
    project(core * 2 + x)
    far_copies[0].wait_recv()
    forward[1].start()
    send(1)
    project(core * 2 + 1 - x)
    forward[0].wait_recv()
    project((1 - core) * 2 + x)
    forward[1].wait_recv()
    project((1 - core) * 2 + 1 - x)

    @pl.loop(0, span // LANES)
    def _(pair):
        attend_pair(pair, rows, reach, span, qkv_ref, segc_ref, segr_ref, att_ref, lse_ref)

    for k in (1, 2):
        take_near(k)
        far_copies[k].wait_recv()
    out_copy.wait_recv()
    for copy in far_copies + weight_copies + forward + [out_copy, seg_copy, small_copy]:
        copy.wait_send()

    @pl.when(moved)
    def _():
        for copy in near_copies:
            copy.wait_send()


def gather_all(
    tokens, cotangent, w_qkv, w_out, prev_logits, routes, segments, w_router, const_proj,
    const_vec, gain_attn, gain_moe,
):
    rows, width = tokens.shape[1:]
    length = segments.shape[1]
    mine = length // 2
    span = width // 2
    vmem = pl.BlockSpec(memory_space=pltpu.VMEM)
    anywhere = pl.BlockSpec(memory_space=pl.ANY)
    return pl.pallas_call(
        functools.partial(gather_kernel, rows, length // 2, w_router.shape[1]),
        in_specs=[anywhere] * 4 + [vmem] * 8,
        out_specs=[vmem] * 12,
        out_shape=[
            shape((length, width), BF16), shape((mine, width), BF16),
            shape((2, SMALL, rows), F32), shape((length, width), BF16),
            shape((length, 3 * span), BF16), shape((length, span), BF16),
            shape((span // LANES, 8, length), F32), shape((SMALL, width), BF16),
            shape((width, 3 * span), BF16), shape((span, width), BF16),
            shape((length, LANES), F32), shape((8, length), F32),
        ],
        scratch_shapes=[
            pltpu.VMEM((2, SMALL, rows), F32),
            pltpu.VMEM((SMALL, span), F32), pltpu.VMEM((SMALL, span), BF16),
            pltpu.VMEM((2, 2, length), jnp.int32),
        ]
        + [pltpu.SemaphoreType.DMA((3,))] * 4
        + [pltpu.SemaphoreType.DMA((8,))] * 2
        + [pltpu.SemaphoreType.DMA((7,))],
        compiler_params=pltpu.CompilerParams(
            collective_id=3, has_side_effects=True, vmem_limit_bytes=60 * 1024 * 1024
        ),
        name="gather_all",
    )(
        tokens, cotangent, w_qkv, w_out, jnp.transpose(prev_logits, (2, 0, 1)),
        jnp.swapaxes(routes, 1, 2), segments, w_router.T, const_proj.T, const_vec.T, gain_attn,
        gain_moe,
    )


def widen(turned):
    pad = jnp.zeros((LANES - turned.shape[0], turned.shape[1]), turned.dtype)
    return jnp.concatenate([turned, pad], axis=0).T


def spread_block(experts, routes, rows, block, refs, send_ref, recv_ref, keep):
    att_own, att_sib, x_ref, g_ref, ctl_ref, w_own, w_sib, small_rows, wide_rows = refs
    residual_ref, mixed_ref, pm_ref, place_ref = keep
    y, x, z, core = position()
    here = pl.ds(pl.multiple_of(block * rows, rows), rows)
    tokens = x_ref[pl.ds(pl.multiple_of((core * 2 + block) * rows, rows), rows), :]
    residual = tokens.astype(F32) + (
        dot(att_own[here, :], w_own[...]) + dot(att_sib[here, :], w_sib[...])
    )
    residual_ref[here, :] = residual
    inverse = lax.rsqrt(jnp.mean(residual * residual, axis=-1, keepdims=True) + NORM_EPS)
    mixed = (residual * inverse * small_rows[15:16, :].astype(F32)).astype(BF16)
    mixed_ref[here, :] = mixed
    logits = dot(mixed, wide_rows[...], ((1,), (1,)))
    ctl = widen(ctl_ref[block])
    lane = lax.broadcasted_iota(jnp.int32, (rows, LANES), 1)
    is_route = lane < routes
    router = jnp.where(is_route, logits + ctl, NEG)
    powers = jnp.exp(router - jnp.max(router, axis=-1, keepdims=True))
    probs = powers / jnp.sum(powers, axis=-1, keepdims=True)
    probs = jnp.where(is_route, probs, 0.0)
    pm = probs
    for const_index in range(2):
        first = column(logits, 8 + 2 * const_index)
        second = column(logits, 9 + 2 * const_index)
        largest = jnp.maximum(first, second)
        first = jnp.exp(first - largest)
        second = jnp.exp(second - largest)
        total = first + second
        pm = jnp.where(lane == 8 + 2 * const_index, first / total, pm)
        pm = jnp.where(lane == 9 + 2 * const_index, second / total, pm)
    pm_ref[here, :] = pm
    chosen = chosen_of(ctl)
    gated = chosen * probs
    earlier = lax.broadcasted_iota(jnp.int32, (rows, rows), 1) < lax.broadcasted_iota(
        jnp.int32, (rows, rows), 0
    )
    rank = dot(earlier.astype(BF16), chosen.astype(BF16))
    lane_f = lane.astype(F32)
    grads = g_ref[here, :].astype(F32)
    for expert in range(experts):
        place = jnp.where(
            (lane_f == column(rank, expert)) & (column(chosen, expert) > 0.0), 1.0, 0.0
        )
        place_ref[here, expert * LANES : (expert + 1) * LANES] = place.astype(BF16)
        pick = place.T.astype(BF16)
        d_part = (column(gated, expert) * grads).astype(BF16)
        send_ref[block, expert, 0] = dot(pick, mixed).astype(BF16)
        send_ref[block, expert, 1] = dot(pick, d_part).astype(BF16)
    recv_ref[block, y * 2 + x] = send_ref[block, y]


def expert_block(block, recv_ref, result_ref, back_ref, weights, keep):
    gate_w, up_w, down_w = weights
    hidden_ref, d_gate_ref, d_up_ref = keep
    y, x, z, core = position()
    peers, _, capacity, width = recv_ref.shape[1:]
    size = peers * capacity
    here = pl.ds(pl.multiple_of(block * size, size), size)
    rows = recv_ref[block, :, 0].reshape(size, width)
    d_rows = recv_ref[block, :, 1].reshape(size, width)
    gate = dot(rows, gate_w[...])
    up = dot(rows, up_w[...])
    sig = jax.nn.sigmoid(gate)
    active = gate * sig
    hidden = (active * up).astype(BF16)
    hidden_ref[here, :] = hidden
    part = dot(hidden, down_w[...]).astype(BF16)
    result_ref[block, :, 0] = part.reshape(peers, capacity, width)
    d_hidden = dot(d_rows, down_w[...], ((1,), (1,)))
    d_gate = (d_hidden * up * sig * (1.0 + gate * (1.0 - sig))).astype(BF16)
    d_up = (d_hidden * active).astype(BF16)
    d_gate_ref[here, :] = d_gate
    d_up_ref[here, :] = d_up
    d_in = dot(d_gate, gate_w[...], ((1,), (1,))) + dot(d_up, up_w[...], ((1,), (1,)))
    result_ref[block, :, 1] = d_in.astype(BF16).reshape(peers, capacity, width)
    back_ref[block, y * 2 + x] = result_ref[block, y * 2 + x]


def combine_block(experts, routes, rows, block, refs, keep, back_ref, outs, small_ref):
    g_ref, ctl_ref, small_rows, wide_rows = refs
    residual_ref, mixed_ref, pm_ref, place_ref = keep
    out_ref, prev_ref, dres_ref, branch_ref = outs
    halves = back_ref.shape[1] // experts
    here = pl.ds(pl.multiple_of(block * rows, rows), rows)
    g_low = g_ref[here, :]
    grads = g_low.astype(F32)
    mixed = mixed_ref[here, :].astype(F32)
    residual = residual_ref[here, :]
    pm = pm_ref[here, :]
    lane = lax.broadcasted_iota(jnp.int32, (rows, LANES), 1)
    chosen = chosen_of(widen(ctl_ref[block]))
    probs = jnp.where(lane < routes, pm, 0.0)
    gated = chosen * probs
    d_probs = jnp.zeros((rows, LANES), F32)
    result = residual
    d_mixed = None
    for expert in range(experts):
        place = place_ref[here, expert * LANES : (expert + 1) * LANES]
        expert_out = None
        for half in range(halves):
            owner = expert * halves + half
            term = dot(place, back_ref[block, owner, 0])
            expert_out = term if expert_out is None else expert_out + term
            term = dot(place, back_ref[block, owner, 1])
            d_mixed = term if d_mixed is None else d_mixed + term
        result = result + column(gated, expert) * expert_out
        d_gate = jnp.sum(expert_out * grads, axis=-1, keepdims=True)
        d_probs = jnp.where(lane == expert, d_gate, d_probs)
    g_mixed = jnp.sum(grads * mixed, axis=-1, keepdims=True)
    g_const = dot(g_low, wide_rows[...], ((1,), (1,)))
    copy = experts + 1
    d_probs = jnp.where(lane == copy, g_mixed, d_probs)
    weight = column(gated, copy)
    d_small = jnp.zeros((rows, LANES), F32)
    for const_index in range(2):
        route = copy + 1 + const_index
        first = column(pm, 8 + 2 * const_index)
        second = column(pm, 9 + 2 * const_index)
        gate = column(gated, route)
        g_vec = column(g_const, 12 + const_index)
        d_probs = jnp.where(lane == route, first * g_mixed + second * g_vec, d_probs)
        weight = weight + gate * first
        vec = small_rows[12 + const_index : 13 + const_index, :].astype(F32)
        result = result + (gate * second) * vec
        d_first = gate * g_mixed
        d_second = gate * g_vec
        mean = first * d_first + second * d_second
        d_small = jnp.where(lane == 8 + 2 * const_index, first * (d_first - mean), d_small)
        d_small = jnp.where(lane == 9 + 2 * const_index, second * (d_second - mean), d_small)
        d_small = jnp.where(lane == 12 + const_index, gate * second, d_small)
    result = result + weight * mixed
    out_ref[block] = result.astype(BF16)
    d_probs = d_probs * chosen
    d_logits = probs * (d_probs - jnp.sum(probs * d_probs, axis=-1, keepdims=True))
    d_small = jnp.where(lane < routes, d_logits, d_small)
    d_mixed = d_mixed + weight * grads
    d_mixed = d_mixed + dot(
        jnp.where(lane < 12, d_small, 0.0), wide_rows[...].astype(F32), precision=HIGHEST
    )
    inverse = lax.rsqrt(jnp.mean(residual * residual, axis=-1, keepdims=True) + NORM_EPS)
    scaled = d_mixed * small_rows[15:16, :].astype(F32)
    mean = jnp.mean(scaled * residual, axis=-1, keepdims=True)
    d_residual = grads + inverse * scaled - residual * (inverse * inverse * inverse * mean)
    dres_ref[here, :] = d_residual
    branch_ref[here, :] = d_residual.astype(BF16)
    d_turned = d_small.T[:SMALL, :]
    prev_ref[block] = d_turned[:8, :]
    sub = lax.broadcasted_iota(jnp.int32, (SMALL, rows), 0)
    small = dot(jnp.where(sub < 12, d_turned, 0.0), mixed, precision=HIGHEST)
    small = small + dot(
        jnp.where((sub >= 12) & (sub < 14), d_turned, 0.0), grads, precision=HIGHEST
    )
    d_gain = jnp.sum(d_mixed * residual * inverse, axis=0, keepdims=True)
    which = lax.broadcasted_iota(jnp.int32, small.shape, 0)
    small_ref[...] += jnp.where(which == 14, d_gain, small)


def layer_kernel(
    experts, routes, rows, blocks,
    att_ref, x_ref, g_ref, ctl_ref, w_own, w_sib, small_rows, gate_ref, up_ref, down_ref,
    out_ref, prev_ref, dres_ref, branch_ref, small_ref, dgate_out, dup_out, ddown_out,
    wide_rows, att_own, att_sib, gate_w, up_w, down_w, residual_ref, mixed_ref, pm_ref, place_ref,
    send_ref, recv_ref, result_ref, back_ref, hidden_ref, d_gate_ref, d_up_ref,
    head_send, head_recv, local_sems, send_sems, recv_sems, back_send, back_recv,
):
    y, x, z, core = position()
    me = y * 2 + x
    sibling = (me, z, 1 - core)
    partners = [(1 - y) * 2 + 1 - x, y * 2 + 1 - x, (1 - y) * 2 + x]
    wanted = [1 - y, y, 1 - y]
    greet([(sibling, True)] + [((place, z, core), True) for place in partners])
    mine = rows * blocks
    mail = Mail(head_send, head_recv)
    pairs = [(gate_ref, gate_w), (up_ref, up_w), (down_ref, down_w)]
    heads = [mail.copy(att_ref.at[1 - core], att_sib, sibling)]
    locals_ = [pltpu.make_async_copy(att_ref.at[core], att_own, local_sems.at[3])]
    for k, (source, target) in enumerate(pairs):
        size = source.shape[0]
        spot = target.at[pl.ds(pl.multiple_of(core * size, size), size)]
        heads.append(mail.copy(source, spot, sibling))
        locals_.append(pltpu.make_async_copy(source, spot, local_sems.at[k]))
    for copy in heads + locals_:
        copy.start()

    def dispatch(block, k):
        return pltpu.make_async_remote_copy(
            src_ref=send_ref.at[block, wanted[k]],
            dst_ref=recv_ref.at[block, me],
            send_sem=send_sems.at[block, k],
            recv_sem=recv_sems.at[block, k],
            device_id=(partners[k], z, core),
            device_id_type=pl.DeviceIdType.MESH,
        )

    def giveback(block, k):
        return pltpu.make_async_remote_copy(
            src_ref=result_ref.at[block, partners[k]],
            dst_ref=back_ref.at[block, me],
            send_sem=back_send.at[block, k],
            recv_sem=back_recv.at[block, k],
            device_id=(partners[k], z, core),
            device_id_type=pl.DeviceIdType.MESH,
        )

    small_ref[...] = jnp.zeros_like(small_ref)
    wide_rows[...] = jnp.zeros_like(wide_rows)
    wide_rows[0:SMALL, :] = small_rows[...]
    heads[0].wait_recv()
    locals_[0].wait()
    keep = (residual_ref, mixed_ref, pm_ref, place_ref)
    spread_refs = (
        att_own, att_sib, x_ref, g_ref, ctl_ref, w_own, w_sib, small_rows, wide_rows
    )

    @pl.loop(0, blocks)
    def _(block):
        spread_block(experts, routes, rows, block, spread_refs, send_ref, recv_ref, keep)
        for k in range(3):
            dispatch(block, k).start()

    for copy in heads[1:]:
        copy.wait_recv()
    for copy in locals_[1:]:
        copy.wait()

    @pl.loop(0, blocks)
    def _(block):
        for k in range(3):
            dispatch(block, k).wait_recv()
        expert_block(
            block, recv_ref, result_ref, back_ref, (gate_w, up_w, down_w),
            (hidden_ref, d_gate_ref, d_up_ref),
        )
        for k in range(3):
            giveback(block, k).start()

    peers, _, capacity, width = recv_ref.shape[1:]
    total = blocks * peers * capacity
    step = 2 * LANES

    @pl.loop(0, width // step)
    def _(chunk):
        span = pl.ds(pl.multiple_of(chunk * step, step), step)
        lhs = recv_ref[:, :, 0, :, span].reshape(total, step).T
        dgate_out[span, :] = dot(lhs, d_gate_ref[...]).astype(BF16)
        dup_out[span, :] = dot(lhs, d_up_ref[...]).astype(BF16)

    @pl.loop(0, hidden_ref.shape[1] // step)
    def _(chunk):
        span = pl.ds(pl.multiple_of(chunk * step, step), step)
        lhs = hidden_ref[:, span].T
        rhs = recv_ref[:, :, 1].reshape(total, width)
        ddown_out[span, :] = dot(lhs, rhs).astype(BF16)

    @pl.loop(0, blocks)
    def _(block):
        for k in range(3):
            giveback(block, k).wait_recv()
        combine_block(
            experts, routes, rows, block, (g_ref, ctl_ref, small_rows, wide_rows),
            keep, back_ref, (out_ref, prev_ref, dres_ref, branch_ref), small_ref,
        )

    for copy in heads:
        copy.wait_send()
    for block in range(blocks):
        for k in range(3):
            dispatch(block, k).wait_send()
            giveback(block, k).wait_send()


def expert_layer(
    experts, routes, rows, attended, x_all, cot_own, ctl, w_own, w_sib, small_all, w_gate,
    w_up, w_down,
):
    mine, width = cot_own.shape
    blocks = mine // rows
    peers = lax.axis_size("ep")
    span = attended.shape[1]
    hidden = w_gate.shape[1]
    vmem = pl.BlockSpec(memory_space=pltpu.VMEM)
    total = blocks * peers * LANES
    grads = [(2 * w.shape[0], w.shape[1]) for w in (w_gate, w_up, w_down)]
    return pl.pallas_call(
        functools.partial(layer_kernel, experts, routes, rows, blocks),
        in_specs=[vmem] * 10,
        out_specs=[vmem] * 8,
        out_shape=[
            shape((blocks, rows, width), BF16), shape((blocks, 8, rows), F32),
            shape((mine, width), F32), shape((mine, width), BF16), shape((SMALL, width), F32),
        ]
        + [shape(dims, BF16) for dims in grads],
        scratch_shapes=[pltpu.VMEM((LANES, width), BF16)]
        + [pltpu.VMEM((mine, span), BF16)] * 2
        + [pltpu.VMEM(dims, BF16) for dims in grads]
        + [
            pltpu.VMEM((mine, width), F32), pltpu.VMEM((mine, width), BF16),
            pltpu.VMEM((mine, LANES), F32), pltpu.VMEM((mine, experts * LANES), BF16),
            pltpu.VMEM((blocks, experts, KINDS, LANES, width), BF16),
        ]
        + [pltpu.VMEM((blocks, peers, KINDS, LANES, width), BF16)] * 3
        + [pltpu.VMEM((total, hidden), BF16)] * 3
        + [
            pltpu.SemaphoreType.DMA((4,)), pltpu.SemaphoreType.DMA((4,)),
            pltpu.SemaphoreType.DMA((4,)),
        ]
        + [pltpu.SemaphoreType.DMA((blocks, 3))] * 4,
        compiler_params=pltpu.CompilerParams(
            collective_id=2, has_side_effects=True, vmem_limit_bytes=62 * 1024 * 1024
        ),
        name="expert_layer",
    )(
        attended.reshape(2, mine, span), x_all, cot_own, ctl, w_own, w_sib, small_all,
        w_gate, w_up, w_down,
    )


class Line:
    def __init__(self, mail, depth, slots):
        self.depth = depth
        self.slots = slots
        self.place = lax.axis_index("dp")
        y, x, z, core = position()
        self.copies = {}
        for way in range(2):
            step_to = 1 if way == 0 else -1
            device = (y * 2 + x, z + step_to, core)
            for step in range(depth - 1):
                for item, (acc, landing) in enumerate(slots):
                    shard = self.shard(way, step)
                    safe = jnp.clip(shard, 0, depth - 1)
                    self.copies[way, step, item] = mail.copy(
                        acc.at[safe], landing.at[way, step], device
                    )

    def shard(self, way, step):
        if way == 0:
            return self.place + self.depth - 1 - step
        return self.place - (self.depth - 1 - step)

    def edge(self, way):
        return self.place == (0 if way == 0 else self.depth - 1)

    def sends(self, way, step):
        shard = self.shard(way, step)
        if way == 0:
            return (shard <= self.depth - 1) & (self.place < self.depth - 1)
        return (shard >= 0) & (self.place > 0)

    def gets(self, way, step):
        if way == 0:
            return (self.place > 0) & (self.shard(way, step + 1) <= self.depth - 1)
        return (self.place < self.depth - 1) & (self.shard(way, step + 1) >= 0)

    def send(self, step, item):
        for way in range(2):
            wanted = self.sends(way, step)
            if step > 0:
                wanted = wanted & jnp.logical_not(self.edge(way))

            @pl.when(wanted)
            def _():
                self.copies[way, step, item].start()

    def send_edge(self, step, item):
        for way in range(2):

            @pl.when(self.sends(way, step) & self.edge(way))
            def _():
                self.copies[way, step, item].start()

    def take(self, step, item):
        acc, landing = self.slots[item]
        for way in range(2):
            shard = jnp.clip(self.shard(way, step + 1), 0, self.depth - 1)

            @pl.when(self.gets(way, step))
            def _():
                self.copies[way, step, item].wait_recv()
                acc[shard] = (
                    acc[shard].astype(F32) + landing[way, step].astype(F32)
                ).astype(BF16)

    def finish(self, item, store):
        acc, landing = self.slots[item]
        store(acc[self.place].astype(F32))
        for way in range(2):

            @pl.when(self.gets(way, self.depth - 2))
            def _():
                self.copies[way, self.depth - 2, item].wait_recv()
                store(landing[way, self.depth - 2].astype(F32), True)

    def close(self):
        for (way, step, item), copy in self.copies.items():

            @pl.when(self.sends(way, step))
            def _():
                copy.wait_send()


class Plane:
    def __init__(self, mail, source, buffers, total):
        y, x, z, core = position()
        self.place = y, x
        self.source = source
        self.buffers = buffers
        self.total = total
        y1_land, x1_land, y1_acc, x1_acc, x2_land, y2_land = buffers
        half = x2_land.shape[0]
        self.low = pl.ds(0, half)
        self.high = pl.ds(half, half)
        across = (y * 2 + 1 - x, z, core)
        along = ((1 - y) * 2 + x, z, core)
        self.first = [
            mail.copy(source.at[1 - y, :, self.low], y1_land, along),
            mail.copy(source.at[:, 1 - x, self.high], x1_land, across),
        ]
        self.second = [
            mail.copy(y1_acc.at[1 - x], x2_land, across),
            mail.copy(x1_acc.at[1 - y], y2_land, along),
        ]

    def start(self):
        for copy in self.first:
            copy.start()

    def middle(self):
        y, x = self.place
        y1_land, x1_land, y1_acc, x1_acc, _, _ = self.buffers
        self.first[0].wait_recv()
        for k in range(2):
            y1_acc[k] = (
                self.source[y, k, self.low].astype(F32) + y1_land[k].astype(F32)
            ).astype(BF16)
        self.second[0].start()
        self.first[1].wait_recv()
        for k in range(2):
            x1_acc[k] = (
                self.source[k, x, self.high].astype(F32) + x1_land[k].astype(F32)
            ).astype(BF16)
        self.second[1].start()

    def end(self):
        y, x = self.place
        _, _, y1_acc, x1_acc, x2_land, y2_land = self.buffers
        shards, size = self.total.shape[0] // 2, self.total.shape[1]
        self.second[0].wait_recv()
        for shard in range(shards):
            part = pl.ds(shard * size, size)
            self.total[shard] = (
                y1_acc[x, part].astype(F32) + x2_land[part].astype(F32)
            ).astype(BF16)
        self.second[1].wait_recv()
        for shard in range(shards):
            part = pl.ds(shard * size, size)
            self.total[shards + shard] = (
                x1_acc[y, part].astype(F32) + y2_land[part].astype(F32)
            ).astype(BF16)

    def close(self):
        for copy in self.first + self.second:
            copy.wait_send()


def back_pair(
    pair, rows, reach, span, qkv_ref, datt_ref, segc_ref, segr_ref, lse_ref, dqkv_ref,
    dk_sum, dv_sum,
):
    length = qkv_ref.shape[0]
    at_q, at_k, at_v = (
        pl.ds(pl.multiple_of(part * span + pair * LANES, LANES), LANES) for part in range(3)
    )
    dk_sum[...] = jnp.zeros_like(dk_sum)
    dv_sum[...] = jnp.zeros_like(dv_sum)
    keys_turned = qkv_ref[:, at_k].T
    for block in range(length // rows):
        start, width = key_span(block, rows, reach)
        here = pl.ds(block * rows, rows)
        there = pl.ds(start, width)
        queries = qkv_ref[here, at_q]
        grads = datt_ref[here, at_q]
        keys = qkv_ref[there, at_k]
        values = qkv_ref[there, at_v]
        seg_k = segc_ref[there, 0:1]
        seg_q = segr_ref[0:1, here]
        key_pos = start + lax.broadcasted_iota(jnp.int32, (width, rows), 0)
        query_pos = block * rows + lax.broadcasted_iota(jnp.int32, (width, rows), 1)
        allowed = (seg_q == seg_k) & (key_pos <= query_pos)
        lane = lax.broadcasted_iota(jnp.int32, (rows, LANES), 1)
        dq_parts = []
        for head in range(2):
            mine = (lane // HEAD) == head
            head_q = jnp.where(mine, queries, 0)
            head_g = jnp.where(mine, grads, 0)
            log_total = lse_ref[pair, head : head + 1, here]
            scores = dot(keys, head_q, ((1,), (1,))) * 0.125
            probs = jnp.exp(jnp.where(allowed, scores, NEG) - log_total)
            d_probs = dot(values, head_g, ((1,), (1,)))
            delta = jnp.sum(probs * d_probs, axis=0, keepdims=True)
            d_scores = (probs * (d_probs - delta)).astype(BF16)
            dv_sum[there, :] += dot(probs.astype(BF16), head_g)
            dk_sum[there, :] += dot(d_scores, head_q)
            turned = keys_turned[head * HEAD : (head + 1) * HEAD, start : start + width]
            dq_parts.append(dot(turned, d_scores))
        dq = jnp.concatenate(dq_parts, axis=0).T * 0.125
        dqkv_ref[here, at_q] = dq.astype(BF16)
    dqkv_ref[:, at_k] = (dk_sum[...] * 0.125).astype(BF16)
    dqkv_ref[:, at_v] = dv_sum[...].astype(BF16)


def back_kernel(depth, rows, reach, *refs):
    (
        gate_any, up_any, down_any, branch_any, wout_any, att_any, qkv_any, segc_any, normed_any,
        wqkv_any, x_any, dres_any, out_ref, prev_ref, lse_ref, segr_ref, small_ref, small_rows,
        gate_out, up_out, down_out, qkv_out, wout_out, small_out, out_home, dtok_home, prev_home,
        gate_land, up_land, down_land, gate_acc, up_acc, down_acc, gate_line, up_line, down_line,
        branch_ref, wout_ref, att_ref, qkv_ref, segc_ref, normed_ref, wqkv_ref, x_ref, dres_ref,
        normed_turned, datt_ref, turned_ref, dqkv_ref, dk_sum, dv_sum, dn_send, dn_recv, dtok_ref,
        dense_ref, y1_land, x1_land, y1_acc, x1_acc, x2_land, y2_land, dense_acc, dense_line,
        tail_ref, ty1_land, tx1_land, ty1_acc, tx1_acc, tx2_land, ty2_land, tail_acc, tail_line,
        dense_sum, dense_sib, tail_sum, tail_sib, small_wide,
        send_sems, recv_sems, local_sems,
    ) = refs
    y, x, z, core = position()
    sibling = (y * 2 + x, z, 1 - core)
    across = (y * 2 + 1 - x, z, core)
    along = ((1 - y) * 2 + x, z, core)
    moved = y != core
    near = ((1 - y) * 2 + x, z, 1 - core)
    far = (core * 2 + 1 - x, z, y)
    greet(
        [
            (sibling, True), (across, True), (along, True),
            (near, moved), (far, moved),
            ((y * 2 + x, z + 1, core), z < depth - 1), ((y * 2 + x, z - 1, core), z > 0),
        ]
    )
    mail = Mail(send_sems, recv_sems)
    length, width = normed_ref.shape
    mine = length // 2
    span = wout_ref.shape[0]
    pairs = span // LANES
    own_rows = pl.ds(pl.multiple_of(core * mine, mine), mine)
    experts = [
        (gate_any, gate_land, gate_acc, gate_line, gate_out),
        (up_any, up_land, up_acc, up_line, up_out),
        (down_any, down_land, down_acc, down_line, down_out),
    ]
    halves = [mail.copy(source.at[:, 1 - core], land, sibling) for source, land, _, _, _ in experts]
    line = Line(mail, depth, [(acc, landing) for _, _, acc, landing, _ in experts])
    branch_copy = mail.copy(branch_any, branch_ref.at[own_rows], sibling)
    loads = [
        pltpu.make_async_copy(source, target, local_sems.at[k])
        for k, (source, target) in enumerate(
            [
                (gate_any.at[:, core], gate_acc), (up_any.at[:, core], up_acc),
                (down_any.at[:, core], down_acc), (branch_any, branch_ref.at[own_rows]),
                (normed_any, normed_ref), (att_any, att_ref), (wout_any, wout_ref),
                (segc_any, segc_ref), (qkv_any, qkv_ref), (wqkv_any, wqkv_ref),
                (x_any.at[own_rows], x_ref), (dres_any, dres_ref),
            ]
        )
    ]
    homes = [(out_ref, out_home), (prev_ref, prev_home), (dtok_ref, dtok_home)]
    nears = [mail.copy(a.at[x], b.at[x], near) for a, b in homes]
    fars = [mail.copy(a.at[1 - x], b.at[x], far) for a, b in homes]
    stays = [
        pltpu.make_async_copy(a.at[x], b.at[x], local_sems.at[len(loads) + k])
        for k, (a, b) in enumerate(homes)
    ]

    def go_near(k):
        @pl.when(moved)
        def _():
            nears[k].start()

        @pl.when(jnp.logical_not(moved))
        def _():
            stays[k].start()

    half_copy = mail.copy(turned_ref.at[1 - core], dense_ref.at[0, core], sibling)
    planes = [
        Plane(
            mail, dense_ref.at[c],
            [b.at[c] for b in (y1_land, x1_land, y1_acc, x1_acc, x2_land, y2_land)],
            dense_acc.at[c],
        )
        for c in range(pairs + 1)
    ] + [
        Plane(
            mail, tail_ref, (ty1_land, tx1_land, ty1_acc, tx1_acc, tx2_land, ty2_land), tail_acc
        )
    ]
    dense = Line(
        mail, depth,
        [(dense_acc.at[c], dense_line.at[c]) for c in range(pairs + 1)] + [(tail_acc, tail_line)],
    )
    chunks = pairs + 2
    size = tail_sum.shape[0]
    half = size // 2
    other = pl.ds(pl.multiple_of((1 - core) * half, 8), half)
    ours = pl.ds(pl.multiple_of(core * half, 8), half)
    sums = [(dense_sum.at[c], dense_sib.at[c]) for c in range(pairs + 1)] + [(tail_sum, tail_sib)]
    lasts = [mail.copy(a.at[other], b, sibling) for a, b in sums]
    dn_copies = [mail.copy(dn_send.at[b], dn_recv.at[b], sibling) for b in range(2)]

    for copy in halves[:1] + [branch_copy] + halves[1:]:
        copy.start()
    for copy in loads:
        copy.start()
    fars[0].start()
    fars[1].start()
    go_near(0)
    go_near(1)

    loads[4].wait()
    normed_turned[...] = normed_ref[...].T
    for item, (_, land, acc, _, _) in enumerate(experts):
        loads[item].wait()
        halves[item].wait_recv()
        for shard in range(depth):
            acc[shard] = (acc[shard].astype(F32) + land[shard].astype(F32)).astype(BF16)
        line.send(0, item)
    for item in range(3):
        line.send_edge(1, item)
    for k in (3, 5, 6, 7):
        loads[k].wait()
    branch_copy.wait_recv()

    @pl.loop(0, length // rows)
    def _(block):
        here = pl.ds(pl.multiple_of(block * rows, rows), rows)
        valid = (segc_ref[here, 0:1] != SEGS - 1.0).astype(F32)
        datt_ref[here, :] = (
            dot(branch_ref[here, :], wout_ref[...], ((1,), (1,))) * valid
        ).astype(BF16)

    att_turned = att_ref[...].T
    for side in range(2):
        part = dot(att_turned, branch_ref[:, side * span : (side + 1) * span]).astype(BF16)
        turned_ref[side] = part.reshape(turned_ref.shape[1:])
    half_copy.start()
    dense_ref[0, core] = turned_ref[core]
    for k in (8, 9):
        loads[k].wait()
    small_wide[...] = jnp.zeros_like(small_wide)

    quarter = width // 4

    @pl.loop(0, pairs)
    def _(pair):
        back_pair(
            pair, rows, reach, span, qkv_ref, datt_ref, segc_ref, segr_ref, lse_ref, dqkv_ref,
            dk_sum, dv_sum,
        )
        columns = [
            pl.ds(pl.multiple_of(part * span + pair * LANES, LANES), LANES) for part in range(3)
        ]

        @pl.loop(0, 4)
        def _(fourth):
            here = pl.ds(pl.multiple_of(fourth * quarter, quarter), quarter)
            d_pair = jnp.concatenate([dqkv_ref[:, at] for at in columns], axis=1)
            weights = jnp.concatenate([wqkv_ref[here, at] for at in columns], axis=1)
            grads = dot(normed_turned[here, :], d_pair)
            dense_ref[1 + pair, fourth // 2, fourth % 2] = grads.astype(BF16)
            gain = jnp.sum(grads * weights.astype(F32), axis=1, keepdims=True)
            lane = lax.broadcasted_iota(jnp.int32, (quarter, LANES), 1)
            small_wide[here, :] += jnp.where(lane == SMALL - 1, gain, 0.0)

        for now in range(pairs):

            @pl.when(pair == now)
            def _():
                planes[now + 1].start()
                if now == 0:
                    half_copy.wait_recv()
                    planes[0].start()
                    for item in range(2):
                        line.take(0, item)
                        line.send(1, item)
                if now >= 1:
                    planes[now - 1].middle()
                if now >= 2:
                    planes[now - 2].end()
                    dense.send(0, now - 2)
                    for step in range(1, depth - 1):
                        dense.send_edge(step, now - 2)
                if now == 1:
                    line.take(0, 2)
                    line.send(1, 2)
                if now == 2:
                    for item in range(2):
                        line.take(1, item)
                        line.send(2, item)

    small_all = small_rows[...].astype(F32)
    gain_column = column(widen(small_all), SMALL - 2)
    lane = lax.broadcasted_iota(jnp.int32, (width, LANES), 1)
    small_grads = jnp.where(
        lane < SMALL - 1, widen(small_ref[...]), small_wide[...] / gain_column
    )
    tail_ref[...] = small_grads.astype(BF16).reshape(tail_ref.shape)
    planes[chunks - 1].start()

    def partial(start, step):
        b = 1 - x if step == 0 else x
        here = pl.ds(pl.multiple_of(start * mine + b * rows, rows), rows)
        return b, dot(dqkv_ref[here, :], wqkv_ref[...], ((1,), (1,)))

    def launch(c):
        planes[c].end()
        dense.send(0, c)
        for step in range(1, depth - 1):
            dense.send_edge(step, c)

    for step in range(2):
        b, value = partial(1 - core, step)
        dn_send[step] = value.astype(BF16)
        dn_copies[step].start()
    planes[pairs - 1].middle()
    launch(pairs - 2)
    for item in range(3):
        line.send_edge(2, item)
    planes[pairs].middle()
    launch(pairs - 1)
    planes[pairs + 1].middle()
    loads[10].wait()
    loads[11].wait()
    gain_row = small_all[SMALL - 2 : SMALL - 1, :]
    for step in range(2):
        b, value = partial(core, step)
        here = pl.ds(pl.multiple_of(b * rows, rows), rows)
        values = x_ref[here, :].astype(F32)
        dn_copies[step].wait_recv()
        d_normed = value + dn_recv[step].astype(F32)
        inverse = lax.rsqrt(jnp.mean(values * values, axis=-1, keepdims=True) + NORM_EPS)
        scaled = d_normed * gain_row
        mean = jnp.mean(scaled * values, axis=-1, keepdims=True)
        result = dres_ref[here, :] + inverse * scaled
        result = result - values * (inverse * inverse * inverse * mean)
        dtok_ref[b] = result.astype(BF16)
        if step == 0:
            fars[2].start()
            launch(pairs)
            launch(pairs + 1)
        else:
            go_near(2)
    line.take(1, 2)
    line.send(2, 2)
    for step in range(depth - 2):
        for c in range(chunks):
            dense.take(step, c)
            dense.send(step + 1, c)
    for item, (_, _, _, _, result) in enumerate(experts):

        def store(value, add=False):
            result[0] = result[0] + value if add else value

        line.finish(item, store)
    for c, (total, _) in enumerate(sums):

        def store(value, add=False):
            total[...] = total[...] + value if add else value

        dense.finish(c, store)
        lasts[c].start()
    for c, (total, land) in enumerate(sums):
        own = total[ours]
        lasts[c].wait_recv()
        theirs = land[...]
        if c == 0:
            for side, value in ((core, own), (1 - core, theirs)):
                wout_out[:, pl.ds(pl.multiple_of(side * span, LANES), span)] = value
        elif c <= pairs:
            for part in range(3):
                for side, value in ((core, own), (1 - core, theirs)):
                    at = part * 2 * span + side * span + (c - 1) * LANES
                    qkv_out[:, pl.ds(pl.multiple_of(at, LANES), LANES)] = value[
                        :, part * LANES : (part + 1) * LANES
                    ]
        else:
            small_out[...] = own + theirs
    for copy in halves + [branch_copy, half_copy] + lasts + dn_copies:
        copy.wait_send()
    for plane in planes:
        plane.close()
    line.close()
    dense.close()
    for copy in fars:
        copy.wait()

    @pl.when(moved)
    def _():
        for copy in nears:
            copy.wait()

    @pl.when(jnp.logical_not(moved))
    def _():
        for copy in stays:
            copy.wait()


def back_all(
    grad_gate, grad_up, grad_down, d_branch, w_out, attended, qkv, seg_col, normed, qkv_weight,
    x_all, d_residual, block_out, d_prev, lse, seg_row, small, small_all,
):
    depth = lax.axis_size("dp")
    experts = [
        grad.reshape(depth, 2, grad.shape[0] // (2 * depth), grad.shape[1])
        for grad in (grad_gate, grad_up, grad_down)
    ]
    length, width = x_all.shape
    mine = length // 2
    span = width // 2
    rows = block_out.shape[1]
    groups = span // LANES + 1
    wide = 3 * LANES
    quarter = width // 4
    size = quarter // depth
    parts = [grad.shape[2:] for grad in experts]
    vmem = pl.BlockSpec(memory_space=pltpu.VMEM)
    anywhere = pl.BlockSpec(memory_space=pl.ANY)
    homes = [block_out.shape, block_out.shape, d_prev.shape]
    kinds = [block_out.dtype, BF16, d_prev.dtype]
    steps = 2 * (depth - 1)
    copies = 3 + 3 * steps + 2 + 6 + (groups + 1) * (4 + steps + 1) + 2

    def plane_buffers(lead, columns):
        return [
            pltpu.VMEM(lead + dims + (columns,), BF16)
            for dims in (
                [(2, 2, quarter)] + [(2, quarter // 2)] * 4 + [(quarter // 2,)] * 2
                + [(depth, size), (2, depth - 1, size)]
            )
        ]

    return pl.pallas_call(
        functools.partial(back_kernel, depth, rows, length // 2),
        in_specs=[anywhere] * 12 + [vmem] * 6,
        out_specs=[vmem] * 6 + [anywhere] * 3,
        out_shape=[shape((1,) + part, F32) for part in parts]
        + [shape((size // 2, 6 * span), F32), shape((size // 2, width), F32)]
        + [shape((size // 2, LANES), F32)]
        + [shape(dims, kind) for dims, kind in zip(homes, kinds)],
        scratch_shapes=[pltpu.VMEM((depth,) + part, BF16) for part in parts] * 2
        + [pltpu.VMEM((2, depth - 1) + part, BF16) for part in parts]
        + [
            pltpu.VMEM((length, width), BF16), pltpu.VMEM((span, width), BF16),
            pltpu.VMEM((length, span), BF16), pltpu.VMEM((length, 3 * span), BF16),
            pltpu.VMEM((length, LANES), F32), pltpu.VMEM((length, width), BF16),
            pltpu.VMEM((width, 3 * span), BF16), pltpu.VMEM((mine, width), BF16),
            pltpu.VMEM((mine, width), F32), pltpu.VMEM((width, length), BF16),
            pltpu.VMEM((length, span), BF16), pltpu.VMEM((2, 2, quarter, span), BF16),
            pltpu.VMEM((length, 3 * span), BF16), pltpu.VMEM((length, LANES), F32),
            pltpu.VMEM((length, LANES), F32), pltpu.VMEM((2, rows, width), BF16),
            pltpu.VMEM((2, rows, width), BF16), pltpu.VMEM((2, rows, width), BF16),
        ]
        + plane_buffers((groups,), wide)
        + plane_buffers((), LANES)
        + [
            pltpu.VMEM((groups, size, wide), F32), pltpu.VMEM((groups, size // 2, wide), F32),
            pltpu.VMEM((size, LANES), F32), pltpu.VMEM((size // 2, LANES), F32),
            pltpu.VMEM((width, LANES), F32),
            pltpu.SemaphoreType.DMA((copies,)),
            pltpu.SemaphoreType.DMA((copies,)),
            pltpu.SemaphoreType.DMA((15,)),
        ],
        compiler_params=pltpu.CompilerParams(
            collective_id=1, has_side_effects=True, vmem_limit_bytes=62 * 1024 * 1024
        ),
        name="back_all",
    )(
        *experts, d_branch, w_out, attended, qkv, seg_col, normed, qkv_weight, x_all, d_residual,
        block_out, d_prev, lse, seg_row, small, small_all,
    )


def deliver_kernel(
    routes,
    out_ref, dtok_ref, prev_ref, qkv_ref, wout_ref, small_ref, gate_ref, up_ref, down_ref,
    out_end, tokens_end, prev_end, gain_a_end, qkv_end, wout_end, gain_m_end, router_end,
    cproj_end, cvec_end, gate_end, up_end, down_end,
):
    for source, target in (
        (out_ref, out_end), (qkv_ref, qkv_end), (wout_ref, wout_end), (gate_ref, gate_end),
        (up_ref, up_end), (down_ref, down_end),
    ):
        target[...] = source[...]
    tokens_end[...] = dtok_ref[...].astype(F32)
    for m in range(2):
        for route in range(routes):
            prev_end[route, m : m + 1, :] = prev_ref[m, route : route + 1, :]
    count = small_ref.shape[0]
    turned = widen(small_ref[...])
    router_end[...] = turned[0:routes, 0:count]
    cproj_end[...] = turned[8:12, 0:count]
    cvec_end[...] = turned[12:14, 0:count]
    gain_m_end[...] = turned[14:15, 0:count].reshape(count)
    gain_a_end[...] = turned[15:16, 0:count].reshape(count)


def deliver(routes, out, dtok, prev, qkv, wout, small, gate, up, down):
    count = small.shape[0]
    vmem = pl.BlockSpec(memory_space=pltpu.VMEM)
    return pl.pallas_call(
        functools.partial(deliver_kernel, routes),
        in_specs=[vmem] * 9,
        out_specs=[vmem] * 13,
        out_shape=[
            shape(out.shape, BF16), shape(dtok.shape, F32), shape((routes, 2, prev.shape[2]), F32),
            shape((count,), F32), shape(qkv.shape, F32), shape(wout.shape, F32),
            shape((count,), F32), shape((routes, count), F32), shape((4, count), F32),
            shape((2, count), F32), shape(gate.shape, F32), shape(up.shape, F32),
            shape(down.shape, F32),
        ],
        compiler_params=params(),
        cost_estimate=cost(1e6, 8e6),
        name="deliver",
    )(out, dtok, prev, qkv, wout, small, gate, up, down)


def one_chip(
    tokens,
    prev_logits,
    segments,
    routes,
    cotangent,
    gain_attn,
    w_qkv,
    w_out,
    gain_moe,
    w_router,
    const_proj,
    const_vec,
    w_gate,
    w_up,
    w_down,
):
    rows = tokens.shape[1]
    route_count = w_router.shape[1]
    experts = route_count - 4
    (
        x_all, cot_own, ctl, normed, qkv, attended, lse, small_all, qkv_weight, out_sib,
        seg_col, seg_row,
    ) = gather_all(
        tokens, cotangent, w_qkv, w_out, prev_logits, routes, segments, w_router, const_proj,
        const_vec, gain_attn, gain_moe,
    )
    (
        block_out, d_prev, d_residual, d_branch, small, grad_gate, grad_up, grad_down,
    ) = expert_layer(
        experts, route_count, rows, attended, x_all, cot_own, ctl, w_out, out_sib, small_all,
        w_gate[0], w_up[0], w_down[0],
    )

    (
        share_gate, share_up, share_down, share_qkv, share_out, share_small, out_home, dtok_home,
        prev_home,
    ) = back_all(
        grad_gate, grad_up, grad_down, d_branch, w_out, attended, qkv, seg_col, normed,
        qkv_weight, x_all, d_residual, block_out, d_prev, lse, seg_row, small, small_all,
    )
    (
        block_out, grad_tokens, grad_prev, gain_a, grad_qkv, grad_out, gain_m, grad_router,
        grad_cproj, grad_cvec, grad_gate, grad_up, grad_down,
    ) = deliver(
        route_count, out_home, dtok_home, prev_home, share_qkv, share_out, share_small,
        share_gate, share_up, share_down,
    )
    return (
        block_out, grad_tokens, jnp.transpose(grad_prev, (1, 2, 0)), gain_a, grad_qkv, grad_out,
        gain_m, grad_router.T, grad_cproj.T, grad_cvec.T, grad_gate, grad_up, grad_down,
    )


def suits(mesh, tokens, w_router, w_gate):
    peers = mesh.shape["ep"]
    rows = tokens.shape[1] // peers
    micro = tokens.shape[0] // (mesh.shape["dp"] * mesh.shape["fs"])
    routes = w_router.shape[1]
    return (
        peers == 4
        and mesh.shape["fs"] == 2
        and micro == 2
        and mesh.shape["dp"] % 2 == 0
        and (routes - 4) * 2 == peers
        and 3 * rows // routes == LANES
        and tokens.shape[2] % (2 * LANES) == 0
    )


def solution(mesh):
    placed = (
        P(("dp", "fs"), "ep", None),
        P(("dp", "fs"), "ep", None),
        P(("dp", "fs"), None),
        P(("dp", "fs"), "ep", None),
        P(("dp", "fs"), "ep", None),
        P("fs"),
        P("fs", None),
        P("fs", None),
        P("fs"),
        P("fs", None),
        P("fs", None),
        P("fs", None),
        P("ep", "fs", None),
        P("ep", "fs", None),
        P("ep", "fs", None),
    )
    def layer(*arrays):
        fits = suits(mesh, arrays[0], arrays[9], arrays[12])
        return mapped(one_chip if fits else shards)(*arrays)

    def mapped(body):
        return jax.shard_map(
            body,
            mesh=mesh,
            in_specs=placed,
            out_specs=(
                P(("dp", "fs"), "ep", None),
                P(("dp", "fs"), "ep", None),
                P(("dp", "fs"), "ep", None),
                P(("ep", "dp", "fs")),
                P(("ep", "dp", "fs"), None),
                P(("ep", "dp", "fs"), None),
                P(("ep", "dp", "fs")),
                P(("ep", "dp", "fs"), None),
                P(("ep", "dp", "fs"), None),
                P(("ep", "dp", "fs"), None),
                P("ep", ("dp", "fs"), None),
                P("ep", ("dp", "fs"), None),
                P("ep", ("dp", "fs"), None),
            ),
            check_vma=False,
        )

    return layer
```

```python
import functools

import jax
import jax.numpy as jnp
from jax import lax
from jax.experimental import pallas as pl
from jax.experimental.pallas import tpu as pltpu
from jax.sharding import PartitionSpec as P

HEAD = 64
SEGS = 4


NORM_EPS = 1e-06
MASK_FILL = -1e30
HIGHEST = lax.Precision.HIGHEST


def rms_scale(values, gains):
    inverse = lax.rsqrt(jnp.mean(values * values, axis=-1, keepdims=True) + NORM_EPS)
    return values * inverse * gains


def small_softmax(logit_rows):
    largest = jnp.max(logit_rows, axis=-1, keepdims=True)
    powers = jnp.exp(logit_rows - largest)
    return powers / jnp.sum(powers, axis=-1, keepdims=True)


def add_tuple(first_tuple, second_tuple):
    if first_tuple is None:
        return second_tuple
    return tuple(
        (first_term + second_term for first_term, second_term in zip(first_tuple, second_tuple))
    )


def shards(
    tokens,
    prev_logits,
    segments,
    routes,
    cotangent,
    gain_attn,
    w_qkv,
    w_out,
    gain_moe,
    w_router,
    const_proj,
    const_vec,
    w_gate,
    w_up,
    w_down,
):
    micro_count, row_count, model_width = tokens.shape
    head_count = model_width // HEAD
    peer_count = lax.axis_size("ep")
    my_index = lax.axis_index("ep")
    route_count = w_router.shape[1]
    expert_count = route_count - 4
    half_count = peer_count // expert_count
    capacity = (3 * row_count // route_count + 7) // 8 * 8
    seq_length = row_count * peer_count
    slot_count = expert_count * capacity
    pos_all = jnp.arange(seq_length, dtype=jnp.int32)
    pos_mine = my_index * row_count + jnp.arange(row_count, dtype=jnp.int32)
    expert_ids = jnp.arange(expert_count, dtype=jnp.int32)
    slot_ids = jnp.arange(slot_count, dtype=jnp.int32)
    route_ids = jnp.arange(route_count, dtype=jnp.int32)
    layer_outputs = []
    input_grads = []
    prev_grads = []
    dense_acc = None
    expert_acc = None
    for step_index in range(micro_count):
        gathered = (
            lax.all_gather(w_qkv, "fs", axis=0, tiled=True),
            lax.all_gather(w_out, "fs", axis=0, tiled=True),
            lax.all_gather(w_router, "fs", axis=0, tiled=True),
            lax.all_gather(const_proj, "fs", axis=0, tiled=True),
            lax.all_gather(const_vec, "fs", axis=0, tiled=True),
            lax.all_gather(gain_attn, "fs", axis=0, tiled=True),
            lax.all_gather(gain_moe, "fs", axis=0, tiled=True),
            lax.all_gather(w_gate, "fs", axis=1, tiled=True),
            lax.all_gather(w_up, "fs", axis=1, tiled=True),
            lax.all_gather(w_down, "fs", axis=1, tiled=True),
        )
        (
            qkv_weight,
            out_weight,
            router_weight,
            cproj_weight,
            cvec_weight,
            attn_gain,
            moe_gain,
            gate_weight,
            up_weight,
            down_weight,
        ) = gathered
        gate_weight = gate_weight[0]
        up_weight = up_weight[0]
        down_weight = down_weight[0]
        attn_gain = attn_gain.astype(jnp.float32)
        moe_gain = moe_gain.astype(jnp.float32)
        router_float = router_weight.astype(jnp.float32)
        cproj_float = cproj_weight.astype(jnp.float32)
        cvec_float = cvec_weight.astype(jnp.float32)
        token_rows = tokens[step_index].astype(jnp.float32)
        seg_all = segments[step_index]
        seg_mine = lax.dynamic_slice_in_dim(seg_all, my_index * row_count, row_count)
        allowed = (seg_mine[:, None] == seg_all[None, :]) & (pos_all[None, :] <= pos_mine[:, None])
        valid_rows = (seg_mine != SEGS - 1).astype(jnp.float32)[:, None]
        normed = rms_scale(token_rows, attn_gain).astype(jnp.bfloat16)
        qkv_rows = jnp.dot(normed, qkv_weight, preferred_element_type=jnp.float32).astype(
            jnp.bfloat16
        )
        queries = qkv_rows[:, :model_width].reshape(row_count, head_count, HEAD)
        keys_local = qkv_rows[:, model_width : 2 * model_width]
        values_local = qkv_rows[:, 2 * model_width :]
        keys_all, values_all = (
            lax.all_gather(keys_local, "ep", axis=0, tiled=True),
            lax.all_gather(values_local, "ep", axis=0, tiled=True),
        )
        key_heads = keys_all.reshape(seq_length, head_count, HEAD)
        value_heads = values_all.reshape(seq_length, head_count, HEAD)
        scores = (
            jnp.einsum("qhd,khd->hqk", queries, key_heads, preferred_element_type=jnp.float32)
            * 0.125
        )
        scores = jnp.where(allowed[None], scores, MASK_FILL)
        largest = jnp.max(scores, axis=-1, keepdims=True)
        powers = jnp.exp(scores - largest)
        row_total = jnp.sum(powers, axis=-1, keepdims=True)
        log_total = largest + jnp.log(row_total)
        attn_probs = powers / row_total
        attended = jnp.einsum(
            "hqk,khd->qhd",
            attn_probs.astype(jnp.bfloat16),
            value_heads,
            preferred_element_type=jnp.float32,
        ).reshape(row_count, model_width)
        attended = (attended * valid_rows).astype(jnp.bfloat16)
        residual = token_rows + jnp.dot(attended, out_weight, preferred_element_type=jnp.float32)
        mixed = rms_scale(residual, moe_gain).astype(jnp.bfloat16)
        mixed_float = mixed.astype(jnp.float32)
        logits = (
            jnp.dot(mixed, router_weight, preferred_element_type=jnp.float32)
            + prev_logits[step_index]
        )
        router_probs = small_softmax(logits)
        route_rows = routes[step_index]
        choose = (route_rows[:, :, None] == route_ids[None, None, :]).astype(jnp.float32)
        gate_values = jnp.sum(choose * router_probs[:, None, :], axis=-1)
        const_logits = jnp.dot(mixed, cproj_weight, preferred_element_type=jnp.float32)
        mixings = []
        const_outs = []
        for const_index in range(2):
            mixing = small_softmax(const_logits[:, 2 * const_index : 2 * const_index + 2])
            mixings.append(mixing)
            const_outs.append(
                mixing[:, :1] * mixed_float + mixing[:, 1:] * cvec_float[:, const_index][None, :]
            )
        pair_route = route_rows.reshape(-1)
        expert_hit = (pair_route[:, None] == expert_ids[None, :]).astype(jnp.int32)
        slot_index = jnp.sum((jnp.cumsum(expert_hit, axis=0) - expert_hit) * expert_hit, axis=1)
        slot_cell = jnp.sum(expert_hit * expert_ids[None, :], axis=1) * capacity + slot_index
        slot_place = jnp.where(jnp.sum(expert_hit, axis=1) > 0, slot_cell, -1)
        slot_table = (slot_ids[:, None] == slot_place[None, :]).astype(jnp.bfloat16)
        pair_rows = jnp.repeat(mixed, 2, axis=0)
        packed = jnp.einsum(
            "sp,pd->sd", slot_table, pair_rows, preferred_element_type=jnp.float32
        ).astype(jnp.bfloat16)
        outgoing = jnp.broadcast_to(
            packed.reshape(expert_count, 1, capacity, model_width),
            (expert_count, half_count, capacity, model_width),
        ).reshape(peer_count, capacity, model_width)
        received = lax.all_to_all(outgoing, "ep", split_axis=0, concat_axis=0, tiled=True)
        flat_rows = received.reshape(-1, model_width)
        gate_part = jnp.dot(flat_rows, gate_weight, preferred_element_type=jnp.float32)
        up_part = jnp.dot(flat_rows, up_weight, preferred_element_type=jnp.float32)
        hidden = (jax.nn.silu(gate_part) * up_part).astype(jnp.bfloat16)
        part_out = (
            jnp.dot(hidden, down_weight, preferred_element_type=jnp.float32)
            .astype(jnp.bfloat16)
            .reshape(received.shape)
        )
        returned_rows = lax.all_to_all(part_out, "ep", split_axis=0, concat_axis=0, tiled=True)
        returned_rows, kept_rows = (returned_rows, received)
        halves = returned_rows.reshape(expert_count, half_count, capacity, model_width)
        pair_ffn = jnp.zeros((2 * row_count, model_width), jnp.float32)
        for half_index in range(half_count):
            pair_ffn = pair_ffn + jnp.einsum(
                "sp,sd->pd",
                slot_table,
                halves[:, half_index].reshape(slot_count, model_width),
                preferred_element_type=jnp.float32,
            )
        expert_out = pair_ffn.reshape(row_count, 2, model_width)
        expert_out = (
            expert_out + choose[:, :, expert_count + 1 : expert_count + 2] * mixed_float[:, None, :]
        )
        for const_index in range(2):
            column = expert_count + 2 + const_index
            expert_out = (
                expert_out + choose[:, :, column : column + 1] * const_outs[const_index][:, None, :]
            )
        result_rows = residual + jnp.sum(gate_values[:, :, None] * expert_out, axis=1)
        layer_outputs.append(result_rows.astype(jnp.bfloat16))
        grad_rows = cotangent[step_index].astype(jnp.float32)
        d_gates = jnp.sum(expert_out * grad_rows[:, None, :], axis=-1)
        d_probs = jnp.sum(choose * d_gates[:, :, None], axis=1)
        d_logits = router_probs * (
            d_probs - jnp.sum(router_probs * d_probs, axis=-1, keepdims=True)
        )
        prev_grads.append(d_logits)
        grad_router = jnp.dot(mixed_float.T, d_logits, precision=HIGHEST)
        d_mixed = jnp.dot(d_logits, router_float.T, precision=HIGHEST)
        weighted = gate_values[:, :, None] * grad_rows[:, None, :]
        d_mixed = d_mixed + jnp.sum(
            choose[:, :, expert_count + 1 : expert_count + 2] * weighted, axis=1
        )
        cproj_grads = []
        cvec_grads = []
        for const_index in range(2):
            column = expert_count + 2 + const_index
            mixing = mixings[const_index]
            d_const = jnp.sum(choose[:, :, column : column + 1] * weighted, axis=1)
            d_mix = jnp.stack(
                [
                    jnp.sum(d_const * mixed_float, axis=-1),
                    jnp.sum(d_const * cvec_float[:, const_index][None, :], axis=-1),
                ],
                axis=-1,
            )
            d_mixlog = mixing * (d_mix - jnp.sum(mixing * d_mix, axis=-1, keepdims=True))
            cproj_grads.append(jnp.dot(mixed_float.T, d_mixlog, precision=HIGHEST))
            cvec_grads.append(jnp.sum(mixing[:, 1:] * d_const, axis=0))
            d_mixed = (
                d_mixed
                + mixing[:, :1] * d_const
                + jnp.dot(
                    d_mixlog,
                    cproj_float[:, 2 * const_index : 2 * const_index + 2].T,
                    precision=HIGHEST,
                )
            )
        grad_cproj = jnp.concatenate(cproj_grads, axis=1)
        grad_cvec = jnp.stack(cvec_grads, axis=1)
        d_pairs = weighted.reshape(2 * row_count, model_width).astype(jnp.bfloat16)
        d_packed = jnp.einsum(
            "sp,pd->sd", slot_table, d_pairs, preferred_element_type=jnp.float32
        ).astype(jnp.bfloat16)
        d_outgoing = jnp.broadcast_to(
            d_packed.reshape(expert_count, 1, capacity, model_width),
            (expert_count, half_count, capacity, model_width),
        ).reshape(peer_count, capacity, model_width)
        d_received = lax.all_to_all(d_outgoing, "ep", split_axis=0, concat_axis=0, tiled=True)
        flat_rows = kept_rows.reshape(-1, model_width)
        flat_grads = d_received.reshape(-1, model_width)
        gate_part = jnp.dot(flat_rows, gate_weight, preferred_element_type=jnp.float32)
        up_part = jnp.dot(flat_rows, up_weight, preferred_element_type=jnp.float32)
        activated = jax.nn.silu(gate_part)
        hidden = (activated * up_part).astype(jnp.bfloat16)
        grad_down = jnp.einsum("rf,rd->fd", hidden, flat_grads, preferred_element_type=jnp.float32)
        d_hidden = jnp.einsum(
            "rd,fd->rf", flat_grads, down_weight, preferred_element_type=jnp.float32
        )
        sigmoid_gate = jax.nn.sigmoid(gate_part)
        d_gate_part = (
            d_hidden * up_part * sigmoid_gate * (1.0 + gate_part * (1.0 - sigmoid_gate))
        ).astype(jnp.bfloat16)
        d_up_part = (d_hidden * activated).astype(jnp.bfloat16)
        grad_gate = jnp.einsum(
            "rd,rf->df", flat_rows, d_gate_part, preferred_element_type=jnp.float32
        )
        grad_up = jnp.einsum("rd,rf->df", flat_rows, d_up_part, preferred_element_type=jnp.float32)
        d_inputs = jnp.einsum(
            "rf,df->rd", d_gate_part, gate_weight, preferred_element_type=jnp.float32
        )
        d_inputs = d_inputs + jnp.einsum(
            "rf,df->rd", d_up_part, up_weight, preferred_element_type=jnp.float32
        )
        d_inputs = d_inputs.astype(jnp.bfloat16).reshape(peer_count, capacity, model_width)
        d_returned = lax.all_to_all(d_inputs, "ep", split_axis=0, concat_axis=0, tiled=True)
        d_halves = d_returned.reshape(expert_count, half_count, capacity, model_width)
        for half_index in range(half_count):
            d_pair_in = jnp.einsum(
                "sp,sd->pd",
                slot_table,
                d_halves[:, half_index].reshape(slot_count, model_width),
                preferred_element_type=jnp.float32,
            )
            d_mixed = d_mixed + jnp.sum(d_pair_in.reshape(row_count, 2, model_width), axis=1)
        expert_acc = add_tuple(expert_acc, (grad_gate, grad_up, grad_down))
        moe_vjp = jax.vjp(rms_scale, residual, moe_gain)[1]
        d_residual_norm, grad_moe_gain = moe_vjp(d_mixed)
        d_residual = grad_rows + d_residual_norm
        d_branch = d_residual.astype(jnp.bfloat16)
        grad_out = jnp.einsum("rd,re->de", attended, d_branch, preferred_element_type=jnp.float32)
        d_attended = (
            jnp.einsum("re,de->rd", d_branch, out_weight, preferred_element_type=jnp.float32)
            * valid_rows
        ).astype(jnp.bfloat16)
        d_heads = d_attended.reshape(row_count, head_count, HEAD)
        scores = (
            jnp.einsum("qhd,khd->hqk", queries, key_heads, preferred_element_type=jnp.float32)
            * 0.125
        )
        scores = jnp.where(allowed[None], scores, MASK_FILL)
        attn_probs = jnp.exp(scores - log_total)
        d_weights = jnp.einsum(
            "qhd,khd->hqk", d_heads, value_heads, preferred_element_type=jnp.float32
        )
        delta_rows = jnp.sum(attn_probs * d_weights, axis=-1, keepdims=True)
        d_scores = (attn_probs * (d_weights - delta_rows)).astype(jnp.bfloat16)
        d_queries = (
            jnp.einsum(
                "hqk,khd->qhd", d_scores, key_heads, preferred_element_type=jnp.float32
            ).reshape(row_count, model_width)
            * 0.125
        )
        d_values = jnp.einsum(
            "hqk,qhd->khd",
            attn_probs.astype(jnp.bfloat16),
            d_heads,
            preferred_element_type=jnp.float32,
        ).reshape(seq_length, model_width)
        d_keys = (
            jnp.einsum(
                "hqk,qhd->khd", d_scores, queries, preferred_element_type=jnp.float32
            ).reshape(seq_length, model_width)
            * 0.125
        )
        d_keys_mine, d_values_mine = (
            lax.psum_scatter(
                d_keys.astype(jnp.bfloat16), "ep", scatter_dimension=0, tiled=True
            ).astype(jnp.float32),
            lax.psum_scatter(
                d_values.astype(jnp.bfloat16), "ep", scatter_dimension=0, tiled=True
            ).astype(jnp.float32),
        )
        d_qkv = jnp.concatenate([d_queries, d_keys_mine, d_values_mine], axis=1).astype(
            jnp.bfloat16
        )
        grad_qkv = jnp.einsum("rd,re->de", normed, d_qkv, preferred_element_type=jnp.float32)
        d_normed = jnp.einsum("re,de->rd", d_qkv, qkv_weight, preferred_element_type=jnp.float32)
        attn_vjp = jax.vjp(rms_scale, token_rows, attn_gain)[1]
        d_tokens_norm, grad_attn_gain = attn_vjp(d_normed)
        input_grads.append(d_residual + d_tokens_norm)
        dense_terms = (
            grad_attn_gain,
            grad_qkv,
            grad_out,
            grad_moe_gain,
            grad_router,
            grad_cproj,
            grad_cvec,
        )
        dense_shares = (
            lax.psum_scatter(dense_terms[0], ("ep", "dp", "fs"), scatter_dimension=0, tiled=True),
            lax.psum_scatter(dense_terms[1], ("ep", "dp", "fs"), scatter_dimension=0, tiled=True),
            lax.psum_scatter(dense_terms[2], ("ep", "dp", "fs"), scatter_dimension=0, tiled=True),
            lax.psum_scatter(dense_terms[3], ("ep", "dp", "fs"), scatter_dimension=0, tiled=True),
            lax.psum_scatter(dense_terms[4], ("ep", "dp", "fs"), scatter_dimension=0, tiled=True),
            lax.psum_scatter(dense_terms[5], ("ep", "dp", "fs"), scatter_dimension=0, tiled=True),
            lax.psum_scatter(dense_terms[6], ("ep", "dp", "fs"), scatter_dimension=0, tiled=True),
        )
        dense_acc = add_tuple(dense_acc, dense_shares)
    expert_shares = (
        lax.psum_scatter(
            expert_acc[0][None].astype(jnp.bfloat16), ("dp", "fs"), scatter_dimension=1, tiled=True
        ).astype(jnp.float32),
        lax.psum_scatter(
            expert_acc[1][None].astype(jnp.bfloat16), ("dp", "fs"), scatter_dimension=1, tiled=True
        ).astype(jnp.float32),
        lax.psum_scatter(
            expert_acc[2][None].astype(jnp.bfloat16), ("dp", "fs"), scatter_dimension=1, tiled=True
        ).astype(jnp.float32),
    )
    return (
        jnp.stack(layer_outputs),
        jnp.stack(input_grads),
        jnp.stack(prev_grads),
        dense_acc[0],
        dense_acc[1],
        dense_acc[2],
        dense_acc[3],
        dense_acc[4],
        dense_acc[5],
        dense_acc[6],
        expert_shares[0],
        expert_shares[1],
        expert_shares[2],
    )


NEG = -1e30
KINDS = 2
SMALL = 16
LANES = 128
F32 = jnp.float32
BF16 = jnp.bfloat16


def dot(lhs, rhs, dims=((1,), (0,)), precision=None):
    return lax.dot_general(
        lhs, rhs, (dims, ((), ())), precision=precision, preferred_element_type=F32
    )


def key_span(block, rows, reach):
    start = max(0, block * rows - reach)
    return start, (block + 1) * rows - start


def column(rows, index):
    return rows[:, index : index + 1]


def chosen_of(ctl):
    lane = lax.broadcasted_iota(jnp.int32, ctl.shape, 1).astype(F32)
    return ((lane == column(ctl, 8)) | (lane == column(ctl, 9))).astype(F32)


def shape(dims, dtype):
    return jax.ShapeDtypeStruct(dims, dtype)


def whole(dims):
    return pl.BlockSpec(dims, lambda *_: (0,) * len(dims))


def per_row(rows, width):
    return pl.BlockSpec((rows, width), lambda i: (i, 0))


def params():
    return pltpu.CompilerParams(vmem_limit_bytes=56 * 1024 * 1024)


def cost(flops, moved):
    return pl.CostEstimate(flops=int(flops), bytes_accessed=int(moved), transcendentals=0)


class Mail:
    def __init__(self, send_sems, recv_sems):
        self.send_sems = send_sems
        self.recv_sems = recv_sems
        self.used = 0

    def copy(self, source, target, device):
        slot = self.used
        self.used = slot + 1
        return pltpu.make_async_remote_copy(
            src_ref=source,
            dst_ref=target,
            send_sem=self.send_sems.at[slot],
            recv_sem=self.recv_sems.at[slot],
            device_id=device,
            device_id_type=pl.DeviceIdType.MESH,
        )


def position():
    place = lax.axis_index("ep")
    return place // 2, place % 2, lax.axis_index("dp"), lax.axis_index("fs")


def greet(devices):
    barrier = pltpu.get_barrier_semaphore()
    total = 0
    for device, present in devices:
        if present is True:
            pl.semaphore_signal(
                barrier, inc=1, device_id=device, device_id_type=pl.DeviceIdType.MESH
            )
            total = total + 1
        else:

            @pl.when(present)
            def _():
                pl.semaphore_signal(
                    barrier, inc=1, device_id=device, device_id_type=pl.DeviceIdType.MESH
                )

            total = total + jnp.where(present, 1, 0)
    pl.semaphore_wait(barrier, total)


def attend_pair(pair, rows, reach, span, qkv_ref, segc_ref, segr_ref, att_ref, lse_ref):
    length = qkv_ref.shape[0]
    at_q, at_k, at_v = (
        pl.ds(pl.multiple_of(part * span + pair * LANES, LANES), LANES) for part in range(3)
    )
    for block in range(length // rows):
        start, width = key_span(block, rows, reach)
        here = pl.ds(block * rows, rows)
        there = pl.ds(start, width)
        queries = qkv_ref[here, at_q]
        keys = qkv_ref[there, at_k]
        values = qkv_ref[there, at_v]
        seg_q = segc_ref[here, 0:1]
        seg_k = segr_ref[0:1, there]
        row_pos = block * rows + lax.broadcasted_iota(jnp.int32, (rows, width), 0)
        col_pos = start + lax.broadcasted_iota(jnp.int32, (rows, width), 1)
        allowed = (seg_q == seg_k) & (col_pos <= row_pos)
        lane = lax.broadcasted_iota(jnp.int32, (rows, LANES), 1)
        outs = []
        logs = []
        for head in range(2):
            mine = (lane // HEAD) == head
            scores = dot(jnp.where(mine, queries, 0), keys, ((1,), (1,))) * 0.125
            scores = jnp.where(allowed, scores, NEG)
            largest = jnp.max(scores, axis=-1, keepdims=True)
            powers = jnp.exp(scores - largest)
            total = jnp.sum(powers, axis=-1, keepdims=True)
            outs.append(dot(powers.astype(BF16), values) / total)
            logs.append(largest + jnp.log(total))
        valid = (seg_q != SEGS - 1.0).astype(F32)
        att = jnp.where(lane < HEAD, outs[0], outs[1]) * valid
        att_ref[here, at_q] = att.astype(BF16)
        both = jnp.where(lane < HEAD, logs[0], logs[1]).T
        lse_ref[pair, 0:1, here] = both[0:1, :]
        lse_ref[pair, 1:2, here] = both[HEAD : HEAD + 1, :]


def gather_kernel(
    rows, reach, routes, experts,
    tok_ref, cot_ref, wqkv_ref, wout_ref, prev_ref, route_ref, seg_ref, router_ref, cproj_ref,
    cvec_ref, gain_a_ref, gain_m_ref,
    x_all, cot_own, ctl_own, normed_ref, qkv_ref, att_ref, lse_ref, small_all, wqkv_all,
    wout_sib, segc_ref, segr_ref, g_rows,
    cot_wide, g_send, ctl_send, small_wide, small_send, seg_all,
    near_send, near_recv, far_send, far_recv, core_send, core_recv, local_sems,
    pack_send, pack_recv,
):
    y, x, z, core = position()
    me = y * 2 + x
    sibling = (me, z, 1 - core)
    moved = y != core
    near = ((1 - y) * 2 + x, z, 1 - core)
    far = (core * 2 + 1 - x, z, y)
    plane = [((y + k // 2) % 2 * 2 + (x + k) % 2) for k in range(4)]
    greet([((plane[k], z, (core + c) % 2), True) for k in range(4) for c in range(2) if k + c > 0])
    span = wqkv_ref.shape[0]
    halves = 4 // experts

    def pack(m, k, target=None):
        return pltpu.make_async_remote_copy(
            src_ref=g_send.at[m, plane[k] // halves],
            dst_ref=g_rows.at[x, core * 2 + m] if target is None else g_rows.at[target],
            send_sem=pack_send.at[m, k],
            recv_sem=pack_recv.at[x, core * 2 + m] if target is None else pack_recv.at[target],
            device_id=(plane[k], z, y),
            device_id_type=pl.DeviceIdType.MESH,
        )

    pack_stays = [
        pltpu.make_async_copy(
            g_send.at[m, y // (halves // 2)], g_rows.at[x, core * 2 + m], local_sems.at[7 + m]
        )
        for m in range(2)
    ]
    cot_load = pltpu.make_async_copy(cot_ref, cot_wide, local_sems.at[9])

    def block_of(index):
        return pl.ds(pl.multiple_of(index * rows, rows), rows)

    within = block_of(x)
    homes = [
        (tok_ref, x_all.at[block_of(me)]),
        (cot_ref, cot_own.at[within]),
        (ctl_send, ctl_own.at[x]),
    ]
    nears = Mail(near_send, near_recv)
    fars = Mail(far_send, far_recv)
    near_copies = [nears.copy(a.at[x], b, near) for a, b in homes]
    far_copies = [fars.copy(a.at[1 - x], b, far) for a, b in homes]
    stay_copies = [
        pltpu.make_async_copy(a.at[x], b, local_sems.at[k]) for k, (a, b) in enumerate(homes)
    ]

    def send(k):
        far_copies[k].start()

        @pl.when(moved)
        def _():
            near_copies[k].start()

        @pl.when(jnp.logical_not(moved))
        def _():
            stay_copies[k].start()

    def take_near(k):
        @pl.when(moved)
        def _():
            near_copies[k].wait_recv()

        @pl.when(jnp.logical_not(moved))
        def _():
            stay_copies[k].wait()

    send(0)
    cot_load.start()
    inner = Mail(core_send, core_recv)
    weight_copies = []
    own_copies = []
    band = pl.ds(pl.multiple_of(core * span, span), span)
    for part in range(3):
        columns = pl.ds(part * span, span)
        for side, copies in ((1 - core, weight_copies), (core, own_copies)):
            source = wqkv_ref.at[
                :, pl.ds(pl.multiple_of(part * 2 * span + side * span, LANES), span)
            ]
            target = wqkv_all.at[band, columns]
            if copies is weight_copies:
                copies.append(inner.copy(source, target, sibling))
            else:
                copies.append(
                    pltpu.make_async_copy(source, target, local_sems.at[3 + part])
                )
    out_copy = inner.copy(wout_ref, wout_sib, sibling)
    seg_copy = inner.copy(seg_ref, seg_all.at[core], sibling)
    seg_own = pltpu.make_async_copy(seg_ref, seg_all.at[core], local_sems.at[6])
    small_copy = inner.copy(small_send, small_all.at[:, band], sibling)
    seg_copy.start()
    seg_own.start()
    for copy in weight_copies + own_copies:
        copy.start()

    small_wide[...] = jnp.zeros_like(small_wide)
    small_wide[0:routes, :] = router_ref[...].astype(F32)
    small_wide[8:12, :] = cproj_ref[...].astype(F32)
    small_wide[12:14, :] = cvec_ref[...].astype(F32)
    small_wide[14:15, :] = gain_a_ref[...].astype(F32).reshape(1, span)
    small_wide[15:16, :] = gain_m_ref[...].astype(F32).reshape(1, span)
    turned = small_wide[...]
    small_send[...] = turned.astype(BF16)
    small_all[:, band] = turned.astype(BF16)
    small_copy.start()
    out_copy.start()
    ctl_send[...] = jnp.zeros_like(ctl_send)
    for m in range(2):
        for route in range(routes):
            ctl_send[m, route : route + 1, :] = prev_ref[route, m : m + 1, :]
        ctl_send[m, 8:10, :] = route_ref[m].astype(F32)
    send(2)
    cot_load.wait()
    earlier = lax.broadcasted_iota(jnp.int32, (rows, rows), 0) < lax.broadcasted_iota(
        jnp.int32, (rows, rows), 1
    )
    slot = lax.broadcasted_iota(jnp.int32, (LANES, rows), 0).astype(F32)
    number = lax.broadcasted_iota(jnp.int32, (8, rows), 0)
    for m in range(2):
        chosen = ((number == route_ref[m, 0:1, :]) | (number == route_ref[m, 1:2, :])).astype(F32)
        rank = dot(chosen.astype(BF16), earlier.astype(BF16))
        for expert in range(experts):
            hit = (slot == rank[expert : expert + 1, :]) & (chosen[expert : expert + 1, :] > 0.0)
            g_send[m, expert] = dot(hit.astype(BF16), cot_wide[m]).astype(BF16)
        for k in range(1, 4):
            pack(m, k).start()

        @pl.when(moved)
        def _():
            pack(m, 0).start()

        @pl.when(jnp.logical_not(moved))
        def _():
            pack_stays[m].start()

    seg_copy.wait_recv()
    seg_own.wait()
    seg_row = seg_all[y, pl.ds(x, 1), :].astype(F32)
    length = seg_row.shape[1]
    segr_ref[...] = jnp.broadcast_to(seg_row, segr_ref.shape)
    segc_ref[...] = jnp.broadcast_to(seg_row, (LANES, length)).T
    small_copy.wait_recv()
    for copy in weight_copies:
        copy.wait_recv()
    for copy in own_copies:
        copy.wait()
    gain = small_all[14:15, :].astype(F32)

    def project(index):
        here = block_of(index)
        values = x_all[here, :].astype(F32)
        inverse = lax.rsqrt(jnp.mean(values * values, axis=-1, keepdims=True) + NORM_EPS)
        normed = (values * inverse * gain).astype(BF16)
        normed_ref[here, :] = normed
        qkv_ref[here, :] = dot(normed, wqkv_all[...]).astype(BF16)

    forward = []
    for step in range(2):
        spot = x_all.at[block_of(core * 2 + (x if step == 0 else 1 - x))]
        forward.append(inner.copy(spot, spot, sibling))
    take_near(0)
    forward[0].start()
    project(core * 2 + x)
    far_copies[0].wait_recv()
    forward[1].start()
    send(1)
    project(core * 2 + 1 - x)
    forward[0].wait_recv()
    project((1 - core) * 2 + x)
    forward[1].wait_recv()
    project((1 - core) * 2 + 1 - x)

    @pl.loop(0, span // LANES)
    def _(pair):
        attend_pair(pair, rows, reach, span, qkv_ref, segc_ref, segr_ref, att_ref, lse_ref)

    for k in (1, 2):
        take_near(k)
        far_copies[k].wait_recv()
    for there in range(2):
        for peer in range(4):
            kept = (y == core) & (x == there) & (core == peer // 2)

            @pl.when(jnp.logical_not(kept))
            def _():
                pack(0, 0, (there, peer)).wait_recv()

    for m in range(2):
        for k in range(1, 4):
            pack(m, k).wait_send()

        @pl.when(moved)
        def _():
            pack(m, 0).wait_send()

        @pl.when(jnp.logical_not(moved))
        def _():
            pack_stays[m].wait()

    out_copy.wait_recv()
    for copy in far_copies + weight_copies + forward + [out_copy, seg_copy, small_copy]:
        copy.wait_send()

    @pl.when(moved)
    def _():
        for copy in near_copies:
            copy.wait_send()


def gather_all(
    experts, tokens, cotangent, w_qkv, w_out, prev_logits, routes, segments, w_router, const_proj,
    const_vec, gain_attn, gain_moe,
):
    rows, width = tokens.shape[1:]
    length = segments.shape[1]
    mine = length // 2
    span = width // 2
    vmem = pl.BlockSpec(memory_space=pltpu.VMEM)
    anywhere = pl.BlockSpec(memory_space=pl.ANY)
    return pl.pallas_call(
        functools.partial(gather_kernel, rows, length // 2, w_router.shape[1], experts),
        in_specs=[anywhere] * 4 + [vmem] * 8,
        out_specs=[vmem] * 13,
        out_shape=[
            shape((length, width), BF16), shape((mine, width), BF16),
            shape((2, SMALL, rows), F32), shape((length, width), BF16),
            shape((length, 3 * span), BF16), shape((length, span), BF16),
            shape((span // LANES, 8, length), F32), shape((SMALL, width), BF16),
            shape((width, 3 * span), BF16), shape((span, width), BF16),
            shape((length, LANES), F32), shape((8, length), F32),
            shape((2, 4, LANES, width), BF16),
        ],
        scratch_shapes=[
            pltpu.VMEM((2, rows, width), BF16), pltpu.VMEM((2, experts, LANES, width), BF16),
            pltpu.VMEM((2, SMALL, rows), F32),
            pltpu.VMEM((SMALL, span), F32), pltpu.VMEM((SMALL, span), BF16),
            pltpu.VMEM((2, 2, length), jnp.int32),
        ]
        + [pltpu.SemaphoreType.DMA((3,))] * 4
        + [pltpu.SemaphoreType.DMA((8,))] * 2
        + [pltpu.SemaphoreType.DMA((10,))]
        + [pltpu.SemaphoreType.DMA((2, 4))] * 2,
        compiler_params=pltpu.CompilerParams(
            collective_id=3, has_side_effects=True, vmem_limit_bytes=60 * 1024 * 1024
        ),
        name="gather_all",
    )(
        tokens, cotangent, w_qkv, w_out, jnp.transpose(prev_logits, (2, 0, 1)),
        jnp.swapaxes(routes, 1, 2), segments, w_router.T, const_proj.T, const_vec.T, gain_attn,
        gain_moe,
    )


def widen(turned):
    pad = jnp.zeros((LANES - turned.shape[0], turned.shape[1]), turned.dtype)
    return jnp.concatenate([turned, pad], axis=0).T


def spread_block(experts, routes, rows, block, refs, sent, got, keep):
    send_ref, gate_send = sent
    recv_ref, gate_recv = got
    att_own, att_sib, x_ref, ctl_ref, w_own, w_sib, small_rows, wide_rows = refs
    residual_ref, mixed_ref, pm_ref, place_ref = keep
    y, x, z, core = position()
    here = pl.ds(pl.multiple_of(block * rows, rows), rows)
    tokens = x_ref[pl.ds(pl.multiple_of((core * 2 + block) * rows, rows), rows), :]
    residual = tokens.astype(F32) + (
        dot(att_own[here, :], w_own[...]) + dot(att_sib[here, :], w_sib[...])
    )
    residual_ref[here, :] = residual
    inverse = lax.rsqrt(jnp.mean(residual * residual, axis=-1, keepdims=True) + NORM_EPS)
    mixed = (residual * inverse * small_rows[15:16, :].astype(F32)).astype(BF16)
    mixed_ref[here, :] = mixed
    logits = dot(mixed, wide_rows[...], ((1,), (1,)))
    ctl = widen(ctl_ref[block])
    lane = lax.broadcasted_iota(jnp.int32, (rows, LANES), 1)
    is_route = lane < routes
    router = jnp.where(is_route, logits + ctl, NEG)
    powers = jnp.exp(router - jnp.max(router, axis=-1, keepdims=True))
    probs = powers / jnp.sum(powers, axis=-1, keepdims=True)
    probs = jnp.where(is_route, probs, 0.0)
    pm = probs
    for const_index in range(2):
        first = column(logits, 8 + 2 * const_index)
        second = column(logits, 9 + 2 * const_index)
        largest = jnp.maximum(first, second)
        first = jnp.exp(first - largest)
        second = jnp.exp(second - largest)
        total = first + second
        pm = jnp.where(lane == 8 + 2 * const_index, first / total, pm)
        pm = jnp.where(lane == 9 + 2 * const_index, second / total, pm)
    pm_ref[here, :] = pm
    chosen = chosen_of(ctl)
    gated = chosen * probs
    earlier = lax.broadcasted_iota(jnp.int32, (rows, rows), 1) < lax.broadcasted_iota(
        jnp.int32, (rows, rows), 0
    )
    rank = dot(earlier.astype(BF16), chosen.astype(BF16))
    lane_f = lane.astype(F32)
    for expert in range(experts):
        place = jnp.where(
            (lane_f == column(rank, expert)) & (column(chosen, expert) > 0.0), 1.0, 0.0
        )
        place_ref[here, expert * LANES : (expert + 1) * LANES] = place.astype(BF16)
        pick = place.T.astype(BF16)
        send_ref[block, expert] = dot(pick, mixed).astype(BF16)
        gates = jnp.sum(place * column(gated, expert), axis=0, keepdims=True)
        gate_send[block, expert] = jnp.broadcast_to(gates, gate_send.shape[2:])
    recv_ref[block, y * 2 + x] = send_ref[block, y]
    gate_recv[block, y * 2 + x] = gate_send[block, y]


def expert_block(block, got, result_ref, back_ref, weights, keep, send):
    recv_ref, gate_recv, g_rows = got
    gate_w, up_w, down_w = weights
    hidden_ref, d_gate_ref, d_up_ref, d_rows_ref = keep
    y, x, z, core = position()
    peers, capacity, width = recv_ref.shape[1:]
    size = peers * capacity
    here = pl.ds(pl.multiple_of(block * size, size), size)
    rows = recv_ref[block].reshape(size, width)
    gate = dot(rows, gate_w[...])
    up = dot(rows, up_w[...])
    sig = jax.nn.sigmoid(gate)
    active = gate * sig
    hidden = (active * up).astype(BF16)
    hidden_ref[here, :] = hidden
    part = dot(hidden, down_w[...]).astype(BF16)
    result_ref[block, :, 0] = part.reshape(peers, capacity, width)
    send(0)
    for peer in range(peers):
        spread = jnp.concatenate([gate_recv[block, peer]] * (capacity // 8), axis=0).T
        d_part = column(spread, 0) * g_rows[block, peer].astype(F32)
        at = pl.ds(pl.multiple_of(block * size + peer * capacity, capacity), capacity)
        d_rows_ref[at, :] = d_part.astype(BF16)
    d_rows = d_rows_ref[here, :]
    d_hidden = dot(d_rows, down_w[...], ((1,), (1,)))
    d_gate = (d_hidden * up * sig * (1.0 + gate * (1.0 - sig))).astype(BF16)
    d_up = (d_hidden * active).astype(BF16)
    d_gate_ref[here, :] = d_gate
    d_up_ref[here, :] = d_up
    d_in = dot(d_gate, gate_w[...], ((1,), (1,))) + dot(d_up, up_w[...], ((1,), (1,)))
    result_ref[block, :, 1] = d_in.astype(BF16).reshape(peers, capacity, width)
    send(1)
    back_ref[block, y * 2 + x] = result_ref[block, y * 2 + x]


def combine_block(experts, routes, rows, block, refs, keep, back_ref, outs, small_ref):
    g_ref, ctl_ref, small_rows, wide_rows = refs
    residual_ref, mixed_ref, pm_ref, place_ref = keep
    out_ref, prev_ref, dres_ref, branch_ref = outs
    halves = back_ref.shape[1] // experts
    here = pl.ds(pl.multiple_of(block * rows, rows), rows)
    g_low = g_ref[here, :]
    grads = g_low.astype(F32)
    mixed = mixed_ref[here, :].astype(F32)
    residual = residual_ref[here, :]
    pm = pm_ref[here, :]
    lane = lax.broadcasted_iota(jnp.int32, (rows, LANES), 1)
    chosen = chosen_of(widen(ctl_ref[block]))
    probs = jnp.where(lane < routes, pm, 0.0)
    gated = chosen * probs
    d_probs = jnp.zeros((rows, LANES), F32)
    result = residual
    d_mixed = None
    for expert in range(experts):
        place = place_ref[here, expert * LANES : (expert + 1) * LANES]
        expert_out = None
        for half in range(halves):
            owner = expert * halves + half
            term = dot(place, back_ref[block, owner, 0])
            expert_out = term if expert_out is None else expert_out + term
            term = dot(place, back_ref[block, owner, 1])
            d_mixed = term if d_mixed is None else d_mixed + term
        result = result + column(gated, expert) * expert_out
        d_gate = jnp.sum(expert_out * grads, axis=-1, keepdims=True)
        d_probs = jnp.where(lane == expert, d_gate, d_probs)
    g_mixed = jnp.sum(grads * mixed, axis=-1, keepdims=True)
    g_const = dot(g_low, wide_rows[...], ((1,), (1,)))
    copy = experts + 1
    d_probs = jnp.where(lane == copy, g_mixed, d_probs)
    weight = column(gated, copy)
    d_small = jnp.zeros((rows, LANES), F32)
    for const_index in range(2):
        route = copy + 1 + const_index
        first = column(pm, 8 + 2 * const_index)
        second = column(pm, 9 + 2 * const_index)
        gate = column(gated, route)
        g_vec = column(g_const, 12 + const_index)
        d_probs = jnp.where(lane == route, first * g_mixed + second * g_vec, d_probs)
        weight = weight + gate * first
        vec = small_rows[12 + const_index : 13 + const_index, :].astype(F32)
        result = result + (gate * second) * vec
        d_first = gate * g_mixed
        d_second = gate * g_vec
        mean = first * d_first + second * d_second
        d_small = jnp.where(lane == 8 + 2 * const_index, first * (d_first - mean), d_small)
        d_small = jnp.where(lane == 9 + 2 * const_index, second * (d_second - mean), d_small)
        d_small = jnp.where(lane == 12 + const_index, gate * second, d_small)
    result = result + weight * mixed
    out_ref[block] = result.astype(BF16)
    d_probs = d_probs * chosen
    d_logits = probs * (d_probs - jnp.sum(probs * d_probs, axis=-1, keepdims=True))
    d_small = jnp.where(lane < routes, d_logits, d_small)
    d_mixed = d_mixed + weight * grads
    d_mixed = d_mixed + dot(
        jnp.where(lane < 12, d_small, 0.0), wide_rows[...].astype(F32), precision=HIGHEST
    )
    inverse = lax.rsqrt(jnp.mean(residual * residual, axis=-1, keepdims=True) + NORM_EPS)
    scaled = d_mixed * small_rows[15:16, :].astype(F32)
    mean = jnp.mean(scaled * residual, axis=-1, keepdims=True)
    d_residual = grads + inverse * scaled - residual * (inverse * inverse * inverse * mean)
    dres_ref[here, :] = d_residual
    branch_ref[here, :] = d_residual.astype(BF16)
    d_turned = d_small.T[:SMALL, :]
    prev_ref[block] = d_turned[:8, :]
    sub = lax.broadcasted_iota(jnp.int32, (SMALL, rows), 0)
    small = dot(jnp.where(sub < 12, d_turned, 0.0), mixed, precision=HIGHEST)
    small = small + dot(
        jnp.where((sub >= 12) & (sub < 14), d_turned, 0.0), grads, precision=HIGHEST
    )
    d_gain = jnp.sum(d_mixed * residual * inverse, axis=0, keepdims=True)
    which = lax.broadcasted_iota(jnp.int32, small.shape, 0)
    small_ref[...] += jnp.where(which == 14, d_gain, small)


def layer_kernel(
    experts, routes, rows, blocks,
    att_ref, x_ref, g_ref, ctl_ref, w_own, w_sib, small_rows, gate_ref, up_ref, down_ref, g_rows,
    out_ref, prev_ref, dres_ref, branch_ref, small_ref, gate_acc, up_acc, down_acc,
    dgate_out, dup_out, ddown_out, gate_land, up_land, down_land, gate_line, up_line, down_line,
    wide_rows, att_own, att_sib, gate_w, up_w, down_w, residual_ref, mixed_ref, pm_ref, place_ref,
    send_ref, gate_send, gate_recv, recv_ref, result_ref, back_ref, hidden_ref, d_gate_ref,
    d_up_ref, d_rows_ref,
    head_send, head_recv, local_sems, send_sems, recv_sems, back_send, back_recv, sum_send, sum_recv,
):
    y, x, z, core = position()
    me = y * 2 + x
    sibling = (me, z, 1 - core)
    partners = [(1 - y) * 2 + 1 - x, y * 2 + 1 - x, (1 - y) * 2 + x]
    wanted = [1 - y, y, 1 - y]
    depth = lax.axis_size("dp")
    greet(
        [(sibling, True)] + [((place, z, core), True) for place in partners]
        + [((me, z + 1, core), z < depth - 1), ((me, z - 1, core), z > 0)]
    )
    sums = Mail(sum_send, sum_recv)
    grads = [
        (dgate_out, gate_land, gate_acc, gate_line), (dup_out, up_land, up_acc, up_line),
        (ddown_out, down_land, down_acc, down_line),
    ]

    def share(ref, shard, side):
        size = ref.shape[0] // (2 * depth)
        return pl.ds(pl.multiple_of((shard * 2 + side) * size, size), size)

    halves = [
        [
            sums.copy(ref.at[share(ref, shard, 1 - core)], land.at[shard], sibling)
            for shard in range(depth)
        ]
        for ref, land, _, _ in grads
    ]
    line = Line(sums, depth, [(acc, landing) for _, _, acc, landing in grads], depth - 2)

    def add_halves(item):
        ref, land, acc, _ = grads[item]
        for shard in range(depth):
            halves[item][shard].wait_recv()
            acc[shard] = (
                ref[share(ref, shard, core)].astype(F32) + land[shard].astype(F32)
            ).astype(BF16)
        line.send(0, item)

    mine = rows * blocks
    mail = Mail(head_send, head_recv)
    pairs = [(gate_ref, gate_w), (up_ref, up_w), (down_ref, down_w)]
    heads = [mail.copy(att_ref.at[1 - core], att_sib, sibling)]
    locals_ = [pltpu.make_async_copy(att_ref.at[core], att_own, local_sems.at[3])]
    for k, (source, target) in enumerate(pairs):
        size = source.shape[0]
        spot = target.at[pl.ds(pl.multiple_of(core * size, size), size)]
        heads.append(mail.copy(source, spot, sibling))
        locals_.append(pltpu.make_async_copy(source, spot, local_sems.at[k]))
    for copy in heads + locals_:
        copy.start()

    def dispatch(block, k, kind):
        source, target = ((send_ref, recv_ref), (gate_send, gate_recv))[kind]
        return pltpu.make_async_remote_copy(
            src_ref=source.at[block, wanted[k]],
            dst_ref=target.at[block, me],
            send_sem=send_sems.at[block, k, kind],
            recv_sem=recv_sems.at[block, k, kind],
            device_id=(partners[k], z, core),
            device_id_type=pl.DeviceIdType.MESH,
        )

    def giveback(block, k, kind):
        return pltpu.make_async_remote_copy(
            src_ref=result_ref.at[block, partners[k], kind],
            dst_ref=back_ref.at[block, me, kind],
            send_sem=back_send.at[block, k, kind],
            recv_sem=back_recv.at[block, k, kind],
            device_id=(partners[k], z, core),
            device_id_type=pl.DeviceIdType.MESH,
        )

    every = [(k, kind) for kind in range(KINDS) for k in range(3)]
    small_ref[...] = jnp.zeros_like(small_ref)
    wide_rows[...] = jnp.zeros_like(wide_rows)
    wide_rows[0:SMALL, :] = small_rows[...]
    heads[0].wait_recv()
    locals_[0].wait()
    keep = (residual_ref, mixed_ref, pm_ref, place_ref)
    spread_refs = (
        att_own, att_sib, x_ref, ctl_ref, w_own, w_sib, small_rows, wide_rows
    )

    @pl.loop(0, blocks)
    def _(block):
        spread_block(
            experts, routes, rows, block, spread_refs, (send_ref, gate_send),
            (recv_ref, gate_recv), keep,
        )
        for k, kind in every:
            dispatch(block, k, kind).start()

    for copy in heads[1:]:
        copy.wait_recv()
    for copy in locals_[1:]:
        copy.wait()

    @pl.loop(0, blocks)
    def _(block):
        for k, kind in every:
            dispatch(block, k, kind).wait_recv()

        def send(kind):
            for k in range(3):
                giveback(block, k, kind).start()

        expert_block(
            block, (recv_ref, gate_recv, g_rows), result_ref, back_ref, (gate_w, up_w, down_w),
            (hidden_ref, d_gate_ref, d_up_ref, d_rows_ref), send,
        )

    peers, capacity, width = recv_ref.shape[1:]
    total = blocks * peers * capacity
    step = 2 * LANES

    @pl.loop(0, width // step)
    def _(chunk):
        span = pl.ds(pl.multiple_of(chunk * step, step), step)
        lhs = recv_ref[:, :, :, span].reshape(total, step).T
        dgate_out[span, :] = dot(lhs, d_gate_ref[...]).astype(BF16)
        dup_out[span, :] = dot(lhs, d_up_ref[...]).astype(BF16)

    for copy in halves[0] + halves[1]:
        copy.start()

    @pl.loop(0, hidden_ref.shape[1] // step)
    def _(chunk):
        span = pl.ds(pl.multiple_of(chunk * step, step), step)
        lhs = hidden_ref[:, span].T
        ddown_out[span, :] = dot(lhs, d_rows_ref[...]).astype(BF16)

    for copy in halves[2]:
        copy.start()
    for item in range(3):
        add_halves(item)
    for step in range(1, depth - 2):
        for item in range(3):
            line.send_edge(step, item)

    @pl.loop(0, blocks)
    def _(block):
        for k, kind in every:
            giveback(block, k, kind).wait_recv()
        combine_block(
            experts, routes, rows, block, (g_ref, ctl_ref, small_rows, wide_rows),
            keep, back_ref, (out_ref, prev_ref, dres_ref, branch_ref), small_ref,
        )

        @pl.when(block == 0)
        def _():
            for step in range(depth - 3):
                for item in range(3):
                    line.take(step, item)
                    line.send(step + 1, item)

    for item in range(3):
        line.take(depth - 3, item)
    for copy in heads + halves[0] + halves[1] + halves[2]:
        copy.wait_send()
    line.close()
    for block in range(blocks):
        for k, kind in every:
            dispatch(block, k, kind).wait_send()
            giveback(block, k, kind).wait_send()


def expert_layer(
    experts, routes, rows, attended, x_all, cot_own, ctl, w_own, w_sib, small_all, w_gate,
    w_up, w_down, g_rows,
):
    mine, width = cot_own.shape
    blocks = mine // rows
    peers = lax.axis_size("ep")
    span = attended.shape[1]
    hidden = w_gate.shape[1]
    vmem = pl.BlockSpec(memory_space=pltpu.VMEM)
    total = blocks * peers * LANES
    grads = [(2 * w.shape[0], w.shape[1]) for w in (w_gate, w_up, w_down)]
    depth = lax.axis_size("dp")
    parts = [(dims[0] // (2 * depth), dims[1]) for dims in grads]
    sums = 3 * depth + 6 * (depth - 2)
    return pl.pallas_call(
        functools.partial(layer_kernel, experts, routes, rows, blocks),
        in_specs=[vmem] * 11,
        out_specs=[vmem] * 8,
        out_shape=[
            shape((blocks, rows, width), BF16), shape((blocks, 8, rows), F32),
            shape((mine, width), F32), shape((mine, width), BF16), shape((SMALL, width), F32),
        ]
        + [shape((depth,) + part, BF16) for part in parts],
        scratch_shapes=[pltpu.VMEM(dims, BF16) for dims in grads]
        + [pltpu.VMEM((depth,) + part, BF16) for part in parts]
        + [pltpu.VMEM((2, depth - 2) + part, BF16) for part in parts]
        + [pltpu.VMEM((LANES, width), BF16)]
        + [pltpu.VMEM((mine, span), BF16)] * 2
        + [pltpu.VMEM(dims, BF16) for dims in grads]
        + [
            pltpu.VMEM((mine, width), F32), pltpu.VMEM((mine, width), BF16),
            pltpu.VMEM((mine, LANES), F32), pltpu.VMEM((mine, experts * LANES), BF16),
            pltpu.VMEM((blocks, experts, LANES, width), BF16),
            pltpu.VMEM((blocks, experts, 8, LANES), F32), pltpu.VMEM((blocks, peers, 8, LANES), F32),
            pltpu.VMEM((blocks, peers, LANES, width), BF16),
        ]
        + [pltpu.VMEM((blocks, peers, KINDS, LANES, width), BF16)] * 2
        + [pltpu.VMEM((total, hidden), BF16)] * 3
        + [pltpu.VMEM((total, width), BF16)]
        + [
            pltpu.SemaphoreType.DMA((4,)), pltpu.SemaphoreType.DMA((4,)),
            pltpu.SemaphoreType.DMA((4,)),
        ]
        + [pltpu.SemaphoreType.DMA((blocks, 3, KINDS))] * 4
        + [pltpu.SemaphoreType.DMA((sums,))] * 2,
        compiler_params=pltpu.CompilerParams(
            collective_id=2, has_side_effects=True, vmem_limit_bytes=62 * 1024 * 1024
        ),
        name="expert_layer",
    )(
        attended.reshape(2, mine, span), x_all, cot_own, ctl, w_own, w_sib, small_all,
        w_gate, w_up, w_down, g_rows,
    )


class Line:
    def __init__(self, mail, depth, slots, steps):
        self.depth = depth
        self.slots = slots
        self.place = lax.axis_index("dp")
        y, x, z, core = position()
        self.copies = {}
        for way in range(2):
            step_to = 1 if way == 0 else -1
            device = (y * 2 + x, z + step_to, core)
            for step in range(steps):
                for item, (acc, landing) in enumerate(slots):
                    shard = self.shard(way, step)
                    safe = jnp.clip(shard, 0, depth - 1)
                    self.copies[way, step, item] = mail.copy(
                        acc.at[safe], landing.at[way, step], device
                    )

    def shard(self, way, step):
        if way == 0:
            return self.place + self.depth - 1 - step
        return self.place - (self.depth - 1 - step)

    def edge(self, way):
        return self.place == (0 if way == 0 else self.depth - 1)

    def sends(self, way, step):
        shard = self.shard(way, step)
        if way == 0:
            return (shard <= self.depth - 1) & (self.place < self.depth - 1)
        return (shard >= 0) & (self.place > 0)

    def gets(self, way, step):
        if way == 0:
            return (self.place > 0) & (self.shard(way, step + 1) <= self.depth - 1)
        return (self.place < self.depth - 1) & (self.shard(way, step + 1) >= 0)

    def send(self, step, item):
        for way in range(2):
            wanted = self.sends(way, step)
            if step > 0:
                wanted = wanted & jnp.logical_not(self.edge(way))

            @pl.when(wanted)
            def _():
                self.copies[way, step, item].start()

    def send_edge(self, step, item):
        for way in range(2):

            @pl.when(self.sends(way, step) & self.edge(way))
            def _():
                self.copies[way, step, item].start()

    def take(self, step, item):
        acc, landing = self.slots[item]
        for way in range(2):
            shard = jnp.clip(self.shard(way, step + 1), 0, self.depth - 1)

            @pl.when(self.gets(way, step))
            def _():
                self.copies[way, step, item].wait_recv()
                acc[shard] = (
                    acc[shard].astype(F32) + landing[way, step].astype(F32)
                ).astype(BF16)

    def finish(self, item, store):
        acc, landing = self.slots[item]
        store(acc[self.place].astype(F32))
        for way in range(2):

            @pl.when(self.gets(way, self.depth - 2))
            def _():
                self.copies[way, self.depth - 2, item].wait_recv()
                store(landing[way, self.depth - 2].astype(F32), True)

    def close(self):
        for (way, step, item), copy in self.copies.items():

            @pl.when(self.sends(way, step))
            def _():
                copy.wait_send()


class Final:
    def __init__(self, mail, depth, slots):
        self.place = lax.axis_index("dp")
        self.depth = depth
        self.slots = slots
        y, x, z, core = position()
        self.copies = {}
        for way in range(2):
            target = z + (1 if way == 0 else -1)
            safe = jnp.clip(target, 0, depth - 1)
            for item, (acc, landing, _) in enumerate(slots):
                self.copies[way, item] = mail.copy(
                    acc.at[safe], landing.at[way], (y * 2 + x, target, core)
                )

    def sends(self, way):
        return self.place < self.depth - 1 if way == 0 else self.place > 0

    def gets(self, way):
        return self.place > 0 if way == 0 else self.place < self.depth - 1

    def start(self):
        for (way, item), copy in self.copies.items():

            @pl.when(self.sends(way))
            def _():
                copy.start()

    def finish(self, item):
        _, landing, result = self.slots[item]
        for way in range(2):

            @pl.when(self.gets(way))
            def _():
                self.copies[way, item].wait_recv()
                result[0] = result[0] + landing[way].astype(F32)

    def close(self):
        for (way, item), copy in self.copies.items():

            @pl.when(self.sends(way))
            def _():
                copy.wait_send()


class Plane:
    def __init__(self, mail, source, buffers, total):
        y, x, z, core = position()
        self.place = y, x
        self.source = source
        self.buffers = buffers
        self.total = total
        y1_land, x1_land, y1_acc, x1_acc, x2_land, y2_land = buffers
        half = x2_land.shape[0]
        self.low = pl.ds(0, half)
        self.high = pl.ds(half, half)
        across = (y * 2 + 1 - x, z, core)
        along = ((1 - y) * 2 + x, z, core)
        self.first = [
            mail.copy(source.at[1 - y, :, self.low], y1_land, along),
            mail.copy(source.at[:, 1 - x, self.high], x1_land, across),
        ]
        self.second = [
            mail.copy(y1_acc.at[1 - x], x2_land, across),
            mail.copy(x1_acc.at[1 - y], y2_land, along),
        ]

    def start(self):
        for copy in self.first:
            copy.start()

    def middle(self):
        y, x = self.place
        y1_land, x1_land, y1_acc, x1_acc, _, _ = self.buffers
        self.first[0].wait_recv()
        for k in range(2):
            y1_acc[k] = (
                self.source[y, k, self.low].astype(F32) + y1_land[k].astype(F32)
            ).astype(BF16)
        self.second[0].start()
        self.first[1].wait_recv()
        for k in range(2):
            x1_acc[k] = (
                self.source[k, x, self.high].astype(F32) + x1_land[k].astype(F32)
            ).astype(BF16)
        self.second[1].start()

    def end(self):
        y, x = self.place
        _, _, y1_acc, x1_acc, x2_land, y2_land = self.buffers
        shards, size = self.total.shape[0] // 2, self.total.shape[1]
        self.second[0].wait_recv()
        for shard in range(shards):
            part = pl.ds(shard * size, size)
            self.total[shard] = (
                y1_acc[x, part].astype(F32) + x2_land[part].astype(F32)
            ).astype(BF16)
        self.second[1].wait_recv()
        for shard in range(shards):
            part = pl.ds(shard * size, size)
            self.total[shards + shard] = (
                x1_acc[y, part].astype(F32) + y2_land[part].astype(F32)
            ).astype(BF16)

    def close(self):
        for copy in self.first + self.second:
            copy.wait_send()


def back_pair(
    pair, rows, reach, span, qkv_ref, datt_ref, segc_ref, segr_ref, lse_ref, dqkv_ref,
    dk_sum, dv_sum,
):
    length = qkv_ref.shape[0]
    at_q, at_k, at_v = (
        pl.ds(pl.multiple_of(part * span + pair * LANES, LANES), LANES) for part in range(3)
    )
    dk_sum[...] = jnp.zeros_like(dk_sum)
    dv_sum[...] = jnp.zeros_like(dv_sum)
    keys_turned = qkv_ref[:, at_k].T
    for block in range(length // rows):
        start, width = key_span(block, rows, reach)
        here = pl.ds(block * rows, rows)
        there = pl.ds(start, width)
        queries = qkv_ref[here, at_q]
        grads = datt_ref[here, at_q]
        keys = qkv_ref[there, at_k]
        values = qkv_ref[there, at_v]
        seg_k = segc_ref[there, 0:1]
        seg_q = segr_ref[0:1, here]
        key_pos = start + lax.broadcasted_iota(jnp.int32, (width, rows), 0)
        query_pos = block * rows + lax.broadcasted_iota(jnp.int32, (width, rows), 1)
        allowed = (seg_q == seg_k) & (key_pos <= query_pos)
        lane = lax.broadcasted_iota(jnp.int32, (rows, LANES), 1)
        dq_parts = []
        for head in range(2):
            mine = (lane // HEAD) == head
            head_q = jnp.where(mine, queries, 0)
            head_g = jnp.where(mine, grads, 0)
            log_total = lse_ref[pair, head : head + 1, here]
            scores = dot(keys, head_q, ((1,), (1,))) * 0.125
            probs = jnp.exp(jnp.where(allowed, scores, NEG) - log_total)
            d_probs = dot(values, head_g, ((1,), (1,)))
            delta = jnp.sum(probs * d_probs, axis=0, keepdims=True)
            d_scores = (probs * (d_probs - delta)).astype(BF16)
            dv_sum[there, :] += dot(probs.astype(BF16), head_g)
            dk_sum[there, :] += dot(d_scores, head_q)
            turned = keys_turned[head * HEAD : (head + 1) * HEAD, start : start + width]
            dq_parts.append(dot(turned, d_scores))
        dq = jnp.concatenate(dq_parts, axis=0).T * 0.125
        dqkv_ref[here, at_q] = dq.astype(BF16)
    dqkv_ref[:, at_k] = (dk_sum[...] * 0.125).astype(BF16)
    dqkv_ref[:, at_v] = dv_sum[...].astype(BF16)


def back_kernel(depth, rows, reach, *refs):
    (
        gate_any, up_any, down_any, branch_any, wout_any, att_any, qkv_any, segc_any, normed_any,
        wqkv_any, x_any, dres_any, out_ref, prev_ref, lse_ref, segr_ref, small_ref, small_rows,
        gate_out, up_out, down_out, qkv_out, wout_out, small_out, out_home, dtok_home, prev_home,
        gate_land, up_land, down_land, gate_own, up_own, down_own, branch_ref, wout_ref, att_ref, qkv_ref, segc_ref, normed_ref, wqkv_ref, x_ref, dres_ref,
        normed_turned, datt_ref, turned_ref, dqkv_ref, dk_sum, dv_sum, dn_send, dn_recv, dtok_ref,
        dense_ref, y1_land, x1_land, y1_acc, x1_acc, x2_land, y2_land, dense_acc, dense_line,
        tail_ref, ty1_land, tx1_land, ty1_acc, tx1_acc, tx2_land, ty2_land, tail_acc, tail_line,
        dense_sum, dense_sib, tail_sum, tail_sib, small_wide,
        send_sems, recv_sems, local_sems,
    ) = refs
    y, x, z, core = position()
    sibling = (y * 2 + x, z, 1 - core)
    across = (y * 2 + 1 - x, z, core)
    along = ((1 - y) * 2 + x, z, core)
    moved = y != core
    near = ((1 - y) * 2 + x, z, 1 - core)
    far = (core * 2 + 1 - x, z, y)
    greet(
        [
            (sibling, True), (across, True), (along, True),
            (near, moved), (far, moved),
            ((y * 2 + x, z + 1, core), z < depth - 1), ((y * 2 + x, z - 1, core), z > 0),
        ]
    )
    mail = Mail(send_sems, recv_sems)
    length, width = normed_ref.shape
    mine = length // 2
    span = wout_ref.shape[0]
    pairs = span // LANES
    own_rows = pl.ds(pl.multiple_of(core * mine, mine), mine)
    final = Final(
        mail, depth,
        [
            (gate_any, gate_land, gate_out), (up_any, up_land, up_out),
            (down_any, down_land, down_out),
        ],
    )
    branch_copy = mail.copy(branch_any, branch_ref.at[own_rows], sibling)
    loads = [
        pltpu.make_async_copy(source, target, local_sems.at[k])
        for k, (source, target) in enumerate(
            [
                (gate_any.at[z], gate_own), (up_any.at[z], up_own),
                (down_any.at[z], down_own), (branch_any, branch_ref.at[own_rows]),
                (normed_any, normed_ref), (att_any, att_ref), (wout_any, wout_ref),
                (segc_any, segc_ref), (qkv_any, qkv_ref), (wqkv_any, wqkv_ref),
                (x_any.at[own_rows], x_ref), (dres_any, dres_ref),
            ]
        )
    ]
    homes = [(out_ref, out_home), (prev_ref, prev_home), (dtok_ref, dtok_home)]
    nears = [mail.copy(a.at[x], b.at[x], near) for a, b in homes]
    fars = [mail.copy(a.at[1 - x], b.at[x], far) for a, b in homes]
    stays = [
        pltpu.make_async_copy(a.at[x], b.at[x], local_sems.at[len(loads) + k])
        for k, (a, b) in enumerate(homes)
    ]

    def go_near(k):
        @pl.when(moved)
        def _():
            nears[k].start()

        @pl.when(jnp.logical_not(moved))
        def _():
            stays[k].start()

    half_copy = mail.copy(turned_ref.at[1 - core], dense_ref.at[0, core], sibling)
    planes = [
        Plane(
            mail, dense_ref.at[c],
            [b.at[c] for b in (y1_land, x1_land, y1_acc, x1_acc, x2_land, y2_land)],
            dense_acc.at[c],
        )
        for c in range(pairs + 1)
    ] + [
        Plane(
            mail, tail_ref, (ty1_land, tx1_land, ty1_acc, tx1_acc, tx2_land, ty2_land), tail_acc
        )
    ]
    dense = Line(
        mail, depth,
        [(dense_acc.at[c], dense_line.at[c]) for c in range(pairs + 1)] + [(tail_acc, tail_line)],
        depth - 1,
    )
    chunks = pairs + 2
    size = tail_sum.shape[0]
    half = size // 2
    other = pl.ds(pl.multiple_of((1 - core) * half, 8), half)
    ours = pl.ds(pl.multiple_of(core * half, 8), half)
    sums = [(dense_sum.at[c], dense_sib.at[c]) for c in range(pairs + 1)] + [(tail_sum, tail_sib)]
    lasts = [mail.copy(a.at[other], b, sibling) for a, b in sums]
    dn_copies = [mail.copy(dn_send.at[b], dn_recv.at[b], sibling) for b in range(2)]

    branch_copy.start()
    final.start()
    for copy in loads[3:] + loads[:3]:
        copy.start()
    fars[0].start()
    fars[1].start()
    go_near(0)
    go_near(1)

    loads[4].wait()
    normed_turned[...] = normed_ref[...].T
    for k in (3, 5, 6, 7):
        loads[k].wait()
    branch_copy.wait_recv()

    @pl.loop(0, length // rows)
    def _(block):
        here = pl.ds(pl.multiple_of(block * rows, rows), rows)
        valid = (segc_ref[here, 0:1] != SEGS - 1.0).astype(F32)
        datt_ref[here, :] = (
            dot(branch_ref[here, :], wout_ref[...], ((1,), (1,))) * valid
        ).astype(BF16)

    att_turned = att_ref[...].T
    for side in range(2):
        part = dot(att_turned, branch_ref[:, side * span : (side + 1) * span]).astype(BF16)
        turned_ref[side] = part.reshape(turned_ref.shape[1:])
    half_copy.start()
    dense_ref[0, core] = turned_ref[core]
    for k in (8, 9):
        loads[k].wait()
    small_wide[...] = jnp.zeros_like(small_wide)

    quarter = width // 4

    @pl.loop(0, pairs)
    def _(pair):
        back_pair(
            pair, rows, reach, span, qkv_ref, datt_ref, segc_ref, segr_ref, lse_ref, dqkv_ref,
            dk_sum, dv_sum,
        )
        columns = [
            pl.ds(pl.multiple_of(part * span + pair * LANES, LANES), LANES) for part in range(3)
        ]

        @pl.loop(0, 4)
        def _(fourth):
            here = pl.ds(pl.multiple_of(fourth * quarter, quarter), quarter)
            d_pair = jnp.concatenate([dqkv_ref[:, at] for at in columns], axis=1)
            weights = jnp.concatenate([wqkv_ref[here, at] for at in columns], axis=1)
            grads = dot(normed_turned[here, :], d_pair)
            dense_ref[1 + pair, fourth // 2, fourth % 2] = grads.astype(BF16)
            gain = jnp.sum(grads * weights.astype(F32), axis=1, keepdims=True)
            lane = lax.broadcasted_iota(jnp.int32, (quarter, LANES), 1)
            small_wide[here, :] += jnp.where(lane == SMALL - 1, gain, 0.0)

        for now in range(pairs):

            @pl.when(pair == now)
            def _():
                planes[now + 1].start()
                if now == 0:
                    half_copy.wait_recv()
                    planes[0].start()
                if now >= 1:
                    planes[now - 1].middle()
                if now >= 2:
                    planes[now - 2].end()
                    dense.send(0, now - 2)
                    for step in range(1, depth - 1):
                        dense.send_edge(step, now - 2)

    small_all = small_rows[...].astype(F32)
    gain_column = column(widen(small_all), SMALL - 2)
    lane = lax.broadcasted_iota(jnp.int32, (width, LANES), 1)
    small_grads = jnp.where(
        lane < SMALL - 1, widen(small_ref[...]), small_wide[...] / gain_column
    )
    tail_ref[...] = small_grads.astype(BF16).reshape(tail_ref.shape)
    planes[chunks - 1].start()

    def partial(start, step):
        b = 1 - x if step == 0 else x
        here = pl.ds(pl.multiple_of(start * mine + b * rows, rows), rows)
        return b, dot(dqkv_ref[here, :], wqkv_ref[...], ((1,), (1,)))

    def launch(c):
        planes[c].end()
        dense.send(0, c)
        for step in range(1, depth - 1):
            dense.send_edge(step, c)

    for step in range(2):
        b, value = partial(1 - core, step)
        dn_send[step] = value.astype(BF16)
        dn_copies[step].start()
    planes[pairs - 1].middle()
    launch(pairs - 2)
    planes[pairs].middle()
    launch(pairs - 1)
    planes[pairs + 1].middle()
    loads[10].wait()
    loads[11].wait()
    gain_row = small_all[SMALL - 2 : SMALL - 1, :]
    for step in range(2):
        b, value = partial(core, step)
        here = pl.ds(pl.multiple_of(b * rows, rows), rows)
        values = x_ref[here, :].astype(F32)
        dn_copies[step].wait_recv()
        d_normed = value + dn_recv[step].astype(F32)
        inverse = lax.rsqrt(jnp.mean(values * values, axis=-1, keepdims=True) + NORM_EPS)
        scaled = d_normed * gain_row
        mean = jnp.mean(scaled * values, axis=-1, keepdims=True)
        result = dres_ref[here, :] + inverse * scaled
        result = result - values * (inverse * inverse * inverse * mean)
        dtok_ref[b] = result.astype(BF16)
        if step == 0:
            fars[2].start()
            launch(pairs)
            launch(pairs + 1)
        else:
            go_near(2)
    for item, (own, result) in enumerate(
        ((gate_own, gate_out), (up_own, up_out), (down_own, down_out))
    ):
        loads[item].wait()
        result[0] = own[...].astype(F32)
        final.finish(item)
    for step in range(depth - 2):
        for c in range(chunks):
            dense.take(step, c)
            dense.send(step + 1, c)
    for c, (total, _) in enumerate(sums):

        def store(value, add=False):
            total[...] = total[...] + value if add else value

        dense.finish(c, store)
        lasts[c].start()
    for c, (total, land) in enumerate(sums):
        own = total[ours]
        lasts[c].wait_recv()
        theirs = land[...]
        if c == 0:
            for side, value in ((core, own), (1 - core, theirs)):
                wout_out[:, pl.ds(pl.multiple_of(side * span, LANES), span)] = value
        elif c <= pairs:
            for part in range(3):
                for side, value in ((core, own), (1 - core, theirs)):
                    at = part * 2 * span + side * span + (c - 1) * LANES
                    qkv_out[:, pl.ds(pl.multiple_of(at, LANES), LANES)] = value[
                        :, part * LANES : (part + 1) * LANES
                    ]
        else:
            small_out[...] = own + theirs
    for copy in [branch_copy, half_copy] + lasts + dn_copies:
        copy.wait_send()
    for plane in planes:
        plane.close()
    final.close()
    dense.close()
    for copy in fars:
        copy.wait()

    @pl.when(moved)
    def _():
        for copy in nears:
            copy.wait()

    @pl.when(jnp.logical_not(moved))
    def _():
        for copy in stays:
            copy.wait()


def back_all(
    grad_gate, grad_up, grad_down, d_branch, w_out, attended, qkv, seg_col, normed, qkv_weight,
    x_all, d_residual, block_out, d_prev, lse, seg_row, small, small_all,
):
    depth = lax.axis_size("dp")
    length, width = x_all.shape
    mine = length // 2
    span = width // 2
    rows = block_out.shape[1]
    groups = span // LANES + 1
    wide = 3 * LANES
    quarter = width // 4
    size = quarter // depth
    parts = [grad.shape[1:] for grad in (grad_gate, grad_up, grad_down)]
    vmem = pl.BlockSpec(memory_space=pltpu.VMEM)
    anywhere = pl.BlockSpec(memory_space=pl.ANY)
    homes = [block_out.shape, block_out.shape, d_prev.shape]
    kinds = [block_out.dtype, BF16, d_prev.dtype]
    steps = 2 * (depth - 1)
    copies = 6 + 2 + 6 + (groups + 1) * (4 + steps + 1) + 2

    def plane_buffers(lead, columns):
        return [
            pltpu.VMEM(lead + dims + (columns,), BF16)
            for dims in (
                [(2, 2, quarter)] + [(2, quarter // 2)] * 4 + [(quarter // 2,)] * 2
                + [(depth, size), (2, depth - 1, size)]
            )
        ]

    return pl.pallas_call(
        functools.partial(back_kernel, depth, rows, length // 2),
        in_specs=[anywhere] * 12 + [vmem] * 6,
        out_specs=[vmem] * 6 + [anywhere] * 3,
        out_shape=[shape((1,) + part, F32) for part in parts]
        + [shape((size // 2, 6 * span), F32), shape((size // 2, width), F32)]
        + [shape((size // 2, LANES), F32)]
        + [shape(dims, kind) for dims, kind in zip(homes, kinds)],
        scratch_shapes=[pltpu.VMEM((2,) + part, BF16) for part in parts]
        + [pltpu.VMEM(part, BF16) for part in parts]
        + [
            pltpu.VMEM((length, width), BF16), pltpu.VMEM((span, width), BF16),
            pltpu.VMEM((length, span), BF16), pltpu.VMEM((length, 3 * span), BF16),
            pltpu.VMEM((length, LANES), F32), pltpu.VMEM((length, width), BF16),
            pltpu.VMEM((width, 3 * span), BF16), pltpu.VMEM((mine, width), BF16),
            pltpu.VMEM((mine, width), F32), pltpu.VMEM((width, length), BF16),
            pltpu.VMEM((length, span), BF16), pltpu.VMEM((2, 2, quarter, span), BF16),
            pltpu.VMEM((length, 3 * span), BF16), pltpu.VMEM((length, LANES), F32),
            pltpu.VMEM((length, LANES), F32), pltpu.VMEM((2, rows, width), BF16),
            pltpu.VMEM((2, rows, width), BF16), pltpu.VMEM((2, rows, width), BF16),
        ]
        + plane_buffers((groups,), wide)
        + plane_buffers((), LANES)
        + [
            pltpu.VMEM((groups, size, wide), F32), pltpu.VMEM((groups, size // 2, wide), F32),
            pltpu.VMEM((size, LANES), F32), pltpu.VMEM((size // 2, LANES), F32),
            pltpu.VMEM((width, LANES), F32),
            pltpu.SemaphoreType.DMA((copies,)),
            pltpu.SemaphoreType.DMA((copies,)),
            pltpu.SemaphoreType.DMA((15,)),
        ],
        compiler_params=pltpu.CompilerParams(
            collective_id=1, has_side_effects=True, vmem_limit_bytes=62 * 1024 * 1024
        ),
        name="back_all",
    )(
        grad_gate, grad_up, grad_down, d_branch, w_out, attended, qkv, seg_col, normed, qkv_weight, x_all, d_residual,
        block_out, d_prev, lse, seg_row, small, small_all,
    )


def deliver_kernel(
    routes,
    out_ref, dtok_ref, prev_ref, qkv_ref, wout_ref, small_ref, gate_ref, up_ref, down_ref,
    out_end, tokens_end, prev_end, gain_a_end, qkv_end, wout_end, gain_m_end, router_end,
    cproj_end, cvec_end, gate_end, up_end, down_end,
):
    for source, target in (
        (out_ref, out_end), (qkv_ref, qkv_end), (wout_ref, wout_end), (gate_ref, gate_end),
        (up_ref, up_end), (down_ref, down_end),
    ):
        target[...] = source[...]
    tokens_end[...] = dtok_ref[...].astype(F32)
    for m in range(2):
        for route in range(routes):
            prev_end[route, m : m + 1, :] = prev_ref[m, route : route + 1, :]
    count = small_ref.shape[0]
    turned = widen(small_ref[...])
    router_end[...] = turned[0:routes, 0:count]
    cproj_end[...] = turned[8:12, 0:count]
    cvec_end[...] = turned[12:14, 0:count]
    gain_m_end[...] = turned[14:15, 0:count].reshape(count)
    gain_a_end[...] = turned[15:16, 0:count].reshape(count)


def deliver(routes, out, dtok, prev, qkv, wout, small, gate, up, down):
    count = small.shape[0]
    vmem = pl.BlockSpec(memory_space=pltpu.VMEM)
    return pl.pallas_call(
        functools.partial(deliver_kernel, routes),
        in_specs=[vmem] * 9,
        out_specs=[vmem] * 13,
        out_shape=[
            shape(out.shape, BF16), shape(dtok.shape, F32), shape((routes, 2, prev.shape[2]), F32),
            shape((count,), F32), shape(qkv.shape, F32), shape(wout.shape, F32),
            shape((count,), F32), shape((routes, count), F32), shape((4, count), F32),
            shape((2, count), F32), shape(gate.shape, F32), shape(up.shape, F32),
            shape(down.shape, F32),
        ],
        compiler_params=params(),
        cost_estimate=cost(1e6, 8e6),
        name="deliver",
    )(out, dtok, prev, qkv, wout, small, gate, up, down)


def one_chip(
    tokens,
    prev_logits,
    segments,
    routes,
    cotangent,
    gain_attn,
    w_qkv,
    w_out,
    gain_moe,
    w_router,
    const_proj,
    const_vec,
    w_gate,
    w_up,
    w_down,
):
    rows = tokens.shape[1]
    route_count = w_router.shape[1]
    experts = route_count - 4
    (
        x_all, cot_own, ctl, normed, qkv, attended, lse, small_all, qkv_weight, out_sib,
        seg_col, seg_row, g_rows,
    ) = gather_all(
        experts, tokens, cotangent, w_qkv, w_out, prev_logits, routes, segments, w_router, const_proj,
        const_vec, gain_attn, gain_moe,
    )
    (
        block_out, d_prev, d_residual, d_branch, small, grad_gate, grad_up, grad_down,
    ) = expert_layer(
        experts, route_count, rows, attended, x_all, cot_own, ctl, w_out, out_sib, small_all,
        w_gate[0], w_up[0], w_down[0], g_rows,
    )

    (
        share_gate, share_up, share_down, share_qkv, share_out, share_small, out_home, dtok_home,
        prev_home,
    ) = back_all(
        grad_gate, grad_up, grad_down, d_branch, w_out, attended, qkv, seg_col, normed,
        qkv_weight, x_all, d_residual, block_out, d_prev, lse, seg_row, small, small_all,
    )
    (
        block_out, grad_tokens, grad_prev, gain_a, grad_qkv, grad_out, gain_m, grad_router,
        grad_cproj, grad_cvec, grad_gate, grad_up, grad_down,
    ) = deliver(
        route_count, out_home, dtok_home, prev_home, share_qkv, share_out, share_small,
        share_gate, share_up, share_down,
    )
    return (
        block_out, grad_tokens, jnp.transpose(grad_prev, (1, 2, 0)), gain_a, grad_qkv, grad_out,
        gain_m, grad_router.T, grad_cproj.T, grad_cvec.T, grad_gate, grad_up, grad_down,
    )


def suits(mesh, tokens, w_router, w_gate):
    peers = mesh.shape["ep"]
    rows = tokens.shape[1] // peers
    micro = tokens.shape[0] // (mesh.shape["dp"] * mesh.shape["fs"])
    routes = w_router.shape[1]
    return (
        peers == 4
        and mesh.shape["fs"] == 2
        and micro == 2
        and mesh.shape["dp"] == 4
        and (routes - 4) * 2 == peers
        and 3 * rows // routes == LANES
        and tokens.shape[2] % (2 * LANES) == 0
    )


def solution(mesh):
    placed = (
        P(("dp", "fs"), "ep", None),
        P(("dp", "fs"), "ep", None),
        P(("dp", "fs"), None),
        P(("dp", "fs"), "ep", None),
        P(("dp", "fs"), "ep", None),
        P("fs"),
        P("fs", None),
        P("fs", None),
        P("fs"),
        P("fs", None),
        P("fs", None),
        P("fs", None),
        P("ep", "fs", None),
        P("ep", "fs", None),
        P("ep", "fs", None),
    )
    def layer(*arrays):
        fits = suits(mesh, arrays[0], arrays[9], arrays[12])
        return mapped(one_chip if fits else shards)(*arrays)

    def mapped(body):
        return jax.shard_map(
            body,
            mesh=mesh,
            in_specs=placed,
            out_specs=(
                P(("dp", "fs"), "ep", None),
                P(("dp", "fs"), "ep", None),
                P(("dp", "fs"), "ep", None),
                P(("ep", "dp", "fs")),
                P(("ep", "dp", "fs"), None),
                P(("ep", "dp", "fs"), None),
                P(("ep", "dp", "fs")),
                P(("ep", "dp", "fs"), None),
                P(("ep", "dp", "fs"), None),
                P(("ep", "dp", "fs"), None),
                P("ep", ("dp", "fs"), None),
                P("ep", ("dp", "fs"), None),
                P("ep", ("dp", "fs"), None),
            ),
            check_vma=False,
        )

    return layer
```

```python
import functools

import jax
import jax.numpy as jnp
from jax import lax
from jax.experimental import pallas as pl
from jax.experimental.pallas import tpu as pltpu
from jax.sharding import PartitionSpec as P

HEAD = 64
SEGS = 4


NORM_EPS = 1e-06
MASK_FILL = -1e30
HIGHEST = lax.Precision.HIGHEST


def rms_scale(values, gains):
    inverse = lax.rsqrt(jnp.mean(values * values, axis=-1, keepdims=True) + NORM_EPS)
    return values * inverse * gains


def small_softmax(logit_rows):
    largest = jnp.max(logit_rows, axis=-1, keepdims=True)
    powers = jnp.exp(logit_rows - largest)
    return powers / jnp.sum(powers, axis=-1, keepdims=True)


def add_tuple(first_tuple, second_tuple):
    if first_tuple is None:
        return second_tuple
    return tuple(
        (first_term + second_term for first_term, second_term in zip(first_tuple, second_tuple))
    )


def shards(
    tokens,
    prev_logits,
    segments,
    routes,
    cotangent,
    gain_attn,
    w_qkv,
    w_out,
    gain_moe,
    w_router,
    const_proj,
    const_vec,
    w_gate,
    w_up,
    w_down,
):
    micro_count, row_count, model_width = tokens.shape
    head_count = model_width // HEAD
    peer_count = lax.axis_size("ep")
    my_index = lax.axis_index("ep")
    route_count = w_router.shape[1]
    expert_count = route_count - 4
    half_count = peer_count // expert_count
    capacity = (3 * row_count // route_count + 7) // 8 * 8
    seq_length = row_count * peer_count
    slot_count = expert_count * capacity
    pos_all = jnp.arange(seq_length, dtype=jnp.int32)
    pos_mine = my_index * row_count + jnp.arange(row_count, dtype=jnp.int32)
    expert_ids = jnp.arange(expert_count, dtype=jnp.int32)
    slot_ids = jnp.arange(slot_count, dtype=jnp.int32)
    route_ids = jnp.arange(route_count, dtype=jnp.int32)
    layer_outputs = []
    input_grads = []
    prev_grads = []
    dense_acc = None
    expert_acc = None
    for step_index in range(micro_count):
        gathered = (
            lax.all_gather(w_qkv, "fs", axis=0, tiled=True),
            lax.all_gather(w_out, "fs", axis=0, tiled=True),
            lax.all_gather(w_router, "fs", axis=0, tiled=True),
            lax.all_gather(const_proj, "fs", axis=0, tiled=True),
            lax.all_gather(const_vec, "fs", axis=0, tiled=True),
            lax.all_gather(gain_attn, "fs", axis=0, tiled=True),
            lax.all_gather(gain_moe, "fs", axis=0, tiled=True),
            lax.all_gather(w_gate, "fs", axis=1, tiled=True),
            lax.all_gather(w_up, "fs", axis=1, tiled=True),
            lax.all_gather(w_down, "fs", axis=1, tiled=True),
        )
        (
            qkv_weight,
            out_weight,
            router_weight,
            cproj_weight,
            cvec_weight,
            attn_gain,
            moe_gain,
            gate_weight,
            up_weight,
            down_weight,
        ) = gathered
        gate_weight = gate_weight[0]
        up_weight = up_weight[0]
        down_weight = down_weight[0]
        attn_gain = attn_gain.astype(jnp.float32)
        moe_gain = moe_gain.astype(jnp.float32)
        router_float = router_weight.astype(jnp.float32)
        cproj_float = cproj_weight.astype(jnp.float32)
        cvec_float = cvec_weight.astype(jnp.float32)
        token_rows = tokens[step_index].astype(jnp.float32)
        seg_all = segments[step_index]
        seg_mine = lax.dynamic_slice_in_dim(seg_all, my_index * row_count, row_count)
        allowed = (seg_mine[:, None] == seg_all[None, :]) & (pos_all[None, :] <= pos_mine[:, None])
        valid_rows = (seg_mine != SEGS - 1).astype(jnp.float32)[:, None]
        normed = rms_scale(token_rows, attn_gain).astype(jnp.bfloat16)
        qkv_rows = jnp.dot(normed, qkv_weight, preferred_element_type=jnp.float32).astype(
            jnp.bfloat16
        )
        queries = qkv_rows[:, :model_width].reshape(row_count, head_count, HEAD)
        keys_local = qkv_rows[:, model_width : 2 * model_width]
        values_local = qkv_rows[:, 2 * model_width :]
        keys_all, values_all = (
            lax.all_gather(keys_local, "ep", axis=0, tiled=True),
            lax.all_gather(values_local, "ep", axis=0, tiled=True),
        )
        key_heads = keys_all.reshape(seq_length, head_count, HEAD)
        value_heads = values_all.reshape(seq_length, head_count, HEAD)
        scores = (
            jnp.einsum("qhd,khd->hqk", queries, key_heads, preferred_element_type=jnp.float32)
            * 0.125
        )
        scores = jnp.where(allowed[None], scores, MASK_FILL)
        largest = jnp.max(scores, axis=-1, keepdims=True)
        powers = jnp.exp(scores - largest)
        row_total = jnp.sum(powers, axis=-1, keepdims=True)
        log_total = largest + jnp.log(row_total)
        attn_probs = powers / row_total
        attended = jnp.einsum(
            "hqk,khd->qhd",
            attn_probs.astype(jnp.bfloat16),
            value_heads,
            preferred_element_type=jnp.float32,
        ).reshape(row_count, model_width)
        attended = (attended * valid_rows).astype(jnp.bfloat16)
        residual = token_rows + jnp.dot(attended, out_weight, preferred_element_type=jnp.float32)
        mixed = rms_scale(residual, moe_gain).astype(jnp.bfloat16)
        mixed_float = mixed.astype(jnp.float32)
        logits = (
            jnp.dot(mixed, router_weight, preferred_element_type=jnp.float32)
            + prev_logits[step_index]
        )
        router_probs = small_softmax(logits)
        route_rows = routes[step_index]
        choose = (route_rows[:, :, None] == route_ids[None, None, :]).astype(jnp.float32)
        gate_values = jnp.sum(choose * router_probs[:, None, :], axis=-1)
        const_logits = jnp.dot(mixed, cproj_weight, preferred_element_type=jnp.float32)
        mixings = []
        const_outs = []
        for const_index in range(2):
            mixing = small_softmax(const_logits[:, 2 * const_index : 2 * const_index + 2])
            mixings.append(mixing)
            const_outs.append(
                mixing[:, :1] * mixed_float + mixing[:, 1:] * cvec_float[:, const_index][None, :]
            )
        pair_route = route_rows.reshape(-1)
        expert_hit = (pair_route[:, None] == expert_ids[None, :]).astype(jnp.int32)
        slot_index = jnp.sum((jnp.cumsum(expert_hit, axis=0) - expert_hit) * expert_hit, axis=1)
        slot_cell = jnp.sum(expert_hit * expert_ids[None, :], axis=1) * capacity + slot_index
        slot_place = jnp.where(jnp.sum(expert_hit, axis=1) > 0, slot_cell, -1)
        slot_table = (slot_ids[:, None] == slot_place[None, :]).astype(jnp.bfloat16)
        pair_rows = jnp.repeat(mixed, 2, axis=0)
        packed = jnp.einsum(
            "sp,pd->sd", slot_table, pair_rows, preferred_element_type=jnp.float32
        ).astype(jnp.bfloat16)
        outgoing = jnp.broadcast_to(
            packed.reshape(expert_count, 1, capacity, model_width),
            (expert_count, half_count, capacity, model_width),
        ).reshape(peer_count, capacity, model_width)
        received = lax.all_to_all(outgoing, "ep", split_axis=0, concat_axis=0, tiled=True)
        flat_rows = received.reshape(-1, model_width)
        gate_part = jnp.dot(flat_rows, gate_weight, preferred_element_type=jnp.float32)
        up_part = jnp.dot(flat_rows, up_weight, preferred_element_type=jnp.float32)
        hidden = (jax.nn.silu(gate_part) * up_part).astype(jnp.bfloat16)
        part_out = (
            jnp.dot(hidden, down_weight, preferred_element_type=jnp.float32)
            .astype(jnp.bfloat16)
            .reshape(received.shape)
        )
        returned_rows = lax.all_to_all(part_out, "ep", split_axis=0, concat_axis=0, tiled=True)
        returned_rows, kept_rows = (returned_rows, received)
        halves = returned_rows.reshape(expert_count, half_count, capacity, model_width)
        pair_ffn = jnp.zeros((2 * row_count, model_width), jnp.float32)
        for half_index in range(half_count):
            pair_ffn = pair_ffn + jnp.einsum(
                "sp,sd->pd",
                slot_table,
                halves[:, half_index].reshape(slot_count, model_width),
                preferred_element_type=jnp.float32,
            )
        expert_out = pair_ffn.reshape(row_count, 2, model_width)
        expert_out = (
            expert_out + choose[:, :, expert_count + 1 : expert_count + 2] * mixed_float[:, None, :]
        )
        for const_index in range(2):
            column = expert_count + 2 + const_index
            expert_out = (
                expert_out + choose[:, :, column : column + 1] * const_outs[const_index][:, None, :]
            )
        result_rows = residual + jnp.sum(gate_values[:, :, None] * expert_out, axis=1)
        layer_outputs.append(result_rows.astype(jnp.bfloat16))
        grad_rows = cotangent[step_index].astype(jnp.float32)
        d_gates = jnp.sum(expert_out * grad_rows[:, None, :], axis=-1)
        d_probs = jnp.sum(choose * d_gates[:, :, None], axis=1)
        d_logits = router_probs * (
            d_probs - jnp.sum(router_probs * d_probs, axis=-1, keepdims=True)
        )
        prev_grads.append(d_logits)
        grad_router = jnp.dot(mixed_float.T, d_logits, precision=HIGHEST)
        d_mixed = jnp.dot(d_logits, router_float.T, precision=HIGHEST)
        weighted = gate_values[:, :, None] * grad_rows[:, None, :]
        d_mixed = d_mixed + jnp.sum(
            choose[:, :, expert_count + 1 : expert_count + 2] * weighted, axis=1
        )
        cproj_grads = []
        cvec_grads = []
        for const_index in range(2):
            column = expert_count + 2 + const_index
            mixing = mixings[const_index]
            d_const = jnp.sum(choose[:, :, column : column + 1] * weighted, axis=1)
            d_mix = jnp.stack(
                [
                    jnp.sum(d_const * mixed_float, axis=-1),
                    jnp.sum(d_const * cvec_float[:, const_index][None, :], axis=-1),
                ],
                axis=-1,
            )
            d_mixlog = mixing * (d_mix - jnp.sum(mixing * d_mix, axis=-1, keepdims=True))
            cproj_grads.append(jnp.dot(mixed_float.T, d_mixlog, precision=HIGHEST))
            cvec_grads.append(jnp.sum(mixing[:, 1:] * d_const, axis=0))
            d_mixed = (
                d_mixed
                + mixing[:, :1] * d_const
                + jnp.dot(
                    d_mixlog,
                    cproj_float[:, 2 * const_index : 2 * const_index + 2].T,
                    precision=HIGHEST,
                )
            )
        grad_cproj = jnp.concatenate(cproj_grads, axis=1)
        grad_cvec = jnp.stack(cvec_grads, axis=1)
        d_pairs = weighted.reshape(2 * row_count, model_width).astype(jnp.bfloat16)
        d_packed = jnp.einsum(
            "sp,pd->sd", slot_table, d_pairs, preferred_element_type=jnp.float32
        ).astype(jnp.bfloat16)
        d_outgoing = jnp.broadcast_to(
            d_packed.reshape(expert_count, 1, capacity, model_width),
            (expert_count, half_count, capacity, model_width),
        ).reshape(peer_count, capacity, model_width)
        d_received = lax.all_to_all(d_outgoing, "ep", split_axis=0, concat_axis=0, tiled=True)
        flat_rows = kept_rows.reshape(-1, model_width)
        flat_grads = d_received.reshape(-1, model_width)
        gate_part = jnp.dot(flat_rows, gate_weight, preferred_element_type=jnp.float32)
        up_part = jnp.dot(flat_rows, up_weight, preferred_element_type=jnp.float32)
        activated = jax.nn.silu(gate_part)
        hidden = (activated * up_part).astype(jnp.bfloat16)
        grad_down = jnp.einsum("rf,rd->fd", hidden, flat_grads, preferred_element_type=jnp.float32)
        d_hidden = jnp.einsum(
            "rd,fd->rf", flat_grads, down_weight, preferred_element_type=jnp.float32
        )
        sigmoid_gate = jax.nn.sigmoid(gate_part)
        d_gate_part = (
            d_hidden * up_part * sigmoid_gate * (1.0 + gate_part * (1.0 - sigmoid_gate))
        ).astype(jnp.bfloat16)
        d_up_part = (d_hidden * activated).astype(jnp.bfloat16)
        grad_gate = jnp.einsum(
            "rd,rf->df", flat_rows, d_gate_part, preferred_element_type=jnp.float32
        )
        grad_up = jnp.einsum("rd,rf->df", flat_rows, d_up_part, preferred_element_type=jnp.float32)
        d_inputs = jnp.einsum(
            "rf,df->rd", d_gate_part, gate_weight, preferred_element_type=jnp.float32
        )
        d_inputs = d_inputs + jnp.einsum(
            "rf,df->rd", d_up_part, up_weight, preferred_element_type=jnp.float32
        )
        d_inputs = d_inputs.astype(jnp.bfloat16).reshape(peer_count, capacity, model_width)
        d_returned = lax.all_to_all(d_inputs, "ep", split_axis=0, concat_axis=0, tiled=True)
        d_halves = d_returned.reshape(expert_count, half_count, capacity, model_width)
        for half_index in range(half_count):
            d_pair_in = jnp.einsum(
                "sp,sd->pd",
                slot_table,
                d_halves[:, half_index].reshape(slot_count, model_width),
                preferred_element_type=jnp.float32,
            )
            d_mixed = d_mixed + jnp.sum(d_pair_in.reshape(row_count, 2, model_width), axis=1)
        expert_acc = add_tuple(expert_acc, (grad_gate, grad_up, grad_down))
        moe_vjp = jax.vjp(rms_scale, residual, moe_gain)[1]
        d_residual_norm, grad_moe_gain = moe_vjp(d_mixed)
        d_residual = grad_rows + d_residual_norm
        d_branch = d_residual.astype(jnp.bfloat16)
        grad_out = jnp.einsum("rd,re->de", attended, d_branch, preferred_element_type=jnp.float32)
        d_attended = (
            jnp.einsum("re,de->rd", d_branch, out_weight, preferred_element_type=jnp.float32)
            * valid_rows
        ).astype(jnp.bfloat16)
        d_heads = d_attended.reshape(row_count, head_count, HEAD)
        scores = (
            jnp.einsum("qhd,khd->hqk", queries, key_heads, preferred_element_type=jnp.float32)
            * 0.125
        )
        scores = jnp.where(allowed[None], scores, MASK_FILL)
        attn_probs = jnp.exp(scores - log_total)
        d_weights = jnp.einsum(
            "qhd,khd->hqk", d_heads, value_heads, preferred_element_type=jnp.float32
        )
        delta_rows = jnp.sum(attn_probs * d_weights, axis=-1, keepdims=True)
        d_scores = (attn_probs * (d_weights - delta_rows)).astype(jnp.bfloat16)
        d_queries = (
            jnp.einsum(
                "hqk,khd->qhd", d_scores, key_heads, preferred_element_type=jnp.float32
            ).reshape(row_count, model_width)
            * 0.125
        )
        d_values = jnp.einsum(
            "hqk,qhd->khd",
            attn_probs.astype(jnp.bfloat16),
            d_heads,
            preferred_element_type=jnp.float32,
        ).reshape(seq_length, model_width)
        d_keys = (
            jnp.einsum(
                "hqk,qhd->khd", d_scores, queries, preferred_element_type=jnp.float32
            ).reshape(seq_length, model_width)
            * 0.125
        )
        d_keys_mine, d_values_mine = (
            lax.psum_scatter(
                d_keys.astype(jnp.bfloat16), "ep", scatter_dimension=0, tiled=True
            ).astype(jnp.float32),
            lax.psum_scatter(
                d_values.astype(jnp.bfloat16), "ep", scatter_dimension=0, tiled=True
            ).astype(jnp.float32),
        )
        d_qkv = jnp.concatenate([d_queries, d_keys_mine, d_values_mine], axis=1).astype(
            jnp.bfloat16
        )
        grad_qkv = jnp.einsum("rd,re->de", normed, d_qkv, preferred_element_type=jnp.float32)
        d_normed = jnp.einsum("re,de->rd", d_qkv, qkv_weight, preferred_element_type=jnp.float32)
        attn_vjp = jax.vjp(rms_scale, token_rows, attn_gain)[1]
        d_tokens_norm, grad_attn_gain = attn_vjp(d_normed)
        input_grads.append(d_residual + d_tokens_norm)
        dense_terms = (
            grad_attn_gain,
            grad_qkv,
            grad_out,
            grad_moe_gain,
            grad_router,
            grad_cproj,
            grad_cvec,
        )
        dense_shares = (
            lax.psum_scatter(dense_terms[0], ("ep", "dp", "fs"), scatter_dimension=0, tiled=True),
            lax.psum_scatter(dense_terms[1], ("ep", "dp", "fs"), scatter_dimension=0, tiled=True),
            lax.psum_scatter(dense_terms[2], ("ep", "dp", "fs"), scatter_dimension=0, tiled=True),
            lax.psum_scatter(dense_terms[3], ("ep", "dp", "fs"), scatter_dimension=0, tiled=True),
            lax.psum_scatter(dense_terms[4], ("ep", "dp", "fs"), scatter_dimension=0, tiled=True),
            lax.psum_scatter(dense_terms[5], ("ep", "dp", "fs"), scatter_dimension=0, tiled=True),
            lax.psum_scatter(dense_terms[6], ("ep", "dp", "fs"), scatter_dimension=0, tiled=True),
        )
        dense_acc = add_tuple(dense_acc, dense_shares)
    expert_shares = (
        lax.psum_scatter(
            expert_acc[0][None].astype(jnp.bfloat16), ("dp", "fs"), scatter_dimension=1, tiled=True
        ).astype(jnp.float32),
        lax.psum_scatter(
            expert_acc[1][None].astype(jnp.bfloat16), ("dp", "fs"), scatter_dimension=1, tiled=True
        ).astype(jnp.float32),
        lax.psum_scatter(
            expert_acc[2][None].astype(jnp.bfloat16), ("dp", "fs"), scatter_dimension=1, tiled=True
        ).astype(jnp.float32),
    )
    return (
        jnp.stack(layer_outputs),
        jnp.stack(input_grads),
        jnp.stack(prev_grads),
        dense_acc[0],
        dense_acc[1],
        dense_acc[2],
        dense_acc[3],
        dense_acc[4],
        dense_acc[5],
        dense_acc[6],
        expert_shares[0],
        expert_shares[1],
        expert_shares[2],
    )


NEG = -1e30
KINDS = 2
SMALL = 16
LANES = 128
F32 = jnp.float32
BF16 = jnp.bfloat16


def dot(lhs, rhs, dims=((1,), (0,)), precision=None):
    return lax.dot_general(
        lhs, rhs, (dims, ((), ())), precision=precision, preferred_element_type=F32
    )


def key_span(block, rows, reach):
    start = max(0, block * rows - reach)
    return start, (block + 1) * rows - start


def column(rows, index):
    return rows[:, index : index + 1]


def chosen_of(ctl):
    lane = lax.broadcasted_iota(jnp.int32, ctl.shape, 1).astype(F32)
    return ((lane == column(ctl, 8)) | (lane == column(ctl, 9))).astype(F32)


def shape(dims, dtype):
    return jax.ShapeDtypeStruct(dims, dtype)


def whole(dims):
    return pl.BlockSpec(dims, lambda *_: (0,) * len(dims))


def per_row(rows, width):
    return pl.BlockSpec((rows, width), lambda i: (i, 0))


def params():
    return pltpu.CompilerParams(vmem_limit_bytes=56 * 1024 * 1024)


def cost(flops, moved):
    return pl.CostEstimate(flops=int(flops), bytes_accessed=int(moved), transcendentals=0)


class Mail:
    def __init__(self, send_sems, recv_sems):
        self.send_sems = send_sems
        self.recv_sems = recv_sems
        self.used = 0

    def copy(self, source, target, device):
        slot = self.used
        self.used = slot + 1
        return pltpu.make_async_remote_copy(
            src_ref=source,
            dst_ref=target,
            send_sem=self.send_sems.at[slot],
            recv_sem=self.recv_sems.at[slot],
            device_id=device,
            device_id_type=pl.DeviceIdType.MESH,
        )


def position():
    place = lax.axis_index("ep")
    return place // 2, place % 2, lax.axis_index("dp"), lax.axis_index("fs")


def greet(devices):
    barrier = pltpu.get_barrier_semaphore()
    total = 0
    for device, present in devices:
        if present is True:
            pl.semaphore_signal(
                barrier, inc=1, device_id=device, device_id_type=pl.DeviceIdType.MESH
            )
            total = total + 1
        else:

            @pl.when(present)
            def _():
                pl.semaphore_signal(
                    barrier, inc=1, device_id=device, device_id_type=pl.DeviceIdType.MESH
                )

            total = total + jnp.where(present, 1, 0)
    pl.semaphore_wait(barrier, total)


def attend_pair(pair, rows, reach, span, qkv_ref, segc_ref, segr_ref, att_ref, lse_ref):
    length = qkv_ref.shape[0]
    at_q, at_k, at_v = (
        pl.ds(pl.multiple_of(part * span + pair * LANES, LANES), LANES) for part in range(3)
    )
    for block in range(length // rows):
        start, width = key_span(block, rows, reach)
        here = pl.ds(block * rows, rows)
        there = pl.ds(start, width)
        queries = qkv_ref[here, at_q] * 0.125
        keys = qkv_ref[there, at_k]
        values = qkv_ref[there, at_v]
        seg_q = segc_ref[here, 0:1]
        seg_k = segr_ref[0:1, there]
        past = width - rows
        order = lax.broadcasted_iota(jnp.int32, (rows, rows), 1) <= lax.broadcasted_iota(
            jnp.int32, (rows, rows), 0
        )

        def masked(scores):
            near = jnp.where((seg_q == seg_k[:, past:]) & order, scores[:, past:], NEG)
            if past == 0:
                return near
            far = jnp.where(seg_q == seg_k[:, :past], scores[:, :past], NEG)
            return jnp.concatenate([far, near], axis=1)

        lane = lax.broadcasted_iota(jnp.int32, (rows, LANES), 1)
        outs = []
        logs = []
        for head in range(2):
            mine = (lane // HEAD) == head
            scores = masked(dot(jnp.where(mine, queries, 0), keys, ((1,), (1,))))
            largest = jnp.max(scores, axis=-1, keepdims=True)
            powers = jnp.exp(scores - largest)
            total = jnp.sum(powers, axis=-1, keepdims=True)
            outs.append(dot(powers.astype(BF16), values) / total)
            logs.append(largest + jnp.log(total))
        valid = (seg_q != SEGS - 1.0).astype(F32)
        att = jnp.where(lane < HEAD, outs[0], outs[1]) * valid
        att_ref[here, at_q] = att.astype(BF16)
        both = jnp.where(lane < HEAD, logs[0], logs[1]).T
        lse_ref[pair, 0:1, here] = both[0:1, :]
        lse_ref[pair, 1:2, here] = both[HEAD : HEAD + 1, :]


def gather_kernel(
    rows, reach, routes, experts,
    tok_ref, cot_ref, wqkv_ref, wout_ref, prev_ref, route_ref, seg_ref, router_ref, cproj_ref,
    cvec_ref, gain_a_ref, gain_m_ref,
    x_out, ctl_own, normed_out, qkv_out, att_ref, lse_ref, small_all, wqkv_out,
    wout_sib, segc_ref, segr_ref, g_rows,
    x_all, normed_ref, qkv_ref, wqkv_all, cot_wide, g_send, ctl_send, small_wide, small_send, seg_all,
    near_send, near_recv, far_send, far_recv, core_send, core_recv, local_sems,
    pack_send, pack_recv,
):
    y, x, z, core = position()
    me = y * 2 + x
    sibling = (me, z, 1 - core)
    moved = y != core
    near = ((1 - y) * 2 + x, z, 1 - core)
    far = (core * 2 + 1 - x, z, y)
    plane = [((y + k // 2) % 2 * 2 + (x + k) % 2) for k in range(4)]
    greet([((plane[k], z, (core + c) % 2), True) for k in range(4) for c in range(2) if k + c > 0])
    span = wqkv_ref.shape[0]
    halves = 4 // experts

    def pack(m, k, target=None):
        return pltpu.make_async_remote_copy(
            src_ref=g_send.at[m, plane[k] // halves],
            dst_ref=g_rows.at[x, core * 2 + m] if target is None else g_rows.at[target],
            send_sem=pack_send.at[m, k],
            recv_sem=pack_recv.at[x, core * 2 + m] if target is None else pack_recv.at[target],
            device_id=(plane[k], z, y),
            device_id_type=pl.DeviceIdType.MESH,
        )

    pack_stays = [
        pltpu.make_async_copy(
            g_send.at[m, y // (halves // 2)], g_rows.at[x, core * 2 + m], local_sems.at[7 + m]
        )
        for m in range(2)
    ]
    cot_load = pltpu.make_async_copy(cot_ref, cot_wide, local_sems.at[9])

    def block_of(index):
        return pl.ds(pl.multiple_of(index * rows, rows), rows)

    homes = [
        (tok_ref, x_all.at[block_of(me)]),
        (ctl_send, ctl_own.at[x]),
    ]
    nears = Mail(near_send, near_recv)
    fars = Mail(far_send, far_recv)
    near_copies = [nears.copy(a.at[x], b, near) for a, b in homes]
    far_copies = [fars.copy(a.at[1 - x], b, far) for a, b in homes]
    stay_copies = [
        pltpu.make_async_copy(a.at[x], b, local_sems.at[k]) for k, (a, b) in enumerate(homes)
    ]

    def send(k):
        far_copies[k].start()

        @pl.when(moved)
        def _():
            near_copies[k].start()

        @pl.when(jnp.logical_not(moved))
        def _():
            stay_copies[k].start()

    def take_near(k):
        @pl.when(moved)
        def _():
            near_copies[k].wait_recv()

        @pl.when(jnp.logical_not(moved))
        def _():
            stay_copies[k].wait()

    send(0)
    cot_load.start()
    inner = Mail(core_send, core_recv)
    weight_copies = []
    own_copies = []
    band = pl.ds(pl.multiple_of(core * span, span), span)
    for part in range(3):
        columns = pl.ds(part * span, span)
        for side, copies in ((1 - core, weight_copies), (core, own_copies)):
            source = wqkv_ref.at[
                :, pl.ds(pl.multiple_of(part * 2 * span + side * span, LANES), span)
            ]
            target = wqkv_all.at[band, columns]
            if copies is weight_copies:
                copies.append(inner.copy(source, target, sibling))
            else:
                copies.append(
                    pltpu.make_async_copy(source, target, local_sems.at[3 + part])
                )
    out_copy = inner.copy(wout_ref, wout_sib, sibling)
    seg_copy = inner.copy(seg_ref, seg_all.at[core], sibling)
    seg_own = pltpu.make_async_copy(seg_ref, seg_all.at[core], local_sems.at[6])
    small_copy = inner.copy(small_send, small_all.at[:, band], sibling)
    seg_copy.start()
    seg_own.start()
    for copy in weight_copies + own_copies:
        copy.start()

    small_wide[...] = jnp.zeros_like(small_wide)
    small_wide[0:routes, :] = router_ref[...].astype(F32)
    small_wide[8:12, :] = cproj_ref[...].astype(F32)
    small_wide[12:14, :] = cvec_ref[...].astype(F32)
    small_wide[14:15, :] = gain_a_ref[...].astype(F32).reshape(1, span)
    small_wide[15:16, :] = gain_m_ref[...].astype(F32).reshape(1, span)
    turned = small_wide[...]
    small_send[...] = turned.astype(BF16)
    small_all[:, band] = turned.astype(BF16)
    small_copy.start()
    out_copy.start()
    ctl_send[...] = jnp.zeros_like(ctl_send)
    for m in range(2):
        for route in range(routes):
            ctl_send[m, route : route + 1, :] = prev_ref[route, m : m + 1, :]
        ctl_send[m, 8:10, :] = route_ref[m].astype(F32)
    send(1)
    cot_load.wait()
    earlier = lax.broadcasted_iota(jnp.int32, (rows, rows), 0) < lax.broadcasted_iota(
        jnp.int32, (rows, rows), 1
    )
    slot = lax.broadcasted_iota(jnp.int32, (LANES, rows), 0).astype(F32)
    number = lax.broadcasted_iota(jnp.int32, (8, rows), 0)
    for m in range(2):
        chosen = ((number == route_ref[m, 0:1, :]) | (number == route_ref[m, 1:2, :])).astype(F32)
        rank = dot(chosen.astype(BF16), earlier.astype(BF16))
        for expert in range(experts):
            hit = (slot == rank[expert : expert + 1, :]) & (chosen[expert : expert + 1, :] > 0.0)
            g_send[m, expert] = dot(hit.astype(BF16), cot_wide[m]).astype(BF16)

    def send_packs():
        for m in range(2):
            for k in range(1, 4):
                pack(m, k).start()

            @pl.when(moved)
            def _():
                pack(m, 0).start()

            @pl.when(jnp.logical_not(moved))
            def _():
                pack_stays[m].start()

    seg_copy.wait_recv()
    seg_own.wait()
    seg_row = seg_all[y, pl.ds(x, 1), :].astype(F32)
    length = seg_row.shape[1]
    segr_ref[...] = jnp.broadcast_to(seg_row, segr_ref.shape)
    segc_ref[...] = jnp.broadcast_to(seg_row, (LANES, length)).T
    small_copy.wait_recv()
    for copy in weight_copies:
        copy.wait_recv()
    for copy in own_copies:
        copy.wait()
    gain = small_all[14:15, :].astype(F32)

    def project(index):
        here = block_of(index)
        values = x_all[here, :].astype(F32)
        inverse = lax.rsqrt(jnp.mean(values * values, axis=-1, keepdims=True) + NORM_EPS)
        normed = (values * inverse * gain).astype(BF16)
        normed_ref[here, :] = normed
        qkv_ref[here, :] = dot(normed, wqkv_all[...]).astype(BF16)

    forward = []
    for step in range(2):
        spot = x_all.at[block_of(core * 2 + (x if step == 0 else 1 - x))]
        forward.append(inner.copy(spot, spot, sibling))
    take_near(0)
    forward[0].start()
    project(core * 2 + x)
    far_copies[0].wait_recv()
    forward[1].start()
    send_packs()
    project(core * 2 + 1 - x)
    forward[0].wait_recv()
    project((1 - core) * 2 + x)
    forward[1].wait_recv()
    project((1 - core) * 2 + 1 - x)

    own_rows = pl.ds(pl.multiple_of(core * 2 * rows, rows), 2 * rows)
    results = [
        pltpu.make_async_copy(source, target, local_sems.at[10 + k])
        for k, (source, target) in enumerate(
            (
                (x_all.at[own_rows], x_out), (normed_ref, normed_out), (qkv_ref, qkv_out),
                (wqkv_all, wqkv_out),
            )
        )
    ]
    for copy in results:
        copy.start()

    @pl.loop(0, span // LANES)
    def _(pair):
        attend_pair(pair, rows, reach, span, qkv_ref, segc_ref, segr_ref, att_ref, lse_ref)

    for copy in results:
        copy.wait()
    take_near(1)
    far_copies[1].wait_recv()
    for there in range(2):
        for peer in range(4):
            kept = (y == core) & (x == there) & (core == peer // 2)

            @pl.when(jnp.logical_not(kept))
            def _():
                pack(0, 0, (there, peer)).wait_recv()

    for m in range(2):
        for k in range(1, 4):
            pack(m, k).wait_send()

        @pl.when(moved)
        def _():
            pack(m, 0).wait_send()

        @pl.when(jnp.logical_not(moved))
        def _():
            pack_stays[m].wait()

    out_copy.wait_recv()
    for copy in far_copies + weight_copies + forward + [out_copy, seg_copy, small_copy]:
        copy.wait_send()

    @pl.when(moved)
    def _():
        for copy in near_copies:
            copy.wait_send()


def gather_all(
    experts, tokens, cotangent, w_qkv, w_out, prev_logits, routes, segments, w_router, const_proj,
    const_vec, gain_attn, gain_moe,
):
    rows, width = tokens.shape[1:]
    length = segments.shape[1]
    span = width // 2
    vmem = pl.BlockSpec(memory_space=pltpu.VMEM)
    anywhere = pl.BlockSpec(memory_space=pl.ANY)
    return pl.pallas_call(
        functools.partial(gather_kernel, rows, length // 2, w_router.shape[1], experts),
        in_specs=[anywhere] * 4 + [vmem] * 8,
        out_specs=[anywhere, vmem, anywhere, anywhere, vmem, vmem, vmem, anywhere, anywhere]
        + [vmem] * 2
        + [anywhere],
        out_shape=[
            shape((length // 2, width), BF16),
            shape((2, SMALL, rows), F32), shape((length, width), BF16),
            shape((length, 3 * span), BF16), shape((length, span), BF16),
            shape((span // LANES, 8, length), F32), shape((SMALL, width), BF16),
            shape((width, 3 * span), BF16), shape((span, width), BF16),
            shape((length, LANES), F32), shape((8, length), F32),
            shape((2, 4, LANES, width), BF16),
        ],
        scratch_shapes=[
            pltpu.VMEM((length, width), BF16), pltpu.VMEM((length, width), BF16),
            pltpu.VMEM((length, 3 * span), BF16), pltpu.VMEM((width, 3 * span), BF16),
            pltpu.VMEM((2, rows, width), BF16), pltpu.VMEM((2, experts, LANES, width), BF16),
            pltpu.VMEM((2, SMALL, rows), F32),
            pltpu.VMEM((SMALL, span), F32), pltpu.VMEM((SMALL, span), BF16),
            pltpu.VMEM((2, 2, length), jnp.int32),
        ]
        + [pltpu.SemaphoreType.DMA((3,))] * 4
        + [pltpu.SemaphoreType.DMA((8,))] * 2
        + [pltpu.SemaphoreType.DMA((14,))]
        + [pltpu.SemaphoreType.DMA((2, 4))] * 2,
        compiler_params=pltpu.CompilerParams(
            collective_id=3, has_side_effects=True, vmem_limit_bytes=60 * 1024 * 1024
        ),
        name="gather_all",
    )(
        tokens, cotangent, w_qkv, w_out, jnp.transpose(prev_logits, (2, 0, 1)),
        jnp.swapaxes(routes, 1, 2), segments, w_router.T, const_proj.T, const_vec.T, gain_attn,
        gain_moe,
    )


def widen(turned):
    pad = jnp.zeros((LANES - turned.shape[0], turned.shape[1]), turned.dtype)
    return jnp.concatenate([turned, pad], axis=0).T


def spread_block(experts, routes, rows, block, refs, sent, got, keep):
    send_ref, gate_send = sent
    recv_ref, gate_recv = got
    att_own, att_sib, x_ref, ctl_ref, w_own, w_sib, small_rows, wide_rows = refs
    residual_ref, mixed_ref, pm_ref, place_ref = keep
    y, x, z, core = position()
    here = pl.ds(pl.multiple_of(block * rows, rows), rows)
    tokens = x_ref[here, :]
    residual = tokens.astype(F32) + (
        dot(att_own[here, :], w_own[...]) + dot(att_sib[here, :], w_sib[...])
    )
    residual_ref[here, :] = residual
    inverse = lax.rsqrt(jnp.mean(residual * residual, axis=-1, keepdims=True) + NORM_EPS)
    mixed = (residual * inverse * small_rows[15:16, :].astype(F32)).astype(BF16)
    mixed_ref[here, :] = mixed
    logits = dot(mixed, wide_rows[...], ((1,), (1,)))
    ctl = widen(ctl_ref[block])
    lane = lax.broadcasted_iota(jnp.int32, (rows, LANES), 1)
    is_route = lane < routes
    router = jnp.where(is_route, logits + ctl, NEG)
    powers = jnp.exp(router - jnp.max(router, axis=-1, keepdims=True))
    probs = powers / jnp.sum(powers, axis=-1, keepdims=True)
    probs = jnp.where(is_route, probs, 0.0)
    pm = probs
    for const_index in range(2):
        first = column(logits, 8 + 2 * const_index)
        second = column(logits, 9 + 2 * const_index)
        largest = jnp.maximum(first, second)
        first = jnp.exp(first - largest)
        second = jnp.exp(second - largest)
        total = first + second
        pm = jnp.where(lane == 8 + 2 * const_index, first / total, pm)
        pm = jnp.where(lane == 9 + 2 * const_index, second / total, pm)
    pm_ref[here, :] = pm
    chosen = chosen_of(ctl)
    gated = chosen * probs
    earlier = lax.broadcasted_iota(jnp.int32, (rows, rows), 1) < lax.broadcasted_iota(
        jnp.int32, (rows, rows), 0
    )
    rank = dot(earlier.astype(BF16), chosen.astype(BF16))
    lane_f = lane.astype(F32)
    for expert in range(experts):
        place = jnp.where(
            (lane_f == column(rank, expert)) & (column(chosen, expert) > 0.0), 1.0, 0.0
        )
        place_ref[here, expert * LANES : (expert + 1) * LANES] = place.astype(BF16)
        pick = place.T.astype(BF16)
        send_ref[block, expert] = dot(pick, mixed).astype(BF16)
        gates = jnp.sum(place * column(gated, expert), axis=0, keepdims=True)
        gate_send[block, expert] = jnp.broadcast_to(gates, gate_send.shape[2:])
    recv_ref[block, y * 2 + x] = send_ref[block, y]
    gate_recv[block, y * 2 + x] = gate_send[block, y]


def expert_block(block, got, result_ref, back_ref, weights, keep, send):
    recv_ref, gate_recv, g_rows = got
    gate_w, up_w, down_w = weights
    hidden_ref, d_gate_ref, d_up_ref, d_rows_ref = keep
    y, x, z, core = position()
    peers, capacity, width = recv_ref.shape[1:]
    size = peers * capacity
    here = pl.ds(pl.multiple_of(block * size, size), size)
    rows = recv_ref[block].reshape(size, width)
    gate = dot(rows, gate_w[...])
    up = dot(rows, up_w[...])
    sig = jax.nn.sigmoid(gate)
    active = gate * sig
    hidden = (active * up).astype(BF16)
    hidden_ref[here, :] = hidden
    part = dot(hidden, down_w[...]).astype(BF16)
    result_ref[block, :, 0] = part.reshape(peers, capacity, width)
    send(0)
    for peer in range(peers):
        spread = jnp.concatenate([gate_recv[block, peer]] * (capacity // 8), axis=0).T
        d_part = column(spread, 0) * g_rows[block, peer].astype(F32)
        at = pl.ds(pl.multiple_of(block * size + peer * capacity, capacity), capacity)
        d_rows_ref[at, :] = d_part.astype(BF16)
    d_rows = d_rows_ref[here, :]
    d_hidden = dot(d_rows, down_w[...], ((1,), (1,)))
    d_gate = (d_hidden * up * sig * (1.0 + gate * (1.0 - sig))).astype(BF16)
    d_up = (d_hidden * active).astype(BF16)
    d_gate_ref[here, :] = d_gate
    d_up_ref[here, :] = d_up
    d_in = dot(d_gate, gate_w[...], ((1,), (1,))) + dot(d_up, up_w[...], ((1,), (1,)))
    result_ref[block, :, 1] = d_in.astype(BF16).reshape(peers, capacity, width)
    send(1)
    back_ref[block, y * 2 + x] = result_ref[block, y * 2 + x]


def combine_forward(experts, routes, rows, block, refs, keep, back_ref, outs, small_ref):
    g_ref, ctl_ref, small_rows, wide_rows = refs
    residual_ref, mixed_ref, pm_ref, place_ref = keep
    out_ref, prev_ref, dres_ref, branch_ref = outs
    halves = back_ref.shape[1] // experts
    here = pl.ds(pl.multiple_of(block * rows, rows), rows)
    g_low = g_ref[here, :]
    grads = g_low.astype(F32)
    mixed = mixed_ref[here, :].astype(F32)
    residual = residual_ref[here, :]
    pm = pm_ref[here, :]
    lane = lax.broadcasted_iota(jnp.int32, (rows, LANES), 1)
    chosen = chosen_of(widen(ctl_ref[block]))
    probs = jnp.where(lane < routes, pm, 0.0)
    gated = chosen * probs
    d_probs = jnp.zeros((rows, LANES), F32)
    result = residual
    for expert in range(experts):
        place = place_ref[here, expert * LANES : (expert + 1) * LANES]
        expert_out = None
        for half in range(halves):
            term = dot(place, back_ref[block, expert * halves + half, 0])
            expert_out = term if expert_out is None else expert_out + term
        result = result + column(gated, expert) * expert_out
        d_gate = jnp.sum(expert_out * grads, axis=-1, keepdims=True)
        d_probs = jnp.where(lane == expert, d_gate, d_probs)
    g_mixed = jnp.sum(grads * mixed, axis=-1, keepdims=True)
    g_const = dot(g_low, wide_rows[...], ((1,), (1,)))
    copy = experts + 1
    d_probs = jnp.where(lane == copy, g_mixed, d_probs)
    weight = column(gated, copy)
    d_small = jnp.zeros((rows, LANES), F32)
    for const_index in range(2):
        route = copy + 1 + const_index
        first = column(pm, 8 + 2 * const_index)
        second = column(pm, 9 + 2 * const_index)
        gate = column(gated, route)
        g_vec = column(g_const, 12 + const_index)
        d_probs = jnp.where(lane == route, first * g_mixed + second * g_vec, d_probs)
        weight = weight + gate * first
        vec = small_rows[12 + const_index : 13 + const_index, :].astype(F32)
        result = result + (gate * second) * vec
        d_first = gate * g_mixed
        d_second = gate * g_vec
        mean = first * d_first + second * d_second
        d_small = jnp.where(lane == 8 + 2 * const_index, first * (d_first - mean), d_small)
        d_small = jnp.where(lane == 9 + 2 * const_index, second * (d_second - mean), d_small)
        d_small = jnp.where(lane == 12 + const_index, gate * second, d_small)
    result = result + weight * mixed
    out_ref[block] = result.astype(BF16)
    d_probs = d_probs * chosen
    d_logits = probs * (d_probs - jnp.sum(probs * d_probs, axis=-1, keepdims=True))
    d_small = jnp.where(lane < routes, d_logits, d_small)
    dres_ref[here, :] = weight * grads + dot(
        jnp.where(lane < 12, d_small, 0.0), wide_rows[...].astype(F32), precision=HIGHEST
    )
    d_turned = d_small.T[:SMALL, :]
    prev_ref[block] = d_turned[:8, :]
    sub = lax.broadcasted_iota(jnp.int32, (SMALL, rows), 0)
    small = dot(jnp.where(sub < 12, d_turned, 0.0), mixed, precision=HIGHEST)
    small_ref[...] += small + dot(
        jnp.where((sub >= 12) & (sub < 14), d_turned, 0.0), grads, precision=HIGHEST
    )


def combine_backward(experts, rows, block, refs, keep, back_ref, outs, small_ref):
    g_ref, ctl_ref, small_rows, wide_rows = refs
    residual_ref, mixed_ref, pm_ref, place_ref = keep
    out_ref, prev_ref, dres_ref, branch_ref = outs
    halves = back_ref.shape[1] // experts
    here = pl.ds(pl.multiple_of(block * rows, rows), rows)
    grads = g_ref[here, :].astype(F32)
    residual = residual_ref[here, :]
    d_mixed = dres_ref[here, :]
    for expert in range(experts):
        place = place_ref[here, expert * LANES : (expert + 1) * LANES]
        for half in range(halves):
            d_mixed = d_mixed + dot(place, back_ref[block, expert * halves + half, 1])
    inverse = lax.rsqrt(jnp.mean(residual * residual, axis=-1, keepdims=True) + NORM_EPS)
    scaled = d_mixed * small_rows[15:16, :].astype(F32)
    mean = jnp.mean(scaled * residual, axis=-1, keepdims=True)
    d_residual = grads + inverse * scaled - residual * (inverse * inverse * inverse * mean)
    dres_ref[here, :] = d_residual
    branch_ref[here, :] = d_residual.astype(BF16)
    small_ref[14:15, :] += jnp.sum(d_mixed * residual * inverse, axis=0, keepdims=True)


def layer_kernel(
    experts, routes, rows, blocks,
    ctl_ref, small_rows, att_ref, cot_ref, x_any, own_any, sib_any, g_any, gate_ref, up_ref,
    down_ref,
    out_ref, prev_ref, dres_ref, branch_ref, small_ref, gate_acc, up_acc, down_acc,
    dgate_out, dup_out, ddown_out, gate_land, up_land, down_land, gate_line, up_line, down_line,
    wide_rows, att_own, att_sib, gate_w, up_w, down_w, residual_ref, mixed_ref, pm_ref, place_ref,
    send_ref, gate_send, gate_recv, recv_ref, result_ref, back_ref, hidden_ref, d_gate_ref,
    d_up_ref, d_rows_ref, g_ref, x_ref, w_own, w_sib, g_rows,
    head_send, head_recv, local_sems, send_sems, recv_sems, back_send, back_recv, sum_send, sum_recv,
    g_sends, g_recvs,
):
    y, x, z, core = position()
    me = y * 2 + x
    sibling = (me, z, 1 - core)
    partners = [(1 - y) * 2 + 1 - x, y * 2 + 1 - x, (1 - y) * 2 + x]
    wanted = [1 - y, y, 1 - y]
    depth = lax.axis_size("dp")
    plane = [((y + k // 2) % 2 * 2 + (x + k) % 2) for k in range(4)]
    greet(
        [((plane[k], z, (core + c) % 2), True) for k in range(4) for c in range(2) if k + c > 0]
        + [((me, z + 1, core), z < depth - 1), ((me, z - 1, core), z > 0)]
    )
    moved = y != core
    g_place = g_ref.at[pl.ds(pl.multiple_of(x * rows, rows), rows)]
    g_mail = Mail(g_sends, g_recvs)
    g_near = g_mail.copy(cot_ref.at[x], g_place, ((1 - y) * 2 + x, z, 1 - core))
    g_far = g_mail.copy(cot_ref.at[1 - x], g_place, (core * 2 + 1 - x, z, y))
    g_stay = pltpu.make_async_copy(cot_ref.at[x], g_place, local_sems.at[4])
    g_far.start()

    @pl.when(moved)
    def _():
        g_near.start()

    @pl.when(jnp.logical_not(moved))
    def _():
        g_stay.start()

    sums = Mail(sum_send, sum_recv)
    grads = [
        (dgate_out, gate_land, gate_acc, gate_line), (dup_out, up_land, up_acc, up_line),
        (ddown_out, down_land, down_acc, down_line),
    ]

    def share(ref, shard, side):
        size = ref.shape[0] // (2 * depth)
        return pl.ds(pl.multiple_of((shard * 2 + side) * size, size), size)

    halves = [
        [
            sums.copy(ref.at[share(ref, shard, 1 - core)], land.at[shard], sibling)
            for shard in range(depth)
        ]
        for ref, land, _, _ in grads
    ]
    line = Line(sums, depth, [(acc, landing) for _, _, acc, landing in grads], range(1))

    def add_halves(item):
        ref, land, acc, _ = grads[item]
        for shard in range(depth):
            halves[item][shard].wait_recv()
            acc[shard] = (
                ref[share(ref, shard, core)].astype(F32) + land[shard].astype(F32)
            ).astype(BF16)
        line.send(0, item)

    mine = rows * blocks
    mail = Mail(head_send, head_recv)
    pairs = [(gate_ref, gate_w), (up_ref, up_w), (down_ref, down_w)]
    heads = [mail.copy(att_ref.at[1 - core], att_sib, sibling)]
    locals_ = [pltpu.make_async_copy(att_ref.at[core], att_own, local_sems.at[3])]
    for k, (source, target) in enumerate(pairs):
        size = source.shape[0]
        spot = target.at[pl.ds(pl.multiple_of(core * size, size), size)]
        heads.append(mail.copy(source, spot, sibling))
        locals_.append(pltpu.make_async_copy(source, spot, local_sems.at[k]))
    loads = [
        pltpu.make_async_copy(source, target, local_sems.at[5 + k])
        for k, (source, target) in enumerate(
            ((x_any, x_ref), (own_any, w_own), (sib_any, w_sib), (g_any, g_rows))
        )
    ]
    heads[0].start()
    locals_[0].start()
    for copy in loads[:3] + heads[1:] + locals_[1:] + loads[3:]:
        copy.start()

    def dispatch(block, k, kind):
        source, target = ((send_ref, recv_ref), (gate_send, gate_recv))[kind]
        return pltpu.make_async_remote_copy(
            src_ref=source.at[block, wanted[k]],
            dst_ref=target.at[block, me],
            send_sem=send_sems.at[block, k, kind],
            recv_sem=recv_sems.at[block, k, kind],
            device_id=(partners[k], z, core),
            device_id_type=pl.DeviceIdType.MESH,
        )

    def giveback(block, k, kind):
        return pltpu.make_async_remote_copy(
            src_ref=result_ref.at[block, partners[k], kind],
            dst_ref=back_ref.at[block, me, kind],
            send_sem=back_send.at[block, k, kind],
            recv_sem=back_recv.at[block, k, kind],
            device_id=(partners[k], z, core),
            device_id_type=pl.DeviceIdType.MESH,
        )

    every = [(k, kind) for kind in range(KINDS) for k in range(3)]
    small_ref[...] = jnp.zeros_like(small_ref)
    wide_rows[...] = jnp.zeros_like(wide_rows)
    wide_rows[0:SMALL, :] = small_rows[...]
    heads[0].wait_recv()
    locals_[0].wait()
    for copy in loads[:3]:
        copy.wait()
    keep = (residual_ref, mixed_ref, pm_ref, place_ref)
    spread_refs = (
        att_own, att_sib, x_ref, ctl_ref, w_own, w_sib, small_rows, wide_rows
    )

    @pl.loop(0, blocks)
    def _(block):
        spread_block(
            experts, routes, rows, block, spread_refs, (send_ref, gate_send),
            (recv_ref, gate_recv), keep,
        )
        for k, kind in every:
            dispatch(block, k, kind).start()

    for copy in heads[1:]:
        copy.wait_recv()
    for copy in locals_[1:] + loads[3:]:
        copy.wait()

    @pl.loop(0, blocks)
    def _(block):
        for k, kind in every:
            dispatch(block, k, kind).wait_recv()

        def send(kind):
            for k in range(3):
                giveback(block, k, kind).start()

        expert_block(
            block, (recv_ref, gate_recv, g_rows), result_ref, back_ref, (gate_w, up_w, down_w),
            (hidden_ref, d_gate_ref, d_up_ref, d_rows_ref), send,
        )

    peers, capacity, width = recv_ref.shape[1:]
    total = blocks * peers * capacity
    step = 2 * LANES

    @pl.loop(0, width // step)
    def _(chunk):
        span = pl.ds(pl.multiple_of(chunk * step, step), step)
        lhs = recv_ref[:, :, :, span].reshape(total, step).T
        dgate_out[span, :] = dot(lhs, d_gate_ref[...]).astype(BF16)
        dup_out[span, :] = dot(lhs, d_up_ref[...]).astype(BF16)

    for copy in halves[0] + halves[1]:
        copy.start()

    @pl.loop(0, hidden_ref.shape[1] // step)
    def _(chunk):
        span = pl.ds(pl.multiple_of(chunk * step, step), step)
        lhs = hidden_ref[:, span].T
        ddown_out[span, :] = dot(lhs, d_rows_ref[...]).astype(BF16)

    for copy in halves[2]:
        copy.start()
    for item in range(3):
        add_halves(item)
    g_far.wait()

    @pl.when(moved)
    def _():
        g_near.wait()

    @pl.when(jnp.logical_not(moved))
    def _():
        g_stay.wait()

    @pl.loop(0, blocks)
    def _(block):
        refs = (g_ref, ctl_ref, small_rows, wide_rows)
        outs = (out_ref, prev_ref, dres_ref, branch_ref)
        for k in range(3):
            giveback(block, k, 0).wait_recv()
        combine_forward(
            experts, routes, rows, block, refs, keep, back_ref, outs, small_ref
        )
        for k in range(3):
            giveback(block, k, 1).wait_recv()
        combine_backward(experts, rows, block, refs, keep, back_ref, outs, small_ref)

    for item in range(3):
        line.take(0, item)
    for copy in heads + halves[0] + halves[1] + halves[2]:
        copy.wait_send()
    line.close()
    for block in range(blocks):
        for k, kind in every:
            dispatch(block, k, kind).wait_send()
            giveback(block, k, kind).wait_send()


def expert_layer(
    experts, routes, rows, attended, x_own, cot, ctl, w_own, w_sib, small_all, w_gate,
    w_up, w_down, g_rows,
):
    blocks, rows, width = cot.shape
    mine = blocks * rows
    peers = lax.axis_size("ep")
    span = attended.shape[1]
    hidden = w_gate.shape[1]
    vmem = pl.BlockSpec(memory_space=pltpu.VMEM)
    total = blocks * peers * LANES
    grads = [(2 * w.shape[0], w.shape[1]) for w in (w_gate, w_up, w_down)]
    depth = lax.axis_size("dp")
    parts = [(dims[0] // (2 * depth), dims[1]) for dims in grads]
    sums = 3 * depth + 6
    return pl.pallas_call(
        functools.partial(layer_kernel, experts, routes, rows, blocks),
        in_specs=[vmem] * 2 + [pl.BlockSpec(memory_space=pl.ANY)] * 9,
        out_specs=[vmem] * 8,
        out_shape=[
            shape((blocks, rows, width), BF16), shape((blocks, 8, rows), F32),
            shape((mine, width), F32), shape((mine, width), BF16), shape((SMALL, width), F32),
        ]
        + [shape((depth,) + part, BF16) for part in parts],
        scratch_shapes=[pltpu.VMEM(dims, BF16) for dims in grads]
        + [pltpu.VMEM((depth,) + part, BF16) for part in parts]
        + [pltpu.VMEM((2, 1) + part, BF16) for part in parts]
        + [pltpu.VMEM((LANES, width), BF16)]
        + [pltpu.VMEM((mine, span), BF16)] * 2
        + [pltpu.VMEM(dims, BF16) for dims in grads]
        + [
            pltpu.VMEM((mine, width), F32), pltpu.VMEM((mine, width), BF16),
            pltpu.VMEM((mine, LANES), F32), pltpu.VMEM((mine, experts * LANES), BF16),
            pltpu.VMEM((blocks, experts, LANES, width), BF16),
            pltpu.VMEM((blocks, experts, 8, LANES), F32), pltpu.VMEM((blocks, peers, 8, LANES), F32),
            pltpu.VMEM((blocks, peers, LANES, width), BF16),
        ]
        + [pltpu.VMEM((blocks, peers, KINDS, LANES, width), BF16)] * 2
        + [pltpu.VMEM((total, hidden), BF16)] * 3
        + [pltpu.VMEM((total, width), BF16), pltpu.VMEM((mine, width), BF16)]
        + [pltpu.VMEM((mine, width), BF16)]
        + [pltpu.VMEM((span, width), BF16)] * 2
        + [pltpu.VMEM((blocks, peers, LANES, width), BF16)]
        + [
            pltpu.SemaphoreType.DMA((4,)), pltpu.SemaphoreType.DMA((4,)),
            pltpu.SemaphoreType.DMA((9,)),
        ]
        + [pltpu.SemaphoreType.DMA((blocks, 3, KINDS))] * 4
        + [pltpu.SemaphoreType.DMA((sums,))] * 2
        + [pltpu.SemaphoreType.DMA((2,))] * 2,
        compiler_params=pltpu.CompilerParams(
            collective_id=2, has_side_effects=True, vmem_limit_bytes=62 * 1024 * 1024
        ),
        name="expert_layer",
    )(
        ctl, small_all, attended.reshape(2, mine, span), cot, x_own, w_own, w_sib, g_rows, w_gate,
        w_up, w_down,
    )


class Line:
    def __init__(self, mail, depth, slots, steps):
        self.depth = depth
        self.slots = slots
        self.first = steps[0]
        self.place = lax.axis_index("dp")
        y, x, z, core = position()
        self.copies = {}
        for way in range(2):
            step_to = 1 if way == 0 else -1
            device = (y * 2 + x, z + step_to, core)
            for step in steps:
                for item, (acc, landing) in enumerate(slots):
                    shard = self.shard(way, step)
                    safe = jnp.clip(shard, 0, depth - 1)
                    self.copies[way, step, item] = mail.copy(
                        acc.at[safe], landing.at[way, step - self.first], device
                    )

    def shard(self, way, step):
        if way == 0:
            return self.place + self.depth - 1 - step
        return self.place - (self.depth - 1 - step)

    def edge(self, way):
        return self.place == (0 if way == 0 else self.depth - 1)

    def sends(self, way, step):
        shard = self.shard(way, step)
        if way == 0:
            return (shard <= self.depth - 1) & (self.place < self.depth - 1)
        return (shard >= 0) & (self.place > 0)

    def gets(self, way, step):
        if way == 0:
            return (self.place > 0) & (self.shard(way, step + 1) <= self.depth - 1)
        return (self.place < self.depth - 1) & (self.shard(way, step + 1) >= 0)

    def send(self, step, item):
        for way in range(2):
            wanted = self.sends(way, step)
            if step > self.first:
                wanted = wanted & jnp.logical_not(self.edge(way))

            @pl.when(wanted)
            def _():
                self.copies[way, step, item].start()

    def send_edge(self, step, item):
        for way in range(2):

            @pl.when(self.sends(way, step) & self.edge(way))
            def _():
                self.copies[way, step, item].start()

    def take(self, step, item):
        acc, landing = self.slots[item]
        for way in range(2):
            shard = jnp.clip(self.shard(way, step + 1), 0, self.depth - 1)

            @pl.when(self.gets(way, step))
            def _():
                self.copies[way, step, item].wait_recv()
                acc[shard] = (
                    acc[shard].astype(F32) + landing[way, step - self.first].astype(F32)
                ).astype(BF16)

    def finish(self, item, store):
        acc, landing = self.slots[item]
        store(acc[self.place].astype(F32))
        for way in range(2):

            @pl.when(self.gets(way, self.depth - 2))
            def _():
                self.copies[way, self.depth - 2, item].wait_recv()
                store(landing[way, self.depth - 2 - self.first].astype(F32), True)

    def close(self):
        for (way, step, item), copy in self.copies.items():

            @pl.when(self.sends(way, step))
            def _():
                copy.wait_send()


class Plane:
    def __init__(self, mail, source, buffers, total):
        y, x, z, core = position()
        self.place = y, x
        self.source = source
        self.buffers = buffers
        self.total = total
        y1_land, x1_land, y1_acc, x1_acc, x2_land, y2_land = buffers
        half = x2_land.shape[0]
        self.low = pl.ds(0, half)
        self.high = pl.ds(half, half)
        across = (y * 2 + 1 - x, z, core)
        along = ((1 - y) * 2 + x, z, core)
        self.first = [
            mail.copy(source.at[1 - y, :, self.low], y1_land, along),
            mail.copy(source.at[:, 1 - x, self.high], x1_land, across),
        ]
        self.second = [
            mail.copy(y1_acc.at[1 - x], x2_land, across),
            mail.copy(x1_acc.at[1 - y], y2_land, along),
        ]

    def start(self):
        for copy in self.first:
            copy.start()

    def middle(self):
        y, x = self.place
        y1_land, x1_land, y1_acc, x1_acc, _, _ = self.buffers
        self.first[0].wait_recv()
        for k in range(2):
            y1_acc[k] = (
                self.source[y, k, self.low].astype(F32) + y1_land[k].astype(F32)
            ).astype(BF16)
        self.second[0].start()
        self.first[1].wait_recv()
        for k in range(2):
            x1_acc[k] = (
                self.source[k, x, self.high].astype(F32) + x1_land[k].astype(F32)
            ).astype(BF16)
        self.second[1].start()

    def end(self):
        y, x = self.place
        _, _, y1_acc, x1_acc, x2_land, y2_land = self.buffers
        shards, size = self.total.shape[0] // 2, self.total.shape[1]
        self.second[0].wait_recv()
        for shard in range(shards):
            part = pl.ds(shard * size, size)
            self.total[shard] = (
                y1_acc[x, part].astype(F32) + x2_land[part].astype(F32)
            ).astype(BF16)
        self.second[1].wait_recv()
        for shard in range(shards):
            part = pl.ds(shard * size, size)
            self.total[shards + shard] = (
                x1_acc[y, part].astype(F32) + y2_land[part].astype(F32)
            ).astype(BF16)

    def close(self):
        for copy in self.first + self.second:
            copy.wait_send()


def back_pair(
    pair, rows, reach, span, qkv_ref, datt_ref, segc_ref, segr_ref, lse_ref, dqkv_ref,
    dk_sum, dv_sum,
):
    length = qkv_ref.shape[0]
    at_q, at_k, at_v = (
        pl.ds(pl.multiple_of(part * span + pair * LANES, LANES), LANES) for part in range(3)
    )
    dk_sum[...] = jnp.zeros_like(dk_sum)
    dv_sum[...] = jnp.zeros_like(dv_sum)
    keys_turned = qkv_ref[:, at_k].T
    for block in range(length // rows):
        start, width = key_span(block, rows, reach)
        here = pl.ds(block * rows, rows)
        there = pl.ds(start, width)
        queries = qkv_ref[here, at_q] * 0.125
        grads = datt_ref[here, at_q]
        keys = qkv_ref[there, at_k]
        values = qkv_ref[there, at_v]
        seg_k = segc_ref[there, 0:1]
        seg_q = segr_ref[0:1, here]
        past = width - rows
        order = lax.broadcasted_iota(jnp.int32, (rows, rows), 0) <= lax.broadcasted_iota(
            jnp.int32, (rows, rows), 1
        )

        def masked(scores):
            near = jnp.where((seg_q == seg_k[past:]) & order, scores[past:], NEG)
            if past == 0:
                return near
            far = jnp.where(seg_q == seg_k[:past], scores[:past], NEG)
            return jnp.concatenate([far, near], axis=0)

        lane = lax.broadcasted_iota(jnp.int32, (rows, LANES), 1)
        dq_parts = []
        for head in range(2):
            mine = (lane // HEAD) == head
            head_q = jnp.where(mine, queries, 0)
            head_g = jnp.where(mine, grads, 0)
            log_total = lse_ref[pair, head : head + 1, here]
            probs = jnp.exp(masked(dot(keys, head_q, ((1,), (1,)))) - log_total)
            d_probs = dot(values, head_g, ((1,), (1,)))
            delta = jnp.sum(probs * d_probs, axis=0, keepdims=True)
            d_scores = (probs * (d_probs - delta)).astype(BF16)
            dv_sum[there, :] += dot(probs.astype(BF16), head_g)
            dk_sum[there, :] += dot(d_scores, head_q)
            turned = keys_turned[head * HEAD : (head + 1) * HEAD, start : start + width]
            dq_parts.append(dot(turned, d_scores))
        dq = jnp.concatenate(dq_parts, axis=0).T * 0.125
        dqkv_ref[here, at_q] = dq.astype(BF16)
    dqkv_ref[:, at_k] = dk_sum[...].astype(BF16)
    dqkv_ref[:, at_v] = dv_sum[...].astype(BF16)


def back_kernel(depth, rows, reach, *refs):
    (
        gate_any, up_any, down_any, branch_any, wout_any, att_any, qkv_any, segc_any, normed_any,
        wqkv_any, x_any, dres_any, out_ref, prev_ref, lse_ref, segr_ref, small_ref, small_rows,
        gate_out, up_out, down_out, qkv_out, wout_out, small_out, out_home, dtok_home, prev_home,
        gate_line, up_line, down_line, gate_acc, up_acc, down_acc, branch_ref, wout_ref, att_ref, qkv_ref, segc_ref, normed_ref, wqkv_ref, x_ref, dres_ref,
        normed_turned, datt_ref, turned_ref, dqkv_ref, dk_sum, dv_sum, dn_send, dn_recv, dtok_ref,
        dense_ref, y1_land, x1_land, y1_acc, x1_acc, x2_land, y2_land, dense_acc, dense_line,
        tail_ref, ty1_land, tx1_land, ty1_acc, tx1_acc, tx2_land, ty2_land, tail_acc, tail_line,
        dense_sum, dense_sib, tail_sum, tail_sib, small_wide,
        send_sems, recv_sems, local_sems,
    ) = refs
    y, x, z, core = position()
    sibling = (y * 2 + x, z, 1 - core)
    across = (y * 2 + 1 - x, z, core)
    along = ((1 - y) * 2 + x, z, core)
    moved = y != core
    near = ((1 - y) * 2 + x, z, 1 - core)
    far = (core * 2 + 1 - x, z, y)
    greet(
        [
            (sibling, True), (across, True), (along, True),
            (near, moved), (far, moved),
            ((y * 2 + x, z + 1, core), z < depth - 1), ((y * 2 + x, z - 1, core), z > 0),
        ]
    )
    mail = Mail(send_sems, recv_sems)
    length, width = normed_ref.shape
    mine = length // 2
    span = wout_ref.shape[0]
    pairs = span // LANES
    own_rows = pl.ds(pl.multiple_of(core * mine, mine), mine)
    shares = [
        (gate_acc, gate_line, gate_out), (up_acc, up_line, up_out), (down_acc, down_line, down_out)
    ]
    line = Line(
        mail, depth, [(acc, landing) for acc, landing, _ in shares], range(1, depth - 1)
    )
    branch_copy = mail.copy(branch_any, branch_ref.at[own_rows], sibling)
    loads = [
        pltpu.make_async_copy(source, target, local_sems.at[k])
        for k, (source, target) in enumerate(
            [
                (gate_any, gate_acc), (up_any, up_acc), (down_any, down_acc), (branch_any, branch_ref.at[own_rows]),
                (normed_any, normed_ref), (att_any, att_ref), (wout_any, wout_ref),
                (segc_any, segc_ref), (qkv_any, qkv_ref), (wqkv_any, wqkv_ref),
                (x_any, x_ref), (dres_any, dres_ref),
            ]
        )
    ]
    homes = [(out_ref, out_home), (prev_ref, prev_home), (dtok_ref, dtok_home)]
    nears = [mail.copy(a.at[x], b.at[x], near) for a, b in homes]
    fars = [mail.copy(a.at[1 - x], b.at[x], far) for a, b in homes]
    stays = [
        pltpu.make_async_copy(a.at[x], b.at[x], local_sems.at[len(loads) + k])
        for k, (a, b) in enumerate(homes)
    ]

    def go_near(k):
        @pl.when(moved)
        def _():
            nears[k].start()

        @pl.when(jnp.logical_not(moved))
        def _():
            stays[k].start()

    half_copy = mail.copy(turned_ref.at[1 - core], dense_ref.at[0, core], sibling)
    planes = [
        Plane(
            mail, dense_ref.at[c],
            [b.at[c] for b in (y1_land, x1_land, y1_acc, x1_acc, x2_land, y2_land)],
            dense_acc.at[c],
        )
        for c in range(pairs + 1)
    ] + [
        Plane(
            mail, tail_ref, (ty1_land, tx1_land, ty1_acc, tx1_acc, tx2_land, ty2_land), tail_acc
        )
    ]
    dense = Line(
        mail, depth,
        [(dense_acc.at[c], dense_line.at[c]) for c in range(pairs + 1)] + [(tail_acc, tail_line)],
        range(depth - 1),
    )
    chunks = pairs + 2
    size = tail_sum.shape[0]
    half = size // 2
    other = pl.ds(pl.multiple_of((1 - core) * half, 8), half)
    ours = pl.ds(pl.multiple_of(core * half, 8), half)
    sums = [(dense_sum.at[c], dense_sib.at[c]) for c in range(pairs + 1)] + [(tail_sum, tail_sib)]
    lasts = [mail.copy(a.at[other], b, sibling) for a, b in sums]
    dn_copies = [mail.copy(dn_send.at[b], dn_recv.at[b], sibling) for b in range(2)]

    branch_copy.start()
    for copy in loads:
        copy.start()
    fars[0].start()
    fars[1].start()
    go_near(0)
    go_near(1)

    for item in range(3):
        loads[item].wait()
        line.send(1, item)
    for item in range(3):
        line.send_edge(2, item)
    loads[4].wait()
    normed_turned[...] = normed_ref[...].T
    for k in (3, 5, 6, 7):
        loads[k].wait()
    branch_copy.wait_recv()

    @pl.loop(0, length // rows)
    def _(block):
        here = pl.ds(pl.multiple_of(block * rows, rows), rows)
        valid = (segc_ref[here, 0:1] != SEGS - 1.0).astype(F32)
        datt_ref[here, :] = (
            dot(branch_ref[here, :], wout_ref[...], ((1,), (1,))) * valid
        ).astype(BF16)

    att_turned = att_ref[...].T
    for side in range(2):
        part = dot(att_turned, branch_ref[:, side * span : (side + 1) * span]).astype(BF16)
        turned_ref[side] = part.reshape(turned_ref.shape[1:])
    half_copy.start()
    dense_ref[0, core] = turned_ref[core]
    for k in (8, 9):
        loads[k].wait()
    small_wide[...] = jnp.zeros_like(small_wide)

    quarter = width // 4

    @pl.loop(0, pairs)
    def _(pair):
        back_pair(
            pair, rows, reach, span, qkv_ref, datt_ref, segc_ref, segr_ref, lse_ref, dqkv_ref,
            dk_sum, dv_sum,
        )
        columns = [
            pl.ds(pl.multiple_of(part * span + pair * LANES, LANES), LANES) for part in range(3)
        ]

        @pl.loop(0, 4)
        def _(fourth):
            here = pl.ds(pl.multiple_of(fourth * quarter, quarter), quarter)
            d_pair = jnp.concatenate([dqkv_ref[:, at] for at in columns], axis=1)
            weights = jnp.concatenate([wqkv_ref[here, at] for at in columns], axis=1)
            grads = dot(normed_turned[here, :], d_pair)
            dense_ref[1 + pair, fourth // 2, fourth % 2] = grads.astype(BF16)
            gain = jnp.sum(grads * weights.astype(F32), axis=1, keepdims=True)
            lane = lax.broadcasted_iota(jnp.int32, (quarter, LANES), 1)
            small_wide[here, :] += jnp.where(lane == SMALL - 1, gain, 0.0)

        for now in range(pairs):

            @pl.when(pair == now)
            def _():
                planes[now + 1].start()
                if now == 0:
                    half_copy.wait_recv()
                    planes[0].start()
                if now == 1:
                    for item in range(3):
                        line.take(1, item)
                        line.send(2, item)
                if now >= 1:
                    planes[now - 1].middle()
                if now >= 2:
                    planes[now - 2].end()
                    dense.send(0, now - 2)
                    for step in range(1, depth - 1):
                        dense.send_edge(step, now - 2)

    small_all = small_rows[...].astype(F32)
    gain_column = column(widen(small_all), SMALL - 2)
    lane = lax.broadcasted_iota(jnp.int32, (width, LANES), 1)
    small_grads = jnp.where(
        lane < SMALL - 1, widen(small_ref[...]), small_wide[...] / gain_column
    )
    tail_ref[...] = small_grads.astype(BF16).reshape(tail_ref.shape)
    planes[chunks - 1].start()

    def partial(start, step):
        b = 1 - x if step == 0 else x
        here = pl.ds(pl.multiple_of(start * mine + b * rows, rows), rows)
        return b, dot(dqkv_ref[here, :], wqkv_ref[...], ((1,), (1,)))

    def launch(c):
        planes[c].end()
        dense.send(0, c)
        for step in range(1, depth - 1):
            dense.send_edge(step, c)

    for step in range(2):
        b, value = partial(1 - core, step)
        dn_send[step] = value.astype(BF16)
        dn_copies[step].start()
    planes[pairs - 1].middle()
    launch(pairs - 2)
    planes[pairs].middle()
    launch(pairs - 1)
    planes[pairs + 1].middle()
    loads[10].wait()
    loads[11].wait()
    gain_row = small_all[SMALL - 2 : SMALL - 1, :]
    for step in range(2):
        b, value = partial(core, step)
        here = pl.ds(pl.multiple_of(b * rows, rows), rows)
        values = x_ref[here, :].astype(F32)
        dn_copies[step].wait_recv()
        d_normed = value + dn_recv[step].astype(F32)
        inverse = lax.rsqrt(jnp.mean(values * values, axis=-1, keepdims=True) + NORM_EPS)
        scaled = d_normed * gain_row
        mean = jnp.mean(scaled * values, axis=-1, keepdims=True)
        result = dres_ref[here, :] + inverse * scaled
        result = result - values * (inverse * inverse * inverse * mean)
        dtok_ref[b] = result.astype(BF16)
        if step == 0:
            fars[2].start()
            launch(pairs)
            launch(pairs + 1)
        else:
            go_near(2)
    for item, (_, _, result) in enumerate(shares):

        def store(value, add=False):
            result[0] = result[0] + value if add else value

        line.finish(item, store)
    for step in range(depth - 2):
        for c in range(chunks):
            dense.take(step, c)
            dense.send(step + 1, c)
    for c, (total, _) in enumerate(sums):

        def store(value, add=False):
            total[...] = total[...] + value if add else value

        dense.finish(c, store)
        lasts[c].start()
    for c, (total, land) in enumerate(sums):
        own = total[ours]
        lasts[c].wait_recv()
        theirs = land[...]
        if c == 0:
            for side, value in ((core, own), (1 - core, theirs)):
                wout_out[:, pl.ds(pl.multiple_of(side * span, LANES), span)] = value
        elif c <= pairs:
            for part in range(3):
                for side, value in ((core, own), (1 - core, theirs)):
                    at = part * 2 * span + side * span + (c - 1) * LANES
                    qkv_out[:, pl.ds(pl.multiple_of(at, LANES), LANES)] = value[
                        :, part * LANES : (part + 1) * LANES
                    ]
        else:
            small_out[...] = own + theirs
    for copy in [branch_copy, half_copy] + lasts + dn_copies:
        copy.wait_send()
    for plane in planes:
        plane.close()
    line.close()
    dense.close()
    for copy in fars:
        copy.wait()

    @pl.when(moved)
    def _():
        for copy in nears:
            copy.wait()

    @pl.when(jnp.logical_not(moved))
    def _():
        for copy in stays:
            copy.wait()


def back_all(
    grad_gate, grad_up, grad_down, d_branch, w_out, attended, qkv, seg_col, normed, qkv_weight,
    x_own, d_residual, block_out, d_prev, lse, seg_row, small, small_all,
):
    depth = lax.axis_size("dp")
    length, width = normed.shape
    mine = length // 2
    span = width // 2
    rows = block_out.shape[1]
    groups = span // LANES + 1
    wide = 3 * LANES
    quarter = width // 4
    size = quarter // depth
    parts = [grad.shape[1:] for grad in (grad_gate, grad_up, grad_down)]
    vmem = pl.BlockSpec(memory_space=pltpu.VMEM)
    anywhere = pl.BlockSpec(memory_space=pl.ANY)
    homes = [block_out.shape, block_out.shape, d_prev.shape]
    kinds = [block_out.dtype, BF16, d_prev.dtype]
    steps = 2 * (depth - 1)
    copies = 6 * (depth - 2) + 2 + 6 + (groups + 1) * (4 + steps + 1) + 2

    def plane_buffers(lead, columns):
        return [
            pltpu.VMEM(lead + dims + (columns,), BF16)
            for dims in (
                [(2, 2, quarter)] + [(2, quarter // 2)] * 4 + [(quarter // 2,)] * 2
                + [(depth, size), (2, depth - 1, size)]
            )
        ]

    return pl.pallas_call(
        functools.partial(back_kernel, depth, rows, length // 2),
        in_specs=[anywhere] * 12 + [vmem] * 6,
        out_specs=[vmem] * 6 + [anywhere] * 3,
        out_shape=[shape((1,) + part, F32) for part in parts]
        + [shape((size // 2, 6 * span), F32), shape((size // 2, width), F32)]
        + [shape((size // 2, LANES), F32)]
        + [shape(dims, kind) for dims, kind in zip(homes, kinds)],
        scratch_shapes=[pltpu.VMEM((2, depth - 2) + part, BF16) for part in parts]
        + [pltpu.VMEM((depth,) + part, BF16) for part in parts]
        + [
            pltpu.VMEM((length, width), BF16), pltpu.VMEM((span, width), BF16),
            pltpu.VMEM((length, span), BF16), pltpu.VMEM((length, 3 * span), BF16),
            pltpu.VMEM((length, LANES), F32), pltpu.VMEM((length, width), BF16),
            pltpu.VMEM((width, 3 * span), BF16), pltpu.VMEM((mine, width), BF16),
            pltpu.VMEM((mine, width), F32), pltpu.VMEM((width, length), BF16),
            pltpu.VMEM((length, span), BF16), pltpu.VMEM((2, 2, quarter, span), BF16),
            pltpu.VMEM((length, 3 * span), BF16), pltpu.VMEM((length, LANES), F32),
            pltpu.VMEM((length, LANES), F32), pltpu.VMEM((2, rows, width), BF16),
            pltpu.VMEM((2, rows, width), BF16), pltpu.VMEM((2, rows, width), BF16),
        ]
        + plane_buffers((groups,), wide)
        + plane_buffers((), LANES)
        + [
            pltpu.VMEM((groups, size, wide), F32), pltpu.VMEM((groups, size // 2, wide), F32),
            pltpu.VMEM((size, LANES), F32), pltpu.VMEM((size // 2, LANES), F32),
            pltpu.VMEM((width, LANES), F32),
            pltpu.SemaphoreType.DMA((copies,)),
            pltpu.SemaphoreType.DMA((copies,)),
            pltpu.SemaphoreType.DMA((15,)),
        ],
        compiler_params=pltpu.CompilerParams(
            collective_id=1, has_side_effects=True, vmem_limit_bytes=62 * 1024 * 1024
        ),
        name="back_all",
    )(
        grad_gate, grad_up, grad_down, d_branch, w_out, attended, qkv, seg_col, normed, qkv_weight, x_own, d_residual,
        block_out, d_prev, lse, seg_row, small, small_all,
    )


def deliver_kernel(
    routes,
    out_ref, dtok_ref, prev_ref, qkv_ref, wout_ref, small_ref, gate_ref, up_ref, down_ref,
    out_end, tokens_end, prev_end, gain_a_end, qkv_end, wout_end, gain_m_end, router_end,
    cproj_end, cvec_end, gate_end, up_end, down_end,
):
    for source, target in (
        (out_ref, out_end), (qkv_ref, qkv_end), (wout_ref, wout_end), (gate_ref, gate_end),
        (up_ref, up_end), (down_ref, down_end),
    ):
        target[...] = source[...]
    tokens_end[...] = dtok_ref[...].astype(F32)
    for m in range(2):
        for route in range(routes):
            prev_end[route, m : m + 1, :] = prev_ref[m, route : route + 1, :]
    count = small_ref.shape[0]
    turned = widen(small_ref[...])
    router_end[...] = turned[0:routes, 0:count]
    cproj_end[...] = turned[8:12, 0:count]
    cvec_end[...] = turned[12:14, 0:count]
    gain_m_end[...] = turned[14:15, 0:count].reshape(count)
    gain_a_end[...] = turned[15:16, 0:count].reshape(count)


def deliver(routes, out, dtok, prev, qkv, wout, small, gate, up, down):
    count = small.shape[0]
    vmem = pl.BlockSpec(memory_space=pltpu.VMEM)
    return pl.pallas_call(
        functools.partial(deliver_kernel, routes),
        in_specs=[vmem] * 9,
        out_specs=[vmem] * 13,
        out_shape=[
            shape(out.shape, BF16), shape(dtok.shape, F32), shape((routes, 2, prev.shape[2]), F32),
            shape((count,), F32), shape(qkv.shape, F32), shape(wout.shape, F32),
            shape((count,), F32), shape((routes, count), F32), shape((4, count), F32),
            shape((2, count), F32), shape(gate.shape, F32), shape(up.shape, F32),
            shape(down.shape, F32),
        ],
        compiler_params=params(),
        cost_estimate=cost(1e6, 8e6),
        name="deliver",
    )(out, dtok, prev, qkv, wout, small, gate, up, down)


def one_chip(
    tokens,
    prev_logits,
    segments,
    routes,
    cotangent,
    gain_attn,
    w_qkv,
    w_out,
    gain_moe,
    w_router,
    const_proj,
    const_vec,
    w_gate,
    w_up,
    w_down,
):
    rows = tokens.shape[1]
    route_count = w_router.shape[1]
    experts = route_count - 4
    (
        x_own, ctl, normed, qkv, attended, lse, small_all, qkv_weight, out_sib,
        seg_col, seg_row, g_rows,
    ) = gather_all(
        experts, tokens, cotangent, w_qkv, w_out, prev_logits, routes, segments, w_router, const_proj,
        const_vec, gain_attn, gain_moe,
    )
    (
        block_out, d_prev, d_residual, d_branch, small, grad_gate, grad_up, grad_down,
    ) = expert_layer(
        experts, route_count, rows, attended, x_own, cotangent, ctl, w_out, out_sib, small_all,
        w_gate[0], w_up[0], w_down[0], g_rows,
    )

    (
        share_gate, share_up, share_down, share_qkv, share_out, share_small, out_home, dtok_home,
        prev_home,
    ) = back_all(
        grad_gate, grad_up, grad_down, d_branch, w_out, attended, qkv, seg_col, normed,
        qkv_weight, x_own, d_residual, block_out, d_prev, lse, seg_row, small, small_all,
    )
    (
        block_out, grad_tokens, grad_prev, gain_a, grad_qkv, grad_out, gain_m, grad_router,
        grad_cproj, grad_cvec, grad_gate, grad_up, grad_down,
    ) = deliver(
        route_count, out_home, dtok_home, prev_home, share_qkv, share_out, share_small,
        share_gate, share_up, share_down,
    )
    return (
        block_out, grad_tokens, jnp.transpose(grad_prev, (1, 2, 0)), gain_a, grad_qkv, grad_out,
        gain_m, grad_router.T, grad_cproj.T, grad_cvec.T, grad_gate, grad_up, grad_down,
    )


def suits(mesh, tokens, w_router, w_gate):
    peers = mesh.shape["ep"]
    rows = tokens.shape[1] // peers
    micro = tokens.shape[0] // (mesh.shape["dp"] * mesh.shape["fs"])
    routes = w_router.shape[1]
    return (
        peers == 4
        and mesh.shape["fs"] == 2
        and micro == 2
        and mesh.shape["dp"] == 4
        and (routes - 4) * 2 == peers
        and 3 * rows // routes == LANES
        and tokens.shape[2] % (2 * LANES) == 0
    )


def solution(mesh):
    placed = (
        P(("dp", "fs"), "ep", None),
        P(("dp", "fs"), "ep", None),
        P(("dp", "fs"), None),
        P(("dp", "fs"), "ep", None),
        P(("dp", "fs"), "ep", None),
        P("fs"),
        P("fs", None),
        P("fs", None),
        P("fs"),
        P("fs", None),
        P("fs", None),
        P("fs", None),
        P("ep", "fs", None),
        P("ep", "fs", None),
        P("ep", "fs", None),
    )
    def layer(*arrays):
        fits = suits(mesh, arrays[0], arrays[9], arrays[12])
        return mapped(one_chip if fits else shards)(*arrays)

    def mapped(body):
        return jax.shard_map(
            body,
            mesh=mesh,
            in_specs=placed,
            out_specs=(
                P(("dp", "fs"), "ep", None),
                P(("dp", "fs"), "ep", None),
                P(("dp", "fs"), "ep", None),
                P(("ep", "dp", "fs")),
                P(("ep", "dp", "fs"), None),
                P(("ep", "dp", "fs"), None),
                P(("ep", "dp", "fs")),
                P(("ep", "dp", "fs"), None),
                P(("ep", "dp", "fs"), None),
                P(("ep", "dp", "fs"), None),
                P("ep", ("dp", "fs"), None),
                P("ep", ("dp", "fs"), None),
                P("ep", ("dp", "fs"), None),
            ),
            check_vma=False,
        )

    return layer
```

```python
import functools

import jax
import jax.numpy as jnp
from jax import lax
from jax.experimental import pallas as pl
from jax.experimental.pallas import tpu as pltpu
from jax.sharding import PartitionSpec as P

HEAD = 64
SEGS = 4


NORM_EPS = 1e-06
MASK_FILL = -1e30
HIGHEST = lax.Precision.HIGHEST


def rms_scale(values, gains):
    inverse = lax.rsqrt(jnp.mean(values * values, axis=-1, keepdims=True) + NORM_EPS)
    return values * inverse * gains


def small_softmax(logit_rows):
    largest = jnp.max(logit_rows, axis=-1, keepdims=True)
    powers = jnp.exp(logit_rows - largest)
    return powers / jnp.sum(powers, axis=-1, keepdims=True)


def add_tuple(first_tuple, second_tuple):
    if first_tuple is None:
        return second_tuple
    return tuple(
        (first_term + second_term for first_term, second_term in zip(first_tuple, second_tuple))
    )


def shards(
    tokens,
    prev_logits,
    segments,
    routes,
    cotangent,
    gain_attn,
    w_qkv,
    w_out,
    gain_moe,
    w_router,
    const_proj,
    const_vec,
    w_gate,
    w_up,
    w_down,
):
    micro_count, row_count, model_width = tokens.shape
    head_count = model_width // HEAD
    peer_count = lax.axis_size("ep")
    my_index = lax.axis_index("ep")
    route_count = w_router.shape[1]
    expert_count = route_count - 4
    half_count = peer_count // expert_count
    capacity = (3 * row_count // route_count + 7) // 8 * 8
    seq_length = row_count * peer_count
    slot_count = expert_count * capacity
    pos_all = jnp.arange(seq_length, dtype=jnp.int32)
    pos_mine = my_index * row_count + jnp.arange(row_count, dtype=jnp.int32)
    expert_ids = jnp.arange(expert_count, dtype=jnp.int32)
    slot_ids = jnp.arange(slot_count, dtype=jnp.int32)
    route_ids = jnp.arange(route_count, dtype=jnp.int32)
    layer_outputs = []
    input_grads = []
    prev_grads = []
    dense_acc = None
    expert_acc = None
    for step_index in range(micro_count):
        gathered = (
            lax.all_gather(w_qkv, "fs", axis=0, tiled=True),
            lax.all_gather(w_out, "fs", axis=0, tiled=True),
            lax.all_gather(w_router, "fs", axis=0, tiled=True),
            lax.all_gather(const_proj, "fs", axis=0, tiled=True),
            lax.all_gather(const_vec, "fs", axis=0, tiled=True),
            lax.all_gather(gain_attn, "fs", axis=0, tiled=True),
            lax.all_gather(gain_moe, "fs", axis=0, tiled=True),
            lax.all_gather(w_gate, "fs", axis=1, tiled=True),
            lax.all_gather(w_up, "fs", axis=1, tiled=True),
            lax.all_gather(w_down, "fs", axis=1, tiled=True),
        )
        (
            qkv_weight,
            out_weight,
            router_weight,
            cproj_weight,
            cvec_weight,
            attn_gain,
            moe_gain,
            gate_weight,
            up_weight,
            down_weight,
        ) = gathered
        gate_weight = gate_weight[0]
        up_weight = up_weight[0]
        down_weight = down_weight[0]
        attn_gain = attn_gain.astype(jnp.float32)
        moe_gain = moe_gain.astype(jnp.float32)
        router_float = router_weight.astype(jnp.float32)
        cproj_float = cproj_weight.astype(jnp.float32)
        cvec_float = cvec_weight.astype(jnp.float32)
        token_rows = tokens[step_index].astype(jnp.float32)
        seg_all = segments[step_index]
        seg_mine = lax.dynamic_slice_in_dim(seg_all, my_index * row_count, row_count)
        allowed = (seg_mine[:, None] == seg_all[None, :]) & (pos_all[None, :] <= pos_mine[:, None])
        valid_rows = (seg_mine != SEGS - 1).astype(jnp.float32)[:, None]
        normed = rms_scale(token_rows, attn_gain).astype(jnp.bfloat16)
        qkv_rows = jnp.dot(normed, qkv_weight, preferred_element_type=jnp.float32).astype(
            jnp.bfloat16
        )
        queries = qkv_rows[:, :model_width].reshape(row_count, head_count, HEAD)
        keys_local = qkv_rows[:, model_width : 2 * model_width]
        values_local = qkv_rows[:, 2 * model_width :]
        keys_all, values_all = (
            lax.all_gather(keys_local, "ep", axis=0, tiled=True),
            lax.all_gather(values_local, "ep", axis=0, tiled=True),
        )
        key_heads = keys_all.reshape(seq_length, head_count, HEAD)
        value_heads = values_all.reshape(seq_length, head_count, HEAD)
        scores = (
            jnp.einsum("qhd,khd->hqk", queries, key_heads, preferred_element_type=jnp.float32)
            * 0.125
        )
        scores = jnp.where(allowed[None], scores, MASK_FILL)
        largest = jnp.max(scores, axis=-1, keepdims=True)
        powers = jnp.exp(scores - largest)
        row_total = jnp.sum(powers, axis=-1, keepdims=True)
        log_total = largest + jnp.log(row_total)
        attn_probs = powers / row_total
        attended = jnp.einsum(
            "hqk,khd->qhd",
            attn_probs.astype(jnp.bfloat16),
            value_heads,
            preferred_element_type=jnp.float32,
        ).reshape(row_count, model_width)
        attended = (attended * valid_rows).astype(jnp.bfloat16)
        residual = token_rows + jnp.dot(attended, out_weight, preferred_element_type=jnp.float32)
        mixed = rms_scale(residual, moe_gain).astype(jnp.bfloat16)
        mixed_float = mixed.astype(jnp.float32)
        logits = (
            jnp.dot(mixed, router_weight, preferred_element_type=jnp.float32)
            + prev_logits[step_index]
        )
        router_probs = small_softmax(logits)
        route_rows = routes[step_index]
        choose = (route_rows[:, :, None] == route_ids[None, None, :]).astype(jnp.float32)
        gate_values = jnp.sum(choose * router_probs[:, None, :], axis=-1)
        const_logits = jnp.dot(mixed, cproj_weight, preferred_element_type=jnp.float32)
        mixings = []
        const_outs = []
        for const_index in range(2):
            mixing = small_softmax(const_logits[:, 2 * const_index : 2 * const_index + 2])
            mixings.append(mixing)
            const_outs.append(
                mixing[:, :1] * mixed_float + mixing[:, 1:] * cvec_float[:, const_index][None, :]
            )
        pair_route = route_rows.reshape(-1)
        expert_hit = (pair_route[:, None] == expert_ids[None, :]).astype(jnp.int32)
        slot_index = jnp.sum((jnp.cumsum(expert_hit, axis=0) - expert_hit) * expert_hit, axis=1)
        slot_cell = jnp.sum(expert_hit * expert_ids[None, :], axis=1) * capacity + slot_index
        slot_place = jnp.where(jnp.sum(expert_hit, axis=1) > 0, slot_cell, -1)
        slot_table = (slot_ids[:, None] == slot_place[None, :]).astype(jnp.bfloat16)
        pair_rows = jnp.repeat(mixed, 2, axis=0)
        packed = jnp.einsum(
            "sp,pd->sd", slot_table, pair_rows, preferred_element_type=jnp.float32
        ).astype(jnp.bfloat16)
        outgoing = jnp.broadcast_to(
            packed.reshape(expert_count, 1, capacity, model_width),
            (expert_count, half_count, capacity, model_width),
        ).reshape(peer_count, capacity, model_width)
        received = lax.all_to_all(outgoing, "ep", split_axis=0, concat_axis=0, tiled=True)
        flat_rows = received.reshape(-1, model_width)
        gate_part = jnp.dot(flat_rows, gate_weight, preferred_element_type=jnp.float32)
        up_part = jnp.dot(flat_rows, up_weight, preferred_element_type=jnp.float32)
        hidden = (jax.nn.silu(gate_part) * up_part).astype(jnp.bfloat16)
        part_out = (
            jnp.dot(hidden, down_weight, preferred_element_type=jnp.float32)
            .astype(jnp.bfloat16)
            .reshape(received.shape)
        )
        returned_rows = lax.all_to_all(part_out, "ep", split_axis=0, concat_axis=0, tiled=True)
        returned_rows, kept_rows = (returned_rows, received)
        halves = returned_rows.reshape(expert_count, half_count, capacity, model_width)
        pair_ffn = jnp.zeros((2 * row_count, model_width), jnp.float32)
        for half_index in range(half_count):
            pair_ffn = pair_ffn + jnp.einsum(
                "sp,sd->pd",
                slot_table,
                halves[:, half_index].reshape(slot_count, model_width),
                preferred_element_type=jnp.float32,
            )
        expert_out = pair_ffn.reshape(row_count, 2, model_width)
        expert_out = (
            expert_out + choose[:, :, expert_count + 1 : expert_count + 2] * mixed_float[:, None, :]
        )
        for const_index in range(2):
            column = expert_count + 2 + const_index
            expert_out = (
                expert_out + choose[:, :, column : column + 1] * const_outs[const_index][:, None, :]
            )
        result_rows = residual + jnp.sum(gate_values[:, :, None] * expert_out, axis=1)
        layer_outputs.append(result_rows.astype(jnp.bfloat16))
        grad_rows = cotangent[step_index].astype(jnp.float32)
        d_gates = jnp.sum(expert_out * grad_rows[:, None, :], axis=-1)
        d_probs = jnp.sum(choose * d_gates[:, :, None], axis=1)
        d_logits = router_probs * (
            d_probs - jnp.sum(router_probs * d_probs, axis=-1, keepdims=True)
        )
        prev_grads.append(d_logits)
        grad_router = jnp.dot(mixed_float.T, d_logits, precision=HIGHEST)
        d_mixed = jnp.dot(d_logits, router_float.T, precision=HIGHEST)
        weighted = gate_values[:, :, None] * grad_rows[:, None, :]
        d_mixed = d_mixed + jnp.sum(
            choose[:, :, expert_count + 1 : expert_count + 2] * weighted, axis=1
        )
        cproj_grads = []
        cvec_grads = []
        for const_index in range(2):
            column = expert_count + 2 + const_index
            mixing = mixings[const_index]
            d_const = jnp.sum(choose[:, :, column : column + 1] * weighted, axis=1)
            d_mix = jnp.stack(
                [
                    jnp.sum(d_const * mixed_float, axis=-1),
                    jnp.sum(d_const * cvec_float[:, const_index][None, :], axis=-1),
                ],
                axis=-1,
            )
            d_mixlog = mixing * (d_mix - jnp.sum(mixing * d_mix, axis=-1, keepdims=True))
            cproj_grads.append(jnp.dot(mixed_float.T, d_mixlog, precision=HIGHEST))
            cvec_grads.append(jnp.sum(mixing[:, 1:] * d_const, axis=0))
            d_mixed = (
                d_mixed
                + mixing[:, :1] * d_const
                + jnp.dot(
                    d_mixlog,
                    cproj_float[:, 2 * const_index : 2 * const_index + 2].T,
                    precision=HIGHEST,
                )
            )
        grad_cproj = jnp.concatenate(cproj_grads, axis=1)
        grad_cvec = jnp.stack(cvec_grads, axis=1)
        d_pairs = weighted.reshape(2 * row_count, model_width).astype(jnp.bfloat16)
        d_packed = jnp.einsum(
            "sp,pd->sd", slot_table, d_pairs, preferred_element_type=jnp.float32
        ).astype(jnp.bfloat16)
        d_outgoing = jnp.broadcast_to(
            d_packed.reshape(expert_count, 1, capacity, model_width),
            (expert_count, half_count, capacity, model_width),
        ).reshape(peer_count, capacity, model_width)
        d_received = lax.all_to_all(d_outgoing, "ep", split_axis=0, concat_axis=0, tiled=True)
        flat_rows = kept_rows.reshape(-1, model_width)
        flat_grads = d_received.reshape(-1, model_width)
        gate_part = jnp.dot(flat_rows, gate_weight, preferred_element_type=jnp.float32)
        up_part = jnp.dot(flat_rows, up_weight, preferred_element_type=jnp.float32)
        activated = jax.nn.silu(gate_part)
        hidden = (activated * up_part).astype(jnp.bfloat16)
        grad_down = jnp.einsum("rf,rd->fd", hidden, flat_grads, preferred_element_type=jnp.float32)
        d_hidden = jnp.einsum(
            "rd,fd->rf", flat_grads, down_weight, preferred_element_type=jnp.float32
        )
        sigmoid_gate = jax.nn.sigmoid(gate_part)
        d_gate_part = (
            d_hidden * up_part * sigmoid_gate * (1.0 + gate_part * (1.0 - sigmoid_gate))
        ).astype(jnp.bfloat16)
        d_up_part = (d_hidden * activated).astype(jnp.bfloat16)
        grad_gate = jnp.einsum(
            "rd,rf->df", flat_rows, d_gate_part, preferred_element_type=jnp.float32
        )
        grad_up = jnp.einsum("rd,rf->df", flat_rows, d_up_part, preferred_element_type=jnp.float32)
        d_inputs = jnp.einsum(
            "rf,df->rd", d_gate_part, gate_weight, preferred_element_type=jnp.float32
        )
        d_inputs = d_inputs + jnp.einsum(
            "rf,df->rd", d_up_part, up_weight, preferred_element_type=jnp.float32
        )
        d_inputs = d_inputs.astype(jnp.bfloat16).reshape(peer_count, capacity, model_width)
        d_returned = lax.all_to_all(d_inputs, "ep", split_axis=0, concat_axis=0, tiled=True)
        d_halves = d_returned.reshape(expert_count, half_count, capacity, model_width)
        for half_index in range(half_count):
            d_pair_in = jnp.einsum(
                "sp,sd->pd",
                slot_table,
                d_halves[:, half_index].reshape(slot_count, model_width),
                preferred_element_type=jnp.float32,
            )
            d_mixed = d_mixed + jnp.sum(d_pair_in.reshape(row_count, 2, model_width), axis=1)
        expert_acc = add_tuple(expert_acc, (grad_gate, grad_up, grad_down))
        moe_vjp = jax.vjp(rms_scale, residual, moe_gain)[1]
        d_residual_norm, grad_moe_gain = moe_vjp(d_mixed)
        d_residual = grad_rows + d_residual_norm
        d_branch = d_residual.astype(jnp.bfloat16)
        grad_out = jnp.einsum("rd,re->de", attended, d_branch, preferred_element_type=jnp.float32)
        d_attended = (
            jnp.einsum("re,de->rd", d_branch, out_weight, preferred_element_type=jnp.float32)
            * valid_rows
        ).astype(jnp.bfloat16)
        d_heads = d_attended.reshape(row_count, head_count, HEAD)
        scores = (
            jnp.einsum("qhd,khd->hqk", queries, key_heads, preferred_element_type=jnp.float32)
            * 0.125
        )
        scores = jnp.where(allowed[None], scores, MASK_FILL)
        attn_probs = jnp.exp(scores - log_total)
        d_weights = jnp.einsum(
            "qhd,khd->hqk", d_heads, value_heads, preferred_element_type=jnp.float32
        )
        delta_rows = jnp.sum(attn_probs * d_weights, axis=-1, keepdims=True)
        d_scores = (attn_probs * (d_weights - delta_rows)).astype(jnp.bfloat16)
        d_queries = (
            jnp.einsum(
                "hqk,khd->qhd", d_scores, key_heads, preferred_element_type=jnp.float32
            ).reshape(row_count, model_width)
            * 0.125
        )
        d_values = jnp.einsum(
            "hqk,qhd->khd",
            attn_probs.astype(jnp.bfloat16),
            d_heads,
            preferred_element_type=jnp.float32,
        ).reshape(seq_length, model_width)
        d_keys = (
            jnp.einsum(
                "hqk,qhd->khd", d_scores, queries, preferred_element_type=jnp.float32
            ).reshape(seq_length, model_width)
            * 0.125
        )
        d_keys_mine, d_values_mine = (
            lax.psum_scatter(
                d_keys.astype(jnp.bfloat16), "ep", scatter_dimension=0, tiled=True
            ).astype(jnp.float32),
            lax.psum_scatter(
                d_values.astype(jnp.bfloat16), "ep", scatter_dimension=0, tiled=True
            ).astype(jnp.float32),
        )
        d_qkv = jnp.concatenate([d_queries, d_keys_mine, d_values_mine], axis=1).astype(
            jnp.bfloat16
        )
        grad_qkv = jnp.einsum("rd,re->de", normed, d_qkv, preferred_element_type=jnp.float32)
        d_normed = jnp.einsum("re,de->rd", d_qkv, qkv_weight, preferred_element_type=jnp.float32)
        attn_vjp = jax.vjp(rms_scale, token_rows, attn_gain)[1]
        d_tokens_norm, grad_attn_gain = attn_vjp(d_normed)
        input_grads.append(d_residual + d_tokens_norm)
        dense_terms = (
            grad_attn_gain,
            grad_qkv,
            grad_out,
            grad_moe_gain,
            grad_router,
            grad_cproj,
            grad_cvec,
        )
        dense_shares = (
            lax.psum_scatter(dense_terms[0], ("ep", "dp", "fs"), scatter_dimension=0, tiled=True),
            lax.psum_scatter(dense_terms[1], ("ep", "dp", "fs"), scatter_dimension=0, tiled=True),
            lax.psum_scatter(dense_terms[2], ("ep", "dp", "fs"), scatter_dimension=0, tiled=True),
            lax.psum_scatter(dense_terms[3], ("ep", "dp", "fs"), scatter_dimension=0, tiled=True),
            lax.psum_scatter(dense_terms[4], ("ep", "dp", "fs"), scatter_dimension=0, tiled=True),
            lax.psum_scatter(dense_terms[5], ("ep", "dp", "fs"), scatter_dimension=0, tiled=True),
            lax.psum_scatter(dense_terms[6], ("ep", "dp", "fs"), scatter_dimension=0, tiled=True),
        )
        dense_acc = add_tuple(dense_acc, dense_shares)
    expert_shares = (
        lax.psum_scatter(
            expert_acc[0][None].astype(jnp.bfloat16), ("dp", "fs"), scatter_dimension=1, tiled=True
        ).astype(jnp.float32),
        lax.psum_scatter(
            expert_acc[1][None].astype(jnp.bfloat16), ("dp", "fs"), scatter_dimension=1, tiled=True
        ).astype(jnp.float32),
        lax.psum_scatter(
            expert_acc[2][None].astype(jnp.bfloat16), ("dp", "fs"), scatter_dimension=1, tiled=True
        ).astype(jnp.float32),
    )
    return (
        jnp.stack(layer_outputs),
        jnp.stack(input_grads),
        jnp.stack(prev_grads),
        dense_acc[0],
        dense_acc[1],
        dense_acc[2],
        dense_acc[3],
        dense_acc[4],
        dense_acc[5],
        dense_acc[6],
        expert_shares[0],
        expert_shares[1],
        expert_shares[2],
    )


NEG = -1e30
KINDS = 2
SMALL = 16
LANES = 128
F32 = jnp.float32
BF16 = jnp.bfloat16


def dot(lhs, rhs, dims=((1,), (0,)), precision=None):
    return lax.dot_general(
        lhs, rhs, (dims, ((), ())), precision=precision, preferred_element_type=F32
    )


def key_span(block, rows, reach):
    start = max(0, block * rows - reach)
    return start, (block + 1) * rows - start


def column(rows, index):
    return rows[:, index : index + 1]


def chosen_of(ctl):
    lane = lax.broadcasted_iota(jnp.int32, ctl.shape, 1).astype(F32)
    return ((lane == column(ctl, 8)) | (lane == column(ctl, 9))).astype(F32)


def shape(dims, dtype):
    return jax.ShapeDtypeStruct(dims, dtype)


def whole(dims):
    return pl.BlockSpec(dims, lambda *_: (0,) * len(dims))


def per_row(rows, width):
    return pl.BlockSpec((rows, width), lambda i: (i, 0))


def params():
    return pltpu.CompilerParams(vmem_limit_bytes=56 * 1024 * 1024)


def cost(flops, moved):
    return pl.CostEstimate(flops=int(flops), bytes_accessed=int(moved), transcendentals=0)


class Mail:
    def __init__(self, send_sems, recv_sems):
        self.send_sems = send_sems
        self.recv_sems = recv_sems
        self.used = 0

    def copy(self, source, target, device):
        slot = self.used
        self.used = slot + 1
        return pltpu.make_async_remote_copy(
            src_ref=source,
            dst_ref=target,
            send_sem=self.send_sems.at[slot],
            recv_sem=self.recv_sems.at[slot],
            device_id=device,
            device_id_type=pl.DeviceIdType.MESH,
        )


def position():
    place = lax.axis_index("ep")
    return place // 2, place % 2, lax.axis_index("dp"), lax.axis_index("fs")


def greet(devices):
    barrier = pltpu.get_barrier_semaphore()
    total = 0
    for device, present in devices:
        if present is True:
            pl.semaphore_signal(
                barrier, inc=1, device_id=device, device_id_type=pl.DeviceIdType.MESH
            )
            total = total + 1
        else:

            @pl.when(present)
            def _():
                pl.semaphore_signal(
                    barrier, inc=1, device_id=device, device_id_type=pl.DeviceIdType.MESH
                )

            total = total + jnp.where(present, 1, 0)
    pl.semaphore_wait(barrier, total)


def attend_pair(pair, rows, reach, span, qkv_ref, segc_ref, segr_ref, att_ref, lse_ref):
    length = qkv_ref.shape[0]
    at_q, at_k, at_v = (
        pl.ds(pl.multiple_of(part * span + pair * LANES, LANES), LANES) for part in range(3)
    )
    for block in range(length // rows):
        start, width = key_span(block, rows, reach)
        here = pl.ds(block * rows, rows)
        there = pl.ds(start, width)
        queries = qkv_ref[here, at_q] * 0.125
        keys = qkv_ref[there, at_k]
        values = qkv_ref[there, at_v]
        seg_q = segc_ref[here, 0:1]
        seg_k = segr_ref[0:1, there]
        past = width - rows
        order = lax.broadcasted_iota(jnp.int32, (rows, rows), 1) <= lax.broadcasted_iota(
            jnp.int32, (rows, rows), 0
        )

        def masked(scores):
            near = jnp.where((seg_q == seg_k[:, past:]) & order, scores[:, past:], NEG)
            if past == 0:
                return near
            far = jnp.where(seg_q == seg_k[:, :past], scores[:, :past], NEG)
            return jnp.concatenate([far, near], axis=1)

        lane = lax.broadcasted_iota(jnp.int32, (rows, LANES), 1)
        outs = []
        logs = []
        for head in range(2):
            mine = (lane // HEAD) == head
            scores = masked(dot(jnp.where(mine, queries, 0), keys, ((1,), (1,))))
            largest = jnp.max(scores, axis=-1, keepdims=True)
            powers = jnp.exp(scores - largest)
            total = jnp.sum(powers, axis=-1, keepdims=True)
            outs.append(dot(powers.astype(BF16), values) / total)
            logs.append(largest + jnp.log(total))
        valid = (seg_q != SEGS - 1.0).astype(F32)
        att = jnp.where(lane < HEAD, outs[0], outs[1]) * valid
        att_ref[here, at_q] = att.astype(BF16)
        both = jnp.where(lane < HEAD, logs[0], logs[1]).T
        lse_ref[pair, 0:1, here] = both[0:1, :]
        lse_ref[pair, 1:2, here] = both[HEAD : HEAD + 1, :]


def gather_kernel(
    rows, reach, routes, experts,
    tok_ref, cot_ref, wqkv_ref, wout_ref, prev_ref, route_ref, seg_ref, router_ref, cproj_ref,
    cvec_ref, gain_a_ref, gain_m_ref,
    x_out, ctl_own, normed_out, qkv_out, att_ref, lse_ref, small_all, wqkv_out,
    wout_sib, segc_ref, segr_ref, g_rows,
    x_all, normed_ref, qkv_ref, wqkv_all, cot_wide, g_send, ctl_send, small_wide, small_send, seg_all,
    near_send, near_recv, far_send, far_recv, core_send, core_recv, local_sems,
    pack_send, pack_recv,
):
    y, x, z, core = position()
    me = y * 2 + x
    sibling = (me, z, 1 - core)
    moved = y != core
    near = ((1 - y) * 2 + x, z, 1 - core)
    far = (core * 2 + 1 - x, z, y)
    plane = [((y + k // 2) % 2 * 2 + (x + k) % 2) for k in range(4)]
    greet([((plane[k], z, (core + c) % 2), True) for k in range(4) for c in range(2) if k + c > 0])
    span = wqkv_ref.shape[0]
    halves = 4 // experts

    def pack(m, k, target=None):
        return pltpu.make_async_remote_copy(
            src_ref=g_send.at[m, plane[k] // halves],
            dst_ref=g_rows.at[x, core * 2 + m] if target is None else g_rows.at[target],
            send_sem=pack_send.at[m, k],
            recv_sem=pack_recv.at[x, core * 2 + m] if target is None else pack_recv.at[target],
            device_id=(plane[k], z, y),
            device_id_type=pl.DeviceIdType.MESH,
        )

    pack_stays = [
        pltpu.make_async_copy(
            g_send.at[m, y // (halves // 2)], g_rows.at[x, core * 2 + m], local_sems.at[7 + m]
        )
        for m in range(2)
    ]
    cot_load = pltpu.make_async_copy(cot_ref, cot_wide, local_sems.at[9])

    def block_of(index):
        return pl.ds(pl.multiple_of(index * rows, rows), rows)

    homes = [
        (tok_ref, x_all.at[block_of(me)]),
        (ctl_send, ctl_own.at[x]),
    ]
    nears = Mail(near_send, near_recv)
    fars = Mail(far_send, far_recv)
    near_copies = [nears.copy(a.at[x], b, near) for a, b in homes]
    far_copies = [fars.copy(a.at[1 - x], b, far) for a, b in homes]
    stay_copies = [
        pltpu.make_async_copy(a.at[x], b, local_sems.at[k]) for k, (a, b) in enumerate(homes)
    ]

    def send(k):
        far_copies[k].start()

        @pl.when(moved)
        def _():
            near_copies[k].start()

        @pl.when(jnp.logical_not(moved))
        def _():
            stay_copies[k].start()

    def take_near(k):
        @pl.when(moved)
        def _():
            near_copies[k].wait_recv()

        @pl.when(jnp.logical_not(moved))
        def _():
            stay_copies[k].wait()

    send(0)
    cot_load.start()
    inner = Mail(core_send, core_recv)
    weight_copies = []
    own_copies = []
    band = pl.ds(pl.multiple_of(core * span, span), span)
    for part in range(3):
        columns = pl.ds(part * span, span)
        for side, copies in ((1 - core, weight_copies), (core, own_copies)):
            source = wqkv_ref.at[
                :, pl.ds(pl.multiple_of(part * 2 * span + side * span, LANES), span)
            ]
            target = wqkv_all.at[band, columns]
            if copies is weight_copies:
                copies.append(inner.copy(source, target, sibling))
            else:
                copies.append(
                    pltpu.make_async_copy(source, target, local_sems.at[3 + part])
                )
    out_copy = inner.copy(wout_ref, wout_sib, sibling)
    seg_copy = inner.copy(seg_ref, seg_all.at[core], sibling)
    seg_own = pltpu.make_async_copy(seg_ref, seg_all.at[core], local_sems.at[6])
    small_copy = inner.copy(small_send, small_all.at[:, band], sibling)
    seg_copy.start()
    seg_own.start()
    for copy in weight_copies + own_copies:
        copy.start()

    small_wide[...] = jnp.zeros_like(small_wide)
    small_wide[0:routes, :] = router_ref[...].astype(F32)
    small_wide[8:12, :] = cproj_ref[...].astype(F32)
    small_wide[12:14, :] = cvec_ref[...].astype(F32)
    small_wide[14:15, :] = gain_a_ref[...].astype(F32).reshape(1, span)
    small_wide[15:16, :] = gain_m_ref[...].astype(F32).reshape(1, span)
    turned = small_wide[...]
    small_send[...] = turned.astype(BF16)
    small_all[:, band] = turned.astype(BF16)
    small_copy.start()
    out_copy.start()
    ctl_send[...] = jnp.zeros_like(ctl_send)
    for m in range(2):
        for route in range(routes):
            ctl_send[m, route : route + 1, :] = prev_ref[route, m : m + 1, :]
        ctl_send[m, 8:10, :] = route_ref[m].astype(F32)
    send(1)
    cot_load.wait()
    earlier = lax.broadcasted_iota(jnp.int32, (rows, rows), 0) < lax.broadcasted_iota(
        jnp.int32, (rows, rows), 1
    )
    slot = lax.broadcasted_iota(jnp.int32, (LANES, rows), 0).astype(F32)
    number = lax.broadcasted_iota(jnp.int32, (8, rows), 0)
    for m in range(2):
        chosen = ((number == route_ref[m, 0:1, :]) | (number == route_ref[m, 1:2, :])).astype(F32)
        rank = dot(chosen.astype(BF16), earlier.astype(BF16))
        for expert in range(experts):
            hit = (slot == rank[expert : expert + 1, :]) & (chosen[expert : expert + 1, :] > 0.0)
            g_send[m, expert] = dot(hit.astype(BF16), cot_wide[m]).astype(BF16)

    def send_packs():
        for m in range(2):
            for k in range(1, 4):
                pack(m, k).start()

            @pl.when(moved)
            def _():
                pack(m, 0).start()

            @pl.when(jnp.logical_not(moved))
            def _():
                pack_stays[m].start()

    seg_copy.wait_recv()
    seg_own.wait()
    seg_row = seg_all[y, pl.ds(x, 1), :].astype(F32)
    length = seg_row.shape[1]
    segr_ref[...] = jnp.broadcast_to(seg_row, segr_ref.shape)
    segc_ref[...] = jnp.broadcast_to(seg_row, (LANES, length)).T
    small_copy.wait_recv()
    for copy in weight_copies:
        copy.wait_recv()
    for copy in own_copies:
        copy.wait()
    gain = small_all[14:15, :].astype(F32)

    def project(index):
        here = block_of(index)
        values = x_all[here, :].astype(F32)
        inverse = lax.rsqrt(jnp.mean(values * values, axis=-1, keepdims=True) + NORM_EPS)
        normed = (values * inverse * gain).astype(BF16)
        normed_ref[here, :] = normed
        qkv_ref[here, :] = dot(normed, wqkv_all[...]).astype(BF16)

    forward = []
    for step in range(2):
        spot = x_all.at[block_of(core * 2 + (x if step == 0 else 1 - x))]
        forward.append(inner.copy(spot, spot, sibling))
    take_near(0)
    forward[0].start()
    project(core * 2 + x)
    far_copies[0].wait_recv()
    forward[1].start()
    send_packs()
    project(core * 2 + 1 - x)
    forward[0].wait_recv()
    project((1 - core) * 2 + x)
    forward[1].wait_recv()
    project((1 - core) * 2 + 1 - x)

    own_rows = pl.ds(pl.multiple_of(core * 2 * rows, rows), 2 * rows)
    results = [
        pltpu.make_async_copy(source, target, local_sems.at[10 + k])
        for k, (source, target) in enumerate(
            (
                (x_all.at[own_rows], x_out), (normed_ref, normed_out), (qkv_ref, qkv_out),
                (wqkv_all, wqkv_out),
            )
        )
    ]
    for copy in results:
        copy.start()

    @pl.loop(0, span // LANES)
    def _(pair):
        attend_pair(pair, rows, reach, span, qkv_ref, segc_ref, segr_ref, att_ref, lse_ref)

    for copy in results:
        copy.wait()
    take_near(1)
    far_copies[1].wait_recv()
    for there in range(2):
        for peer in range(4):
            kept = (y == core) & (x == there) & (core == peer // 2)

            @pl.when(jnp.logical_not(kept))
            def _():
                pack(0, 0, (there, peer)).wait_recv()

    for m in range(2):
        for k in range(1, 4):
            pack(m, k).wait_send()

        @pl.when(moved)
        def _():
            pack(m, 0).wait_send()

        @pl.when(jnp.logical_not(moved))
        def _():
            pack_stays[m].wait()

    out_copy.wait_recv()
    for copy in far_copies + weight_copies + forward + [out_copy, seg_copy, small_copy]:
        copy.wait_send()

    @pl.when(moved)
    def _():
        for copy in near_copies:
            copy.wait_send()


def gather_all(
    experts, tokens, cotangent, w_qkv, w_out, prev_logits, routes, segments, w_router, const_proj,
    const_vec, gain_attn, gain_moe,
):
    rows, width = tokens.shape[1:]
    length = segments.shape[1]
    span = width // 2
    vmem = pl.BlockSpec(memory_space=pltpu.VMEM)
    anywhere = pl.BlockSpec(memory_space=pl.ANY)
    return pl.pallas_call(
        functools.partial(gather_kernel, rows, length // 2, w_router.shape[1], experts),
        in_specs=[anywhere] * 4 + [vmem] * 8,
        out_specs=[anywhere, vmem, anywhere, anywhere, vmem, vmem, vmem, anywhere, anywhere]
        + [vmem] * 2
        + [anywhere],
        out_shape=[
            shape((length // 2, width), BF16),
            shape((2, SMALL, rows), F32), shape((length, width), BF16),
            shape((length, 3 * span), BF16), shape((length, span), BF16),
            shape((span // LANES, 8, length), F32), shape((SMALL, width), BF16),
            shape((width, 3 * span), BF16), shape((span, width), BF16),
            shape((length, LANES), F32), shape((8, length), F32),
            shape((2, 4, LANES, width), BF16),
        ],
        scratch_shapes=[
            pltpu.VMEM((length, width), BF16), pltpu.VMEM((length, width), BF16),
            pltpu.VMEM((length, 3 * span), BF16), pltpu.VMEM((width, 3 * span), BF16),
            pltpu.VMEM((2, rows, width), BF16), pltpu.VMEM((2, experts, LANES, width), BF16),
            pltpu.VMEM((2, SMALL, rows), F32),
            pltpu.VMEM((SMALL, span), F32), pltpu.VMEM((SMALL, span), BF16),
            pltpu.VMEM((2, 2, length), jnp.int32),
        ]
        + [pltpu.SemaphoreType.DMA((3,))] * 4
        + [pltpu.SemaphoreType.DMA((8,))] * 2
        + [pltpu.SemaphoreType.DMA((14,))]
        + [pltpu.SemaphoreType.DMA((2, 4))] * 2,
        compiler_params=pltpu.CompilerParams(
            collective_id=3, has_side_effects=True, vmem_limit_bytes=60 * 1024 * 1024
        ),
        name="gather_all",
    )(
        tokens, cotangent, w_qkv, w_out, jnp.transpose(prev_logits, (2, 0, 1)),
        jnp.swapaxes(routes, 1, 2), segments, w_router.T, const_proj.T, const_vec.T, gain_attn,
        gain_moe,
    )


def widen(turned):
    pad = jnp.zeros((LANES - turned.shape[0], turned.shape[1]), turned.dtype)
    return jnp.concatenate([turned, pad], axis=0).T


def spread_block(experts, routes, rows, block, refs, sent, got, keep):
    send_ref, gate_send = sent
    recv_ref, gate_recv = got
    att_own, att_sib, x_ref, ctl_ref, w_own, w_sib, small_rows, wide_rows = refs
    residual_ref, mixed_ref, pm_ref, place_ref = keep
    y, x, z, core = position()
    here = pl.ds(pl.multiple_of(block * rows, rows), rows)
    tokens = x_ref[here, :]
    residual = tokens.astype(F32) + (
        dot(att_own[here, :], w_own[...]) + dot(att_sib[here, :], w_sib[...])
    )
    residual_ref[here, :] = residual
    inverse = lax.rsqrt(jnp.mean(residual * residual, axis=-1, keepdims=True) + NORM_EPS)
    mixed = (residual * inverse * small_rows[15:16, :].astype(F32)).astype(BF16)
    mixed_ref[here, :] = mixed
    logits = dot(mixed, wide_rows[...], ((1,), (1,)))
    ctl = widen(ctl_ref[block])
    lane = lax.broadcasted_iota(jnp.int32, (rows, LANES), 1)
    is_route = lane < routes
    router = jnp.where(is_route, logits + ctl, NEG)
    powers = jnp.exp(router - jnp.max(router, axis=-1, keepdims=True))
    probs = powers / jnp.sum(powers, axis=-1, keepdims=True)
    probs = jnp.where(is_route, probs, 0.0)
    pm = probs
    for const_index in range(2):
        first = column(logits, 8 + 2 * const_index)
        second = column(logits, 9 + 2 * const_index)
        largest = jnp.maximum(first, second)
        first = jnp.exp(first - largest)
        second = jnp.exp(second - largest)
        total = first + second
        pm = jnp.where(lane == 8 + 2 * const_index, first / total, pm)
        pm = jnp.where(lane == 9 + 2 * const_index, second / total, pm)
    pm_ref[here, :] = pm
    chosen = chosen_of(ctl)
    gated = chosen * probs
    earlier = lax.broadcasted_iota(jnp.int32, (rows, rows), 1) < lax.broadcasted_iota(
        jnp.int32, (rows, rows), 0
    )
    rank = dot(earlier.astype(BF16), chosen.astype(BF16))
    lane_f = lane.astype(F32)
    for expert in range(experts):
        place = jnp.where(
            (lane_f == column(rank, expert)) & (column(chosen, expert) > 0.0), 1.0, 0.0
        )
        place_ref[here, expert * LANES : (expert + 1) * LANES] = place.astype(BF16)
        pick = place.T.astype(BF16)
        send_ref[block, expert] = dot(pick, mixed).astype(BF16)
        gates = jnp.sum(place * column(gated, expert), axis=0, keepdims=True)
        gate_send[block, expert] = jnp.broadcast_to(gates, gate_send.shape[2:])
    recv_ref[block, y * 2 + x] = send_ref[block, y]
    gate_recv[block, y * 2 + x] = gate_send[block, y]


def expert_block(block, got, result_ref, back_ref, weights, keep, send):
    recv_ref, gate_recv, g_rows = got
    gate_w, up_w, down_w = weights
    hidden_ref, d_gate_ref, d_up_ref, d_rows_ref = keep
    y, x, z, core = position()
    peers, capacity, width = recv_ref.shape[1:]
    size = peers * capacity
    here = pl.ds(pl.multiple_of(block * size, size), size)
    rows = recv_ref[block].reshape(size, width)
    gate = dot(rows, gate_w[...])
    up = dot(rows, up_w[...])
    sig = jax.nn.sigmoid(gate)
    active = gate * sig
    hidden = (active * up).astype(BF16)
    hidden_ref[here, :] = hidden
    part = dot(hidden, down_w[...]).astype(BF16)
    result_ref[block, :, 0] = part.reshape(peers, capacity, width)
    send(0)
    for peer in range(peers):
        spread = jnp.concatenate([gate_recv[block, peer]] * (capacity // 8), axis=0).T
        d_part = column(spread, 0) * g_rows[block, peer].astype(F32)
        at = pl.ds(pl.multiple_of(block * size + peer * capacity, capacity), capacity)
        d_rows_ref[at, :] = d_part.astype(BF16)
    d_rows = d_rows_ref[here, :]
    d_hidden = dot(d_rows, down_w[...], ((1,), (1,)))
    d_gate = (d_hidden * up * sig * (1.0 + gate * (1.0 - sig))).astype(BF16)
    d_up = (d_hidden * active).astype(BF16)
    d_gate_ref[here, :] = d_gate
    d_up_ref[here, :] = d_up
    d_in = dot(d_gate, gate_w[...], ((1,), (1,))) + dot(d_up, up_w[...], ((1,), (1,)))
    result_ref[block, :, 1] = d_in.astype(BF16).reshape(peers, capacity, width)
    send(1)
    back_ref[block, y * 2 + x] = result_ref[block, y * 2 + x]


def combine_forward(experts, routes, rows, block, refs, keep, back_ref, outs, small_ref):
    g_ref, ctl_ref, small_rows, wide_rows = refs
    residual_ref, mixed_ref, pm_ref, place_ref = keep
    out_ref, prev_ref, dres_ref, branch_ref = outs
    halves = back_ref.shape[1] // experts
    here = pl.ds(pl.multiple_of(block * rows, rows), rows)
    g_low = g_ref[here, :]
    grads = g_low.astype(F32)
    mixed = mixed_ref[here, :].astype(F32)
    residual = residual_ref[here, :]
    pm = pm_ref[here, :]
    lane = lax.broadcasted_iota(jnp.int32, (rows, LANES), 1)
    chosen = chosen_of(widen(ctl_ref[block]))
    probs = jnp.where(lane < routes, pm, 0.0)
    gated = chosen * probs
    d_probs = jnp.zeros((rows, LANES), F32)
    result = residual
    for expert in range(experts):
        place = place_ref[here, expert * LANES : (expert + 1) * LANES]
        expert_out = None
        for half in range(halves):
            term = dot(place, back_ref[block, expert * halves + half, 0])
            expert_out = term if expert_out is None else expert_out + term
        result = result + column(gated, expert) * expert_out
        d_gate = jnp.sum(expert_out * grads, axis=-1, keepdims=True)
        d_probs = jnp.where(lane == expert, d_gate, d_probs)
    g_mixed = jnp.sum(grads * mixed, axis=-1, keepdims=True)
    g_const = dot(g_low, wide_rows[...], ((1,), (1,)))
    copy = experts + 1
    d_probs = jnp.where(lane == copy, g_mixed, d_probs)
    weight = column(gated, copy)
    d_small = jnp.zeros((rows, LANES), F32)
    for const_index in range(2):
        route = copy + 1 + const_index
        first = column(pm, 8 + 2 * const_index)
        second = column(pm, 9 + 2 * const_index)
        gate = column(gated, route)
        g_vec = column(g_const, 12 + const_index)
        d_probs = jnp.where(lane == route, first * g_mixed + second * g_vec, d_probs)
        weight = weight + gate * first
        vec = small_rows[12 + const_index : 13 + const_index, :].astype(F32)
        result = result + (gate * second) * vec
        d_first = gate * g_mixed
        d_second = gate * g_vec
        mean = first * d_first + second * d_second
        d_small = jnp.where(lane == 8 + 2 * const_index, first * (d_first - mean), d_small)
        d_small = jnp.where(lane == 9 + 2 * const_index, second * (d_second - mean), d_small)
        d_small = jnp.where(lane == 12 + const_index, gate * second, d_small)
    result = result + weight * mixed
    out_ref[block] = result.astype(BF16)
    d_probs = d_probs * chosen
    d_logits = probs * (d_probs - jnp.sum(probs * d_probs, axis=-1, keepdims=True))
    d_small = jnp.where(lane < routes, d_logits, d_small)
    dres_ref[here, :] = weight * grads + dot(
        jnp.where(lane < 12, d_small, 0.0), wide_rows[...].astype(F32), precision=HIGHEST
    )
    d_turned = d_small.T[:SMALL, :]
    prev_ref[block] = d_turned[:8, :]
    sub = lax.broadcasted_iota(jnp.int32, (SMALL, rows), 0)
    small = dot(jnp.where(sub < 12, d_turned, 0.0), mixed, precision=HIGHEST)
    small_ref[...] += small + dot(
        jnp.where((sub >= 12) & (sub < 14), d_turned, 0.0), grads, precision=HIGHEST
    )


def combine_backward(experts, rows, block, refs, keep, back_ref, outs, small_ref):
    g_ref, ctl_ref, small_rows, wide_rows = refs
    residual_ref, mixed_ref, pm_ref, place_ref = keep
    out_ref, prev_ref, dres_ref, branch_ref = outs
    halves = back_ref.shape[1] // experts
    here = pl.ds(pl.multiple_of(block * rows, rows), rows)
    grads = g_ref[here, :].astype(F32)
    residual = residual_ref[here, :]
    d_mixed = dres_ref[here, :]
    for expert in range(experts):
        place = place_ref[here, expert * LANES : (expert + 1) * LANES]
        for half in range(halves):
            d_mixed = d_mixed + dot(place, back_ref[block, expert * halves + half, 1])
    inverse = lax.rsqrt(jnp.mean(residual * residual, axis=-1, keepdims=True) + NORM_EPS)
    scaled = d_mixed * small_rows[15:16, :].astype(F32)
    mean = jnp.mean(scaled * residual, axis=-1, keepdims=True)
    d_residual = grads + inverse * scaled - residual * (inverse * inverse * inverse * mean)
    dres_ref[here, :] = d_residual
    branch_ref[here, :] = d_residual.astype(BF16)
    small_ref[14:15, :] += jnp.sum(d_mixed * residual * inverse, axis=0, keepdims=True)


def layer_kernel(
    experts, routes, rows, blocks,
    ctl_ref, small_rows, att_ref, cot_ref, x_any, own_any, sib_any, g_any, gate_ref, up_ref,
    down_ref,
    out_end, prev_ref, dres_end, branch_end, small_ref, gate_acc, up_acc, down_acc,
    dgate_out, dup_out, ddown_out, gate_land, up_land, down_land, gate_line, up_line, down_line,
    wide_rows, att_own, att_sib, gate_w, up_w, down_w, residual_ref, mixed_ref, pm_ref, place_ref,
    send_ref, gate_send, gate_recv, recv_ref, result_ref, back_ref, hidden_ref, d_gate_ref,
    d_up_ref, d_rows_ref, g_ref, x_ref, w_own, w_sib, g_rows, out_ref, dres_ref, branch_ref, end_sems,
    head_send, head_recv, local_sems, send_sems, recv_sems, back_send, back_recv, sum_send, sum_recv,
    g_sends, g_recvs,
):
    y, x, z, core = position()
    me = y * 2 + x
    sibling = (me, z, 1 - core)
    partners = [(1 - y) * 2 + 1 - x, y * 2 + 1 - x, (1 - y) * 2 + x]
    wanted = [1 - y, y, 1 - y]
    depth = lax.axis_size("dp")
    plane = [((y + k // 2) % 2 * 2 + (x + k) % 2) for k in range(4)]
    greet(
        [((plane[k], z, (core + c) % 2), True) for k in range(4) for c in range(2) if k + c > 0]
        + [((me, z + 1, core), z < depth - 1), ((me, z - 1, core), z > 0)]
    )
    moved = y != core
    g_place = g_ref.at[pl.ds(pl.multiple_of(x * rows, rows), rows)]
    g_mail = Mail(g_sends, g_recvs)
    g_near = g_mail.copy(cot_ref.at[x], g_place, ((1 - y) * 2 + x, z, 1 - core))
    g_far = g_mail.copy(cot_ref.at[1 - x], g_place, (core * 2 + 1 - x, z, y))
    g_stay = pltpu.make_async_copy(cot_ref.at[x], g_place, local_sems.at[4])
    g_far.start()

    @pl.when(moved)
    def _():
        g_near.start()

    @pl.when(jnp.logical_not(moved))
    def _():
        g_stay.start()

    sums = Mail(sum_send, sum_recv)
    grads = [
        (dgate_out, gate_land, gate_acc, gate_line), (dup_out, up_land, up_acc, up_line),
        (ddown_out, down_land, down_acc, down_line),
    ]

    def share(ref, shard, side):
        size = ref.shape[0] // (2 * depth)
        return pl.ds(pl.multiple_of((shard * 2 + side) * size, size), size)

    halves = [
        [
            sums.copy(ref.at[share(ref, shard, 1 - core)], land.at[shard], sibling)
            for shard in range(depth)
        ]
        for ref, land, _, _ in grads
    ]
    line = Line(sums, depth, [(acc, landing) for _, _, acc, landing in grads], range(1))

    def add_halves(item):
        ref, land, acc, _ = grads[item]
        for shard in range(depth):
            halves[item][shard].wait_recv()
            acc[shard] = (
                ref[share(ref, shard, core)].astype(F32) + land[shard].astype(F32)
            ).astype(BF16)
        line.send(0, item)

    mine = rows * blocks
    mail = Mail(head_send, head_recv)
    pairs = [(gate_ref, gate_w), (up_ref, up_w), (down_ref, down_w)]
    heads = [mail.copy(att_ref.at[1 - core], att_sib, sibling)]
    locals_ = [pltpu.make_async_copy(att_ref.at[core], att_own, local_sems.at[3])]
    for k, (source, target) in enumerate(pairs):
        size = source.shape[0]
        spot = target.at[pl.ds(pl.multiple_of(core * size, size), size)]
        heads.append(mail.copy(source, spot, sibling))
        locals_.append(pltpu.make_async_copy(source, spot, local_sems.at[k]))
    loads = [
        pltpu.make_async_copy(source, target, local_sems.at[5 + k])
        for k, (source, target) in enumerate(
            ((x_any, x_ref), (own_any, w_own), (sib_any, w_sib), (g_any, g_rows))
        )
    ]
    heads[0].start()
    locals_[0].start()
    for copy in loads[:3] + heads[1:] + locals_[1:] + loads[3:]:
        copy.start()

    def dispatch(block, k, kind):
        source, target = ((send_ref, recv_ref), (gate_send, gate_recv))[kind]
        return pltpu.make_async_remote_copy(
            src_ref=source.at[block, wanted[k]],
            dst_ref=target.at[block, me],
            send_sem=send_sems.at[block, k, kind],
            recv_sem=recv_sems.at[block, k, kind],
            device_id=(partners[k], z, core),
            device_id_type=pl.DeviceIdType.MESH,
        )

    def giveback(block, k, kind):
        return pltpu.make_async_remote_copy(
            src_ref=result_ref.at[block, partners[k], kind],
            dst_ref=back_ref.at[block, me, kind],
            send_sem=back_send.at[block, k, kind],
            recv_sem=back_recv.at[block, k, kind],
            device_id=(partners[k], z, core),
            device_id_type=pl.DeviceIdType.MESH,
        )

    def ends(block):
        here = pl.ds(pl.multiple_of(block * rows, rows), rows)
        return [
            pltpu.make_async_copy(out_ref.at[block], out_end.at[block], end_sems.at[block, 0]),
            pltpu.make_async_copy(dres_ref.at[here], dres_end.at[here], end_sems.at[block, 1]),
            pltpu.make_async_copy(branch_ref.at[here], branch_end.at[here], end_sems.at[block, 2]),
        ]

    every = [(k, kind) for kind in range(KINDS) for k in range(3)]
    small_ref[...] = jnp.zeros_like(small_ref)
    wide_rows[...] = jnp.zeros_like(wide_rows)
    wide_rows[0:SMALL, :] = small_rows[...]
    heads[0].wait_recv()
    locals_[0].wait()
    for copy in loads[:3]:
        copy.wait()
    keep = (residual_ref, mixed_ref, pm_ref, place_ref)
    spread_refs = (
        att_own, att_sib, x_ref, ctl_ref, w_own, w_sib, small_rows, wide_rows
    )

    @pl.loop(0, blocks)
    def _(block):
        spread_block(
            experts, routes, rows, block, spread_refs, (send_ref, gate_send),
            (recv_ref, gate_recv), keep,
        )
        for k, kind in every:
            dispatch(block, k, kind).start()

    for copy in heads[1:]:
        copy.wait_recv()
    for copy in locals_[1:] + loads[3:]:
        copy.wait()

    @pl.loop(0, blocks)
    def _(block):
        for k, kind in every:
            dispatch(block, k, kind).wait_recv()

        def send(kind):
            for k in range(3):
                giveback(block, k, kind).start()

        expert_block(
            block, (recv_ref, gate_recv, g_rows), result_ref, back_ref, (gate_w, up_w, down_w),
            (hidden_ref, d_gate_ref, d_up_ref, d_rows_ref), send,
        )

    peers, capacity, width = recv_ref.shape[1:]
    total = blocks * peers * capacity
    step = 2 * LANES

    @pl.loop(0, width // step)
    def _(chunk):
        span = pl.ds(pl.multiple_of(chunk * step, step), step)
        lhs = recv_ref[:, :, :, span].reshape(total, step).T
        dgate_out[span, :] = dot(lhs, d_gate_ref[...]).astype(BF16)
        dup_out[span, :] = dot(lhs, d_up_ref[...]).astype(BF16)

    for copy in halves[0] + halves[1]:
        copy.start()

    @pl.loop(0, hidden_ref.shape[1] // step)
    def _(chunk):
        span = pl.ds(pl.multiple_of(chunk * step, step), step)
        lhs = hidden_ref[:, span].T
        ddown_out[span, :] = dot(lhs, d_rows_ref[...]).astype(BF16)

    for copy in halves[2]:
        copy.start()
    for item in range(3):
        add_halves(item)
    g_far.wait()

    @pl.when(moved)
    def _():
        g_near.wait()

    @pl.when(jnp.logical_not(moved))
    def _():
        g_stay.wait()

    @pl.loop(0, blocks)
    def _(block):
        refs = (g_ref, ctl_ref, small_rows, wide_rows)
        outs = (out_ref, prev_ref, dres_ref, branch_ref)
        for k in range(3):
            giveback(block, k, 0).wait_recv()
        combine_forward(
            experts, routes, rows, block, refs, keep, back_ref, outs, small_ref
        )
        for k in range(3):
            giveback(block, k, 1).wait_recv()
        combine_backward(experts, rows, block, refs, keep, back_ref, outs, small_ref)
        for copy in ends(block):
            copy.start()

    for item in range(3):
        line.take(0, item)
    for block in range(blocks):
        for copy in ends(block):
            copy.wait()
    for copy in heads + halves[0] + halves[1] + halves[2]:
        copy.wait_send()
    line.close()
    for block in range(blocks):
        for k, kind in every:
            dispatch(block, k, kind).wait_send()
            giveback(block, k, kind).wait_send()


def expert_layer(
    experts, routes, rows, attended, x_own, cot, ctl, w_own, w_sib, small_all, w_gate,
    w_up, w_down, g_rows,
):
    blocks, rows, width = cot.shape
    mine = blocks * rows
    peers = lax.axis_size("ep")
    span = attended.shape[1]
    hidden = w_gate.shape[1]
    vmem = pl.BlockSpec(memory_space=pltpu.VMEM)
    anywhere = pl.BlockSpec(memory_space=pl.ANY)
    total = blocks * peers * LANES
    grads = [(2 * w.shape[0], w.shape[1]) for w in (w_gate, w_up, w_down)]
    depth = lax.axis_size("dp")
    parts = [(dims[0] // (2 * depth), dims[1]) for dims in grads]
    sums = 3 * depth + 6
    return pl.pallas_call(
        functools.partial(layer_kernel, experts, routes, rows, blocks),
        in_specs=[vmem] * 2 + [anywhere] * 9,
        out_specs=[anywhere, vmem, anywhere, anywhere] + [vmem] * 4,
        out_shape=[
            shape((blocks, rows, width), BF16), shape((blocks, 8, rows), F32),
            shape((mine, width), F32), shape((mine, width), BF16), shape((SMALL, width), F32),
        ]
        + [shape((depth,) + part, BF16) for part in parts],
        scratch_shapes=[pltpu.VMEM(dims, BF16) for dims in grads]
        + [pltpu.VMEM((depth,) + part, BF16) for part in parts]
        + [pltpu.VMEM((2, 1) + part, BF16) for part in parts]
        + [pltpu.VMEM((LANES, width), BF16)]
        + [pltpu.VMEM((mine, span), BF16)] * 2
        + [pltpu.VMEM(dims, BF16) for dims in grads]
        + [
            pltpu.VMEM((mine, width), F32), pltpu.VMEM((mine, width), BF16),
            pltpu.VMEM((mine, LANES), F32), pltpu.VMEM((mine, experts * LANES), BF16),
            pltpu.VMEM((blocks, experts, LANES, width), BF16),
            pltpu.VMEM((blocks, experts, 8, LANES), F32), pltpu.VMEM((blocks, peers, 8, LANES), F32),
            pltpu.VMEM((blocks, peers, LANES, width), BF16),
        ]
        + [pltpu.VMEM((blocks, peers, KINDS, LANES, width), BF16)] * 2
        + [pltpu.VMEM((total, hidden), BF16)] * 3
        + [pltpu.VMEM((total, width), BF16), pltpu.VMEM((mine, width), BF16)]
        + [pltpu.VMEM((mine, width), BF16)]
        + [pltpu.VMEM((span, width), BF16)] * 2
        + [
            pltpu.VMEM((blocks, peers, LANES, width), BF16),
            pltpu.VMEM((blocks, rows, width), BF16), pltpu.VMEM((mine, width), F32),
            pltpu.VMEM((mine, width), BF16), pltpu.SemaphoreType.DMA((blocks, 3)),
        ]
        + [
            pltpu.SemaphoreType.DMA((4,)), pltpu.SemaphoreType.DMA((4,)),
            pltpu.SemaphoreType.DMA((9,)),
        ]
        + [pltpu.SemaphoreType.DMA((blocks, 3, KINDS))] * 4
        + [pltpu.SemaphoreType.DMA((sums,))] * 2
        + [pltpu.SemaphoreType.DMA((2,))] * 2,
        compiler_params=pltpu.CompilerParams(
            collective_id=2, has_side_effects=True, vmem_limit_bytes=62 * 1024 * 1024
        ),
        name="expert_layer",
    )(
        ctl, small_all, attended.reshape(2, mine, span), cot, x_own, w_own, w_sib, g_rows, w_gate,
        w_up, w_down,
    )


class Line:
    def __init__(self, mail, depth, slots, steps):
        self.depth = depth
        self.slots = slots
        self.first = steps[0]
        self.place = lax.axis_index("dp")
        y, x, z, core = position()
        self.copies = {}
        for way in range(2):
            step_to = 1 if way == 0 else -1
            device = (y * 2 + x, z + step_to, core)
            for step in steps:
                for item, (acc, landing) in enumerate(slots):
                    shard = self.shard(way, step)
                    safe = jnp.clip(shard, 0, depth - 1)
                    self.copies[way, step, item] = mail.copy(
                        acc.at[safe], landing.at[way, step - self.first], device
                    )

    def shard(self, way, step):
        if way == 0:
            return self.place + self.depth - 1 - step
        return self.place - (self.depth - 1 - step)

    def edge(self, way):
        return self.place == (0 if way == 0 else self.depth - 1)

    def sends(self, way, step):
        shard = self.shard(way, step)
        if way == 0:
            return (shard <= self.depth - 1) & (self.place < self.depth - 1)
        return (shard >= 0) & (self.place > 0)

    def gets(self, way, step):
        if way == 0:
            return (self.place > 0) & (self.shard(way, step + 1) <= self.depth - 1)
        return (self.place < self.depth - 1) & (self.shard(way, step + 1) >= 0)

    def send(self, step, item):
        for way in range(2):
            wanted = self.sends(way, step)
            if step > self.first:
                wanted = wanted & jnp.logical_not(self.edge(way))

            @pl.when(wanted)
            def _():
                self.copies[way, step, item].start()

    def send_edge(self, step, item):
        for way in range(2):

            @pl.when(self.sends(way, step) & self.edge(way))
            def _():
                self.copies[way, step, item].start()

    def take(self, step, item):
        acc, landing = self.slots[item]
        for way in range(2):
            shard = jnp.clip(self.shard(way, step + 1), 0, self.depth - 1)

            @pl.when(self.gets(way, step))
            def _():
                self.copies[way, step, item].wait_recv()
                acc[shard] = (
                    acc[shard].astype(F32) + landing[way, step - self.first].astype(F32)
                ).astype(BF16)

    def finish(self, item, store):
        acc, landing = self.slots[item]
        store(acc[self.place].astype(F32))
        for way in range(2):

            @pl.when(self.gets(way, self.depth - 2))
            def _():
                self.copies[way, self.depth - 2, item].wait_recv()
                store(landing[way, self.depth - 2 - self.first].astype(F32), True)

    def close(self):
        for (way, step, item), copy in self.copies.items():

            @pl.when(self.sends(way, step))
            def _():
                copy.wait_send()


class Plane:
    def __init__(self, mail, source, buffers, total):
        y, x, z, core = position()
        self.place = y, x
        self.source = source
        self.buffers = buffers
        self.total = total
        y1_land, x1_land, y1_acc, x1_acc, x2_land, y2_land = buffers
        half = x2_land.shape[0]
        self.low = pl.ds(0, half)
        self.high = pl.ds(half, half)
        across = (y * 2 + 1 - x, z, core)
        along = ((1 - y) * 2 + x, z, core)
        self.first = [
            mail.copy(source.at[1 - y, :, self.low], y1_land, along),
            mail.copy(source.at[:, 1 - x, self.high], x1_land, across),
        ]
        self.second = [
            mail.copy(y1_acc.at[1 - x], x2_land, across),
            mail.copy(x1_acc.at[1 - y], y2_land, along),
        ]

    def start(self):
        for copy in self.first:
            copy.start()

    def middle(self):
        y, x = self.place
        y1_land, x1_land, y1_acc, x1_acc, _, _ = self.buffers
        self.first[0].wait_recv()
        for k in range(2):
            y1_acc[k] = (
                self.source[y, k, self.low].astype(F32) + y1_land[k].astype(F32)
            ).astype(BF16)
        self.second[0].start()
        self.first[1].wait_recv()
        for k in range(2):
            x1_acc[k] = (
                self.source[k, x, self.high].astype(F32) + x1_land[k].astype(F32)
            ).astype(BF16)
        self.second[1].start()

    def end(self):
        y, x = self.place
        _, _, y1_acc, x1_acc, x2_land, y2_land = self.buffers
        shards, size = self.total.shape[0] // 2, self.total.shape[1]
        self.second[0].wait_recv()
        for shard in range(shards):
            part = pl.ds(shard * size, size)
            self.total[shard] = (
                y1_acc[x, part].astype(F32) + x2_land[part].astype(F32)
            ).astype(BF16)
        self.second[1].wait_recv()
        for shard in range(shards):
            part = pl.ds(shard * size, size)
            self.total[shards + shard] = (
                x1_acc[y, part].astype(F32) + y2_land[part].astype(F32)
            ).astype(BF16)

    def close(self):
        for copy in self.first + self.second:
            copy.wait_send()


def back_pair(
    pair, rows, reach, span, qkv_ref, datt_ref, segc_ref, segr_ref, lse_ref, dqkv_ref,
    dk_sum, dv_sum,
):
    length = qkv_ref.shape[0]
    at_q, at_k, at_v = (
        pl.ds(pl.multiple_of(part * span + pair * LANES, LANES), LANES) for part in range(3)
    )
    dk_sum[...] = jnp.zeros_like(dk_sum)
    dv_sum[...] = jnp.zeros_like(dv_sum)
    keys_turned = qkv_ref[:, at_k].T
    for block in range(length // rows):
        start, width = key_span(block, rows, reach)
        here = pl.ds(block * rows, rows)
        there = pl.ds(start, width)
        queries = qkv_ref[here, at_q] * 0.125
        grads = datt_ref[here, at_q]
        keys = qkv_ref[there, at_k]
        values = qkv_ref[there, at_v]
        seg_k = segc_ref[there, 0:1]
        seg_q = segr_ref[0:1, here]
        past = width - rows
        order = lax.broadcasted_iota(jnp.int32, (rows, rows), 0) <= lax.broadcasted_iota(
            jnp.int32, (rows, rows), 1
        )

        def masked(scores):
            near = jnp.where((seg_q == seg_k[past:]) & order, scores[past:], NEG)
            if past == 0:
                return near
            far = jnp.where(seg_q == seg_k[:past], scores[:past], NEG)
            return jnp.concatenate([far, near], axis=0)

        lane = lax.broadcasted_iota(jnp.int32, (rows, LANES), 1)
        dq_parts = []
        for head in range(2):
            mine = (lane // HEAD) == head
            head_q = jnp.where(mine, queries, 0)
            head_g = jnp.where(mine, grads, 0)
            log_total = lse_ref[pair, head : head + 1, here]
            probs = jnp.exp(masked(dot(keys, head_q, ((1,), (1,)))) - log_total)
            d_probs = dot(values, head_g, ((1,), (1,)))
            delta = jnp.sum(probs * d_probs, axis=0, keepdims=True)
            d_scores = (probs * (d_probs - delta)).astype(BF16)
            dv_sum[there, :] += dot(probs.astype(BF16), head_g)
            dk_sum[there, :] += dot(d_scores, head_q)
            turned = keys_turned[head * HEAD : (head + 1) * HEAD, start : start + width]
            dq_parts.append(dot(turned, d_scores))
        dq = jnp.concatenate(dq_parts, axis=0).T * 0.125
        dqkv_ref[here, at_q] = dq.astype(BF16)
    dqkv_ref[:, at_k] = dk_sum[...].astype(BF16)
    dqkv_ref[:, at_v] = dv_sum[...].astype(BF16)


def back_kernel(depth, rows, reach, *refs):
    (
        gate_any, up_any, down_any, branch_any, wout_any, att_any, qkv_any, segc_any, normed_any,
        wqkv_any, x_any, dres_any, out_ref, prev_ref, lse_ref, segr_ref, small_ref, small_rows,
        gate_out, up_out, down_out, qkv_out, wout_out, small_out, out_home, dtok_home, prev_home,
        gate_line, up_line, down_line, gate_acc, up_acc, down_acc, branch_ref, wout_ref, att_ref, qkv_ref, segc_ref, normed_ref, wqkv_ref, x_ref, dres_ref,
        normed_turned, datt_ref, turned_ref, dqkv_ref, dk_sum, dv_sum, dn_send, dn_recv, dtok_ref,
        dense_ref, y1_land, x1_land, y1_acc, x1_acc, x2_land, y2_land, dense_acc, dense_line,
        tail_ref, ty1_land, tx1_land, ty1_acc, tx1_acc, tx2_land, ty2_land, tail_acc, tail_line,
        dense_sum, dense_sib, tail_sum, tail_sib, small_wide,
        send_sems, recv_sems, local_sems,
    ) = refs
    y, x, z, core = position()
    sibling = (y * 2 + x, z, 1 - core)
    across = (y * 2 + 1 - x, z, core)
    along = ((1 - y) * 2 + x, z, core)
    moved = y != core
    near = ((1 - y) * 2 + x, z, 1 - core)
    far = (core * 2 + 1 - x, z, y)
    greet(
        [
            (sibling, True), (across, True), (along, True),
            (near, moved), (far, moved),
            ((y * 2 + x, z + 1, core), z < depth - 1), ((y * 2 + x, z - 1, core), z > 0),
        ]
    )
    mail = Mail(send_sems, recv_sems)
    length, width = normed_ref.shape
    mine = length // 2
    span = wout_ref.shape[0]
    pairs = span // LANES
    own_rows = pl.ds(pl.multiple_of(core * mine, mine), mine)
    shares = [
        (gate_acc, gate_line, gate_out), (up_acc, up_line, up_out), (down_acc, down_line, down_out)
    ]
    line = Line(
        mail, depth, [(acc, landing) for acc, landing, _ in shares], range(1, depth - 1)
    )
    branch_copy = mail.copy(branch_any, branch_ref.at[own_rows], sibling)
    loads = [
        pltpu.make_async_copy(source, target, local_sems.at[k])
        for k, (source, target) in enumerate(
            [
                (gate_any, gate_acc), (up_any, up_acc), (down_any, down_acc), (branch_any, branch_ref.at[own_rows]),
                (normed_any, normed_ref), (att_any, att_ref), (wout_any, wout_ref),
                (segc_any, segc_ref), (qkv_any, qkv_ref), (wqkv_any, wqkv_ref),
                (x_any, x_ref), (dres_any, dres_ref),
            ]
        )
    ]
    homes = [(out_ref, out_home), (prev_ref, prev_home), (dtok_ref, dtok_home)]
    nears = [mail.copy(a.at[x], b.at[x], near) for a, b in homes]
    fars = [mail.copy(a.at[1 - x], b.at[x], far) for a, b in homes]
    stays = [
        pltpu.make_async_copy(a.at[x], b.at[x], local_sems.at[len(loads) + k])
        for k, (a, b) in enumerate(homes)
    ]

    def go_near(k):
        @pl.when(moved)
        def _():
            nears[k].start()

        @pl.when(jnp.logical_not(moved))
        def _():
            stays[k].start()

    half_copy = mail.copy(turned_ref.at[1 - core], dense_ref.at[0, core], sibling)
    planes = [
        Plane(
            mail, dense_ref.at[c],
            [b.at[c] for b in (y1_land, x1_land, y1_acc, x1_acc, x2_land, y2_land)],
            dense_acc.at[c],
        )
        for c in range(pairs + 1)
    ] + [
        Plane(
            mail, tail_ref, (ty1_land, tx1_land, ty1_acc, tx1_acc, tx2_land, ty2_land), tail_acc
        )
    ]
    dense = Line(
        mail, depth,
        [(dense_acc.at[c], dense_line.at[c]) for c in range(pairs + 1)] + [(tail_acc, tail_line)],
        range(depth - 1),
    )
    chunks = pairs + 2
    size = tail_sum.shape[0]
    half = size // 2
    other = pl.ds(pl.multiple_of((1 - core) * half, 8), half)
    ours = pl.ds(pl.multiple_of(core * half, 8), half)
    sums = [(dense_sum.at[c], dense_sib.at[c]) for c in range(pairs + 1)] + [(tail_sum, tail_sib)]
    lasts = [mail.copy(a.at[other], b, sibling) for a, b in sums]
    dn_copies = [mail.copy(dn_send.at[b], dn_recv.at[b], sibling) for b in range(2)]

    branch_copy.start()
    for copy in loads:
        copy.start()
    fars[0].start()
    fars[1].start()
    go_near(0)
    go_near(1)

    for item in range(3):
        loads[item].wait()
        line.send(1, item)
    for item in range(3):
        line.send_edge(2, item)
    loads[4].wait()
    normed_turned[...] = normed_ref[...].T
    for k in (3, 5, 6, 7):
        loads[k].wait()
    branch_copy.wait_recv()

    @pl.loop(0, length // rows)
    def _(block):
        here = pl.ds(pl.multiple_of(block * rows, rows), rows)
        valid = (segc_ref[here, 0:1] != SEGS - 1.0).astype(F32)
        datt_ref[here, :] = (
            dot(branch_ref[here, :], wout_ref[...], ((1,), (1,))) * valid
        ).astype(BF16)

    att_turned = att_ref[...].T
    for side in range(2):
        part = dot(att_turned, branch_ref[:, side * span : (side + 1) * span]).astype(BF16)
        turned_ref[side] = part.reshape(turned_ref.shape[1:])
    half_copy.start()
    dense_ref[0, core] = turned_ref[core]
    for k in (8, 9):
        loads[k].wait()
    small_wide[...] = jnp.zeros_like(small_wide)

    quarter = width // 4

    @pl.loop(0, pairs)
    def _(pair):
        back_pair(
            pair, rows, reach, span, qkv_ref, datt_ref, segc_ref, segr_ref, lse_ref, dqkv_ref,
            dk_sum, dv_sum,
        )
        columns = [
            pl.ds(pl.multiple_of(part * span + pair * LANES, LANES), LANES) for part in range(3)
        ]

        @pl.loop(0, 4)
        def _(fourth):
            here = pl.ds(pl.multiple_of(fourth * quarter, quarter), quarter)
            d_pair = jnp.concatenate([dqkv_ref[:, at] for at in columns], axis=1)
            weights = jnp.concatenate([wqkv_ref[here, at] for at in columns], axis=1)
            grads = dot(normed_turned[here, :], d_pair)
            dense_ref[1 + pair, fourth // 2, fourth % 2] = grads.astype(BF16)
            gain = jnp.sum(grads * weights.astype(F32), axis=1, keepdims=True)
            lane = lax.broadcasted_iota(jnp.int32, (quarter, LANES), 1)
            small_wide[here, :] += jnp.where(lane == SMALL - 1, gain, 0.0)

        for now in range(pairs):

            @pl.when(pair == now)
            def _():
                planes[now + 1].start()
                if now == 0:
                    half_copy.wait_recv()
                    planes[0].start()
                if now == 1:
                    for item in range(3):
                        line.take(1, item)
                        line.send(2, item)
                if now >= 1:
                    planes[now - 1].middle()
                if now >= 2:
                    planes[now - 2].end()
                    dense.send(0, now - 2)
                    for step in range(1, depth - 1):
                        dense.send_edge(step, now - 2)

    small_all = small_rows[...].astype(F32)
    gain_column = column(widen(small_all), SMALL - 2)
    lane = lax.broadcasted_iota(jnp.int32, (width, LANES), 1)
    small_grads = jnp.where(
        lane < SMALL - 1, widen(small_ref[...]), small_wide[...] / gain_column
    )
    tail_ref[...] = small_grads.astype(BF16).reshape(tail_ref.shape)
    planes[chunks - 1].start()

    def partial(start, step):
        b = 1 - x if step == 0 else x
        here = pl.ds(pl.multiple_of(start * mine + b * rows, rows), rows)
        return b, dot(dqkv_ref[here, :], wqkv_ref[...], ((1,), (1,)))

    def launch(c):
        planes[c].end()
        dense.send(0, c)
        for step in range(1, depth - 1):
            dense.send_edge(step, c)

    for step in range(2):
        b, value = partial(1 - core, step)
        dn_send[step] = value.astype(BF16)
        dn_copies[step].start()
    planes[pairs - 1].middle()
    launch(pairs - 2)
    planes[pairs].middle()
    launch(pairs - 1)
    planes[pairs + 1].middle()
    loads[10].wait()
    loads[11].wait()
    gain_row = small_all[SMALL - 2 : SMALL - 1, :]
    for step in range(2):
        b, value = partial(core, step)
        here = pl.ds(pl.multiple_of(b * rows, rows), rows)
        values = x_ref[here, :].astype(F32)
        dn_copies[step].wait_recv()
        d_normed = value + dn_recv[step].astype(F32)
        inverse = lax.rsqrt(jnp.mean(values * values, axis=-1, keepdims=True) + NORM_EPS)
        scaled = d_normed * gain_row
        mean = jnp.mean(scaled * values, axis=-1, keepdims=True)
        result = dres_ref[here, :] + inverse * scaled
        result = result - values * (inverse * inverse * inverse * mean)
        dtok_ref[b] = result.astype(BF16)
        if step == 0:
            fars[2].start()
            launch(pairs)
            launch(pairs + 1)
        else:
            go_near(2)
    for item, (_, _, result) in enumerate(shares):

        def store(value, add=False):
            result[0] = result[0] + value if add else value

        line.finish(item, store)
    for step in range(depth - 2):
        for c in range(chunks):
            dense.take(step, c)
            dense.send(step + 1, c)
    for c, (total, _) in enumerate(sums):

        def store(value, add=False):
            total[...] = total[...] + value if add else value

        dense.finish(c, store)
        lasts[c].start()
    for c, (total, land) in enumerate(sums):
        own = total[ours]
        lasts[c].wait_recv()
        theirs = land[...]
        if c == 0:
            for side, value in ((core, own), (1 - core, theirs)):
                wout_out[:, pl.ds(pl.multiple_of(side * span, LANES), span)] = value
        elif c <= pairs:
            for part in range(3):
                for side, value in ((core, own), (1 - core, theirs)):
                    at = part * 2 * span + side * span + (c - 1) * LANES
                    qkv_out[:, pl.ds(pl.multiple_of(at, LANES), LANES)] = value[
                        :, part * LANES : (part + 1) * LANES
                    ]
        else:
            small_out[...] = own + theirs
    for copy in [branch_copy, half_copy] + lasts + dn_copies:
        copy.wait_send()
    for plane in planes:
        plane.close()
    line.close()
    dense.close()
    for copy in fars:
        copy.wait()

    @pl.when(moved)
    def _():
        for copy in nears:
            copy.wait()

    @pl.when(jnp.logical_not(moved))
    def _():
        for copy in stays:
            copy.wait()


def back_all(
    grad_gate, grad_up, grad_down, d_branch, w_out, attended, qkv, seg_col, normed, qkv_weight,
    x_own, d_residual, block_out, d_prev, lse, seg_row, small, small_all,
):
    depth = lax.axis_size("dp")
    length, width = normed.shape
    mine = length // 2
    span = width // 2
    rows = block_out.shape[1]
    groups = span // LANES + 1
    wide = 3 * LANES
    quarter = width // 4
    size = quarter // depth
    parts = [grad.shape[1:] for grad in (grad_gate, grad_up, grad_down)]
    vmem = pl.BlockSpec(memory_space=pltpu.VMEM)
    anywhere = pl.BlockSpec(memory_space=pl.ANY)
    homes = [block_out.shape, block_out.shape, d_prev.shape]
    kinds = [block_out.dtype, BF16, d_prev.dtype]
    steps = 2 * (depth - 1)
    copies = 6 * (depth - 2) + 2 + 6 + (groups + 1) * (4 + steps + 1) + 2

    def plane_buffers(lead, columns):
        return [
            pltpu.VMEM(lead + dims + (columns,), BF16)
            for dims in (
                [(2, 2, quarter)] + [(2, quarter // 2)] * 4 + [(quarter // 2,)] * 2
                + [(depth, size), (2, depth - 1, size)]
            )
        ]

    return pl.pallas_call(
        functools.partial(back_kernel, depth, rows, length // 2),
        in_specs=[anywhere] * 12 + [vmem] * 6,
        out_specs=[vmem] * 6 + [anywhere] * 3,
        out_shape=[shape((1,) + part, F32) for part in parts]
        + [shape((size // 2, 6 * span), F32), shape((size // 2, width), F32)]
        + [shape((size // 2, LANES), F32)]
        + [shape(dims, kind) for dims, kind in zip(homes, kinds)],
        scratch_shapes=[pltpu.VMEM((2, depth - 2) + part, BF16) for part in parts]
        + [pltpu.VMEM((depth,) + part, BF16) for part in parts]
        + [
            pltpu.VMEM((length, width), BF16), pltpu.VMEM((span, width), BF16),
            pltpu.VMEM((length, span), BF16), pltpu.VMEM((length, 3 * span), BF16),
            pltpu.VMEM((length, LANES), F32), pltpu.VMEM((length, width), BF16),
            pltpu.VMEM((width, 3 * span), BF16), pltpu.VMEM((mine, width), BF16),
            pltpu.VMEM((mine, width), F32), pltpu.VMEM((width, length), BF16),
            pltpu.VMEM((length, span), BF16), pltpu.VMEM((2, 2, quarter, span), BF16),
            pltpu.VMEM((length, 3 * span), BF16), pltpu.VMEM((length, LANES), F32),
            pltpu.VMEM((length, LANES), F32), pltpu.VMEM((2, rows, width), BF16),
            pltpu.VMEM((2, rows, width), BF16), pltpu.VMEM((2, rows, width), BF16),
        ]
        + plane_buffers((groups,), wide)
        + plane_buffers((), LANES)
        + [
            pltpu.VMEM((groups, size, wide), F32), pltpu.VMEM((groups, size // 2, wide), F32),
            pltpu.VMEM((size, LANES), F32), pltpu.VMEM((size // 2, LANES), F32),
            pltpu.VMEM((width, LANES), F32),
            pltpu.SemaphoreType.DMA((copies,)),
            pltpu.SemaphoreType.DMA((copies,)),
            pltpu.SemaphoreType.DMA((15,)),
        ],
        compiler_params=pltpu.CompilerParams(
            collective_id=1, has_side_effects=True, vmem_limit_bytes=62 * 1024 * 1024
        ),
        name="back_all",
    )(
        grad_gate, grad_up, grad_down, d_branch, w_out, attended, qkv, seg_col, normed, qkv_weight, x_own, d_residual,
        block_out, d_prev, lse, seg_row, small, small_all,
    )


def deliver_kernel(
    routes,
    out_ref, dtok_ref, prev_ref, qkv_ref, wout_ref, small_ref, gate_ref, up_ref, down_ref,
    out_end, tokens_end, prev_end, gain_a_end, qkv_end, wout_end, gain_m_end, router_end,
    cproj_end, cvec_end, gate_end, up_end, down_end,
):
    for source, target in (
        (out_ref, out_end), (qkv_ref, qkv_end), (wout_ref, wout_end), (gate_ref, gate_end),
        (up_ref, up_end), (down_ref, down_end),
    ):
        target[...] = source[...]
    tokens_end[...] = dtok_ref[...].astype(F32)
    for m in range(2):
        for route in range(routes):
            prev_end[route, m : m + 1, :] = prev_ref[m, route : route + 1, :]
    count = small_ref.shape[0]
    turned = widen(small_ref[...])
    router_end[...] = turned[0:routes, 0:count]
    cproj_end[...] = turned[8:12, 0:count]
    cvec_end[...] = turned[12:14, 0:count]
    gain_m_end[...] = turned[14:15, 0:count].reshape(count)
    gain_a_end[...] = turned[15:16, 0:count].reshape(count)


def deliver(routes, out, dtok, prev, qkv, wout, small, gate, up, down):
    count = small.shape[0]
    vmem = pl.BlockSpec(memory_space=pltpu.VMEM)
    return pl.pallas_call(
        functools.partial(deliver_kernel, routes),
        in_specs=[vmem] * 9,
        out_specs=[vmem] * 13,
        out_shape=[
            shape(out.shape, BF16), shape(dtok.shape, F32), shape((routes, 2, prev.shape[2]), F32),
            shape((count,), F32), shape(qkv.shape, F32), shape(wout.shape, F32),
            shape((count,), F32), shape((routes, count), F32), shape((4, count), F32),
            shape((2, count), F32), shape(gate.shape, F32), shape(up.shape, F32),
            shape(down.shape, F32),
        ],
        compiler_params=params(),
        cost_estimate=cost(1e6, 8e6),
        name="deliver",
    )(out, dtok, prev, qkv, wout, small, gate, up, down)


def one_chip(
    tokens,
    prev_logits,
    segments,
    routes,
    cotangent,
    gain_attn,
    w_qkv,
    w_out,
    gain_moe,
    w_router,
    const_proj,
    const_vec,
    w_gate,
    w_up,
    w_down,
):
    rows = tokens.shape[1]
    route_count = w_router.shape[1]
    experts = route_count - 4
    (
        x_own, ctl, normed, qkv, attended, lse, small_all, qkv_weight, out_sib,
        seg_col, seg_row, g_rows,
    ) = gather_all(
        experts, tokens, cotangent, w_qkv, w_out, prev_logits, routes, segments, w_router, const_proj,
        const_vec, gain_attn, gain_moe,
    )
    (
        block_out, d_prev, d_residual, d_branch, small, grad_gate, grad_up, grad_down,
    ) = expert_layer(
        experts, route_count, rows, attended, x_own, cotangent, ctl, w_out, out_sib, small_all,
        w_gate[0], w_up[0], w_down[0], g_rows,
    )

    (
        share_gate, share_up, share_down, share_qkv, share_out, share_small, out_home, dtok_home,
        prev_home,
    ) = back_all(
        grad_gate, grad_up, grad_down, d_branch, w_out, attended, qkv, seg_col, normed,
        qkv_weight, x_own, d_residual, block_out, d_prev, lse, seg_row, small, small_all,
    )
    (
        block_out, grad_tokens, grad_prev, gain_a, grad_qkv, grad_out, gain_m, grad_router,
        grad_cproj, grad_cvec, grad_gate, grad_up, grad_down,
    ) = deliver(
        route_count, out_home, dtok_home, prev_home, share_qkv, share_out, share_small,
        share_gate, share_up, share_down,
    )
    return (
        block_out, grad_tokens, jnp.transpose(grad_prev, (1, 2, 0)), gain_a, grad_qkv, grad_out,
        gain_m, grad_router.T, grad_cproj.T, grad_cvec.T, grad_gate, grad_up, grad_down,
    )


def suits(mesh, tokens, w_router, w_gate):
    peers = mesh.shape["ep"]
    rows = tokens.shape[1] // peers
    micro = tokens.shape[0] // (mesh.shape["dp"] * mesh.shape["fs"])
    routes = w_router.shape[1]
    return (
        peers == 4
        and mesh.shape["fs"] == 2
        and micro == 2
        and mesh.shape["dp"] == 4
        and (routes - 4) * 2 == peers
        and 3 * rows // routes == LANES
        and tokens.shape[2] % (2 * LANES) == 0
    )


def solution(mesh):
    placed = (
        P(("dp", "fs"), "ep", None),
        P(("dp", "fs"), "ep", None),
        P(("dp", "fs"), None),
        P(("dp", "fs"), "ep", None),
        P(("dp", "fs"), "ep", None),
        P("fs"),
        P("fs", None),
        P("fs", None),
        P("fs"),
        P("fs", None),
        P("fs", None),
        P("fs", None),
        P("ep", "fs", None),
        P("ep", "fs", None),
        P("ep", "fs", None),
    )
    def layer(*arrays):
        fits = suits(mesh, arrays[0], arrays[9], arrays[12])
        return mapped(one_chip if fits else shards)(*arrays)

    def mapped(body):
        return jax.shard_map(
            body,
            mesh=mesh,
            in_specs=placed,
            out_specs=(
                P(("dp", "fs"), "ep", None),
                P(("dp", "fs"), "ep", None),
                P(("dp", "fs"), "ep", None),
                P(("ep", "dp", "fs")),
                P(("ep", "dp", "fs"), None),
                P(("ep", "dp", "fs"), None),
                P(("ep", "dp", "fs")),
                P(("ep", "dp", "fs"), None),
                P(("ep", "dp", "fs"), None),
                P(("ep", "dp", "fs"), None),
                P("ep", ("dp", "fs"), None),
                P("ep", ("dp", "fs"), None),
                P("ep", ("dp", "fs"), None),
            ),
            check_vma=False,
        )

    return layer
```
